32 devices in a mesh: dp: 16 (over z, x, core), tensor: 2 (over y).
Axes of the slice: x: 2, y: 2, z: 4, core: 2. Of those that a mesh axis runs over, the one named last changes fastest.
Arguments:
- tokens: bfloat16 [6144, 2048], P(('dp', 'tensor')), may hold values from -6 to 6
- attn_gain: bfloat16 [2048], P('dp'), may hold values from 0.5 to 1.5
- q_weight: bfloat16 [2048, 4096], P('dp', 'tensor'), may hold values from -0.125 to 0.125
- key_matrix: bfloat16 [2048, 512], P('dp', 'tensor'), may hold values from -0.125 to 0.125
- value_matrix: bfloat16 [2048, 512], P('dp', 'tensor'), may hold values from -0.125 to 0.125
- o_weight: bfloat16 [4096, 2048], P('tensor', 'dp'), may hold values from -0.75 to 0.75
- query_norm_gain: bfloat16 [128], P('dp'), may hold values from 0.5 to 1.5
- k_gain: bfloat16 [128], P('dp'), may hold values from 0.5 to 1.5
- ffn_gain: bfloat16 [2048], P('dp'), may hold values from 0.5 to 1.5
- router_weight: bfloat16 [2048, 32], P('dp'), may hold values from -0.024902344 to 0.024902344
- gate_weight: bfloat16 [32, 2048, 768], P('dp', None, 'tensor'), may hold values from -0.125 to 0.125
- up_weight: bfloat16 [32, 2048, 768], P('dp', None, 'tensor'), may hold values from -0.125 to 0.125
- down_weight: bfloat16 [32, 768, 2048], P('dp', 'tensor'), may hold values from -0.625 to 0.625
- expert_ids: int32 [6144, 8], P('dp'), may hold values from 0 to 31, all different within a row; in each aligned block of 384 rows (0 to 383, 384 to 767, ...) at most 120 rows name the same one
- cotangent: bfloat16 [6144, 2048], P(('dp', 'tensor')), may hold values from -6 to 6
Outputs:
- output: bfloat16 [6144, 2048], P(('dp', 'tensor'))
- tokens_grad: float32 [6144, 2048], P(('dp', 'tensor'))
- attn_gain_grad: float32 [2048], P('dp')
- q_weight_grad: float32 [2048, 4096], P('dp', 'tensor')
- k_weight_grad: float32 [2048, 512], P('dp', 'tensor')
- v_weight_grad: float32 [2048, 512], P('dp', 'tensor')
- o_weight_grad: float32 [4096, 2048], P('tensor', 'dp')
- q_gain_grad: float32 [128], P('dp')
- k_gain_grad: float32 [128], P('dp')
- ffn_gain_grad: float32 [2048], P('dp')
- router_weight_grad: float32 [2048, 32], P('dp')
- gate_weight_grad: float32 [32, 2048, 768], P('dp', None, 'tensor')
- up_weight_grad: float32 [32, 2048, 768], P('dp', None, 'tensor')
- down_weight_grad: float32 [32, 768, 2048], P('dp', 'tensor')
The draws below stay inside these ranges and needn't reach their ends.
Inputs may be any that keep to these rules, and one draw needn't show every extreme that they name: `expert_ids`: each row names 8 different experts. Among the 384 tokens of one sequence (the rows of one device) no expert is named more than 120 times, a bound that some block reaches.
All inputs are finite; a program needn't handle non-finite values.
Results may differ from the reference program's by a relative error of at most 0.019.
Values may be sent and summed in bfloat16 or wider, within the bound.
No kernel may reach another device: no remote copies, remote signals or barrier semaphores. Data moves between devices by JAX's collectives and lax.ppermute only.
A program may use at most 320 MiB of HBM per device.

```python
import math
from functools import partial
import jax
import jax.numpy as jnp
import numpy as np
from jax import lax

MODEL_WIDTH = 2048
QUERY_HEAD_COUNT = 32
KEY_VALUE_HEADS = 4
HEAD_ENTRIES = 128
FF = 768
TOP = 8
EXPERTS = 32
SEQ = 384
TOKENS = 6144
CAP = 120
N_DP = 16
N_TENSOR = 2


def shard_levels(key, shape, cuts, low, top_value):
    level = 1.0
    for axis_at, blocks in cuts:
        heights = jax.random.uniform(jax.random.fold_in(jax.random.fold_in(key, 6), axis_at), (blocks,), jnp.float32, low / len(cuts), top_value / len(cuts))
        level = level * jnp.repeat(jnp.exp(heights), shape[axis_at] // blocks).reshape((-1,) + (1,) * (len(shape) - 1 - axis_at))
    return level


def deal_out(key, own, number, rows, number_of, top, bound, lean):
    order = jax.random.permutation(key, number_of)
    packed, ordinary = load_shares(number_of, rows * top, bound, lean, True), load_shares(number_of, rows * top, bound, lean, False)
    places = jnp.arange(number_of)

    def named(lengths, turn):
        used = int((lengths > 0).sum())
        fixed = max(1, used // 4)
        shifted = fixed + (places - fixed + turn * (used - fixed)) % max(1, number_of - fixed)
        return jnp.zeros((number_of,), jnp.int32).at[order[jnp.where(places < fixed, places, shifted)]].set(jnp.asarray(lengths, jnp.int32))

    lengths = jnp.where(number % 4 == 0, named(packed, number // 4), named(ordinary, number - number // 4 - 1))
    mixed = jax.random.permutation(jax.random.fold_in(own, 3), number_of)
    donor, taker = mixed[0:number_of // 2 * 2:2], mixed[1:number_of // 2 * 2:2]
    margin = jnp.minimum(lengths[donor] - 1, bound - lengths[taker]) // 2
    margin = jnp.where((donor == order[0]) | (taker == order[0]) | (lengths[taker] == 0), 0, jnp.maximum(margin, 0))
    shifted = jax.random.randint(jax.random.fold_in(own, 4), (number_of // 2,), 0, 1 << 20) % (margin + 1)
    lengths = lengths.at[donor].add(-shifted).at[taker].add(shifted)
    members = jnp.searchsorted(jnp.cumsum(lengths), jnp.arange(rows * top), side="right").astype(jnp.int32)
    grid = members.reshape(top, rows).T
    grid = grid[jax.random.permutation(jax.random.fold_in(own, 1), rows)]
    turn = jax.random.randint(jax.random.fold_in(own, 2), (rows, 1), 0, top)
    return jnp.take_along_axis(grid, (jnp.arange(top)[None, :] + turn) % top, axis=1)


def load_shares(number_of, total, bound, slope, full):
    portions = [(1 << 20) // math.isqrt(grade ** slope) + 1 for grade in range(1, number_of + 1)]
    largest = bound if full else min(bound, max(-(-total // number_of), total * portions[0] // sum(portions)))
    least = 1 if total - largest >= number_of - 1 else 0
    counts, rest = [largest] + [least] * (number_of - 1), total - largest - least * (number_of - 1)
    while rest > 0:
        free = [i for i in range(1, number_of) if counts[i] < largest] or [i for i in range(1, number_of) if counts[i] < bound]
        mass, remaining = sum([portions[i] for i in free]), rest
        for i in free:
            addition = min(bound - counts[i], max(1, remaining * portions[i] // mass), rest)
            counts[i] = counts[i] + addition
            rest = rest - addition
    return np.array(counts)


def gaussian(key, shape, deviation, bound, cuts=(), kind=jnp.bfloat16):
    array = deviation * jax.random.normal(key, shape, jnp.float32)
    if cuts:
        array = array * shard_levels(key, shape, cuts, -0.22, 0.18)
    return jnp.clip(array, -bound, bound).astype(kind)


def setup_inputs(seed: int = 0) -> dict:
    keys = jax.random.split(jax.random.key(seed), 16)
    tokens = gaussian(keys[0], (TOKENS, MODEL_WIDTH), 1.0, 6.0, ((0, 32),))
    attn_gain = jnp.clip(1.0 + 0.1 * jax.random.normal(keys[1], (MODEL_WIDTH,), jnp.float32), 0.5, 1.5).astype(jnp.bfloat16)
    q_weight = gaussian(keys[2], (MODEL_WIDTH, QUERY_HEAD_COUNT * HEAD_ENTRIES), MODEL_WIDTH ** -0.5, 0.125, ((0, 16), (1, 2)))
    key_matrix = gaussian(keys[3], (MODEL_WIDTH, KEY_VALUE_HEADS * HEAD_ENTRIES), MODEL_WIDTH ** -0.5, 0.125, ((0, 16), (1, 2)))
    value_matrix = gaussian(keys[4], (MODEL_WIDTH, KEY_VALUE_HEADS * HEAD_ENTRIES), MODEL_WIDTH ** -0.5, 0.125, ((0, 16), (1, 2)))
    o_weight = gaussian(keys[5], (QUERY_HEAD_COUNT * HEAD_ENTRIES, MODEL_WIDTH), (QUERY_HEAD_COUNT * HEAD_ENTRIES // 64) ** -0.5, 0.75, ((0, 2), (1, 16)))
    query_norm_gain = jnp.clip(1.0 + 0.1 * jax.random.normal(keys[6], (HEAD_ENTRIES,), jnp.float32), 0.5, 1.5).astype(jnp.bfloat16)
    k_gain = jnp.clip(1.0 + 0.1 * jax.random.normal(keys[7], (HEAD_ENTRIES,), jnp.float32), 0.5, 1.5).astype(jnp.bfloat16)
    ffn_gain = jnp.clip(1.0 + 0.1 * jax.random.normal(keys[8], (MODEL_WIDTH,), jnp.float32), 0.5, 1.5).astype(jnp.bfloat16)
    router_weight = jnp.clip(jax.random.uniform(keys[9], (MODEL_WIDTH, EXPERTS), jnp.float32, -0.024902344, 0.024902344) * shard_levels(keys[9], (MODEL_WIDTH, EXPERTS), ((0, 16),), -0.4, 0.0), -0.024902344, 0.024902344).astype(jnp.bfloat16)
    gate_weight = gaussian(keys[10], (EXPERTS, MODEL_WIDTH, FF), MODEL_WIDTH ** -0.5, 0.125, ((0, 16), (2, 2)))
    up_weight = gaussian(keys[11], (EXPERTS, MODEL_WIDTH, FF), MODEL_WIDTH ** -0.5, 0.125, ((0, 16), (2, 2)))
    down_weight = gaussian(keys[12], (EXPERTS, FF, MODEL_WIDTH), (FF // 8) ** -0.5, 0.625, ((0, 16), (1, 2)))
    expert_ids_keys = jax.random.split(jax.random.fold_in(keys[13], 1), TOKENS // SEQ)
    expert_ids_turns = jax.random.permutation(jax.random.fold_in(keys[13], 3), TOKENS // SEQ)
    expert_ids = jax.vmap(lambda own, number: deal_out(jax.random.fold_in(keys[13], 2), own, number, SEQ, EXPERTS, TOP, CAP, 2))(expert_ids_keys, expert_ids_turns).reshape((TOKENS, TOP))
    cotangent = gaussian(keys[14], (TOKENS, MODEL_WIDTH), 1.0, 6.0, ((0, 32),))
    return dict(tokens=tokens, attn_gain=attn_gain, q_weight=q_weight, key_matrix=key_matrix, value_matrix=value_matrix, o_weight=o_weight, query_norm_gain=query_norm_gain, k_gain=k_gain, ffn_gain=ffn_gain, router_weight=router_weight, gate_weight=gate_weight, up_weight=up_weight, down_weight=down_weight, expert_ids=expert_ids, cotangent=cotangent)


EPSILON = 1e-06
ROPE_THETA = 1000000.0
EXACT_PRECISION = lax.Precision.HIGHEST

@jax.custom_vjp
def lower_precision(v):
    return lax.optimization_barrier(v.astype(jnp.bfloat16)).astype(jnp.float32)

@jax.custom_vjp
def lower_precision_back(v):
    return v

def low_keep(v):
    return (lower_precision(v), None)

def low_pass(kept, grad):
    return (grad,)

def back_keep(v):
    return (v, None)

def back_low(kept, grad):
    return (lower_precision(grad),)
lower_precision.defvjp(low_keep, low_pass)
lower_precision_back.defvjp(back_keep, back_low)

def root_mean_norm(value_rows, gain):
    return value_rows * lax.rsqrt(lax.optimization_barrier(jnp.mean(value_rows * value_rows, axis=-1, keepdims=True)) + EPSILON) * gain

def apply_rotary(value_rows, cosine_lookup, sine_lookup):
    half_size = value_rows.shape[-1] // 2
    first_half = value_rows[..., :half_size]
    second_half = value_rows[..., half_size:]
    return jnp.concatenate([first_half * cosine_lookup - second_half * sine_lookup, second_half * cosine_lookup + first_half * sine_lookup], axis=-1)

def rope_tables(length_tokens):
    half_size = HEAD_ENTRIES // 2
    inverse = ROPE_THETA ** (-(jnp.arange(half_size, dtype=jnp.float32) * 2.0 / HEAD_ENTRIES))
    angles = jnp.arange(length_tokens, dtype=jnp.float32)[:, None] * inverse[None, :]
    return (jnp.cos(angles)[:, None, :], jnp.sin(angles)[:, None, :])

def attend(weights, rows):
    attn_gain, q_weight, key_matrix, value_matrix, o_weight, query_norm_gain, k_gain = weights
    length_tokens = rows.shape[0]
    group_width = QUERY_HEAD_COUNT // KEY_VALUE_HEADS
    normalized_input = lower_precision(root_mean_norm(rows, attn_gain))
    query_unrotated = lower_precision_back(jnp.dot(normalized_input, q_weight, precision=EXACT_PRECISION)).reshape(length_tokens, QUERY_HEAD_COUNT, HEAD_ENTRIES)
    key_unrotated = lower_precision_back(jnp.dot(normalized_input, key_matrix, precision=EXACT_PRECISION)).reshape(length_tokens, KEY_VALUE_HEADS, HEAD_ENTRIES)
    value_rows = lower_precision(lower_precision_back(jnp.dot(normalized_input, value_matrix, precision=EXACT_PRECISION))).reshape(length_tokens, KEY_VALUE_HEADS, HEAD_ENTRIES)
    cosine_lookup, sine_lookup = rope_tables(length_tokens)
    query_rows = lower_precision(apply_rotary(root_mean_norm(query_unrotated, query_norm_gain), cosine_lookup, sine_lookup)).reshape(length_tokens, KEY_VALUE_HEADS, group_width, HEAD_ENTRIES)
    keys_rot = lower_precision(apply_rotary(root_mean_norm(key_unrotated, k_gain), cosine_lookup, sine_lookup))
    scores = lower_precision_back(jnp.einsum('qhgd,khd->hgqk', query_rows, keys_rot, precision=EXACT_PRECISION) * HEAD_ENTRIES ** (-0.5))
    causal = jnp.arange(length_tokens)[:, None] >= jnp.arange(length_tokens)[None, :]
    exponent = jnp.where(causal, jnp.exp(scores), 0.0)
    probs_low = lower_precision(exponent / lax.optimization_barrier(jnp.sum(exponent, axis=-1, keepdims=True)))
    context = jnp.einsum('hgqk,khd->qhgd', probs_low, value_rows, precision=EXACT_PRECISION).reshape(length_tokens, QUERY_HEAD_COUNT * HEAD_ENTRIES)
    context = lower_precision(lower_precision_back(context))
    return lower_precision_back(jnp.dot(context, o_weight, precision=EXACT_PRECISION))

def expert_block(padded, expert_items):
    row_index, gate_w, up_w, down_w = expert_items
    inputs = padded[row_index]
    block_width = FF // N_TENSOR
    summed = jnp.zeros((row_index.shape[0], MODEL_WIDTH), jnp.float32)
    for block_idx in range(N_TENSOR):
        lower_col = block_idx * block_width
        inputs_half = lower_precision_back(inputs)
        gate_proj = lower_precision_back(jnp.dot(inputs_half, gate_w[:, lower_col:lower_col + block_width], precision=EXACT_PRECISION))
        up_proj = lower_precision_back(jnp.dot(inputs_half, up_w[:, lower_col:lower_col + block_width], precision=EXACT_PRECISION))
        activated = lower_precision(jax.nn.silu(gate_proj) * up_proj)
        summed = summed + lower_precision(lower_precision_back(jnp.dot(activated, down_w[lower_col:lower_col + block_width, :], precision=EXACT_PRECISION)))
    return summed

def slot_tables(expert_ids):
    pair_count = SEQ * TOP
    grouped = expert_ids.reshape(N_DP, pair_count)
    onehot = (grouped[:, :, None] == jnp.arange(EXPERTS, dtype=jnp.int32)[None, None, :]).astype(jnp.int32)
    earlier = jnp.cumsum(onehot, axis=1) - onehot
    slots = lax.optimization_barrier(jnp.sum(earlier * onehot, axis=2)).astype(jnp.int32)
    group_index = jnp.arange(N_DP, dtype=jnp.int32)[:, None]
    row_in_expert = (group_index * CAP + slots).astype(jnp.int32)
    token_index = (group_index * SEQ + jnp.arange(pair_count, dtype=jnp.int32)[None, :] // TOP).astype(jnp.int32)
    table = jnp.full((EXPERTS, N_DP * CAP), TOKENS, jnp.int32).at[grouped, row_in_expert].set(token_index)
    slot_index = (grouped * (N_DP * CAP) + row_in_expert).reshape(TOKENS, TOP).astype(jnp.int32)
    return (table, slot_index)

def forward(expert_ids, table, slot_index, tokens, attn_gain, q_weight, key_matrix, value_matrix, o_weight, query_norm_gain, k_gain, ffn_gain, router_weight, gate_weight, up_weight, down_weight):
    weights = (attn_gain, q_weight, key_matrix, value_matrix, o_weight, query_norm_gain, k_gain)
    sequences = tokens.reshape(TOKENS // SEQ, SEQ, MODEL_WIDTH)
    attended = lax.map(partial(jax.checkpoint(attend), weights), sequences).reshape(TOKENS, MODEL_WIDTH)
    hidden = tokens + attended
    normalized_input = lower_precision(root_mean_norm(hidden, ffn_gain))
    logits = jnp.dot(normalized_input, router_weight, precision=EXACT_PRECISION)
    chosen = jnp.exp(jnp.take_along_axis(logits, expert_ids, axis=1))
    gates = chosen / lax.optimization_barrier(jnp.sum(chosen, axis=1, keepdims=True))
    padded = jnp.concatenate([normalized_input, jnp.zeros((1, MODEL_WIDTH), normalized_input.dtype)], axis=0)
    expert_out = lax.map(partial(jax.checkpoint(expert_block), padded), (table, gate_weight, up_weight, down_weight))
    flat_out = expert_out.reshape(EXPERTS * N_DP * CAP, MODEL_WIDTH)
    mixed = jnp.zeros((TOKENS, MODEL_WIDTH), hidden.dtype)
    for column in range(TOP):
        mixed = mixed + gates[:, column:column + 1] * flat_out[slot_index[:, column]]
    return hidden + mixed

def reference(tokens, attn_gain, q_weight, key_matrix, value_matrix, o_weight, query_norm_gain, k_gain, ffn_gain, router_weight, gate_weight, up_weight, down_weight, expert_ids, cotangent):
    table, slot_index = slot_tables(expert_ids)
    floats = [argument.astype(jnp.float32) for argument in (tokens, attn_gain, q_weight, key_matrix, value_matrix, o_weight, query_norm_gain, k_gain, ffn_gain, router_weight, gate_weight, up_weight, down_weight)]
    result, pullback = jax.vjp(partial(forward, expert_ids, table, slot_index), *floats)
    grads = pullback(cotangent.astype(jnp.float32))
    return (result.astype(jnp.bfloat16), grads[0], grads[1], grads[2], grads[3], grads[4], grads[5], grads[6], grads[7], grads[8], grads[9], grads[10], grads[11], grads[12])
```

```python
import jax
import jax.numpy as jnp
from jax import lax
from jax.sharding import PartitionSpec as P

HEAD = 128
EPS = 1e-06
THETA = 1000000.0
BF = jnp.bfloat16
F32 = jnp.float32


def dot(a, b, ca, cb):
    return lax.dot_general(a, b, (((ca,), (cb,)), ((), ())), preferred_element_type=F32)


def rms(v, gain):
    return v * lax.rsqrt(jnp.mean(v * v, axis=-1, keepdims=True) + EPS) * gain


def rms_back(v, gain, u):
    inv = lax.rsqrt(jnp.mean(v * v, axis=-1, keepdims=True) + EPS)
    ug = u * gain
    grad = ug * inv - v * (jnp.mean(ug * v, axis=-1, keepdims=True) * inv * inv * inv)
    return grad, u * v * inv


def rope(v, cos, sin):
    a, b = v[..., : HEAD // 2], v[..., HEAD // 2 :]
    return jnp.concatenate([a * cos - b * sin, b * cos + a * sin], axis=-1)


def rope_back(v, cos, sin):
    a, b = v[..., : HEAD // 2], v[..., HEAD // 2 :]
    return jnp.concatenate([a * cos + b * sin, b * cos - a * sin], axis=-1)


def rope_tables(count):
    inverse = THETA ** (-(jnp.arange(HEAD // 2, dtype=F32) * 2.0 / HEAD))
    angles = jnp.arange(count, dtype=F32)[:, None] * inverse[None, :]
    return jnp.cos(angles)[:, None, :], jnp.sin(angles)[:, None, :]


def split2(v):
    high = v.astype(BF)
    return high, (v - high.astype(F32)).astype(BF)


def gather_dp(v):
    return lax.all_gather(v, "dp", axis=0, tiled=True)


def gather_all(v):
    return lax.all_gather(v, ("dp", "tensor"), axis=0, tiled=True)


def scatter_all(v):
    return lax.psum_scatter(v, ("dp", "tensor"), scatter_dimension=0, tiled=True)


def scatter_dp(v):
    return lax.psum_scatter(v, "dp", scatter_dimension=0, tiled=True)


def pieces(width, dp, seq):
    count = 1 if dp * seq <= 8192 else 4
    step = width // count // 128 * 128
    edges = [step * i for i in range(count)] + [width]
    return list(zip(edges[:-1], edges[1:]))


def after(v, earlier):
    return v if earlier is None else lax.optimization_barrier((v, earlier))[0]


def dispatch(pick, own, dp, seq, earlier):
    blocks = []
    for low, high in pieces(own.shape[1], dp, seq):
        every = gather_all(after(own[:, low:high], earlier)).reshape(dp, seq, high - low)
        block = jnp.einsum("gest,gtd->gesd", pick, every, preferred_element_type=F32).astype(BF)
        blocks.append(block)
        earlier = block if len(pieces(own.shape[1], dp, seq)) > 1 else None
    return jnp.concatenate(blocks, axis=3)


def combine(pick, rows, dp, seq, earlier):
    blocks = []
    for low, high in pieces(rows.shape[3], dp, seq):
        tok = jnp.einsum(
            "gest,gesd->gtd",
            pick,
            after(rows[:, :, :, low:high], earlier),
            preferred_element_type=F32,
        ).astype(BF)
        blocks.append(scatter_all(tok.reshape(dp * seq, high - low)))
        earlier = blocks[-1] if len(pieces(rows.shape[3], dp, seq)) > 1 else None
    return jnp.concatenate(blocks, axis=1).astype(F32)


def pad_to(v, width):
    return jnp.pad(v, ((0, 0), (0, width - v.shape[1])))


def lanes(count):
    return -(-count // 128) * 128


def on_device(
    tokens,
    attn_gain,
    q_weight,
    key_matrix,
    value_matrix,
    o_weight,
    query_norm_gain,
    k_gain,
    ffn_gain,
    router_weight,
    gate_weight,
    up_weight,
    down_weight,
    expert_ids,
    cotangent,
):
    dp = lax.axis_size("dp")
    tensor = lax.axis_size("tensor")
    dp_at = lax.axis_index("dp")
    own, width = tokens.shape
    seq = expert_ids.shape[0]
    begin = lax.axis_index("tensor") * own
    local = gate_weight.shape[0]
    experts = local * dp
    slots = 10 * seq * expert_ids.shape[1] // (8 * experts)
    slots = -(-slots // 16) * 16
    shard = q_weight.shape[0]
    gshard = query_norm_gain.shape[0]
    hq = q_weight.shape[1] // HEAD
    hk = key_matrix.shape[1] // HEAD
    group = hq // hk
    qkv_width = (hq + 2 * hk) * HEAD

    arange_e = jnp.arange(experts, dtype=jnp.int32)
    own_ids = lax.dynamic_slice_in_dim(expert_ids, begin, own, 0)
    own_mask = jnp.any(own_ids[:, :, None] == arange_e[None, None, :], axis=1)

    gain_rows = jnp.stack(
        [
            attn_gain,
            ffn_gain,
            jnp.pad(query_norm_gain, (0, shard - gshard)),
            jnp.pad(k_gain, (0, shard - gshard)),
        ],
        axis=1,
    )
    small = pad_to(jnp.concatenate([router_weight, gain_rows], axis=1), lanes(experts + 4))
    all_in = gather_dp(jnp.concatenate([q_weight, key_matrix, value_matrix, small], axis=1))
    layer_in = lax.all_gather(tokens, "tensor", axis=0, tiled=True)
    o_t = gather_dp(o_weight.T)
    mask_all = gather_all(pad_to(own_mask.astype(BF), lanes(experts))).reshape(dp, seq, -1)

    w_qkv = all_in[:, :qkv_width]
    router = all_in[:, qkv_width : qkv_width + experts]
    gains = all_in[:, qkv_width + experts : qkv_width + experts + 4].astype(F32)
    attn_gain32 = gains[:, 0]
    ffn_gain32 = gains[:, 1]
    q_gain32 = gains[:, 2].reshape(dp, shard)[:, :gshard].reshape(-1)
    k_gain32 = gains[:, 3].reshape(dp, shard)[:, :gshard].reshape(-1)

    residual = layer_in.astype(F32)
    normed = rms(residual, attn_gain32).astype(BF)
    qkv = dot(normed, w_qkv, 1, 0)
    cos, sin = rope_tables(seq)
    q_raw = qkv[:, : hq * HEAD].reshape(seq, hq, HEAD)
    k_raw = qkv[:, hq * HEAD : (hq + hk) * HEAD].reshape(seq, hk, HEAD)
    v_low = qkv[:, (hq + hk) * HEAD :].astype(BF).reshape(seq, hk, HEAD)
    q_low = rope(rms(q_raw, q_gain32), cos, sin).astype(BF).reshape(seq, hk, group, HEAD)
    k_low = rope(rms(k_raw, k_gain32), cos, sin).astype(BF)
    causal = jnp.arange(seq)[:, None] >= jnp.arange(seq)[None, :]
    scale = HEAD ** (-0.5)
    scores = jnp.einsum("qhgd,khd->hgqk", q_low, k_low, preferred_element_type=F32) * scale
    expo = jnp.where(causal, jnp.exp(scores), 0.0)
    total = jnp.sum(expo, axis=-1, keepdims=True)
    probs = expo / total
    context = jnp.einsum("hgqk,khd->qhgd", probs.astype(BF), v_low, preferred_element_type=F32)
    context = context.reshape(seq, hq * HEAD).astype(BF)
    attn_part = dot(context, o_t, 1, 1).astype(BF)
    attn_own = lax.psum_scatter(attn_part, "tensor", scatter_dimension=0, tiled=True)
    hidden = tokens.astype(F32) + attn_own.astype(F32)

    ffn_in = rms(hidden, ffn_gain32).astype(BF)
    logits = dot(ffn_in, router, 1, 0)
    chosen = jnp.where(own_mask, jnp.exp(logits), 0.0)
    gates = chosen / jnp.sum(chosen, axis=1, keepdims=True)
    gate_high, gate_low = split2(gates)
    gate_x = pad_to(jnp.concatenate([gate_high, gate_low], axis=1), lanes(2 * experts))
    gate_all = gather_all(gate_x).reshape(dp, seq, -1)

    mask = lax.dynamic_slice_in_dim(mask_all, dp_at * local, local, 2)
    before = (jnp.arange(seq)[:, None] > jnp.arange(seq)[None, :]).astype(BF)
    rank = jnp.einsum("ab,gbe->gea", before, mask, preferred_element_type=F32)
    rank = jnp.where(jnp.swapaxes(mask, 1, 2) > 0, rank, -1.0)
    pick = (rank[:, :, None, :] == jnp.arange(slots, dtype=F32)[None, None, :, None]).astype(BF)

    cots = dispatch(pick, cotangent, dp, seq, None)
    rows = dispatch(pick, ffn_in, dp, seq, None if dp * seq <= 8192 else cots)
    gate_tok = lax.dynamic_slice_in_dim(gate_all, dp_at * local, local, 2).astype(
        F32
    ) + lax.dynamic_slice_in_dim(gate_all, experts + dp_at * local, local, 2).astype(F32)
    gate_slot = jnp.sum(pick.astype(F32) * jnp.swapaxes(gate_tok, 1, 2)[:, :, None, :], axis=3)

    g_proj = jnp.einsum("gesd,edf->gesf", rows, gate_weight, preferred_element_type=F32)
    u_proj = jnp.einsum("gesd,edf->gesf", rows, up_weight, preferred_element_type=F32)
    d_act = jnp.einsum("gesd,efd->gesf", cots, down_weight, preferred_element_type=F32)
    sig = 1.0 / (1.0 + jnp.exp(-g_proj))
    silu = g_proj * sig
    act = silu * u_proj
    scaled = (act * gate_slot[..., None]).astype(BF)
    d_gate_slot = jnp.sum(act * d_act, axis=3)
    d_act = d_act * gate_slot[..., None]
    d_g = (d_act * u_proj * sig * (1.0 + g_proj * (1.0 - sig))).astype(BF)
    d_u = (d_act * silu).astype(BF)
    d_rows = (
        jnp.einsum("gesf,edf->gesd", d_g, gate_weight, preferred_element_type=F32)
        + jnp.einsum("gesf,edf->gesd", d_u, up_weight, preferred_element_type=F32)
    ).astype(BF)
    dg_high, dg_low = split2(d_gate_slot)
    column = jnp.arange(lanes(2 * experts))
    mine = dp_at * local + jnp.arange(local)
    high_col = (column[None, :] == mine[:, None])[None, :, None, :]
    low_col = (column[None, :] == experts + mine[:, None])[None, :, None, :]
    extra = jnp.where(high_col, dg_high[..., None], jnp.where(low_col, dg_low[..., None], 0.0))
    d_rows = jnp.concatenate([d_rows, extra.astype(BF)], axis=3)
    d_sum = combine(pick, d_rows, dp, seq, None)

    y_rows = jnp.einsum("gesf,efd->gesd", scaled, down_weight, preferred_element_type=F32)
    y_sum = combine(pick, y_rows.astype(BF), dp, seq, None if dp * seq <= 8192 else d_sum)
    output = (hidden + y_sum).astype(BF)
    down_grad = jnp.einsum("gesf,gesd->efd", scaled, cots, preferred_element_type=F32)
    gate_grad = jnp.einsum("gesd,gesf->edf", rows, d_g, preferred_element_type=F32)
    up_grad = jnp.einsum("gesd,gesf->edf", rows, d_u, preferred_element_type=F32)

    d_gates = d_sum[:, width : width + experts] + d_sum[:, width + experts : width + 2 * experts]
    d_logits = gates * (d_gates - jnp.sum(gates * d_gates, axis=1, keepdims=True))
    d_high, d_low = split2(d_logits)
    d_ffn = d_sum[:, :width] + dot(d_high, router, 1, 1) + dot(d_low, router, 1, 1)
    router_part = dot(ffn_in, d_high, 0, 0) + dot(ffn_in, d_low, 0, 0)
    d_hidden, ffn_gain_rows = rms_back(hidden, ffn_gain32, d_ffn)
    ffn_gain_part = jnp.sum(ffn_gain_rows, axis=0)
    d_hidden = d_hidden + cotangent.astype(F32)
    d_attn = lax.all_gather(d_hidden.astype(BF), "tensor", axis=0, tiled=True)

    o_part = dot(d_attn, context, 0, 0).astype(BF)
    d_context = dot(d_attn, o_t, 1, 0).astype(BF).reshape(seq, hk, group, HEAD)
    d_probs = jnp.einsum("qhgd,khd->hgqk", d_context, v_low, preferred_element_type=F32)
    d_values = jnp.einsum("hgqk,qhgd->khd", probs.astype(BF), d_context, preferred_element_type=F32)
    d_scores = probs * (d_probs - jnp.sum(probs * d_probs, axis=-1, keepdims=True))
    d_scores = d_scores.astype(BF)
    d_q = jnp.einsum("hgqk,khd->qhgd", d_scores, k_low, preferred_element_type=F32) * scale
    d_k = jnp.einsum("hgqk,qhgd->khd", d_scores, q_low, preferred_element_type=F32) * scale
    d_q_raw, q_gain_rows = rms_back(q_raw, q_gain32, rope_back(d_q.reshape(seq, hq, HEAD), cos, sin))
    d_k_raw, k_gain_rows = rms_back(k_raw, k_gain32, rope_back(d_k, cos, sin))
    d_qkv = jnp.concatenate(
        [
            d_q_raw.reshape(seq, hq * HEAD).astype(BF),
            d_k_raw.reshape(seq, hk * HEAD).astype(BF),
            d_values.reshape(seq, hk * HEAD).astype(BF),
        ],
        axis=1,
    )
    d_normed = dot(d_qkv, w_qkv, 1, 1).astype(BF)
    d_normed = lax.psum_scatter(d_normed, "tensor", scatter_dimension=0, tiled=True).astype(F32)
    qkv_part = dot(normed, d_qkv, 0, 0).astype(BF)
    d_tokens, attn_gain_rows = rms_back(tokens.astype(F32), attn_gain32, d_normed)
    tokens_grad = d_tokens + d_hidden

    o_sum = scatter_dp(o_part).astype(F32)
    qkv_sum = scatter_dp(qkv_part).astype(F32)
    spread = lambda v: jnp.pad(v.reshape(dp, gshard), ((0, 0), (0, shard - gshard))).reshape(-1)
    small_part = jnp.concatenate(
        [
            router_part,
            jnp.stack(
                [
                    jnp.sum(attn_gain_rows, axis=0),
                    ffn_gain_part,
                    spread(jnp.sum(q_gain_rows, axis=(0, 1))),
                    spread(jnp.sum(k_gain_rows, axis=(0, 1))),
                ],
                axis=1,
            ),
        ],
        axis=1,
    )
    small_part = pad_to(small_part, lanes(experts + 4))
    small_sum = lax.psum(scatter_dp(small_part), "tensor")
    return (
        output,
        tokens_grad,
        small_sum[:, experts],
        qkv_sum[:, : hq * HEAD],
        qkv_sum[:, hq * HEAD : (hq + hk) * HEAD],
        qkv_sum[:, (hq + hk) * HEAD :],
        o_sum.T,
        small_sum[:gshard, experts + 2],
        small_sum[:gshard, experts + 3],
        small_sum[:, experts + 1],
        small_sum[:, :experts],
        gate_grad,
        up_grad,
        down_grad,
    )


def solution(mesh):
    rows = P(("dp", "tensor"), None)
    both = P("dp", "tensor")
    return jax.shard_map(
        on_device,
        mesh=mesh,
        in_specs=(
            rows,
            P("dp"),
            both,
            both,
            both,
            P("tensor", "dp"),
            P("dp"),
            P("dp"),
            P("dp"),
            P("dp", None),
            P("dp", None, "tensor"),
            P("dp", None, "tensor"),
            P("dp", "tensor", None),
            P("dp", None),
            rows,
        ),
        out_specs=(
            rows,
            rows,
            P("dp"),
            both,
            both,
            both,
            P("tensor", "dp"),
            P("dp"),
            P("dp"),
            P("dp"),
            P("dp", None),
            P("dp", None, "tensor"),
            P("dp", None, "tensor"),
            P("dp", "tensor", None),
        ),
        check_vma=False,
    )
```

```python
import jax
import jax.numpy as jnp
from jax import lax
from jax.experimental import pallas as pl
from jax.experimental.pallas import tpu as pltpu
from jax.sharding import PartitionSpec as P

HEAD = 128
EPS = 1e-06
THETA = 1000000.0
BF = jnp.bfloat16
F32 = jnp.float32


def dot(a, b, ca, cb):
    return lax.dot_general(a, b, (((ca,), (cb,)), ((), ())), preferred_element_type=F32)


def rms(v, gain):
    return v * lax.rsqrt(jnp.mean(v * v, axis=-1, keepdims=True) + EPS) * gain


def rms_back(v, gain, u):
    inv = lax.rsqrt(jnp.mean(v * v, axis=-1, keepdims=True) + EPS)
    ug = u * gain
    grad = ug * inv - v * (jnp.mean(ug * v, axis=-1, keepdims=True) * inv * inv * inv)
    return grad, u * v * inv


def rope(v, cos, sin):
    a, b = v[..., : HEAD // 2], v[..., HEAD // 2 :]
    return jnp.concatenate([a * cos - b * sin, b * cos + a * sin], axis=-1)


def rope_back(v, cos, sin):
    a, b = v[..., : HEAD // 2], v[..., HEAD // 2 :]
    return jnp.concatenate([a * cos + b * sin, b * cos - a * sin], axis=-1)


def rope_tables(count):
    inverse = THETA ** (-(jnp.arange(HEAD // 2, dtype=F32) * 2.0 / HEAD))
    angles = jnp.arange(count, dtype=F32)[:, None] * inverse[None, :]
    return jnp.cos(angles)[:, None, :], jnp.sin(angles)[:, None, :]


def split2(v):
    high = v.astype(BF)
    return high, (v - high.astype(F32)).astype(BF)


def gather_dp(v):
    return lax.all_gather(v, "dp", axis=0, tiled=True)


def gather_all(v):
    return lax.all_gather(v, ("dp", "tensor"), axis=0, tiled=True)


def scatter_all(v):
    return lax.psum_scatter(v, ("dp", "tensor"), scatter_dimension=0, tiled=True)


def scatter_dp(v):
    return lax.psum_scatter(v, "dp", scatter_dimension=0, tiled=True)


def pieces(width, dp, seq):
    count = 1 if dp * seq <= 8192 else 4
    step = width // count // 128 * 128
    edges = [step * i for i in range(count)] + [width]
    return list(zip(edges[:-1], edges[1:]))


def after(v, earlier):
    return v if earlier is None else lax.optimization_barrier((v, earlier))[0]


def dispatch(pick, own, dp, seq, earlier):
    blocks = []
    for low, high in pieces(own.shape[1], dp, seq):
        every = gather_all(after(own[:, low:high], earlier)).reshape(dp, seq, high - low)
        block = jnp.einsum("gest,gtd->gesd", pick, every, preferred_element_type=F32).astype(BF)
        blocks.append(block)
        earlier = block if len(pieces(own.shape[1], dp, seq)) > 1 else None
    return jnp.concatenate(blocks, axis=3)


def combine(pick, rows, dp, seq, earlier):
    blocks = []
    for low, high in pieces(rows.shape[3], dp, seq):
        tok = jnp.einsum(
            "gest,gesd->gtd",
            pick,
            after(rows[:, :, :, low:high], earlier),
            preferred_element_type=F32,
        ).astype(BF)
        blocks.append(scatter_all(tok.reshape(dp * seq, high - low)))
        earlier = blocks[-1] if len(pieces(rows.shape[3], dp, seq)) > 1 else None
    return jnp.concatenate(blocks, axis=1).astype(F32)


GRID = [(z, x, c) for z in range(4) for x in range(2) for c in range(2)]
SPLIT = (0, 768, 1536, 1792, 2048)


def at(z, x, c):
    return z % 4 * 4 + x % 2 * 2 + c % 2


def shift_z(v, k):
    return lax.ppermute(v, "dp", [(at(z, x, c), at(z + k, x, c)) for z, x, c in GRID])


def swap_x(v):
    return lax.ppermute(v, "dp", [(at(z, x, c), at(z, x + 1, c)) for z, x, c in GRID])


def swap_c(v):
    return lax.ppermute(v, "dp", [(at(z, x, c), at(z, x, c + 1)) for z, x, c in GRID])


def swap_y(v):
    return lax.ppermute(v, "tensor", [(0, 1), (1, 0)])


def gather_z(v, way):
    one, three = shift_z(v, 1), shift_z(v, -1)
    two = shift_z(one, 1) if way > 0 else shift_z(three, -1)
    return jnp.stack([v, one, two, three])


def add2(a, b):
    return (a.astype(F32) + b.astype(F32)).astype(BF)


def reduce_z(v, way):
    if way > 0:
        one = shift_z(add2(v[1], shift_z(v[2], -1)), -1)
        three = shift_z(v[3], 1)
    else:
        three = shift_z(add2(v[3], shift_z(v[2], 1)), 1)
        one = shift_z(v[1], -1)
    return (v[0].astype(F32) + one.astype(F32) + three.astype(F32)).astype(BF)


def gather_rel(v1, v2, v5, v6):
    w5 = jnp.stack([v5, swap_x(v5)])
    w6 = jnp.stack([v6, swap_y(v6)])
    s1 = gather_z(v1, 1)
    s2 = gather_z(v2, -1)
    w5 = jnp.stack([w5, swap_y(w5)], axis=1)
    w6 = jnp.stack([w6, swap_x(w6)], axis=0)
    s1 = jnp.stack([s1, swap_x(s1)], axis=1)
    s2 = jnp.stack([s2, swap_y(s2)], axis=1)
    o5 = gather_z(w5, 1)
    o6 = gather_z(w6, -1)
    first = (s1, swap_y(s1), s2, swap_x(s2), o5, o6)
    second = tuple(swap_c(v) for v in first)
    return first, second


def scatter_rel(near, far):
    def core(i):
        n = near[i].shape[1] // 2
        both = add2(near[i], swap_c(far[i]))
        return both.reshape(4, 2, 2, n, both.shape[2])

    p5, p6, p1, p2 = core(2), core(3), core(0), core(1)
    p5 = reduce_z(p5, 1)
    p6 = reduce_z(p6, -1)
    p1 = add2(p1[:, :, 0], swap_y(p1[:, :, 1]))
    p2 = add2(p2[:, 0], swap_x(p2[:, 1]))
    p5 = add2(p5[:, 0], swap_y(p5[:, 1]))
    p6 = add2(p6[0], swap_x(p6[1]))
    p1 = add2(p1[:, 0], swap_x(p1[:, 1]))
    p2 = add2(p2[:, 0], swap_y(p2[:, 1]))
    p5 = add2(p5[0], swap_x(p5[1]))
    p6 = add2(p6[0], swap_y(p6[1]))
    return reduce_z(p1, 1), reduce_z(p2, -1), p5, p6


def nn(a, b):
    return lax.dot_general(a, b, (((1,), (0,)), ((), ())), preferred_element_type=F32)


def nt(a, b):
    return lax.dot_general(a, b, (((1,), (1,)), ((), ())), preferred_element_type=F32)


def pick_rows(rank, slots):
    at_slot = lax.broadcasted_iota(jnp.int32, (slots, rank.shape[1]), 0).astype(F32)
    return jnp.concatenate(
        [(rank[e : e + 1, :] == at_slot).astype(F32).astype(BF) for e in range(rank.shape[0])],
        axis=0,
    )


def pick_cols(rank, slots):
    at_slot = lax.broadcasted_iota(jnp.int32, (rank.shape[0], slots), 1).astype(F32)
    return jnp.concatenate(
        [(rank[:, e : e + 1] == at_slot).astype(F32).astype(BF) for e in range(rank.shape[1])],
        axis=1,
    )


def cot_kernel(where, rank, cot_a, cot_b, down, cots, d_act):
    slots = cots.shape[2] // 2
    for dx, cot in enumerate((cot_a, cot_b)):
        both = nn(pick_rows(rank[dx], slots), cot[0]).astype(BF)
        for e in range(2):
            cots[e, 0, dx * slots : (dx + 1) * slots, :] = both[e * slots : (e + 1) * slots]
    for e in range(2):
        d_act[e, 0] = nt(cots[e, 0], down[e])


def expert_kernel(
    rank, rank_t, cols, d_act, x1a, x1b, x2a, x2b, x5, x6, w_gate, w_up,
    rows, scaled, d_g, d_u, t1, t2, t5, t6, back,
):
    slots = rows.shape[2] // 2
    n = x1a.shape[1]
    gates = []
    for dx, x2 in enumerate((x2a, x2b)):
        pick = pick_rows(rank[dx], slots)
        block1 = nn(pick[:, :n], x1a[dx]) + nn(pick[:, n:], x1b[dx])
        block2 = nn(pick, x2[0])
        block5 = nn(pick, x5[dx])
        block6 = nn(pick, x6[dx])
        low = dx * slots
        for e in range(2):
            part = slice(e * slots, (e + 1) * slots)
            rows[e, 0, low : low + slots, 0:768] = block1[part].astype(BF)
            rows[e, 0, low : low + slots, 768:1536] = block2[part].astype(BF)
            rows[e, 0, low : low + slots, 1536:1792] = block5[part, :256].astype(BF)
            rows[e, 0, low : low + slots, 1792:2048] = block6[part].astype(BF)
            both = cols[e, 0:1, :] + cols[e, 1:2, :]
            gates.append(jnp.sum(block5[part, 256:] * both, axis=1, keepdims=True))
    extras = []
    for e in range(2):
        gate = jnp.concatenate([gates[e], gates[2 + e]], axis=0)
        g = nn(rows[e, 0], w_gate[e])
        u = nn(rows[e, 0], w_up[e])
        da = d_act[e, 0]
        sig = 1.0 / (1.0 + jnp.exp(-g))
        silu = g * sig
        act = silu * u
        scaled[e, 0] = (act * gate).astype(BF)
        d_gate = jnp.sum(act * da, axis=1, keepdims=True)
        da = da * gate
        dg = (da * u * sig * (1.0 + g * (1.0 - sig))).astype(BF)
        du = (da * silu).astype(BF)
        d_g[e, 0] = dg
        d_u[e, 0] = du
        high = d_gate.astype(BF).astype(F32)
        extras.append(high * cols[e, 0:1, :] + (d_gate - high) * cols[e, 1:2, :])
        dr = (nt(dg, w_gate[e]) + nt(du, w_up[e])).astype(BF)
        for dx in range(2):
            back[dx, e * slots : (e + 1) * slots, :] = dr[dx * slots : (dx + 1) * slots]
    for dx in range(2):
        pick_t = pick_cols(rank_t[dx], slots)
        t1[dx] = nn(pick_t, back[dx, :, 0:768]).astype(BF)
        t2[dx] = nn(pick_t, back[dx, :, 768:1536]).astype(BF)
        t5[dx, :, 0:256] = nn(pick_t, back[dx, :, 1536:1792]).astype(BF)
        t6[dx] = nn(pick_t, back[dx, :, 1792:2048]).astype(BF)
        extra = jnp.concatenate(
            [extras[e][dx * slots : (dx + 1) * slots] for e in range(2)], axis=0
        ).astype(BF)
        t5[dx, :, 256:] = nn(pick_t, extra).astype(BF)


def out_kernel(rank_t, scaled, down, t1, t2, t5, t6, back):
    slots = scaled.shape[2] // 2
    for e in range(2):
        y = nn(scaled[e, 0], down[e]).astype(BF)
        for dx in range(2):
            back[dx, e * slots : (e + 1) * slots, :] = y[dx * slots : (dx + 1) * slots]
    for dx in range(2):
        pick_t = pick_cols(rank_t[dx], slots)
        for t, low, high in zip((t1, t2, t5, t6), SPLIT[:-1], SPLIT[1:]):
            t[dx] = nn(pick_t, back[dx, :, low:high]).astype(BF)


def pair(*tail):
    return pl.BlockSpec((2, *tail), lambda i, *_: (i,) + (0,) * len(tail))


def one(*tail):
    return pl.BlockSpec((1, *tail), lambda i, *_: (i,) + (0,) * len(tail))


def by_expert(*tail):
    return pl.BlockSpec((2, 1, *tail), lambda i, *_: (0, i) + (0,) * len(tail))


def fixed(*shape):
    return pl.BlockSpec(
        shape, lambda i, *_: (0,) * len(shape), pipeline_mode=pl.Buffered(1)
    )


def shaped(shape, kind):
    return jax.ShapeDtypeStruct(shape, kind)


LIMIT = pltpu.CompilerParams(vmem_limit_bytes=60000 * 1024)


def run_cots(where, rank, cot_all, down, slots):
    seq, width = cot_all.shape[1:]
    ff = down.shape[1]
    return pl.pallas_call(
        cot_kernel,
        grid_spec=pltpu.PrefetchScalarGridSpec(
            num_scalar_prefetch=1,
            grid=(4,),
            in_specs=[
                pair(2, seq),
                pl.BlockSpec((1, seq, width), lambda i, w: (w[2 * i], 0, 0)),
                pl.BlockSpec((1, seq, width), lambda i, w: (w[2 * i + 1], 0, 0)),
                fixed(2, ff, width),
            ],
            out_specs=[by_expert(2 * slots, width), by_expert(2 * slots, ff)],
        ),
        out_shape=[shaped((2, 4, 2 * slots, width), BF), shaped((2, 4, 2 * slots, ff), F32)],
        compiler_params=LIMIT,
        name="cots",
    )(where, rank, cot_all, cot_all, down)


def run_experts(rank, rank_t, cols, d_act, parts, w_gate, w_up, slots):
    s1, s1y, s2, s2x, o5, o6 = parts
    n = s1.shape[2]
    seq, width, ff = 2 * n, w_gate.shape[1], w_gate.shape[2]
    flat = lambda v, lead: v.reshape(lead, -1, v.shape[-1])
    tail = [768, 768, 384, 256]
    return pl.pallas_call(
        expert_kernel,
        grid=(4,),
        in_specs=[
            pair(2, seq),
            pair(seq, 2),
            fixed(*cols.shape),
            by_expert(2 * slots, ff),
            pair(n, 768),
            pair(n, 768),
            one(seq, 768),
            one(seq, 768),
            pair(seq, 384),
            pair(seq, 256),
            fixed(2, width, ff),
            fixed(2, width, ff),
        ],
        out_specs=[
            by_expert(2 * slots, width),
            by_expert(2 * slots, ff),
            by_expert(2 * slots, ff),
            by_expert(2 * slots, ff),
        ]
        + [pair(seq, w) for w in tail],
        out_shape=[
            shaped((2, 4, 2 * slots, width), BF),
            shaped((2, 4, 2 * slots, ff), BF),
            shaped((2, 4, 2 * slots, ff), BF),
            shaped((2, 4, 2 * slots, ff), BF),
        ]
        + [shaped((8, seq, w), BF) for w in tail],
        scratch_shapes=[pltpu.VMEM((2, 2 * slots, width), BF)],
        compiler_params=LIMIT,
        name="experts",
    )(
        rank, rank_t, cols, d_act, flat(s1, 8), flat(s1y, 8), flat(s2, 4), flat(s2x, 4),
        flat(o5, 8), flat(o6, 8), w_gate, w_up,
    )


def run_outs(rank_t, scaled, down, slots):
    seq, ff, width = rank_t.shape[1], down.shape[1], down.shape[2]
    tail = [b - a for a, b in zip(SPLIT[:-1], SPLIT[1:])]
    return pl.pallas_call(
        out_kernel,
        grid=(4,),
        in_specs=[pair(seq, 2), by_expert(2 * slots, ff), fixed(2, ff, width)],
        out_specs=[pair(seq, w) for w in tail],
        out_shape=[shaped((8, seq, w), BF) for w in tail],
        scratch_shapes=[pltpu.VMEM((2, 2 * slots, width), BF)],
        compiler_params=LIMIT,
        name="outs",
    )(rank_t, scaled, down)


def flip(v, axis, y):
    a, b = jnp.split(v, 2, axis=axis)
    return jnp.where(y == 0, v, jnp.concatenate([b, a], axis=axis))


def moe_small(
    ids_all, cot_all, ffn_in, gate_x, gate_weight, up_weight, down_weight, experts, slots
):
    dp_at = lax.axis_index("dp")
    y = lax.axis_index("tensor")
    seq = ids_all.shape[1]
    mine = dp_at * 2 + jnp.arange(2, dtype=jnp.int32)
    mask = jnp.any(ids_all[:, None, :, :] == mine[None, :, None, None], axis=3)
    before = (jnp.arange(seq)[:, None] < jnp.arange(seq)[None, :]).astype(BF)
    rank = jnp.einsum("gea,ab->geb", mask.astype(BF), before, preferred_element_type=F32)
    rank = jnp.where(mask, rank, -1.0)
    d = jnp.arange(16)
    dc, dz, dx = d // 8, d // 2 % 4, d % 2
    where = (dp_at // 4 - dz) % 4 * 4 + (dp_at // 2 % 2 + dx) % 2 * 2 + (dp_at % 2 + dc) % 2
    rank = jnp.take(rank, where, axis=0)
    rank_rel = flip(rank, 2, y)
    rank_t = jnp.swapaxes(rank_rel, 1, 2)
    column = jnp.arange(128)
    cols = (
        column[None, None, :] == (mine[:, None] + jnp.array([[0, experts]]))[:, :, None]
    ).astype(F32)
    half = lambda v, k: v[8 * k : 8 * k + 8]
    where = where.astype(jnp.int32)

    cots, d_act = zip(*[run_cots(half(where, k), half(rank, k), cot_all, down_weight, slots) for k in (0, 1)])
    v1, v2, v5, v6 = [ffn_in[:, a:b] for a, b in zip(SPLIT[:-1], SPLIT[1:])]
    parts = gather_rel(v1, v2, jnp.concatenate([v5, gate_x], axis=1), v6)
    far = run_experts(half(rank_rel, 1), half(rank_t, 1), cols, d_act[1], parts[1], gate_weight, up_weight, slots)
    near = run_experts(half(rank_rel, 0), half(rank_t, 0), cols, d_act[0], parts[0], gate_weight, up_weight, slots)
    d1, d2, d5, d6 = scatter_rel(near[4:], far[4:])
    d_sum = jnp.concatenate([d1, d2, d5[:, :256], d6, d5[:, 256:]], axis=1).astype(F32)
    outs = [run_outs(half(rank_t, k), (near, far)[k][1], down_weight, slots) for k in (0, 1)]
    y_sum = jnp.concatenate(scatter_rel(outs[0], outs[1]), axis=1).astype(F32)
    total = lambda spec, a, b: jnp.einsum(spec, near[a], near[b], preferred_element_type=F32) + jnp.einsum(
        spec, far[a], far[b], preferred_element_type=F32
    )
    gate_grad = total("egsd,egsf->edf", 0, 2)
    up_grad = total("egsd,egsf->edf", 0, 3)
    down_grad = jnp.einsum(
        "egsf,egsd->efd", near[1], cots[0], preferred_element_type=F32
    ) + jnp.einsum("egsf,egsd->efd", far[1], cots[1], preferred_element_type=F32)
    return d_sum, y_sum, gate_grad, up_grad, down_grad


def moe_large(
    ids_all, cotangent, ffn_in, gate_x, gate_weight, up_weight, down_weight, experts, slots
):
    dp, seq = ids_all.shape[:2]
    local = gate_weight.shape[0]
    dp_at = lax.axis_index("dp")
    mine = dp_at * local + jnp.arange(local, dtype=jnp.int32)
    mask = jnp.any(ids_all[:, :, None, :] == mine[None, None, :, None], axis=3).astype(BF)
    gate_all = gather_all(gate_x).reshape(dp, seq, -1)
    before = (jnp.arange(seq)[:, None] > jnp.arange(seq)[None, :]).astype(BF)
    rank = jnp.einsum("ab,gbe->gea", before, mask, preferred_element_type=F32)
    rank = jnp.where(jnp.swapaxes(mask, 1, 2) > 0, rank, -1.0)
    pick = (rank[:, :, None, :] == jnp.arange(slots, dtype=F32)[None, None, :, None]).astype(BF)

    cots = dispatch(pick, cotangent, dp, seq, None)
    rows = dispatch(pick, ffn_in, dp, seq, cots)
    gate_tok = lax.dynamic_slice_in_dim(gate_all, dp_at * local, local, 2).astype(
        F32
    ) + lax.dynamic_slice_in_dim(gate_all, experts + dp_at * local, local, 2).astype(F32)
    gate_slot = jnp.sum(pick.astype(F32) * jnp.swapaxes(gate_tok, 1, 2)[:, :, None, :], axis=3)

    g_proj = jnp.einsum("gesd,edf->gesf", rows, gate_weight, preferred_element_type=F32)
    u_proj = jnp.einsum("gesd,edf->gesf", rows, up_weight, preferred_element_type=F32)
    d_act = jnp.einsum("gesd,efd->gesf", cots, down_weight, preferred_element_type=F32)
    sig = 1.0 / (1.0 + jnp.exp(-g_proj))
    silu = g_proj * sig
    act = silu * u_proj
    scaled = (act * gate_slot[..., None]).astype(BF)
    d_gate_slot = jnp.sum(act * d_act, axis=3)
    d_act = d_act * gate_slot[..., None]
    d_g = (d_act * u_proj * sig * (1.0 + g_proj * (1.0 - sig))).astype(BF)
    d_u = (d_act * silu).astype(BF)
    d_rows = (
        jnp.einsum("gesf,edf->gesd", d_g, gate_weight, preferred_element_type=F32)
        + jnp.einsum("gesf,edf->gesd", d_u, up_weight, preferred_element_type=F32)
    ).astype(BF)
    dg_high, dg_low = split2(d_gate_slot)
    column = jnp.arange(lanes(2 * experts))
    high_col = (column[None, :] == mine[:, None])[None, :, None, :]
    low_col = (column[None, :] == experts + mine[:, None])[None, :, None, :]
    extra = jnp.where(high_col, dg_high[..., None], jnp.where(low_col, dg_low[..., None], 0.0))
    d_rows = jnp.concatenate([d_rows, extra.astype(BF)], axis=3)
    d_sum = combine(pick, d_rows, dp, seq, None)

    y_rows = jnp.einsum("gesf,efd->gesd", scaled, down_weight, preferred_element_type=F32)
    y_sum = combine(pick, y_rows.astype(BF), dp, seq, d_sum)
    down_grad = jnp.einsum("gesf,gesd->efd", scaled, cots, preferred_element_type=F32)
    gate_grad = jnp.einsum("gesd,gesf->edf", rows, d_g, preferred_element_type=F32)
    up_grad = jnp.einsum("gesd,gesf->edf", rows, d_u, preferred_element_type=F32)

    return d_sum, y_sum, gate_grad, up_grad, down_grad


def pad_to(v, width):
    return jnp.pad(v, ((0, 0), (0, width - v.shape[1])))


def lanes(count):
    return -(-count // 128) * 128


def on_device(
    tokens,
    attn_gain,
    q_weight,
    key_matrix,
    value_matrix,
    o_weight,
    query_norm_gain,
    k_gain,
    ffn_gain,
    router_weight,
    gate_weight,
    up_weight,
    down_weight,
    expert_ids,
    cotangent,
):
    dp = lax.axis_size("dp")
    tensor = lax.axis_size("tensor")
    dp_at = lax.axis_index("dp")
    own, width = tokens.shape
    seq = expert_ids.shape[0]
    begin = lax.axis_index("tensor") * own
    local = gate_weight.shape[0]
    experts = local * dp
    slots = 10 * seq * expert_ids.shape[1] // (8 * experts)
    slots = -(-slots // 16) * 16
    shard = q_weight.shape[0]
    gshard = query_norm_gain.shape[0]
    hq = q_weight.shape[1] // HEAD
    hk = key_matrix.shape[1] // HEAD
    group = hq // hk
    qkv_width = (hq + 2 * hk) * HEAD
    top = expert_ids.shape[1]
    fast = (dp, tensor, local, seq, width) == (16, 2, 2, 384, 2048)

    arange_e = jnp.arange(experts, dtype=jnp.int32)
    own_ids = lax.dynamic_slice_in_dim(expert_ids, begin, own, 0)
    own_mask = jnp.any(own_ids[:, :, None] == arange_e[None, None, :], axis=1)

    gain_rows = jnp.stack(
        [
            attn_gain,
            ffn_gain,
            jnp.pad(query_norm_gain, (0, shard - gshard)),
            jnp.pad(k_gain, (0, shard - gshard)),
        ],
        axis=1,
    )
    ids_rows = expert_ids.reshape(shard, -1).astype(BF)
    small = jnp.concatenate([router_weight, gain_rows, ids_rows], axis=1)
    small = pad_to(small, lanes(small.shape[1]))
    all_in = gather_dp(jnp.concatenate([q_weight, key_matrix, value_matrix, small], axis=1))
    layer_in = lax.all_gather(tokens, "tensor", axis=0, tiled=True)
    o_t = gather_dp(o_weight.T)
    if fast:
        cot_all = gather_all(cotangent).reshape(dp, seq, width)

    w_qkv = all_in[:, :qkv_width]
    router = all_in[:, qkv_width : qkv_width + experts]
    gains = all_in[:, qkv_width + experts : qkv_width + experts + 4].astype(F32)
    ids_all = all_in[:, qkv_width + experts + 4 :][:, : seq * top // shard]
    ids_all = ids_all.astype(jnp.int32).reshape(dp, seq, top)
    attn_gain32 = gains[:, 0]
    ffn_gain32 = gains[:, 1]
    q_gain32 = gains[:, 2].reshape(dp, shard)[:, :gshard].reshape(-1)
    k_gain32 = gains[:, 3].reshape(dp, shard)[:, :gshard].reshape(-1)

    residual = layer_in.astype(F32)
    normed = rms(residual, attn_gain32).astype(BF)
    qkv = dot(normed, w_qkv, 1, 0)
    cos, sin = rope_tables(seq)
    q_raw = qkv[:, : hq * HEAD].reshape(seq, hq, HEAD)
    k_raw = qkv[:, hq * HEAD : (hq + hk) * HEAD].reshape(seq, hk, HEAD)
    v_low = qkv[:, (hq + hk) * HEAD :].astype(BF).reshape(seq, hk, HEAD)
    q_low = rope(rms(q_raw, q_gain32), cos, sin).astype(BF).reshape(seq, hk, group, HEAD)
    k_low = rope(rms(k_raw, k_gain32), cos, sin).astype(BF)
    causal = jnp.arange(seq)[:, None] >= jnp.arange(seq)[None, :]
    scale = HEAD ** (-0.5)
    scores = jnp.einsum("qhgd,khd->hgqk", q_low, k_low, preferred_element_type=F32) * scale
    expo = jnp.where(causal, jnp.exp(scores), 0.0)
    total = jnp.sum(expo, axis=-1, keepdims=True)
    probs = expo / total
    context = jnp.einsum("hgqk,khd->qhgd", probs.astype(BF), v_low, preferred_element_type=F32)
    context = context.reshape(seq, hq * HEAD).astype(BF)
    attn_part = dot(context, o_t, 1, 1).astype(BF)
    attn_own = lax.psum_scatter(attn_part, "tensor", scatter_dimension=0, tiled=True)
    hidden = tokens.astype(F32) + attn_own.astype(F32)

    ffn_in = rms(hidden, ffn_gain32).astype(BF)
    logits = dot(ffn_in, router, 1, 0)
    chosen = jnp.where(own_mask, jnp.exp(logits), 0.0)
    gates = chosen / jnp.sum(chosen, axis=1, keepdims=True)
    gate_high, gate_low = split2(gates)
    gate_x = pad_to(jnp.concatenate([gate_high, gate_low], axis=1), lanes(2 * experts))
    args = (gate_weight, up_weight, down_weight, experts, slots)
    if fast:
        d_sum, y_sum, gate_grad, up_grad, down_grad = moe_small(
            ids_all, cot_all, ffn_in, gate_x, *args
        )
    else:
        d_sum, y_sum, gate_grad, up_grad, down_grad = moe_large(
            ids_all, cotangent, ffn_in, gate_x, *args
        )
    output = (hidden + y_sum).astype(BF)

    d_gates = d_sum[:, width : width + experts] + d_sum[:, width + experts : width + 2 * experts]
    d_logits = gates * (d_gates - jnp.sum(gates * d_gates, axis=1, keepdims=True))
    d_high, d_low = split2(d_logits)
    d_ffn = d_sum[:, :width] + dot(d_high, router, 1, 1) + dot(d_low, router, 1, 1)
    router_part = dot(ffn_in, d_high, 0, 0) + dot(ffn_in, d_low, 0, 0)
    d_hidden, ffn_gain_rows = rms_back(hidden, ffn_gain32, d_ffn)
    ffn_gain_part = jnp.sum(ffn_gain_rows, axis=0)
    d_hidden = d_hidden + cotangent.astype(F32)
    d_attn = lax.all_gather(d_hidden.astype(BF), "tensor", axis=0, tiled=True)

    o_part = dot(d_attn, context, 0, 0).astype(BF)
    d_context = dot(d_attn, o_t, 1, 0).astype(BF).reshape(seq, hk, group, HEAD)
    d_probs = jnp.einsum("qhgd,khd->hgqk", d_context, v_low, preferred_element_type=F32)
    d_values = jnp.einsum("hgqk,qhgd->khd", probs.astype(BF), d_context, preferred_element_type=F32)
    d_scores = probs * (d_probs - jnp.sum(probs * d_probs, axis=-1, keepdims=True))
    d_scores = d_scores.astype(BF)
    d_q = jnp.einsum("hgqk,khd->qhgd", d_scores, k_low, preferred_element_type=F32) * scale
    d_k = jnp.einsum("hgqk,qhgd->khd", d_scores, q_low, preferred_element_type=F32) * scale
    d_q_raw, q_gain_rows = rms_back(q_raw, q_gain32, rope_back(d_q.reshape(seq, hq, HEAD), cos, sin))
    d_k_raw, k_gain_rows = rms_back(k_raw, k_gain32, rope_back(d_k, cos, sin))
    d_qkv = jnp.concatenate(
        [
            d_q_raw.reshape(seq, hq * HEAD).astype(BF),
            d_k_raw.reshape(seq, hk * HEAD).astype(BF),
            d_values.reshape(seq, hk * HEAD).astype(BF),
        ],
        axis=1,
    )
    d_normed = dot(d_qkv, w_qkv, 1, 1).astype(BF)
    d_normed = lax.psum_scatter(d_normed, "tensor", scatter_dimension=0, tiled=True).astype(F32)
    qkv_part = dot(normed, d_qkv, 0, 0).astype(BF)
    d_tokens, attn_gain_rows = rms_back(tokens.astype(F32), attn_gain32, d_normed)
    tokens_grad = d_tokens + d_hidden

    o_sum = scatter_dp(o_part).astype(F32)
    qkv_sum = scatter_dp(qkv_part).astype(F32)
    spread = lambda v: jnp.pad(v.reshape(dp, gshard), ((0, 0), (0, shard - gshard))).reshape(-1)
    small_part = jnp.concatenate(
        [
            router_part,
            jnp.stack(
                [
                    jnp.sum(attn_gain_rows, axis=0),
                    ffn_gain_part,
                    spread(jnp.sum(q_gain_rows, axis=(0, 1))),
                    spread(jnp.sum(k_gain_rows, axis=(0, 1))),
                ],
                axis=1,
            ),
        ],
        axis=1,
    )
    small_part = pad_to(small_part, lanes(experts + 4))
    small_sum = lax.psum(scatter_dp(small_part), "tensor")
    return (
        output,
        tokens_grad,
        small_sum[:, experts],
        qkv_sum[:, : hq * HEAD],
        qkv_sum[:, hq * HEAD : (hq + hk) * HEAD],
        qkv_sum[:, (hq + hk) * HEAD :],
        o_sum.T,
        small_sum[:gshard, experts + 2],
        small_sum[:gshard, experts + 3],
        small_sum[:, experts + 1],
        small_sum[:, :experts],
        gate_grad,
        up_grad,
        down_grad,
    )


def solution(mesh):
    rows = P(("dp", "tensor"), None)
    both = P("dp", "tensor")
    return jax.shard_map(
        on_device,
        mesh=mesh,
        in_specs=(
            rows,
            P("dp"),
            both,
            both,
            both,
            P("tensor", "dp"),
            P("dp"),
            P("dp"),
            P("dp"),
            P("dp", None),
            P("dp", None, "tensor"),
            P("dp", None, "tensor"),
            P("dp", "tensor", None),
            P("dp", None),
            rows,
        ),
        out_specs=(
            rows,
            rows,
            P("dp"),
            both,
            both,
            both,
            P("tensor", "dp"),
            P("dp"),
            P("dp"),
            P("dp"),
            P("dp", None),
            P("dp", None, "tensor"),
            P("dp", None, "tensor"),
            P("dp", "tensor", None),
        ),
        check_vma=False,
    )
```

```python
import jax
import jax.numpy as jnp
from jax import lax
from jax.experimental import pallas as pl
from jax.experimental.pallas import tpu as pltpu
from jax.sharding import PartitionSpec as P

HEAD = 128
EPS = 1e-06
THETA = 1000000.0
BF = jnp.bfloat16
F32 = jnp.float32


def dot(a, b, ca, cb):
    return lax.dot_general(a, b, (((ca,), (cb,)), ((), ())), preferred_element_type=F32)


def rms(v, gain):
    return v * lax.rsqrt(jnp.mean(v * v, axis=-1, keepdims=True) + EPS) * gain


def rms_back(v, gain, u):
    inv = lax.rsqrt(jnp.mean(v * v, axis=-1, keepdims=True) + EPS)
    ug = u * gain
    grad = ug * inv - v * (jnp.mean(ug * v, axis=-1, keepdims=True) * inv * inv * inv)
    return grad, u * v * inv


def rope(v, cos, sin):
    a, b = v[..., : HEAD // 2], v[..., HEAD // 2 :]
    return jnp.concatenate([a * cos - b * sin, b * cos + a * sin], axis=-1)


def rope_back(v, cos, sin):
    a, b = v[..., : HEAD // 2], v[..., HEAD // 2 :]
    return jnp.concatenate([a * cos + b * sin, b * cos - a * sin], axis=-1)


def rope_tables(count):
    inverse = THETA ** (-(jnp.arange(HEAD // 2, dtype=F32) * 2.0 / HEAD))
    angles = jnp.arange(count, dtype=F32)[:, None] * inverse[None, :]
    return jnp.cos(angles)[:, None, :], jnp.sin(angles)[:, None, :]


def split2(v):
    high = v.astype(BF)
    return high, (v - high.astype(F32)).astype(BF)


def gather_dp(v):
    return lax.all_gather(v, "dp", axis=0, tiled=True)


def gather_all(v):
    return lax.all_gather(v, ("dp", "tensor"), axis=0, tiled=True)


def scatter_all(v):
    return lax.psum_scatter(v, ("dp", "tensor"), scatter_dimension=0, tiled=True)


def scatter_dp(v):
    return lax.psum_scatter(v, "dp", scatter_dimension=0, tiled=True)


def pieces(width, dp, seq):
    count = 1 if dp * seq <= 8192 else 4
    step = width // count // 128 * 128
    edges = [step * i for i in range(count)] + [width]
    return list(zip(edges[:-1], edges[1:]))


def after(v, earlier):
    return v if earlier is None else lax.optimization_barrier((v, earlier))[0]


def dispatch(pick, own, dp, seq, earlier):
    blocks = []
    for low, high in pieces(own.shape[1], dp, seq):
        every = gather_all(after(own[:, low:high], earlier)).reshape(dp, seq, high - low)
        block = jnp.einsum("gest,gtd->gesd", pick, every, preferred_element_type=F32).astype(BF)
        blocks.append(block)
        earlier = block if len(pieces(own.shape[1], dp, seq)) > 1 else None
    return jnp.concatenate(blocks, axis=3)


def combine(pick, rows, dp, seq, earlier):
    blocks = []
    for low, high in pieces(rows.shape[3], dp, seq):
        tok = jnp.einsum(
            "gest,gesd->gtd",
            pick,
            after(rows[:, :, :, low:high], earlier),
            preferred_element_type=F32,
        ).astype(BF)
        blocks.append(scatter_all(tok.reshape(dp * seq, high - low)))
        earlier = blocks[-1] if len(pieces(rows.shape[3], dp, seq)) > 1 else None
    return jnp.concatenate(blocks, axis=1).astype(F32)


GRID = [(z, x, c) for z in range(4) for x in range(2) for c in range(2)]
SPLIT = (0, 768, 1536, 1792, 2048)


def at(z, x, c):
    return z % 4 * 4 + x % 2 * 2 + c % 2


def shift_z(v, k):
    return lax.ppermute(v, "dp", [(at(z, x, c), at(z + k, x, c)) for z, x, c in GRID])


def swap_x(v):
    return lax.ppermute(v, "dp", [(at(z, x, c), at(z, x + 1, c)) for z, x, c in GRID])


def swap_c(v):
    return lax.ppermute(v, "dp", [(at(z, x, c), at(z, x, c + 1)) for z, x, c in GRID])


def swap_y(v):
    return lax.ppermute(v, "tensor", [(0, 1), (1, 0)])


def gather_y(v):
    other = swap_y(v)
    first = lax.axis_index("tensor") == 0
    return jnp.concatenate([jnp.where(first, v, other), jnp.where(first, other, v)])


def scatter_y(v):
    a, b = jnp.split(v, 2)
    first = lax.axis_index("tensor") == 0
    kept, sent = jnp.where(first, a, b), jnp.where(first, b, a)
    return kept.astype(F32) + swap_y(sent.astype(BF)).astype(F32)


def gather_z(v, way):
    one, three = shift_z(v, 1), shift_z(v, -1)
    two = shift_z(one, 1) if way > 0 else shift_z(three, -1)
    return jnp.stack([v, one, two, three])


def add2(a, b):
    return (a.astype(F32) + b.astype(F32)).astype(BF)


def reduce_z(v, way):
    if way > 0:
        one = shift_z(add2(v[1], shift_z(v[2], -1)), -1)
        three = shift_z(v[3], 1)
    else:
        three = shift_z(add2(v[3], shift_z(v[2], 1)), 1)
        one = shift_z(v[1], -1)
    return (v[0].astype(F32) + one.astype(F32) + three.astype(F32)).astype(BF)


def gather_rel(v1, v2, v5, v6):
    w5 = jnp.stack([v5, swap_x(v5)])
    w6 = jnp.stack([v6, swap_y(v6)])
    s1 = gather_z(v1, 1)
    s2 = gather_z(v2, -1)
    w5 = jnp.stack([w5, swap_y(w5)])
    w6 = jnp.stack([w6, swap_x(w6)])
    s1 = jnp.stack([s1, swap_x(s1)])
    s2 = jnp.stack([s2, swap_y(s2)])
    o5 = gather_z(w5, 1)
    o6 = gather_z(w6, -1)
    first = (s1, swap_y(s1), s2, swap_x(s2), o5, o6)
    second = tuple(swap_c(v) for v in first)
    return first, second


def tied(v, w):
    return lax.optimization_barrier((v, w))


def scatter_core(near, far):
    p5, p6, p1, p2 = [add2(near[i], swap_c(far[i])) for i in (2, 3, 0, 1)]
    return p1, p2, p5, p6


def scatter_first(p1, p2, p5, p6):
    p5 = reduce_z(p5, 1)
    p6 = reduce_z(p6, -1)
    p1 = add2(p1[0], swap_y(p1[1]))
    p2 = add2(p2[0], swap_x(p2[1]))
    return p1, p2, p5, p6


def scatter_second(p1, p2, p5, p6):
    p5 = add2(p5[0], swap_y(p5[1]))
    p6 = add2(p6[0], swap_x(p6[1]))
    p1 = add2(p1[0], swap_x(p1[1]))
    p2 = add2(p2[0], swap_y(p2[1]))
    return p1, p2, p5, p6


def scatter_last(p1, p2, p5, p6):
    p5 = add2(p5[0], swap_x(p5[1]))
    p6 = add2(p6[0], swap_y(p6[1]))
    return reduce_z(p1, 1), reduce_z(p2, -1), p5, p6


def scatter_blocks(v):
    d = jnp.arange(16)
    v = jnp.take(v, sequence_at(d // 8, d // 2 % 4, d % 2), axis=0)
    v = (v[:8] + swap_c(v[8:])).reshape(4, 2, *v.shape[1:])
    v = v[:, 0] + swap_x(v[:, 1])
    one = shift_z(v[1] + shift_z(v[2], -1), -1)
    return v[0] + one + shift_z(v[3], 1)


def sequence_at(dc, dz, dx):
    at = lax.axis_index("dp")
    return (at // 4 - dz) % 4 * 4 + (at // 2 % 2 + dx) % 2 * 2 + (at % 2 + dc) % 2


def nn(a, b):
    return lax.dot_general(a, b, (((1,), (0,)), ((), ())), preferred_element_type=F32)


def nt(a, b):
    return lax.dot_general(a, b, (((1,), (1,)), ((), ())), preferred_element_type=F32)


def pick_rows(rank, slots):
    at_slot = lax.broadcasted_iota(jnp.int32, (slots, rank.shape[1]), 0).astype(F32)
    return jnp.concatenate(
        [(rank[e : e + 1, :] == at_slot).astype(F32).astype(BF) for e in range(rank.shape[0])],
        axis=0,
    )


def pick_cols(rank, slots):
    at_slot = lax.broadcasted_iota(jnp.int32, (rank.shape[0], slots), 1).astype(F32)
    return jnp.concatenate(
        [(rank[:, e : e + 1] == at_slot).astype(F32).astype(BF) for e in range(rank.shape[1])],
        axis=1,
    )


def cot_kernel(where, rank, cot_a, cot_b, down, cots, d_act):
    slots = cots.shape[2] // 2
    for dx, cot in enumerate((cot_a, cot_b)):
        both = nn(pick_rows(rank[dx], slots), cot[0]).astype(BF)
        for e in range(2):
            cots[e, 0, dx * slots : (dx + 1) * slots, :] = both[e * slots : (e + 1) * slots]
    for e in range(2):
        d_act[e, 0] = nt(cots[e, 0], down[e])


def expert_kernel(
    rank, rank_t, cols, d_act, x1a, x1b, x2a, x2b, x5, x6, w_gate, w_up,
    rows, scaled, d_g, d_u, t1, t2, t5, t6, back,
):
    slots = rows.shape[2] // 2
    n = x1a.shape[2]
    gates = []
    for dx, x2 in enumerate((x2a, x2b)):
        pick = pick_rows(rank[dx], slots)
        low, high = pick[:, :n], pick[:, n:]
        block1 = nn(low, x1a[dx, 0]) + nn(high, x1b[dx, 0])
        block2 = nn(low, x2[0, 0]) + nn(high, x2[1, 0])
        block5 = nn(low, x5[0, 0, dx]) + nn(high, x5[0, 1, dx])
        block6 = nn(low, x6[0, dx, 0]) + nn(high, x6[0, dx, 1])
        low = dx * slots
        for e in range(2):
            part = slice(e * slots, (e + 1) * slots)
            rows[e, 0, low : low + slots, 0:768] = block1[part].astype(BF)
            rows[e, 0, low : low + slots, 768:1536] = block2[part].astype(BF)
            rows[e, 0, low : low + slots, 1536:1792] = block5[part, :256].astype(BF)
            rows[e, 0, low : low + slots, 1792:2048] = block6[part].astype(BF)
            both = cols[e, 0:1, :] + cols[e, 1:2, :]
            gates.append(jnp.sum(block5[part, 256:] * both, axis=1, keepdims=True))
    extras = []
    for e in range(2):
        gate = jnp.concatenate([gates[e], gates[2 + e]], axis=0)
        g = nn(rows[e, 0], w_gate[e])
        u = nn(rows[e, 0], w_up[e])
        da = d_act[e, 0]
        sig = 1.0 / (1.0 + jnp.exp(-g))
        silu = g * sig
        act = silu * u
        scaled[e, 0] = (act * gate).astype(BF)
        d_gate = jnp.sum(act * da, axis=1, keepdims=True)
        da = da * gate
        dg = (da * u * sig * (1.0 + g * (1.0 - sig))).astype(BF)
        du = (da * silu).astype(BF)
        d_g[e, 0] = dg
        d_u[e, 0] = du
        high = d_gate.astype(BF).astype(F32)
        extras.append(high * cols[e, 0:1, :] + (d_gate - high) * cols[e, 1:2, :])
        dr = (nt(dg, w_gate[e]) + nt(du, w_up[e])).astype(BF)
        for dx in range(2):
            back[dx, e * slots : (e + 1) * slots, :] = dr[dx * slots : (dx + 1) * slots]
    extra = [
        jnp.concatenate([extras[e][dx * slots : (dx + 1) * slots] for e in range(2)], axis=0)
        for dx in range(2)
    ]
    put_back(rank_t, back, t1, t2, t5, t6, slots, extra)


def put_back(rank_t, back, t1, t2, t5, t6, slots, extra=None):
    for dx in range(2):
        pick_t = pick_cols(rank_t[dx], slots)
        n = pick_t.shape[0] // 2
        p1, p2, p5, p6 = [
            nn(pick_t, back[dx, :, a:b]).astype(BF) for a, b in zip(SPLIT[:-1], SPLIT[1:])
        ]
        for dy in range(2):
            half = slice(dy * n, (dy + 1) * n)
            t1[dy, dx, 0] = p1[half]
            t2[dx, dy, 0] = p2[half]
            t5[0, dy, dx, :, 0:256] = p5[half]
            t6[0, dx, dy] = p6[half]
        if extra is not None:
            p7 = nn(pick_t, extra[dx].astype(BF)).astype(BF)
            for dy in range(2):
                t5[0, dy, dx, :, 256:] = p7[dy * n : (dy + 1) * n]


def out_kernel(rank_t, scaled, down, t1, t2, t5, t6, back):
    slots = scaled.shape[2] // 2
    for e in range(2):
        y = nn(scaled[e, 0], down[e]).astype(BF)
        for dx in range(2):
            back[dx, e * slots : (e + 1) * slots, :] = y[dx * slots : (dx + 1) * slots]
    put_back(rank_t, back, t1, t2, t5, t6, slots)


def pair(*tail):
    return pl.BlockSpec((2, *tail), lambda i, *_: (i,) + (0,) * len(tail))


def z_last(*lead):
    def spec(rows, columns):
        return pl.BlockSpec(
            (*lead, 1, rows, columns), lambda i, *_: (0,) * len(lead) + (i, 0, 0)
        )

    return spec


def z_first(rows, columns):
    return pl.BlockSpec((1, 2, 2, rows, columns), lambda i, *_: (i, 0, 0, 0, 0))


def block_specs(n, extra):
    return [z_last(2, 2)(n, 768), z_last(2, 2)(n, 768), z_first(n, 256 + extra), z_first(n, 256)]


def block_shapes(n, extra):
    shapes = [(2, 2, 4, n, 768), (2, 2, 4, n, 768), (4, 2, 2, n, 256 + extra), (4, 2, 2, n, 256)]
    return [shaped(v, BF) for v in shapes]


def by_expert(*tail):
    return pl.BlockSpec((2, 1, *tail), lambda i, *_: (0, i) + (0,) * len(tail))


def fixed(*shape):
    return pl.BlockSpec(
        shape, lambda i, *_: (0,) * len(shape), pipeline_mode=pl.Buffered(1)
    )


def shaped(shape, kind):
    return jax.ShapeDtypeStruct(shape, kind)


LIMIT = pltpu.CompilerParams(vmem_limit_bytes=60000 * 1024)


def run_cots(where, rank, cot_all, down, slots):
    seq, width = cot_all.shape[1:]
    ff = down.shape[1]
    return pl.pallas_call(
        cot_kernel,
        grid_spec=pltpu.PrefetchScalarGridSpec(
            num_scalar_prefetch=1,
            grid=(4,),
            in_specs=[
                pair(2, seq),
                pl.BlockSpec((1, seq, width), lambda i, w: (w[2 * i], 0, 0)),
                pl.BlockSpec((1, seq, width), lambda i, w: (w[2 * i + 1], 0, 0)),
                fixed(2, ff, width),
            ],
            out_specs=[by_expert(2 * slots, width), by_expert(2 * slots, ff)],
        ),
        out_shape=[shaped((2, 4, 2 * slots, width), BF), shaped((2, 4, 2 * slots, ff), F32)],
        compiler_params=LIMIT,
        name="cots",
    )(where, rank, cot_all, cot_all, down)


def run_experts(rank, rank_t, cols, d_act, parts, w_gate, w_up, slots):
    s1, s1y, s2, s2x, o5, o6 = parts
    n = s1.shape[2]
    seq, width, ff = 2 * n, w_gate.shape[1], w_gate.shape[2]
    return pl.pallas_call(
        expert_kernel,
        grid=(4,),
        in_specs=[
            pair(2, seq),
            pair(seq, 2),
            fixed(*cols.shape),
            by_expert(2 * slots, ff),
            z_last(2)(n, 768),
            z_last(2)(n, 768),
            z_last(2)(n, 768),
            z_last(2)(n, 768),
            z_first(n, 384),
            z_first(n, 256),
            fixed(2, width, ff),
            fixed(2, width, ff),
        ],
        out_specs=[
            by_expert(2 * slots, width),
            by_expert(2 * slots, ff),
            by_expert(2 * slots, ff),
            by_expert(2 * slots, ff),
        ]
        + block_specs(n, 128),
        out_shape=[
            shaped((2, 4, 2 * slots, width), BF),
            shaped((2, 4, 2 * slots, ff), BF),
            shaped((2, 4, 2 * slots, ff), BF),
            shaped((2, 4, 2 * slots, ff), BF),
        ]
        + block_shapes(n, 128),
        scratch_shapes=[pltpu.VMEM((2, 2 * slots, width), BF)],
        compiler_params=LIMIT,
        name="experts",
    )(
        rank, rank_t, cols, d_act, s1, s1y, s2, s2x, o5, o6, w_gate, w_up,
    )


def run_outs(rank_t, scaled, down, slots):
    seq, ff, width = rank_t.shape[1], down.shape[1], down.shape[2]
    return pl.pallas_call(
        out_kernel,
        grid=(4,),
        in_specs=[pair(seq, 2), by_expert(2 * slots, ff), fixed(2, ff, width)],
        out_specs=block_specs(seq // 2, 0),
        out_shape=block_shapes(seq // 2, 0),
        scratch_shapes=[pltpu.VMEM((2, 2 * slots, width), BF)],
        compiler_params=LIMIT,
        name="outs",
    )(rank_t, scaled, down)


def flip(v, axis, y):
    a, b = jnp.split(v, 2, axis=axis)
    return jnp.where(y == 0, v, jnp.concatenate([b, a], axis=axis))


def moe_small(
    ids_all, cot_all, ffn_in, gate_x, gate_weight, up_weight, down_weight, experts, slots
):
    dp_at = lax.axis_index("dp")
    y = lax.axis_index("tensor")
    seq = ids_all.shape[1]
    mine = dp_at * 2 + jnp.arange(2, dtype=jnp.int32)
    mask = jnp.any(ids_all[:, None, :, :] == mine[None, :, None, None], axis=3)
    before = (jnp.arange(seq)[:, None] < jnp.arange(seq)[None, :]).astype(BF)
    rank = jnp.einsum("gea,ab->geb", mask.astype(BF), before, preferred_element_type=F32)
    rank = jnp.where(mask, rank, -1.0)
    d = jnp.arange(16)
    where = sequence_at(d // 8, d // 2 % 4, d % 2)
    rank = jnp.take(rank, where, axis=0)
    rank_rel = flip(rank, 2, y)
    rank_t = jnp.swapaxes(rank_rel, 1, 2)
    column = jnp.arange(128)
    cols = (
        column[None, None, :] == (mine[:, None] + jnp.array([[0, experts]]))[:, :, None]
    ).astype(F32)
    half = lambda v, k: v[8 * k : 8 * k + 8]
    where = where.astype(jnp.int32)

    cots, d_act = zip(*[run_cots(half(where, k), half(rank, k), cot_all, down_weight, slots) for k in (0, 1)])
    v1, v2, v5, v6 = [ffn_in[:, a:b] for a, b in zip(SPLIT[:-1], SPLIT[1:])]
    parts = gather_rel(v1, v2, jnp.concatenate([v5, gate_x], axis=1), v6)
    far = run_experts(half(rank_rel, 1), half(rank_t, 1), cols, d_act[1], parts[1], gate_weight, up_weight, slots)
    near = run_experts(half(rank_rel, 0), half(rank_t, 0), cols, d_act[0], parts[0], gate_weight, up_weight, slots)
    outs = [run_outs(half(rank_t, k), (near, far)[k][1], down_weight, slots) for k in (0, 1)]
    total = lambda spec, a, b: jnp.einsum(spec, a[0], b[0], preferred_element_type=F32) + jnp.einsum(
        spec, a[1], b[1], preferred_element_type=F32
    )
    kept = lambda i: (near[i], far[i])
    gate_grad = total("egsd,egsf->edf", kept(0), kept(2))
    up_grad = total("egsd,egsf->edf", kept(0), kept(3))
    down_grad = total("egsf,egsd->efd", kept(1), cots)
    step = scatter_second(*scatter_first(*scatter_core(near[4:], far[4:])))
    outs = scatter_core(*outs)
    step, (outs, gate_grad, up_grad, down_grad) = tied(step, (outs, gate_grad, up_grad, down_grad))
    d1, d2, d5, d6 = scatter_last(*step)
    d_sum = jnp.concatenate([d1, d2, d5[:, :256], d6, d5[:, 256:]], axis=1)
    d_sum, y_sum = tied(d_sum, outs)
    d_sum = d_sum.astype(F32)
    return d_sum, y_sum, gate_grad, up_grad, down_grad


def moe_large(
    ids_all, cotangent, ffn_in, gate_x, gate_weight, up_weight, down_weight, experts, slots
):
    dp, seq = ids_all.shape[:2]
    local = gate_weight.shape[0]
    dp_at = lax.axis_index("dp")
    mine = dp_at * local + jnp.arange(local, dtype=jnp.int32)
    mask = jnp.any(ids_all[:, :, None, :] == mine[None, None, :, None], axis=3).astype(BF)
    gate_all = gather_all(gate_x).reshape(dp, seq, -1)
    before = (jnp.arange(seq)[:, None] > jnp.arange(seq)[None, :]).astype(BF)
    rank = jnp.einsum("ab,gbe->gea", before, mask, preferred_element_type=F32)
    rank = jnp.where(jnp.swapaxes(mask, 1, 2) > 0, rank, -1.0)
    pick = (rank[:, :, None, :] == jnp.arange(slots, dtype=F32)[None, None, :, None]).astype(BF)

    cots = dispatch(pick, cotangent, dp, seq, None)
    rows = dispatch(pick, ffn_in, dp, seq, cots)
    gate_tok = lax.dynamic_slice_in_dim(gate_all, dp_at * local, local, 2).astype(
        F32
    ) + lax.dynamic_slice_in_dim(gate_all, experts + dp_at * local, local, 2).astype(F32)
    gate_slot = jnp.sum(pick.astype(F32) * jnp.swapaxes(gate_tok, 1, 2)[:, :, None, :], axis=3)

    g_proj = jnp.einsum("gesd,edf->gesf", rows, gate_weight, preferred_element_type=F32)
    u_proj = jnp.einsum("gesd,edf->gesf", rows, up_weight, preferred_element_type=F32)
    d_act = jnp.einsum("gesd,efd->gesf", cots, down_weight, preferred_element_type=F32)
    sig = 1.0 / (1.0 + jnp.exp(-g_proj))
    silu = g_proj * sig
    act = silu * u_proj
    scaled = (act * gate_slot[..., None]).astype(BF)
    d_gate_slot = jnp.sum(act * d_act, axis=3)
    d_act = d_act * gate_slot[..., None]
    d_g = (d_act * u_proj * sig * (1.0 + g_proj * (1.0 - sig))).astype(BF)
    d_u = (d_act * silu).astype(BF)
    d_rows = (
        jnp.einsum("gesf,edf->gesd", d_g, gate_weight, preferred_element_type=F32)
        + jnp.einsum("gesf,edf->gesd", d_u, up_weight, preferred_element_type=F32)
    ).astype(BF)
    dg_high, dg_low = split2(d_gate_slot)
    column = jnp.arange(lanes(2 * experts))
    high_col = (column[None, :] == mine[:, None])[None, :, None, :]
    low_col = (column[None, :] == experts + mine[:, None])[None, :, None, :]
    extra = jnp.where(high_col, dg_high[..., None], jnp.where(low_col, dg_low[..., None], 0.0))
    d_rows = jnp.concatenate([d_rows, extra.astype(BF)], axis=3)
    d_sum = combine(pick, d_rows, dp, seq, None)

    y_rows = jnp.einsum("gesf,efd->gesd", scaled, down_weight, preferred_element_type=F32)
    y_sum = combine(pick, y_rows.astype(BF), dp, seq, d_sum)
    down_grad = jnp.einsum("gesf,gesd->efd", scaled, cots, preferred_element_type=F32)
    gate_grad = jnp.einsum("gesd,gesf->edf", rows, d_g, preferred_element_type=F32)
    up_grad = jnp.einsum("gesd,gesf->edf", rows, d_u, preferred_element_type=F32)

    return d_sum, y_sum, gate_grad, up_grad, down_grad


def pad_to(v, width):
    return jnp.pad(v, ((0, 0), (0, width - v.shape[1])))


def lanes(count):
    return -(-count // 128) * 128


def on_device(
    tokens,
    attn_gain,
    q_weight,
    key_matrix,
    value_matrix,
    o_weight,
    query_norm_gain,
    k_gain,
    ffn_gain,
    router_weight,
    gate_weight,
    up_weight,
    down_weight,
    expert_ids,
    cotangent,
):
    dp = lax.axis_size("dp")
    tensor = lax.axis_size("tensor")
    dp_at = lax.axis_index("dp")
    own, width = tokens.shape
    seq = expert_ids.shape[0]
    begin = lax.axis_index("tensor") * own
    local = gate_weight.shape[0]
    experts = local * dp
    slots = 10 * seq * expert_ids.shape[1] // (8 * experts)
    slots = -(-slots // 16) * 16
    shard = q_weight.shape[0]
    gshard = query_norm_gain.shape[0]
    hq = q_weight.shape[1] // HEAD
    hk = key_matrix.shape[1] // HEAD
    group = hq // hk
    qkv_width = (hq + 2 * hk) * HEAD
    top = expert_ids.shape[1]
    fast = (dp, tensor, local, seq, width) == (16, 2, 2, 384, 2048)

    arange_e = jnp.arange(experts, dtype=jnp.int32)
    own_ids = lax.dynamic_slice_in_dim(expert_ids, begin, own, 0)
    own_mask = jnp.any(own_ids[:, :, None] == arange_e[None, None, :], axis=1)

    gain_rows = jnp.stack(
        [
            attn_gain,
            ffn_gain,
            jnp.pad(query_norm_gain, (0, shard - gshard)),
            jnp.pad(k_gain, (0, shard - gshard)),
        ],
        axis=1,
    )
    ids_rows = expert_ids.reshape(shard, -1).astype(BF)
    small = jnp.concatenate([router_weight, gain_rows, ids_rows], axis=1)
    small = pad_to(small, lanes(small.shape[1]))
    all_in = gather_dp(jnp.concatenate([q_weight, key_matrix, value_matrix, small], axis=1))
    layer_in = gather_y(tokens)
    o_t = gather_dp(o_weight.T)
    if fast:
        cot_all = gather_dp(gather_y(cotangent)).reshape(dp, seq, width)

    w_qkv = all_in[:, :qkv_width]
    router = all_in[:, qkv_width : qkv_width + experts]
    gains = all_in[:, qkv_width + experts : qkv_width + experts + 4].astype(F32)
    ids_all = all_in[:, qkv_width + experts + 4 :][:, : seq * top // shard]
    ids_all = ids_all.astype(jnp.int32).reshape(dp, seq, top)
    attn_gain32 = gains[:, 0]
    ffn_gain32 = gains[:, 1]
    q_gain32 = gains[:, 2].reshape(dp, shard)[:, :gshard].reshape(-1)
    k_gain32 = gains[:, 3].reshape(dp, shard)[:, :gshard].reshape(-1)

    residual = layer_in.astype(F32)
    normed = rms(residual, attn_gain32).astype(BF)
    qkv = dot(normed, w_qkv, 1, 0)
    cos, sin = rope_tables(seq)
    q_raw = qkv[:, : hq * HEAD].reshape(seq, hq, HEAD)
    k_raw = qkv[:, hq * HEAD : (hq + hk) * HEAD].reshape(seq, hk, HEAD)
    v_low = qkv[:, (hq + hk) * HEAD :].astype(BF).reshape(seq, hk, HEAD)
    q_low = rope(rms(q_raw, q_gain32), cos, sin).astype(BF).reshape(seq, hk, group, HEAD)
    k_low = rope(rms(k_raw, k_gain32), cos, sin).astype(BF)
    causal = jnp.arange(seq)[:, None] >= jnp.arange(seq)[None, :]
    scale = HEAD ** (-0.5)
    scores = jnp.einsum("qhgd,khd->hgqk", q_low, k_low, preferred_element_type=F32) * scale
    expo = jnp.where(causal, jnp.exp(scores), 0.0)
    total = jnp.sum(expo, axis=-1, keepdims=True)
    probs = expo / total
    context = jnp.einsum("hgqk,khd->qhgd", probs.astype(BF), v_low, preferred_element_type=F32)
    context = context.reshape(seq, hq * HEAD).astype(BF)
    hidden = tokens.astype(F32) + scatter_y(dot(context, o_t, 1, 1))

    ffn_in = rms(hidden, ffn_gain32).astype(BF)
    logits = dot(ffn_in, router, 1, 0)
    chosen = jnp.where(own_mask, jnp.exp(logits), 0.0)
    gates = chosen / jnp.sum(chosen, axis=1, keepdims=True)
    gate_high, gate_low = split2(gates)
    gate_x = pad_to(jnp.concatenate([gate_high, gate_low], axis=1), lanes(2 * experts))
    args = (gate_weight, up_weight, down_weight, experts, slots)
    if fast:
        d_sum, y_sum, gate_grad, up_grad, down_grad = moe_small(
            ids_all, cot_all, ffn_in, gate_x, *args
        )
    else:
        d_sum, y_sum, gate_grad, up_grad, down_grad = moe_large(
            ids_all, cotangent, ffn_in, gate_x, *args
        )
    d_gates = d_sum[:, width : width + experts] + d_sum[:, width + experts : width + 2 * experts]
    d_logits = gates * (d_gates - jnp.sum(gates * d_gates, axis=1, keepdims=True))
    d_high, d_low = split2(d_logits)
    d_ffn = d_sum[:, :width] + dot(d_high, router, 1, 1) + dot(d_low, router, 1, 1)
    router_part = dot(ffn_in, d_high, 0, 0) + dot(ffn_in, d_low, 0, 0)
    d_hidden, ffn_gain_rows = rms_back(hidden, ffn_gain32, d_ffn)
    ffn_gain_part = jnp.sum(ffn_gain_rows, axis=0)
    d_hidden = d_hidden + cotangent.astype(F32)
    d_attn = gather_y(d_hidden.astype(BF))

    o_part = dot(d_attn, context, 0, 0).astype(BF)
    d_attn, o_part = tied(d_attn, o_part)
    o_sum = scatter_dp(o_part).astype(F32)
    if fast:
        y_sum = scatter_first(*y_sum)
    d_context = dot(d_attn, o_t, 1, 0).astype(BF).reshape(seq, hk, group, HEAD)
    d_probs = jnp.einsum("qhgd,khd->hgqk", d_context, v_low, preferred_element_type=F32)
    d_values = jnp.einsum("hgqk,qhgd->khd", probs.astype(BF), d_context, preferred_element_type=F32)
    d_scores = probs * (d_probs - jnp.sum(probs * d_probs, axis=-1, keepdims=True))
    d_scores = d_scores.astype(BF)
    if fast:
        d_scores, y_sum = tied(d_scores, y_sum)
        y_sum = scatter_second(*y_sum)
    d_q = jnp.einsum("hgqk,khd->qhgd", d_scores, k_low, preferred_element_type=F32) * scale
    d_k = jnp.einsum("hgqk,qhgd->khd", d_scores, q_low, preferred_element_type=F32) * scale
    d_q_raw, q_gain_rows = rms_back(q_raw, q_gain32, rope_back(d_q.reshape(seq, hq, HEAD), cos, sin))
    d_k_raw, k_gain_rows = rms_back(k_raw, k_gain32, rope_back(d_k, cos, sin))
    d_qkv = jnp.concatenate(
        [
            d_q_raw.reshape(seq, hq * HEAD).astype(BF),
            d_k_raw.reshape(seq, hk * HEAD).astype(BF),
            d_values.reshape(seq, hk * HEAD).astype(BF),
        ],
        axis=1,
    )
    qkv_part = dot(normed, d_qkv, 0, 0).astype(BF)
    if fast:
        qkv_part, y_sum = tied(qkv_part, y_sum)
        y_sum = jnp.concatenate(scatter_last(*y_sum), axis=1).astype(F32)
    d_qkv, qkv_part = tied(d_qkv, qkv_part)
    qkv_sum = scatter_dp(qkv_part).astype(F32)
    output = (hidden + y_sum).astype(BF)
    d_normed = scatter_y(dot(d_qkv, w_qkv, 1, 1))
    d_tokens, attn_gain_rows = rms_back(tokens.astype(F32), attn_gain32, d_normed)
    tokens_grad = d_tokens + d_hidden

    spread = lambda v: jnp.pad(v.reshape(dp, gshard), ((0, 0), (0, shard - gshard))).reshape(-1)
    small_part = jnp.concatenate(
        [
            router_part,
            jnp.stack(
                [
                    jnp.sum(attn_gain_rows, axis=0),
                    ffn_gain_part,
                    spread(jnp.sum(q_gain_rows, axis=(0, 1))),
                    spread(jnp.sum(k_gain_rows, axis=(0, 1))),
                ],
                axis=1,
            ),
        ],
        axis=1,
    )
    small_part = pad_to(small_part, lanes(experts + 4))
    if fast:
        small_sum = scatter_blocks(small_part.reshape(dp, shard, -1))
    else:
        small_sum = scatter_dp(small_part)
    small_sum = small_sum + swap_y(small_sum)
    return (
        output,
        tokens_grad,
        small_sum[:, experts],
        qkv_sum[:, : hq * HEAD],
        qkv_sum[:, hq * HEAD : (hq + hk) * HEAD],
        qkv_sum[:, (hq + hk) * HEAD :],
        o_sum.T,
        small_sum[:gshard, experts + 2],
        small_sum[:gshard, experts + 3],
        small_sum[:, experts + 1],
        small_sum[:, :experts],
        gate_grad,
        up_grad,
        down_grad,
    )


def solution(mesh):
    rows = P(("dp", "tensor"), None)
    both = P("dp", "tensor")
    return jax.shard_map(
        on_device,
        mesh=mesh,
        in_specs=(
            rows,
            P("dp"),
            both,
            both,
            both,
            P("tensor", "dp"),
            P("dp"),
            P("dp"),
            P("dp"),
            P("dp", None),
            P("dp", None, "tensor"),
            P("dp", None, "tensor"),
            P("dp", "tensor", None),
            P("dp", None),
            rows,
        ),
        out_specs=(
            rows,
            rows,
            P("dp"),
            both,
            both,
            both,
            P("tensor", "dp"),
            P("dp"),
            P("dp"),
            P("dp"),
            P("dp", None),
            P("dp", None, "tensor"),
            P("dp", None, "tensor"),
            P("dp", "tensor", None),
        ),
        check_vma=False,
    )
```

```python
import jax
import jax.numpy as jnp
from jax import lax
from jax.experimental import pallas as pl
from jax.experimental.pallas import tpu as pltpu
from jax.sharding import PartitionSpec as P

HEAD = 128
EPS = 1e-06
THETA = 1000000.0
BF = jnp.bfloat16
F32 = jnp.float32


def dot(a, b, ca, cb):
    return lax.dot_general(a, b, (((ca,), (cb,)), ((), ())), preferred_element_type=F32)


def rms(v, gain):
    return v * lax.rsqrt(jnp.mean(v * v, axis=-1, keepdims=True) + EPS) * gain


def rms_back(v, gain, u):
    inv = lax.rsqrt(jnp.mean(v * v, axis=-1, keepdims=True) + EPS)
    ug = u * gain
    grad = ug * inv - v * (jnp.mean(ug * v, axis=-1, keepdims=True) * inv * inv * inv)
    return grad, u * v * inv


def rope(v, cos, sin):
    a, b = v[..., : HEAD // 2], v[..., HEAD // 2 :]
    return jnp.concatenate([a * cos - b * sin, b * cos + a * sin], axis=-1)


def rope_back(v, cos, sin):
    a, b = v[..., : HEAD // 2], v[..., HEAD // 2 :]
    return jnp.concatenate([a * cos + b * sin, b * cos - a * sin], axis=-1)


def rope_tables(count):
    inverse = THETA ** (-(jnp.arange(HEAD // 2, dtype=F32) * 2.0 / HEAD))
    angles = jnp.arange(count, dtype=F32)[:, None] * inverse[None, :]
    return jnp.cos(angles)[:, None, :], jnp.sin(angles)[:, None, :]


def split2(v):
    high = v.astype(BF)
    return high, (v - high.astype(F32)).astype(BF)


def gather_dp(v):
    return lax.all_gather(v, "dp", axis=0, tiled=True)


def gather_all(v):
    return lax.all_gather(v, ("dp", "tensor"), axis=0, tiled=True)


def scatter_all(v):
    return lax.psum_scatter(v, ("dp", "tensor"), scatter_dimension=0, tiled=True)


def scatter_dp(v):
    return lax.psum_scatter(v, "dp", scatter_dimension=0, tiled=True)


def pieces(width, dp, seq):
    count = 1 if dp * seq <= 8192 else 4
    step = width // count // 128 * 128
    edges = [step * i for i in range(count)] + [width]
    return list(zip(edges[:-1], edges[1:]))


def after(v, earlier):
    return v if earlier is None else lax.optimization_barrier((v, earlier))[0]


def dispatch(pick, own, dp, seq, earlier):
    blocks = []
    for low, high in pieces(own.shape[1], dp, seq):
        every = gather_all(after(own[:, low:high], earlier)).reshape(dp, seq, high - low)
        block = jnp.einsum("gest,gtd->gesd", pick, every, preferred_element_type=F32).astype(BF)
        blocks.append(block)
        earlier = block if len(pieces(own.shape[1], dp, seq)) > 1 else None
    return jnp.concatenate(blocks, axis=3)


def combine(pick, rows, dp, seq, earlier):
    blocks = []
    for low, high in pieces(rows.shape[3], dp, seq):
        tok = jnp.einsum(
            "gest,gesd->gtd",
            pick,
            after(rows[:, :, :, low:high], earlier),
            preferred_element_type=F32,
        ).astype(BF)
        blocks.append(scatter_all(tok.reshape(dp * seq, high - low)))
        earlier = blocks[-1] if len(pieces(rows.shape[3], dp, seq)) > 1 else None
    return jnp.concatenate(blocks, axis=1).astype(F32)


GRID = [(z, x, c) for z in range(4) for x in range(2) for c in range(2)]
SPLIT = (0, 768, 1536, 1792, 2048)


def at(z, x, c):
    return z % 4 * 4 + x % 2 * 2 + c % 2


def shift_z(v, k):
    return lax.ppermute(v, "dp", [(at(z, x, c), at(z + k, x, c)) for z, x, c in GRID])


def swap_x(v):
    return lax.ppermute(v, "dp", [(at(z, x, c), at(z, x + 1, c)) for z, x, c in GRID])


def swap_c(v):
    return lax.ppermute(v, "dp", [(at(z, x, c), at(z, x, c + 1)) for z, x, c in GRID])


def swap_y(v):
    return lax.ppermute(v, "tensor", [(0, 1), (1, 0)])


def gather_y(v):
    other = swap_y(v)
    first = lax.axis_index("tensor") == 0
    return jnp.concatenate([jnp.where(first, v, other), jnp.where(first, other, v)])


def scatter_y(v):
    a, b = jnp.split(v, 2)
    first = lax.axis_index("tensor") == 0
    kept, sent = jnp.where(first, a, b), jnp.where(first, b, a)
    return kept.astype(F32) + swap_y(sent.astype(BF)).astype(F32)


def gather_z(v, way):
    one, three = shift_z(v, 1), shift_z(v, -1)
    two = shift_z(one, 1) if way > 0 else shift_z(three, -1)
    return jnp.stack([v, one, two, three])


def add2(a, b):
    return (a.astype(F32) + b.astype(F32)).astype(BF)


def reduce_z(v, way):
    if way > 0:
        one = shift_z(add2(v[1], shift_z(v[2], -1)), -1)
        three = shift_z(v[3], 1)
    else:
        three = shift_z(add2(v[3], shift_z(v[2], 1)), 1)
        one = shift_z(v[1], -1)
    return (v[0].astype(F32) + one.astype(F32) + three.astype(F32)).astype(BF)


def tied(v, w):
    return lax.optimization_barrier((v, w))


def gather_rel(v1, v2, v5, v6, aside):
    w5 = jnp.stack([v5, swap_x(v5)])
    w6 = jnp.stack([v6, swap_y(v6)])
    s1 = gather_z(v1, 1)
    s2 = gather_z(v2, -1)
    w5 = jnp.stack([w5, swap_y(w5)])
    w6 = jnp.stack([w6, swap_x(w6)])
    s1, s2, w5, w6 = lax.optimization_barrier((s1, s2, w5, w6))
    s1x, s2y = swap_x(s1), swap_y(s2)
    five = [shift_z(w5, 1), shift_z(w5, -1)]
    six = [shift_z(w6, 1), shift_z(w6, -1)]
    (five, six), (s1x, s2y) = tied((five, six), (s1x, s2y))
    s1 = jnp.stack([s1, s1x])
    s2 = jnp.stack([s2, s2y])
    s1y, s2x = swap_y(s1), swap_x(s2)
    o5 = jnp.stack([w5, five[0], shift_z(five[0], 1), five[1]])
    o6 = jnp.stack([w6, six[0], shift_z(six[1], -1), six[1]])
    (s1y, s2x), aside = tied((s1y, s2x), aside)
    first = (s1, s1y, s2, s2x, o5, o6)
    return first, tuple(swap_c(v) for v in first), aside


def scatter_core(near, far):
    p5, p6, p1, p2 = [add2(near[i], swap_c(far[i])) for i in (2, 3, 0, 1)]
    return lax.optimization_barrier((p1, p2, p5, p6))


def scatter_first(p1, p2, p5, p6):
    p5 = reduce_z(p5, 1)
    p6 = reduce_z(p6, -1)
    p1 = add2(p1[0], swap_y(p1[1]))
    p2 = add2(p2[0], swap_x(p2[1]))
    return p1, p2, p5, p6


def scatter_second(p1, p2, p5, p6):
    p5 = add2(p5[0], swap_y(p5[1]))
    p6 = add2(p6[0], swap_x(p6[1]))
    p1 = add2(p1[0], swap_x(p1[1]))
    p2 = add2(p2[0], swap_y(p2[1]))
    return p1, p2, p5, p6


def scatter_last(p1, p2, p5, p6):
    p5 = add2(p5[0], swap_x(p5[1]))
    p6 = add2(p6[0], swap_y(p6[1]))
    return reduce_z(p1, 1), reduce_z(p2, -1), p5, p6


def scatter_blocks(v):
    d = jnp.arange(16)
    v = jnp.take(v, sequence_at(d // 8, d // 2 % 4, d % 2), axis=0)
    v = (v[:8] + swap_c(v[8:])).reshape(4, 2, *v.shape[1:])
    v = v[:, 0] + swap_x(v[:, 1])
    one = shift_z(v[1] + shift_z(v[2], -1), -1)
    return v[0] + one + shift_z(v[3], 1)


def sequence_at(dc, dz, dx):
    at = lax.axis_index("dp")
    return (at // 4 - dz) % 4 * 4 + (at // 2 % 2 + dx) % 2 * 2 + (at % 2 + dc) % 2


def nn(a, b):
    return lax.dot_general(a, b, (((1,), (0,)), ((), ())), preferred_element_type=F32)


def nt(a, b):
    return lax.dot_general(a, b, (((1,), (1,)), ((), ())), preferred_element_type=F32)


def pick_rows(rank, slots):
    at_slot = lax.broadcasted_iota(jnp.int32, (slots, rank.shape[1]), 0).astype(F32)
    return jnp.concatenate(
        [(rank[e : e + 1, :] == at_slot).astype(F32).astype(BF) for e in range(rank.shape[0])],
        axis=0,
    )


def pick_cols(rank, slots):
    at_slot = lax.broadcasted_iota(jnp.int32, (rank.shape[0], slots), 1).astype(F32)
    return jnp.concatenate(
        [(rank[:, e : e + 1] == at_slot).astype(F32).astype(BF) for e in range(rank.shape[1])],
        axis=1,
    )


def cot_kernel(where, rank, cot_a, cot_b, down, cots, d_act):
    slots = cots.shape[2] // 2
    for dx, cot in enumerate((cot_a, cot_b)):
        both = nn(pick_rows(rank[dx], slots), cot[0]).astype(BF)
        for e in range(2):
            cots[e, 0, dx * slots : (dx + 1) * slots, :] = both[e * slots : (e + 1) * slots]
    for e in range(2):
        d_act[e, 0] = nt(cots[e, 0], down[e])


def expert_kernel(
    rank, rank_t, cols, d_act, x1a, x1b, x2a, x2b, x5, x6, w_gate, w_up,
    rows, scaled, d_g, d_u, t1, t2, t5, t6, back,
):
    slots = rows.shape[2] // 2
    n = x1a.shape[2]
    gates = []
    for dx, x2 in enumerate((x2a, x2b)):
        pick = pick_rows(rank[dx], slots)
        low, high = pick[:, :n], pick[:, n:]
        block1 = nn(low, x1a[dx, 0]) + nn(high, x1b[dx, 0])
        block2 = nn(low, x2[0, 0]) + nn(high, x2[1, 0])
        block5 = nn(low, x5[0, 0, dx]) + nn(high, x5[0, 1, dx])
        block6 = nn(low, x6[0, dx, 0]) + nn(high, x6[0, dx, 1])
        low = dx * slots
        for e in range(2):
            part = slice(e * slots, (e + 1) * slots)
            rows[e, 0, low : low + slots, 0:768] = block1[part].astype(BF)
            rows[e, 0, low : low + slots, 768:1536] = block2[part].astype(BF)
            rows[e, 0, low : low + slots, 1536:1792] = block5[part, :256].astype(BF)
            rows[e, 0, low : low + slots, 1792:2048] = block6[part].astype(BF)
            both = cols[e, 0:1, :] + cols[e, 1:2, :]
            gates.append(jnp.sum(block5[part, 256:] * both, axis=1, keepdims=True))
    extras = []
    for e in range(2):
        gate = jnp.concatenate([gates[e], gates[2 + e]], axis=0)
        g = nn(rows[e, 0], w_gate[e])
        u = nn(rows[e, 0], w_up[e])
        da = d_act[e, 0]
        sig = 1.0 / (1.0 + jnp.exp(-g))
        silu = g * sig
        act = silu * u
        scaled[e, 0] = (act * gate).astype(BF)
        d_gate = jnp.sum(act * da, axis=1, keepdims=True)
        da = da * gate
        dg = (da * u * sig * (1.0 + g * (1.0 - sig))).astype(BF)
        du = (da * silu).astype(BF)
        d_g[e, 0] = dg
        d_u[e, 0] = du
        high = d_gate.astype(BF).astype(F32)
        extras.append(high * cols[e, 0:1, :] + (d_gate - high) * cols[e, 1:2, :])
        dr = (nt(dg, w_gate[e]) + nt(du, w_up[e])).astype(BF)
        for dx in range(2):
            back[dx, e * slots : (e + 1) * slots, :] = dr[dx * slots : (dx + 1) * slots]
    extra = [
        jnp.concatenate([extras[e][dx * slots : (dx + 1) * slots] for e in range(2)], axis=0)
        for dx in range(2)
    ]
    put_back(rank_t, back, t1, t2, t5, t6, slots, extra)


def put_back(rank_t, back, t1, t2, t5, t6, slots, extra=None):
    for dx in range(2):
        pick_t = pick_cols(rank_t[dx], slots)
        n = pick_t.shape[0] // 2
        p1, p2, p5, p6 = [
            nn(pick_t, back[dx, :, a:b]).astype(BF) for a, b in zip(SPLIT[:-1], SPLIT[1:])
        ]
        for dy in range(2):
            half = slice(dy * n, (dy + 1) * n)
            t1[dy, dx, 0] = p1[half]
            t2[dx, dy, 0] = p2[half]
            t5[0, dy, dx, :, 0:256] = p5[half]
            t6[0, dx, dy] = p6[half]
        if extra is not None:
            p7 = nn(pick_t, extra[dx].astype(BF)).astype(BF)
            for dy in range(2):
                t5[0, dy, dx, :, 256:] = p7[dy * n : (dy + 1) * n]


def out_kernel(rank_t, scaled, down, t1, t2, t5, t6, back):
    slots = scaled.shape[2] // 2
    for e in range(2):
        y = nn(scaled[e, 0], down[e]).astype(BF)
        for dx in range(2):
            back[dx, e * slots : (e + 1) * slots, :] = y[dx * slots : (dx + 1) * slots]
    put_back(rank_t, back, t1, t2, t5, t6, slots)


def pair(*tail):
    return pl.BlockSpec((2, *tail), lambda i, *_: (i,) + (0,) * len(tail))


def z_last(*lead):
    def spec(rows, columns):
        return pl.BlockSpec(
            (*lead, 1, rows, columns), lambda i, *_: (0,) * len(lead) + (i, 0, 0)
        )

    return spec


def z_first(rows, columns):
    return pl.BlockSpec((1, 2, 2, rows, columns), lambda i, *_: (i, 0, 0, 0, 0))


def block_specs(n, extra):
    return [z_last(2, 2)(n, 768), z_last(2, 2)(n, 768), z_first(n, 256 + extra), z_first(n, 256)]


def block_shapes(n, extra):
    shapes = [(2, 2, 4, n, 768), (2, 2, 4, n, 768), (4, 2, 2, n, 256 + extra), (4, 2, 2, n, 256)]
    return [shaped(v, BF) for v in shapes]


def by_expert(*tail):
    return pl.BlockSpec((2, 1, *tail), lambda i, *_: (0, i) + (0,) * len(tail))


def fixed(*shape):
    return pl.BlockSpec(
        shape, lambda i, *_: (0,) * len(shape), pipeline_mode=pl.Buffered(1)
    )


def shaped(shape, kind):
    return jax.ShapeDtypeStruct(shape, kind)


LIMIT = pltpu.CompilerParams(vmem_limit_bytes=60000 * 1024)


def run_cots(where, rank, cot_all, down, slots):
    seq, width = cot_all.shape[1:]
    ff = down.shape[1]
    return pl.pallas_call(
        cot_kernel,
        grid_spec=pltpu.PrefetchScalarGridSpec(
            num_scalar_prefetch=1,
            grid=(4,),
            in_specs=[
                pair(2, seq),
                pl.BlockSpec((1, seq, width), lambda i, w: (w[2 * i], 0, 0)),
                pl.BlockSpec((1, seq, width), lambda i, w: (w[2 * i + 1], 0, 0)),
                fixed(2, ff, width),
            ],
            out_specs=[by_expert(2 * slots, width), by_expert(2 * slots, ff)],
        ),
        out_shape=[shaped((2, 4, 2 * slots, width), BF), shaped((2, 4, 2 * slots, ff), F32)],
        compiler_params=LIMIT,
        name="cots",
    )(where, rank, cot_all, cot_all, down)


def run_experts(rank, rank_t, cols, d_act, parts, w_gate, w_up, slots):
    s1, s1y, s2, s2x, o5, o6 = parts
    n = s1.shape[2]
    seq, width, ff = 2 * n, w_gate.shape[1], w_gate.shape[2]
    return pl.pallas_call(
        expert_kernel,
        grid=(4,),
        in_specs=[
            pair(2, seq),
            pair(seq, 2),
            fixed(*cols.shape),
            by_expert(2 * slots, ff),
            z_last(2)(n, 768),
            z_last(2)(n, 768),
            z_last(2)(n, 768),
            z_last(2)(n, 768),
            z_first(n, 384),
            z_first(n, 256),
            fixed(2, width, ff),
            fixed(2, width, ff),
        ],
        out_specs=[
            by_expert(2 * slots, width),
            by_expert(2 * slots, ff),
            by_expert(2 * slots, ff),
            by_expert(2 * slots, ff),
        ]
        + block_specs(n, 128),
        out_shape=[
            shaped((2, 4, 2 * slots, width), BF),
            shaped((2, 4, 2 * slots, ff), BF),
            shaped((2, 4, 2 * slots, ff), BF),
            shaped((2, 4, 2 * slots, ff), BF),
        ]
        + block_shapes(n, 128),
        scratch_shapes=[pltpu.VMEM((2, 2 * slots, width), BF)],
        compiler_params=LIMIT,
        name="experts",
    )(
        rank, rank_t, cols, d_act, s1, s1y, s2, s2x, o5, o6, w_gate, w_up,
    )


def run_outs(rank_t, scaled, down, slots):
    seq, ff, width = rank_t.shape[1], down.shape[1], down.shape[2]
    return pl.pallas_call(
        out_kernel,
        grid=(4,),
        in_specs=[pair(seq, 2), by_expert(2 * slots, ff), fixed(2, ff, width)],
        out_specs=block_specs(seq // 2, 0),
        out_shape=block_shapes(seq // 2, 0),
        scratch_shapes=[pltpu.VMEM((2, 2 * slots, width), BF)],
        compiler_params=LIMIT,
        name="outs",
    )(rank_t, scaled, down)


def flip(v, axis, y):
    a, b = jnp.split(v, 2, axis=axis)
    return jnp.where(y == 0, v, jnp.concatenate([b, a], axis=axis))


def slot_plan(ids_all, experts):
    y = lax.axis_index("tensor")
    seq = ids_all.shape[1]
    mine = lax.axis_index("dp") * 2 + jnp.arange(2, dtype=jnp.int32)
    mask = jnp.any(ids_all[:, None, :, :] == mine[None, :, None, None], axis=3)
    before = (jnp.arange(seq)[:, None] < jnp.arange(seq)[None, :]).astype(BF)
    rank = jnp.einsum("gea,ab->geb", mask.astype(BF), before, preferred_element_type=F32)
    rank = jnp.where(mask, rank, -1.0)
    d = jnp.arange(16)
    where = sequence_at(d // 8, d // 2 % 4, d % 2)
    rank = jnp.take(rank, where, axis=0)
    rank_rel = flip(rank, 2, y)
    rank_t = jnp.swapaxes(rank_rel, 1, 2)
    column = jnp.arange(128)
    cols = (
        column[None, None, :] == (mine[:, None] + jnp.array([[0, experts]]))[:, :, None]
    ).astype(F32)
    halves = lambda v: (v[:8], v[8:])
    return halves(where.astype(jnp.int32)), halves(rank), halves(rank_rel), halves(rank_t), cols


def moe_small(plan, cot_all, ffn_in, gate_x, gate_weight, up_weight, down_weight, slots):
    where, rank, rank_rel, rank_t, cols = plan
    both = [run_cots(where[k], rank[k], cot_all, down_weight, slots) for k in (0, 1)]
    v1, v2, v5, v6 = [ffn_in[:, a:b] for a, b in zip(SPLIT[:-1], SPLIT[1:])]
    *parts, both = gather_rel(v1, v2, jnp.concatenate([v5, gate_x], axis=1), v6, both)
    cots, d_act = zip(*both)
    far, near = [
        run_experts(
            rank_rel[k], rank_t[k], cols, d_act[k], parts[k], gate_weight, up_weight, slots
        )
        for k in (1, 0)
    ]
    step = scatter_core(near[4:], far[4:])
    (near, far, cots), step = tied((near[:4], far[:4], cots), step)
    kept = lambda i: (near[i], far[i])
    outs = scatter_core(*[run_outs(rank_t[k], kept(1)[k], down_weight, slots) for k in (0, 1)])
    total = lambda spec, a, b: jnp.einsum(spec, a[0], b[0], preferred_element_type=F32) + jnp.einsum(
        spec, a[1], b[1], preferred_element_type=F32
    )
    gate_grad = total("egsd,egsf->edf", kept(0), kept(2))
    up_grad = total("egsd,egsf->edf", kept(0), kept(3))
    down_grad = total("egsf,egsd->efd", kept(1), cots)
    step = scatter_second(*scatter_first(*step))
    step, (outs, gate_grad, up_grad, down_grad) = tied(step, (outs, gate_grad, up_grad, down_grad))
    d1, d2, d5, d6 = scatter_last(*step)
    d_sum = jnp.concatenate([d1, d2, d5[:, :256], d6, d5[:, 256:]], axis=1)
    d_sum, y_sum = tied(d_sum, outs)
    d_sum = d_sum.astype(F32)
    return d_sum, y_sum, gate_grad, up_grad, down_grad


def moe_large(
    ids_all, cotangent, ffn_in, gate_x, gate_weight, up_weight, down_weight, experts, slots
):
    dp, seq = ids_all.shape[:2]
    local = gate_weight.shape[0]
    dp_at = lax.axis_index("dp")
    mine = dp_at * local + jnp.arange(local, dtype=jnp.int32)
    mask = jnp.any(ids_all[:, :, None, :] == mine[None, None, :, None], axis=3).astype(BF)
    gate_all = gather_all(gate_x).reshape(dp, seq, -1)
    before = (jnp.arange(seq)[:, None] > jnp.arange(seq)[None, :]).astype(BF)
    rank = jnp.einsum("ab,gbe->gea", before, mask, preferred_element_type=F32)
    rank = jnp.where(jnp.swapaxes(mask, 1, 2) > 0, rank, -1.0)
    pick = (rank[:, :, None, :] == jnp.arange(slots, dtype=F32)[None, None, :, None]).astype(BF)

    cots = dispatch(pick, cotangent, dp, seq, None)
    rows = dispatch(pick, ffn_in, dp, seq, cots)
    gate_tok = lax.dynamic_slice_in_dim(gate_all, dp_at * local, local, 2).astype(
        F32
    ) + lax.dynamic_slice_in_dim(gate_all, experts + dp_at * local, local, 2).astype(F32)
    gate_slot = jnp.sum(pick.astype(F32) * jnp.swapaxes(gate_tok, 1, 2)[:, :, None, :], axis=3)

    g_proj = jnp.einsum("gesd,edf->gesf", rows, gate_weight, preferred_element_type=F32)
    u_proj = jnp.einsum("gesd,edf->gesf", rows, up_weight, preferred_element_type=F32)
    d_act = jnp.einsum("gesd,efd->gesf", cots, down_weight, preferred_element_type=F32)
    sig = 1.0 / (1.0 + jnp.exp(-g_proj))
    silu = g_proj * sig
    act = silu * u_proj
    scaled = (act * gate_slot[..., None]).astype(BF)
    d_gate_slot = jnp.sum(act * d_act, axis=3)
    d_act = d_act * gate_slot[..., None]
    d_g = (d_act * u_proj * sig * (1.0 + g_proj * (1.0 - sig))).astype(BF)
    d_u = (d_act * silu).astype(BF)
    d_rows = (
        jnp.einsum("gesf,edf->gesd", d_g, gate_weight, preferred_element_type=F32)
        + jnp.einsum("gesf,edf->gesd", d_u, up_weight, preferred_element_type=F32)
    ).astype(BF)
    dg_high, dg_low = split2(d_gate_slot)
    column = jnp.arange(lanes(2 * experts))
    high_col = (column[None, :] == mine[:, None])[None, :, None, :]
    low_col = (column[None, :] == experts + mine[:, None])[None, :, None, :]
    extra = jnp.where(high_col, dg_high[..., None], jnp.where(low_col, dg_low[..., None], 0.0))
    d_rows = jnp.concatenate([d_rows, extra.astype(BF)], axis=3)
    d_sum = combine(pick, d_rows, dp, seq, None)

    y_rows = jnp.einsum("gesf,efd->gesd", scaled, down_weight, preferred_element_type=F32)
    y_sum = combine(pick, y_rows.astype(BF), dp, seq, d_sum)
    down_grad = jnp.einsum("gesf,gesd->efd", scaled, cots, preferred_element_type=F32)
    gate_grad = jnp.einsum("gesd,gesf->edf", rows, d_g, preferred_element_type=F32)
    up_grad = jnp.einsum("gesd,gesf->edf", rows, d_u, preferred_element_type=F32)

    return d_sum, y_sum, gate_grad, up_grad, down_grad


def pad_to(v, width):
    return jnp.pad(v, ((0, 0), (0, width - v.shape[1])))


def lanes(count):
    return -(-count // 128) * 128


def on_device(
    tokens,
    attn_gain,
    q_weight,
    key_matrix,
    value_matrix,
    o_weight,
    query_norm_gain,
    k_gain,
    ffn_gain,
    router_weight,
    gate_weight,
    up_weight,
    down_weight,
    expert_ids,
    cotangent,
):
    dp = lax.axis_size("dp")
    tensor = lax.axis_size("tensor")
    dp_at = lax.axis_index("dp")
    own, width = tokens.shape
    seq = expert_ids.shape[0]
    begin = lax.axis_index("tensor") * own
    local = gate_weight.shape[0]
    experts = local * dp
    slots = 10 * seq * expert_ids.shape[1] // (8 * experts)
    slots = -(-slots // 16) * 16
    shard = q_weight.shape[0]
    gshard = query_norm_gain.shape[0]
    hq = q_weight.shape[1] // HEAD
    hk = key_matrix.shape[1] // HEAD
    group = hq // hk
    qkv_width = (hq + 2 * hk) * HEAD
    top = expert_ids.shape[1]
    fast = (dp, tensor, local, seq, width) == (16, 2, 2, 384, 2048)

    arange_e = jnp.arange(experts, dtype=jnp.int32)
    own_ids = lax.dynamic_slice_in_dim(expert_ids, begin, own, 0)
    own_mask = jnp.any(own_ids[:, :, None] == arange_e[None, None, :], axis=1)

    gain_rows = jnp.stack(
        [
            attn_gain,
            ffn_gain,
            jnp.pad(query_norm_gain, (0, shard - gshard)),
            jnp.pad(k_gain, (0, shard - gshard)),
        ],
        axis=1,
    )
    ids_rows = expert_ids.reshape(shard, -1).astype(BF)
    small = jnp.concatenate([router_weight, gain_rows, ids_rows], axis=1)
    small = pad_to(small, lanes(small.shape[1]))
    all_in = gather_dp(jnp.concatenate([q_weight, key_matrix, value_matrix, small], axis=1))
    layer_in = gather_y(tokens)
    o_t = gather_dp(o_weight.T)
    if fast:
        cot_all = gather_dp(gather_y(cotangent)).reshape(dp, seq, width)

    w_qkv = all_in[:, :qkv_width]
    router = all_in[:, qkv_width : qkv_width + experts]
    gains = all_in[:, qkv_width + experts : qkv_width + experts + 4].astype(F32)
    ids_all = all_in[:, qkv_width + experts + 4 :][:, : seq * top // shard]
    ids_all = ids_all.astype(jnp.int32).reshape(dp, seq, top)
    attn_gain32 = gains[:, 0]
    ffn_gain32 = gains[:, 1]
    q_gain32 = gains[:, 2].reshape(dp, shard)[:, :gshard].reshape(-1)
    k_gain32 = gains[:, 3].reshape(dp, shard)[:, :gshard].reshape(-1)

    residual = layer_in.astype(F32)
    normed = rms(residual, attn_gain32).astype(BF)
    qkv = dot(normed, w_qkv, 1, 0)
    cos, sin = rope_tables(seq)
    q_raw = qkv[:, : hq * HEAD].reshape(seq, hq, HEAD)
    k_raw = qkv[:, hq * HEAD : (hq + hk) * HEAD].reshape(seq, hk, HEAD)
    v_low = qkv[:, (hq + hk) * HEAD :].astype(BF).reshape(seq, hk, HEAD)
    q_low = rope(rms(q_raw, q_gain32), cos, sin).astype(BF).reshape(seq, hk, group, HEAD)
    k_low = rope(rms(k_raw, k_gain32), cos, sin).astype(BF)
    causal = jnp.arange(seq)[:, None] >= jnp.arange(seq)[None, :]
    scale = HEAD ** (-0.5)
    scores = jnp.einsum("qhgd,khd->hgqk", q_low, k_low, preferred_element_type=F32) * scale
    expo = jnp.where(causal, jnp.exp(scores), 0.0)
    total = jnp.sum(expo, axis=-1, keepdims=True)
    probs = expo / total
    context = jnp.einsum("hgqk,khd->qhgd", probs.astype(BF), v_low, preferred_element_type=F32)
    context = context.reshape(seq, hq * HEAD).astype(BF)
    if fast:
        context, plan = tied(context, slot_plan(ids_all, experts))
    hidden = tokens.astype(F32) + scatter_y(dot(context, o_t, 1, 1))

    ffn_in = rms(hidden, ffn_gain32).astype(BF)
    logits = dot(ffn_in, router, 1, 0)
    chosen = jnp.where(own_mask, jnp.exp(logits), 0.0)
    gates = chosen / jnp.sum(chosen, axis=1, keepdims=True)
    gate_high, gate_low = split2(gates)
    gate_x = pad_to(jnp.concatenate([gate_high, gate_low], axis=1), lanes(2 * experts))
    args = (gate_weight, up_weight, down_weight)
    if fast:
        d_sum, y_sum, gate_grad, up_grad, down_grad = moe_small(
            plan, cot_all, ffn_in, gate_x, *args, slots
        )
    else:
        d_sum, y_sum, gate_grad, up_grad, down_grad = moe_large(
            ids_all, cotangent, ffn_in, gate_x, *args, experts, slots
        )
    d_gates = d_sum[:, width : width + experts] + d_sum[:, width + experts : width + 2 * experts]
    d_logits = gates * (d_gates - jnp.sum(gates * d_gates, axis=1, keepdims=True))
    d_high, d_low = split2(d_logits)
    d_ffn = d_sum[:, :width] + dot(d_high, router, 1, 1) + dot(d_low, router, 1, 1)
    router_part = dot(ffn_in, d_high, 0, 0) + dot(ffn_in, d_low, 0, 0)
    d_hidden, ffn_gain_rows = rms_back(hidden, ffn_gain32, d_ffn)
    ffn_gain_part = jnp.sum(ffn_gain_rows, axis=0)
    d_hidden = d_hidden + cotangent.astype(F32)
    d_attn = gather_y(d_hidden.astype(BF))

    o_part = dot(d_attn, context, 0, 0).astype(BF)
    d_attn, o_part = tied(d_attn, o_part)
    o_sum = scatter_dp(o_part).astype(F32)
    if fast:
        y_sum = scatter_first(*y_sum)
    d_context = dot(d_attn, o_t, 1, 0).astype(BF).reshape(seq, hk, group, HEAD)
    d_probs = jnp.einsum("qhgd,khd->hgqk", d_context, v_low, preferred_element_type=F32)
    d_values = jnp.einsum("hgqk,qhgd->khd", probs.astype(BF), d_context, preferred_element_type=F32)
    d_scores = probs * (d_probs - jnp.sum(probs * d_probs, axis=-1, keepdims=True))
    d_scores = d_scores.astype(BF)
    if fast:
        d_scores, y_sum = tied(d_scores, y_sum)
        y_sum = scatter_second(*y_sum)
    d_q = jnp.einsum("hgqk,khd->qhgd", d_scores, k_low, preferred_element_type=F32) * scale
    d_k = jnp.einsum("hgqk,qhgd->khd", d_scores, q_low, preferred_element_type=F32) * scale
    d_q_raw, q_gain_rows = rms_back(q_raw, q_gain32, rope_back(d_q.reshape(seq, hq, HEAD), cos, sin))
    d_k_raw, k_gain_rows = rms_back(k_raw, k_gain32, rope_back(d_k, cos, sin))
    d_qkv = jnp.concatenate(
        [
            d_q_raw.reshape(seq, hq * HEAD).astype(BF),
            d_k_raw.reshape(seq, hk * HEAD).astype(BF),
            d_values.reshape(seq, hk * HEAD).astype(BF),
        ],
        axis=1,
    )
    qkv_part = dot(normed, d_qkv, 0, 0).astype(BF)
    if fast:
        qkv_part, y_sum = tied(qkv_part, y_sum)
        y_sum = jnp.concatenate(scatter_last(*y_sum), axis=1).astype(F32)
    d_qkv, qkv_part = tied(d_qkv, qkv_part)
    qkv_sum = scatter_dp(qkv_part).astype(F32)
    output = (hidden + y_sum).astype(BF)
    d_normed = scatter_y(dot(d_qkv, w_qkv, 1, 1))
    d_tokens, attn_gain_rows = rms_back(tokens.astype(F32), attn_gain32, d_normed)
    tokens_grad = d_tokens + d_hidden

    spread = lambda v: jnp.pad(v.reshape(dp, gshard), ((0, 0), (0, shard - gshard))).reshape(-1)
    small_part = jnp.concatenate(
        [
            router_part,
            jnp.stack(
                [
                    jnp.sum(attn_gain_rows, axis=0),
                    ffn_gain_part,
                    spread(jnp.sum(q_gain_rows, axis=(0, 1))),
                    spread(jnp.sum(k_gain_rows, axis=(0, 1))),
                ],
                axis=1,
            ),
        ],
        axis=1,
    )
    small_part = pad_to(small_part, lanes(experts + 4))
    if fast:
        small_sum = scatter_blocks(small_part.reshape(dp, shard, -1))
    else:
        small_sum = scatter_dp(small_part)
    small_sum = small_sum + swap_y(small_sum)
    return (
        output,
        tokens_grad,
        small_sum[:, experts],
        qkv_sum[:, : hq * HEAD],
        qkv_sum[:, hq * HEAD : (hq + hk) * HEAD],
        qkv_sum[:, (hq + hk) * HEAD :],
        o_sum.T,
        small_sum[:gshard, experts + 2],
        small_sum[:gshard, experts + 3],
        small_sum[:, experts + 1],
        small_sum[:, :experts],
        gate_grad,
        up_grad,
        down_grad,
    )


def solution(mesh):
    rows = P(("dp", "tensor"), None)
    both = P("dp", "tensor")
    return jax.shard_map(
        on_device,
        mesh=mesh,
        in_specs=(
            rows,
            P("dp"),
            both,
            both,
            both,
            P("tensor", "dp"),
            P("dp"),
            P("dp"),
            P("dp"),
            P("dp", None),
            P("dp", None, "tensor"),
            P("dp", None, "tensor"),
            P("dp", "tensor", None),
            P("dp", None),
            rows,
        ),
        out_specs=(
            rows,
            rows,
            P("dp"),
            both,
            both,
            both,
            P("tensor", "dp"),
            P("dp"),
            P("dp"),
            P("dp"),
            P("dp", None),
            P("dp", None, "tensor"),
            P("dp", None, "tensor"),
            P("dp", "tensor", None),
        ),
        check_vma=False,
    )
```

```python
import jax
import jax.numpy as jnp
from jax import lax
from jax.experimental import pallas as pl
from jax.experimental.pallas import tpu as pltpu
from jax.sharding import PartitionSpec as P

HEAD = 128
EPS = 1e-06
THETA = 1000000.0
BF = jnp.bfloat16
F32 = jnp.float32


def dot(a, b, ca, cb):
    return lax.dot_general(a, b, (((ca,), (cb,)), ((), ())), preferred_element_type=F32)


def rms(v, gain):
    return v * lax.rsqrt(jnp.mean(v * v, axis=-1, keepdims=True) + EPS) * gain


def rms_back(v, gain, u):
    inv = lax.rsqrt(jnp.mean(v * v, axis=-1, keepdims=True) + EPS)
    ug = u * gain
    grad = ug * inv - v * (jnp.mean(ug * v, axis=-1, keepdims=True) * inv * inv * inv)
    return grad, u * v * inv


def rope(v, cos, sin):
    a, b = v[..., : HEAD // 2], v[..., HEAD // 2 :]
    return jnp.concatenate([a * cos - b * sin, b * cos + a * sin], axis=-1)


def rope_back(v, cos, sin):
    a, b = v[..., : HEAD // 2], v[..., HEAD // 2 :]
    return jnp.concatenate([a * cos + b * sin, b * cos - a * sin], axis=-1)


def rope_tables(count):
    inverse = THETA ** (-(jnp.arange(HEAD // 2, dtype=F32) * 2.0 / HEAD))
    angles = jnp.arange(count, dtype=F32)[:, None] * inverse[None, :]
    return jnp.cos(angles)[:, None, :], jnp.sin(angles)[:, None, :]


def split2(v):
    high = v.astype(BF)
    return high, (v - high.astype(F32)).astype(BF)


def gather_dp(v):
    return lax.all_gather(v, "dp", axis=0, tiled=True)


def gather_all(v):
    return lax.all_gather(v, ("dp", "tensor"), axis=0, tiled=True)


def scatter_all(v):
    return lax.psum_scatter(v, ("dp", "tensor"), scatter_dimension=0, tiled=True)


def scatter_dp(v):
    return lax.psum_scatter(v, "dp", scatter_dimension=0, tiled=True)


def pieces(width, dp, seq):
    count = 1 if dp * seq <= 8192 else 4
    step = width // count // 128 * 128
    edges = [step * i for i in range(count)] + [width]
    return list(zip(edges[:-1], edges[1:]))


def after(v, earlier):
    return v if earlier is None else lax.optimization_barrier((v, earlier))[0]


def dispatch(pick, own, dp, seq, earlier):
    blocks = []
    for low, high in pieces(own.shape[1], dp, seq):
        every = gather_all(after(own[:, low:high], earlier)).reshape(dp, seq, high - low)
        block = jnp.einsum("gest,gtd->gesd", pick, every, preferred_element_type=F32).astype(BF)
        blocks.append(block)
        earlier = block if len(pieces(own.shape[1], dp, seq)) > 1 else None
    return jnp.concatenate(blocks, axis=3)


def combine(pick, rows, dp, seq, earlier):
    blocks = []
    for low, high in pieces(rows.shape[3], dp, seq):
        tok = jnp.einsum(
            "gest,gesd->gtd",
            pick,
            after(rows[:, :, :, low:high], earlier),
            preferred_element_type=F32,
        ).astype(BF)
        blocks.append(scatter_all(tok.reshape(dp * seq, high - low)))
        earlier = blocks[-1] if len(pieces(rows.shape[3], dp, seq)) > 1 else None
    return jnp.concatenate(blocks, axis=1).astype(F32)


GRID = [(z, x, c) for z in range(4) for x in range(2) for c in range(2)]
SPLIT = (0, 768, 1536, 1792, 2048)


def at(z, x, c):
    return z % 4 * 4 + x % 2 * 2 + c % 2


def shift_z(v, k):
    return lax.ppermute(v, "dp", [(at(z, x, c), at(z + k, x, c)) for z, x, c in GRID])


def swap_x(v):
    return lax.ppermute(v, "dp", [(at(z, x, c), at(z, x + 1, c)) for z, x, c in GRID])


def swap_c(v):
    return lax.ppermute(v, "dp", [(at(z, x, c), at(z, x, c + 1)) for z, x, c in GRID])


def swap_y(v):
    return lax.ppermute(v, "tensor", [(0, 1), (1, 0)])


def gather_y(v):
    other = swap_y(v)
    first = lax.axis_index("tensor") == 0
    return jnp.concatenate([jnp.where(first, v, other), jnp.where(first, other, v)])


def scatter_y(v):
    a, b = jnp.split(v, 2)
    first = lax.axis_index("tensor") == 0
    kept, sent = jnp.where(first, a, b), jnp.where(first, b, a)
    return kept.astype(F32) + swap_y(sent.astype(BF)).astype(F32)


def gather_z(v, way):
    one, three = shift_z(v, 1), shift_z(v, -1)
    two = shift_z(one, 1) if way > 0 else shift_z(three, -1)
    return jnp.stack([v, one, two, three])


def add2(a, b):
    return (a.astype(F32) + b.astype(F32)).astype(BF)


def reduce_z(v, way, two=None):
    two = shift_z(v[2], -way) if two is None else two
    if way > 0:
        one = shift_z(add2(v[1], two), -1)
        three = shift_z(v[3], 1)
    else:
        three = shift_z(add2(v[3], two), 1)
        one = shift_z(v[1], -1)
    return (v[0].astype(F32) + one.astype(F32) + three.astype(F32)).astype(BF)


def tied(v, w):
    return lax.optimization_barrier((v, w))


def gather_rel(v1, v2, v5, v6, aside):
    w5 = jnp.stack([v5, swap_x(v5)])
    w6 = jnp.stack([v6, swap_y(v6)])
    s1 = gather_z(v1, 1)
    s2 = gather_z(v2, -1)
    w5 = jnp.stack([w5, swap_y(w5)])
    w6 = jnp.stack([w6, swap_x(w6)])
    s1, s2, w5, w6 = lax.optimization_barrier((s1, s2, w5, w6))
    s1x, s2y = swap_x(s1), swap_y(s2)
    five = [shift_z(w5, 1), shift_z(w5, -1)]
    six = [shift_z(w6, 1), shift_z(w6, -1)]
    (five, six), (s1x, s2y) = tied((five, six), (s1x, s2y))
    s1 = jnp.stack([s1, s1x])
    s2 = jnp.stack([s2, s2y])
    s1y, s2x = swap_y(s1), swap_x(s2)
    o5 = jnp.stack([w5, five[0], shift_z(five[0], 1), five[1]])
    o6 = jnp.stack([w6, six[0], shift_z(six[1], -1), six[1]])
    (s1y, s2x), aside = tied((s1y, s2x), aside)
    first = (s1, s1y, s2, s2x, o5, o6)
    return first, tuple(swap_c(v) for v in first), aside


def scatter_core(near, far):
    p5, p6, p1, p2 = [add2(near[i], swap_c(far[i])) for i in (2, 3, 0, 1)]
    return lax.optimization_barrier((p1, p2, p5, p6))


def scatter_first(p1, p2, p5, p6, aside=None):
    two5, two6 = shift_z(p5[2], -1), shift_z(p6[2], 1)
    (two5, two6), aside = tied((two5, two6), aside)
    p5 = reduce_z(p5, 1, two5)
    p6 = reduce_z(p6, -1, two6)
    p1 = add2(p1[0], swap_y(p1[1]))
    p2 = add2(p2[0], swap_x(p2[1]))
    return (p1, p2, p5, p6), aside


def scatter_second(p1, p2, p5, p6):
    p5 = add2(p5[0], swap_y(p5[1]))
    p6 = add2(p6[0], swap_x(p6[1]))
    p1 = add2(p1[0], swap_x(p1[1]))
    p2 = add2(p2[0], swap_y(p2[1]))
    return p1, p2, p5, p6


def scatter_last(p1, p2, p5, p6):
    p5 = add2(p5[0], swap_x(p5[1]))
    p6 = add2(p6[0], swap_y(p6[1]))
    return reduce_z(p1, 1), reduce_z(p2, -1), p5, p6


def scatter_rows(near, far):
    a, b = [add2(n, swap_c(f)) for n, f in zip(near, far)]
    a, b = lax.optimization_barrier((a, b))
    b = reduce_z(b, -1)
    a = add2(a[0], swap_x(a[1]))
    b = add2(b[0], swap_x(b[1]))
    return jnp.concatenate([reduce_z(a, 1), b], axis=1)


def scatter_blocks(v):
    d = jnp.arange(16)
    v = jnp.take(v, sequence_at(d // 8, d // 2 % 4, d % 2), axis=0)
    v = (v[:8] + swap_c(v[8:])).reshape(4, 2, *v.shape[1:])
    v = v[:, 0] + swap_x(v[:, 1])
    one = shift_z(v[1] + shift_z(v[2], -1), -1)
    return v[0] + one + shift_z(v[3], 1)


def sequence_at(dc, dz, dx):
    at = lax.axis_index("dp")
    return (at // 4 - dz) % 4 * 4 + (at // 2 % 2 + dx) % 2 * 2 + (at % 2 + dc) % 2


def nn(a, b):
    return lax.dot_general(a, b, (((1,), (0,)), ((), ())), preferred_element_type=F32)


def nt(a, b):
    return lax.dot_general(a, b, (((1,), (1,)), ((), ())), preferred_element_type=F32)


def pick_rows(rank, slots):
    at_slot = lax.broadcasted_iota(jnp.int32, (slots, rank.shape[1]), 0).astype(F32)
    return jnp.concatenate(
        [(rank[e : e + 1, :] == at_slot).astype(F32).astype(BF) for e in range(rank.shape[0])],
        axis=0,
    )


def pick_cols(rank, slots):
    at_slot = lax.broadcasted_iota(jnp.int32, (rank.shape[0], slots), 1).astype(F32)
    return jnp.concatenate(
        [(rank[:, e : e + 1] == at_slot).astype(F32).astype(BF) for e in range(rank.shape[1])],
        axis=1,
    )


def cot_kernel(where, rank, cot_a, cot_b, down, cots, d_act):
    slots = cots.shape[2] // 2
    for dx, cot in enumerate((cot_a, cot_b)):
        both = nn(pick_rows(rank[dx], slots), cot[0]).astype(BF)
        for e in range(2):
            cots[e, 0, dx * slots : (dx + 1) * slots, :] = both[e * slots : (e + 1) * slots]
    for e in range(2):
        d_act[e, 0] = nt(cots[e, 0], down[e])


def expert_kernel(
    rank, rank_t, cols, d_act, x1a, x1b, x2a, x2b, x5, x6, w_gate, w_up,
    rows, scaled, d_g, d_u, t1, t2, t5, t6, back,
):
    slots = rows.shape[2] // 2
    n = x1a.shape[2]
    gates = []
    for dx, x2 in enumerate((x2a, x2b)):
        pick = pick_rows(rank[dx], slots)
        low, high = pick[:, :n], pick[:, n:]
        block1 = nn(low, x1a[dx, 0]) + nn(high, x1b[dx, 0])
        block2 = nn(low, x2[0, 0]) + nn(high, x2[1, 0])
        block5 = nn(low, x5[0, 0, dx]) + nn(high, x5[0, 1, dx])
        block6 = nn(low, x6[0, dx, 0]) + nn(high, x6[0, dx, 1])
        low = dx * slots
        for e in range(2):
            part = slice(e * slots, (e + 1) * slots)
            rows[e, 0, low : low + slots, 0:768] = block1[part].astype(BF)
            rows[e, 0, low : low + slots, 768:1536] = block2[part].astype(BF)
            rows[e, 0, low : low + slots, 1536:1792] = block5[part, :256].astype(BF)
            rows[e, 0, low : low + slots, 1792:2048] = block6[part].astype(BF)
            both = cols[e, 0:1, :] + cols[e, 1:2, :]
            gates.append(jnp.sum(block5[part, 256:] * both, axis=1, keepdims=True))
    extras = []
    for e in range(2):
        gate = jnp.concatenate([gates[e], gates[2 + e]], axis=0)
        g = nn(rows[e, 0], w_gate[e])
        u = nn(rows[e, 0], w_up[e])
        da = d_act[e, 0]
        sig = 1.0 / (1.0 + jnp.exp(-g))
        silu = g * sig
        act = silu * u
        scaled[e, 0] = (act * gate).astype(BF)
        d_gate = jnp.sum(act * da, axis=1, keepdims=True)
        da = da * gate
        dg = (da * u * sig * (1.0 + g * (1.0 - sig))).astype(BF)
        du = (da * silu).astype(BF)
        d_g[e, 0] = dg
        d_u[e, 0] = du
        high = d_gate.astype(BF).astype(F32)
        extras.append(high * cols[e, 0:1, :] + (d_gate - high) * cols[e, 1:2, :])
        dr = (nt(dg, w_gate[e]) + nt(du, w_up[e])).astype(BF)
        for dx in range(2):
            back[dx, e * slots : (e + 1) * slots, :] = dr[dx * slots : (dx + 1) * slots]
    extra = [
        jnp.concatenate([extras[e][dx * slots : (dx + 1) * slots] for e in range(2)], axis=0)
        for dx in range(2)
    ]
    put_back(rank_t, back, t1, t2, t5, t6, slots, extra)


def put_back(rank_t, back, t1, t2, t5, t6, slots, extra=None):
    for dx in range(2):
        pick_t = pick_cols(rank_t[dx], slots)
        n = pick_t.shape[0] // 2
        p1, p2, p5, p6 = [
            nn(pick_t, back[dx, :, a:b]).astype(BF) for a, b in zip(SPLIT[:-1], SPLIT[1:])
        ]
        for dy in range(2):
            half = slice(dy * n, (dy + 1) * n)
            t1[dy, dx, 0] = p1[half]
            t2[dx, dy, 0] = p2[half]
            t5[0, dy, dx, :, 0:256] = p5[half]
            t6[0, dx, dy] = p6[half]
        if extra is not None:
            p7 = nn(pick_t, extra[dx].astype(BF)).astype(BF)
            for dy in range(2):
                t5[0, dy, dx, :, 256:] = p7[dy * n : (dy + 1) * n]


def out_kernel(rank_t, scaled, down, t1, t2, t5, t6, back):
    slots = scaled.shape[2] // 2
    for e in range(2):
        y = nn(scaled[e, 0], down[e]).astype(BF)
        for dx in range(2):
            back[dx, e * slots : (e + 1) * slots, :] = y[dx * slots : (dx + 1) * slots]
    put_back(rank_t, back, t1, t2, t5, t6, slots)


def grad_kernel(where, left, right, a, b):
    both = lax.dot_general(
        left[...], right[...], (((0,), (0,)), ((), ())), preferred_element_type=F32
    ).astype(BF)
    width = a.shape[-1]
    a[0, 0] = both[:, :width]
    b[0, 0] = both[:, width:]


def run_grad(where, left, right):
    count, columns = right.shape
    width = columns * 9 // 16 // 128 * 128
    shard = left.shape[1] // 16
    return pl.pallas_call(
        grad_kernel,
        grid_spec=pltpu.PrefetchScalarGridSpec(
            num_scalar_prefetch=1,
            grid=(2, 4),
            in_specs=[
                pl.BlockSpec((count, shard), lambda dx, dz, w: (0, w[2 * dz + dx])),
                pl.BlockSpec((count, columns), lambda dx, dz, w: (0, 0)),
            ],
            out_specs=[
                pl.BlockSpec((1, 1, shard, width), lambda dx, dz, w: (dx, dz, 0, 0)),
                pl.BlockSpec((1, 1, shard, columns - width), lambda dx, dz, w: (dz, dx, 0, 0)),
            ],
        ),
        out_shape=[
            shaped((2, 4, shard, width), BF),
            shaped((4, 2, shard, columns - width), BF),
        ],
        compiler_params=LIMIT,
        name="grad",
    )(where, left, right)


def pair(*tail):
    return pl.BlockSpec((2, *tail), lambda i, *_: (i,) + (0,) * len(tail))


def z_last(*lead):
    def spec(rows, columns):
        return pl.BlockSpec(
            (*lead, 1, rows, columns), lambda i, *_: (0,) * len(lead) + (i, 0, 0)
        )

    return spec


def z_first(rows, columns):
    return pl.BlockSpec((1, 2, 2, rows, columns), lambda i, *_: (i, 0, 0, 0, 0))


def block_specs(n, extra):
    return [z_last(2, 2)(n, 768), z_last(2, 2)(n, 768), z_first(n, 256 + extra), z_first(n, 256)]


def block_shapes(n, extra):
    shapes = [(2, 2, 4, n, 768), (2, 2, 4, n, 768), (4, 2, 2, n, 256 + extra), (4, 2, 2, n, 256)]
    return [shaped(v, BF) for v in shapes]


def by_expert(*tail):
    return pl.BlockSpec((2, 1, *tail), lambda i, *_: (0, i) + (0,) * len(tail))


def fixed(*shape):
    return pl.BlockSpec(
        shape, lambda i, *_: (0,) * len(shape), pipeline_mode=pl.Buffered(1)
    )


def shaped(shape, kind):
    return jax.ShapeDtypeStruct(shape, kind)


LIMIT = pltpu.CompilerParams(vmem_limit_bytes=60000 * 1024)


def run_cots(where, rank, cot_all, down, slots):
    seq, width = cot_all.shape[1:]
    ff = down.shape[1]
    return pl.pallas_call(
        cot_kernel,
        grid_spec=pltpu.PrefetchScalarGridSpec(
            num_scalar_prefetch=1,
            grid=(4,),
            in_specs=[
                pair(2, seq),
                pl.BlockSpec((1, seq, width), lambda i, w: (w[2 * i], 0, 0)),
                pl.BlockSpec((1, seq, width), lambda i, w: (w[2 * i + 1], 0, 0)),
                fixed(2, ff, width),
            ],
            out_specs=[by_expert(2 * slots, width), by_expert(2 * slots, ff)],
        ),
        out_shape=[shaped((2, 4, 2 * slots, width), BF), shaped((2, 4, 2 * slots, ff), F32)],
        compiler_params=LIMIT,
        name="cots",
    )(where, rank, cot_all, cot_all, down)


def run_experts(rank, rank_t, cols, d_act, parts, w_gate, w_up, slots):
    s1, s1y, s2, s2x, o5, o6 = parts
    n = s1.shape[2]
    seq, width, ff = 2 * n, w_gate.shape[1], w_gate.shape[2]
    return pl.pallas_call(
        expert_kernel,
        grid=(4,),
        in_specs=[
            pair(2, seq),
            pair(seq, 2),
            fixed(*cols.shape),
            by_expert(2 * slots, ff),
            z_last(2)(n, 768),
            z_last(2)(n, 768),
            z_last(2)(n, 768),
            z_last(2)(n, 768),
            z_first(n, 384),
            z_first(n, 256),
            fixed(2, width, ff),
            fixed(2, width, ff),
        ],
        out_specs=[
            by_expert(2 * slots, width),
            by_expert(2 * slots, ff),
            by_expert(2 * slots, ff),
            by_expert(2 * slots, ff),
        ]
        + block_specs(n, 128),
        out_shape=[
            shaped((2, 4, 2 * slots, width), BF),
            shaped((2, 4, 2 * slots, ff), BF),
            shaped((2, 4, 2 * slots, ff), BF),
            shaped((2, 4, 2 * slots, ff), BF),
        ]
        + block_shapes(n, 128),
        scratch_shapes=[pltpu.VMEM((2, 2 * slots, width), BF)],
        compiler_params=LIMIT,
        name="experts",
    )(
        rank, rank_t, cols, d_act, s1, s1y, s2, s2x, o5, o6, w_gate, w_up,
    )


def run_outs(rank_t, scaled, down, slots):
    seq, ff, width = rank_t.shape[1], down.shape[1], down.shape[2]
    return pl.pallas_call(
        out_kernel,
        grid=(4,),
        in_specs=[pair(seq, 2), by_expert(2 * slots, ff), fixed(2, ff, width)],
        out_specs=block_specs(seq // 2, 0),
        out_shape=block_shapes(seq // 2, 0),
        scratch_shapes=[pltpu.VMEM((2, 2 * slots, width), BF)],
        compiler_params=LIMIT,
        name="outs",
    )(rank_t, scaled, down)


def flip(v, axis, y):
    a, b = jnp.split(v, 2, axis=axis)
    return jnp.where(y == 0, v, jnp.concatenate([b, a], axis=axis))


def slot_plan(ids_all, experts):
    y = lax.axis_index("tensor")
    seq = ids_all.shape[1]
    mine = lax.axis_index("dp") * 2 + jnp.arange(2, dtype=jnp.int32)
    mask = jnp.any(ids_all[:, None, :, :] == mine[None, :, None, None], axis=3)
    before = (jnp.arange(seq)[:, None] < jnp.arange(seq)[None, :]).astype(BF)
    rank = jnp.einsum("gea,ab->geb", mask.astype(BF), before, preferred_element_type=F32)
    rank = jnp.where(mask, rank, -1.0)
    d = jnp.arange(16)
    where = sequence_at(d // 8, d // 2 % 4, d % 2)
    rank = jnp.take(rank, where, axis=0)
    rank_rel = flip(rank, 2, y)
    rank_t = jnp.swapaxes(rank_rel, 1, 2)
    column = jnp.arange(128)
    cols = (
        column[None, None, :] == (mine[:, None] + jnp.array([[0, experts]]))[:, :, None]
    ).astype(F32)
    halves = lambda v: (v[:8], v[8:])
    return halves(where.astype(jnp.int32)), halves(rank), halves(rank_rel), halves(rank_t), cols


def moe_small(plan, cot_all, ffn_in, gate_x, gate_weight, up_weight, down_weight, slots):
    where, rank, rank_rel, rank_t, cols = plan
    both = [run_cots(where[k], rank[k], cot_all, down_weight, slots) for k in (0, 1)]
    v1, v2, v5, v6 = [ffn_in[:, a:b] for a, b in zip(SPLIT[:-1], SPLIT[1:])]
    *parts, both = gather_rel(v1, v2, jnp.concatenate([v5, gate_x], axis=1), v6, both)
    cots, d_act = zip(*both)
    far, near = [
        run_experts(
            rank_rel[k], rank_t[k], cols, d_act[k], parts[k], gate_weight, up_weight, slots
        )
        for k in (1, 0)
    ]
    step = scatter_core(near[4:], far[4:])
    step, (near, far, cots) = scatter_first(*step, (near[:4], far[:4], cots))
    kept = lambda i: (near[i], far[i])
    outs = [run_outs(rank_t[k], kept(1)[k], down_weight, slots) for k in (0, 1)]
    total = lambda spec, a, b: jnp.einsum(spec, a[0], b[0], preferred_element_type=F32) + jnp.einsum(
        spec, a[1], b[1], preferred_element_type=F32
    )
    gate_grad = total("egsd,egsf->edf", kept(0), kept(2))
    down_grad = total("egsf,egsd->efd", kept(1), cots)
    step, (outs, down_grad, gate_grad) = tied(step, (outs, down_grad, gate_grad))
    step, rows, d_up = lax.optimization_barrier((scatter_second(*step), kept(0), kept(3)))
    up_grad = total("egsd,egsf->edf", rows, d_up)
    d1, d2, d5, d6 = scatter_last(*step)
    outs = scatter_core(*outs)
    d_sum = jnp.concatenate([d1, d2, d5[:, :256], d6, d5[:, 256:]], axis=1)
    d_sum, (y_sum, up_grad) = tied(d_sum, (outs, up_grad))
    d_sum = d_sum.astype(F32)
    return d_sum, y_sum, gate_grad, up_grad, down_grad


def moe_large(
    ids_all, cotangent, ffn_in, gate_x, gate_weight, up_weight, down_weight, experts, slots
):
    dp, seq = ids_all.shape[:2]
    local = gate_weight.shape[0]
    dp_at = lax.axis_index("dp")
    mine = dp_at * local + jnp.arange(local, dtype=jnp.int32)
    mask = jnp.any(ids_all[:, :, None, :] == mine[None, None, :, None], axis=3).astype(BF)
    gate_all = gather_all(gate_x).reshape(dp, seq, -1)
    before = (jnp.arange(seq)[:, None] > jnp.arange(seq)[None, :]).astype(BF)
    rank = jnp.einsum("ab,gbe->gea", before, mask, preferred_element_type=F32)
    rank = jnp.where(jnp.swapaxes(mask, 1, 2) > 0, rank, -1.0)
    pick = (rank[:, :, None, :] == jnp.arange(slots, dtype=F32)[None, None, :, None]).astype(BF)

    cots = dispatch(pick, cotangent, dp, seq, None)
    rows = dispatch(pick, ffn_in, dp, seq, cots)
    gate_tok = lax.dynamic_slice_in_dim(gate_all, dp_at * local, local, 2).astype(
        F32
    ) + lax.dynamic_slice_in_dim(gate_all, experts + dp_at * local, local, 2).astype(F32)
    gate_slot = jnp.sum(pick.astype(F32) * jnp.swapaxes(gate_tok, 1, 2)[:, :, None, :], axis=3)

    g_proj = jnp.einsum("gesd,edf->gesf", rows, gate_weight, preferred_element_type=F32)
    u_proj = jnp.einsum("gesd,edf->gesf", rows, up_weight, preferred_element_type=F32)
    d_act = jnp.einsum("gesd,efd->gesf", cots, down_weight, preferred_element_type=F32)
    sig = 1.0 / (1.0 + jnp.exp(-g_proj))
    silu = g_proj * sig
    act = silu * u_proj
    scaled = (act * gate_slot[..., None]).astype(BF)
    d_gate_slot = jnp.sum(act * d_act, axis=3)
    d_act = d_act * gate_slot[..., None]
    d_g = (d_act * u_proj * sig * (1.0 + g_proj * (1.0 - sig))).astype(BF)
    d_u = (d_act * silu).astype(BF)
    d_rows = (
        jnp.einsum("gesf,edf->gesd", d_g, gate_weight, preferred_element_type=F32)
        + jnp.einsum("gesf,edf->gesd", d_u, up_weight, preferred_element_type=F32)
    ).astype(BF)
    dg_high, dg_low = split2(d_gate_slot)
    column = jnp.arange(lanes(2 * experts))
    high_col = (column[None, :] == mine[:, None])[None, :, None, :]
    low_col = (column[None, :] == experts + mine[:, None])[None, :, None, :]
    extra = jnp.where(high_col, dg_high[..., None], jnp.where(low_col, dg_low[..., None], 0.0))
    d_rows = jnp.concatenate([d_rows, extra.astype(BF)], axis=3)
    d_sum = combine(pick, d_rows, dp, seq, None)

    y_rows = jnp.einsum("gesf,efd->gesd", scaled, down_weight, preferred_element_type=F32)
    y_sum = combine(pick, y_rows.astype(BF), dp, seq, d_sum)
    down_grad = jnp.einsum("gesf,gesd->efd", scaled, cots, preferred_element_type=F32)
    gate_grad = jnp.einsum("gesd,gesf->edf", rows, d_g, preferred_element_type=F32)
    up_grad = jnp.einsum("gesd,gesf->edf", rows, d_u, preferred_element_type=F32)

    return d_sum, y_sum, gate_grad, up_grad, down_grad


def pad_to(v, width):
    return jnp.pad(v, ((0, 0), (0, width - v.shape[1])))


def lanes(count):
    return -(-count // 128) * 128


def on_device(
    tokens,
    attn_gain,
    q_weight,
    key_matrix,
    value_matrix,
    o_weight,
    query_norm_gain,
    k_gain,
    ffn_gain,
    router_weight,
    gate_weight,
    up_weight,
    down_weight,
    expert_ids,
    cotangent,
):
    dp = lax.axis_size("dp")
    tensor = lax.axis_size("tensor")
    dp_at = lax.axis_index("dp")
    own, width = tokens.shape
    seq = expert_ids.shape[0]
    begin = lax.axis_index("tensor") * own
    local = gate_weight.shape[0]
    experts = local * dp
    slots = 10 * seq * expert_ids.shape[1] // (8 * experts)
    slots = -(-slots // 16) * 16
    shard = q_weight.shape[0]
    gshard = query_norm_gain.shape[0]
    hq = q_weight.shape[1] // HEAD
    hk = key_matrix.shape[1] // HEAD
    group = hq // hk
    qkv_width = (hq + 2 * hk) * HEAD
    top = expert_ids.shape[1]
    fast = (dp, tensor, local, seq, width) == (16, 2, 2, 384, 2048)

    arange_e = jnp.arange(experts, dtype=jnp.int32)
    own_ids = lax.dynamic_slice_in_dim(expert_ids, begin, own, 0)
    own_mask = jnp.any(own_ids[:, :, None] == arange_e[None, None, :], axis=1)

    gain_rows = jnp.stack(
        [
            attn_gain,
            ffn_gain,
            jnp.pad(query_norm_gain, (0, shard - gshard)),
            jnp.pad(k_gain, (0, shard - gshard)),
        ],
        axis=1,
    )
    ids_rows = expert_ids.reshape(shard, -1).astype(BF)
    small = jnp.concatenate([router_weight, gain_rows, ids_rows], axis=1)
    small = pad_to(small, lanes(small.shape[1]))
    small_end = qkv_width + small.shape[1]
    all_in = gather_dp(
        jnp.concatenate([q_weight, key_matrix, value_matrix, small, o_weight.T], axis=1)
    )
    layer_in = gather_y(tokens)
    o_t = all_in[:, small_end:]
    if fast:
        cot_all = gather_dp(gather_y(cotangent)).reshape(dp, seq, width)

    w_qkv = all_in[:, :qkv_width]
    router = all_in[:, qkv_width : qkv_width + experts]
    gains = all_in[:, qkv_width + experts : qkv_width + experts + 4].astype(F32)
    ids_all = all_in[:, qkv_width + experts + 4 :][:, : seq * top // shard]
    ids_all = ids_all.astype(jnp.int32).reshape(dp, seq, top)
    attn_gain32 = gains[:, 0]
    ffn_gain32 = gains[:, 1]
    q_gain32 = gains[:, 2].reshape(dp, shard)[:, :gshard].reshape(-1)
    k_gain32 = gains[:, 3].reshape(dp, shard)[:, :gshard].reshape(-1)

    residual = layer_in.astype(F32)
    normed = rms(residual, attn_gain32).astype(BF)
    qkv = dot(normed, w_qkv, 1, 0)
    cos, sin = rope_tables(seq)
    q_raw = qkv[:, : hq * HEAD].reshape(seq, hq, HEAD)
    k_raw = qkv[:, hq * HEAD : (hq + hk) * HEAD].reshape(seq, hk, HEAD)
    v_low = qkv[:, (hq + hk) * HEAD :].astype(BF).reshape(seq, hk, HEAD)
    q_low = rope(rms(q_raw, q_gain32), cos, sin).astype(BF).reshape(seq, hk, group, HEAD)
    k_low = rope(rms(k_raw, k_gain32), cos, sin).astype(BF)
    causal = jnp.arange(seq)[:, None] >= jnp.arange(seq)[None, :]
    scale = HEAD ** (-0.5)
    scores = jnp.einsum("qhgd,khd->hgqk", q_low, k_low, preferred_element_type=F32) * scale
    expo = jnp.where(causal, jnp.exp(scores), 0.0)
    total = jnp.sum(expo, axis=-1, keepdims=True)
    probs = expo / total
    context = jnp.einsum("hgqk,khd->qhgd", probs.astype(BF), v_low, preferred_element_type=F32)
    context = context.reshape(seq, hq * HEAD).astype(BF)
    if fast:
        context, plan = tied(context, slot_plan(ids_all, experts))
    hidden = tokens.astype(F32) + scatter_y(dot(context, o_t, 1, 1))

    ffn_in = rms(hidden, ffn_gain32).astype(BF)
    logits = dot(ffn_in, router, 1, 0)
    chosen = jnp.where(own_mask, jnp.exp(logits), 0.0)
    gates = chosen / jnp.sum(chosen, axis=1, keepdims=True)
    gate_high, gate_low = split2(gates)
    gate_x = pad_to(jnp.concatenate([gate_high, gate_low], axis=1), lanes(2 * experts))
    args = (gate_weight, up_weight, down_weight)
    if fast:
        d_sum, y_sum, gate_grad, up_grad, down_grad = moe_small(
            plan, cot_all, ffn_in, gate_x, *args, slots
        )
    else:
        d_sum, y_sum, gate_grad, up_grad, down_grad = moe_large(
            ids_all, cotangent, ffn_in, gate_x, *args, experts, slots
        )
    d_gates = d_sum[:, width : width + experts] + d_sum[:, width + experts : width + 2 * experts]
    d_logits = gates * (d_gates - jnp.sum(gates * d_gates, axis=1, keepdims=True))
    d_high, d_low = split2(d_logits)
    d_ffn = d_sum[:, :width] + dot(d_high, router, 1, 1) + dot(d_low, router, 1, 1)
    router_part = dot(ffn_in, d_high, 0, 0) + dot(ffn_in, d_low, 0, 0)
    d_hidden, ffn_gain_rows = rms_back(hidden, ffn_gain32, d_ffn)
    ffn_gain_part = jnp.sum(ffn_gain_rows, axis=0)
    d_hidden = d_hidden + cotangent.astype(F32)
    d_attn = gather_y(d_hidden.astype(BF))

    o_part = dot(d_attn, context, 0, 0).astype(BF)
    d_attn, o_part = tied(d_attn, o_part)
    o_sum = scatter_dp(o_part).astype(F32)
    if fast:
        y_sum = scatter_first(*y_sum)[0]
    d_context = dot(d_attn, o_t, 1, 0).astype(BF).reshape(seq, hk, group, HEAD)
    d_probs = jnp.einsum("qhgd,khd->hgqk", d_context, v_low, preferred_element_type=F32)
    d_values = jnp.einsum("hgqk,qhgd->khd", probs.astype(BF), d_context, preferred_element_type=F32)
    d_scores = probs * (d_probs - jnp.sum(probs * d_probs, axis=-1, keepdims=True))
    d_scores = d_scores.astype(BF)
    if fast:
        d_scores, y_sum = tied(d_scores, y_sum)
        y_sum = scatter_second(*y_sum)
    d_q = jnp.einsum("hgqk,khd->qhgd", d_scores, k_low, preferred_element_type=F32) * scale
    d_k = jnp.einsum("hgqk,qhgd->khd", d_scores, q_low, preferred_element_type=F32) * scale
    d_q_raw, q_gain_rows = rms_back(q_raw, q_gain32, rope_back(d_q.reshape(seq, hq, HEAD), cos, sin))
    d_k_raw, k_gain_rows = rms_back(k_raw, k_gain32, rope_back(d_k, cos, sin))
    d_qkv = jnp.concatenate(
        [
            d_q_raw.reshape(seq, hq * HEAD).astype(BF),
            d_k_raw.reshape(seq, hk * HEAD).astype(BF),
            d_values.reshape(seq, hk * HEAD).astype(BF),
        ],
        axis=1,
    )
    if fast:
        far, near = [run_grad(plan[0][k], normed, d_qkv) for k in (1, 0)]
        (far, near), y_sum = tied((far, near), y_sum)
        y_sum = jnp.concatenate(scatter_last(*y_sum), axis=1).astype(F32)
        d_qkv, (far, near) = tied(d_qkv, (far, near))
        qkv_sum = scatter_rows(near, far).astype(F32)
    else:
        qkv_sum = scatter_dp(dot(normed, d_qkv, 0, 0).astype(BF)).astype(F32)
    output = (hidden + y_sum).astype(BF)
    d_normed = scatter_y(dot(d_qkv, w_qkv, 1, 1))
    d_tokens, attn_gain_rows = rms_back(tokens.astype(F32), attn_gain32, d_normed)
    tokens_grad = d_tokens + d_hidden

    spread = lambda v: jnp.pad(v.reshape(dp, gshard), ((0, 0), (0, shard - gshard))).reshape(-1)
    small_part = jnp.concatenate(
        [
            router_part,
            jnp.stack(
                [
                    jnp.sum(attn_gain_rows, axis=0),
                    ffn_gain_part,
                    spread(jnp.sum(q_gain_rows, axis=(0, 1))),
                    spread(jnp.sum(k_gain_rows, axis=(0, 1))),
                ],
                axis=1,
            ),
        ],
        axis=1,
    )
    small_part = pad_to(small_part, lanes(experts + 4))
    if fast:
        small_sum = scatter_blocks(small_part.reshape(dp, shard, -1))
    else:
        small_sum = scatter_dp(small_part)
    small_sum = small_sum + swap_y(small_sum)
    return (
        output,
        tokens_grad,
        small_sum[:, experts],
        qkv_sum[:, : hq * HEAD],
        qkv_sum[:, hq * HEAD : (hq + hk) * HEAD],
        qkv_sum[:, (hq + hk) * HEAD :],
        o_sum.T,
        small_sum[:gshard, experts + 2],
        small_sum[:gshard, experts + 3],
        small_sum[:, experts + 1],
        small_sum[:, :experts],
        gate_grad,
        up_grad,
        down_grad,
    )


def solution(mesh):
    rows = P(("dp", "tensor"), None)
    both = P("dp", "tensor")
    return jax.shard_map(
        on_device,
        mesh=mesh,
        in_specs=(
            rows,
            P("dp"),
            both,
            both,
            both,
            P("tensor", "dp"),
            P("dp"),
            P("dp"),
            P("dp"),
            P("dp", None),
            P("dp", None, "tensor"),
            P("dp", None, "tensor"),
            P("dp", "tensor", None),
            P("dp", None),
            rows,
        ),
        out_specs=(
            rows,
            rows,
            P("dp"),
            both,
            both,
            both,
            P("tensor", "dp"),
            P("dp"),
            P("dp"),
            P("dp"),
            P("dp", None),
            P("dp", None, "tensor"),
            P("dp", None, "tensor"),
            P("dp", "tensor", None),
        ),
        check_vma=False,
    )
```

```python
import jax
import jax.numpy as jnp
from jax import lax
from jax.experimental import pallas as pl
from jax.experimental.pallas import tpu as pltpu
from jax.sharding import PartitionSpec as P

HEAD = 128
EPS = 1e-06
THETA = 1000000.0
BF = jnp.bfloat16
F32 = jnp.float32


def dot(a, b, ca, cb):
    return lax.dot_general(a, b, (((ca,), (cb,)), ((), ())), preferred_element_type=F32)


def rms(v, gain):
    return v * lax.rsqrt(jnp.mean(v * v, axis=-1, keepdims=True) + EPS) * gain


def rms_back(v, gain, u):
    inv = lax.rsqrt(jnp.mean(v * v, axis=-1, keepdims=True) + EPS)
    ug = u * gain
    grad = ug * inv - v * (jnp.mean(ug * v, axis=-1, keepdims=True) * inv * inv * inv)
    return grad, u * v * inv


def rope(v, cos, sin):
    a, b = v[..., : HEAD // 2], v[..., HEAD // 2 :]
    return jnp.concatenate([a * cos - b * sin, b * cos + a * sin], axis=-1)


def rope_back(v, cos, sin):
    a, b = v[..., : HEAD // 2], v[..., HEAD // 2 :]
    return jnp.concatenate([a * cos + b * sin, b * cos - a * sin], axis=-1)


def rope_tables(count):
    inverse = THETA ** (-(jnp.arange(HEAD // 2, dtype=F32) * 2.0 / HEAD))
    angles = jnp.arange(count, dtype=F32)[:, None] * inverse[None, :]
    return jnp.cos(angles)[:, None, :], jnp.sin(angles)[:, None, :]


def split2(v):
    high = v.astype(BF)
    return high, (v - high.astype(F32)).astype(BF)


def gather_dp(v):
    return lax.all_gather(v, "dp", axis=0, tiled=True)


def gather_all(v):
    return lax.all_gather(v, ("dp", "tensor"), axis=0, tiled=True)


def scatter_all(v):
    return lax.psum_scatter(v, ("dp", "tensor"), scatter_dimension=0, tiled=True)


def scatter_dp(v):
    return lax.psum_scatter(v, "dp", scatter_dimension=0, tiled=True)


def pieces(width, dp, seq):
    count = 1 if dp * seq <= 8192 else 4
    step = width // count // 128 * 128
    edges = [step * i for i in range(count)] + [width]
    return list(zip(edges[:-1], edges[1:]))


def after(v, earlier):
    return v if earlier is None else lax.optimization_barrier((v, earlier))[0]


def dispatch(pick, own, dp, seq, earlier):
    blocks = []
    for low, high in pieces(own.shape[1], dp, seq):
        every = gather_all(after(own[:, low:high], earlier)).reshape(dp, seq, high - low)
        block = jnp.einsum("gest,gtd->gesd", pick, every, preferred_element_type=F32).astype(BF)
        blocks.append(block)
        earlier = block if len(pieces(own.shape[1], dp, seq)) > 1 else None
    return jnp.concatenate(blocks, axis=3)


def combine(pick, rows, dp, seq, earlier):
    blocks = []
    for low, high in pieces(rows.shape[3], dp, seq):
        tok = jnp.einsum(
            "gest,gesd->gtd",
            pick,
            after(rows[:, :, :, low:high], earlier),
            preferred_element_type=F32,
        ).astype(BF)
        blocks.append(scatter_all(tok.reshape(dp * seq, high - low)))
        earlier = blocks[-1] if len(pieces(rows.shape[3], dp, seq)) > 1 else None
    return jnp.concatenate(blocks, axis=1).astype(F32)


GRID = [(z, x, c) for z in range(4) for x in range(2) for c in range(2)]
SPLIT = (0, 768, 1536, 1792, 2048)


def at(z, x, c):
    return z % 4 * 4 + x % 2 * 2 + c % 2


def shift_z(v, k):
    return lax.ppermute(v, "dp", [(at(z, x, c), at(z + k, x, c)) for z, x, c in GRID])


def swap_x(v):
    return lax.ppermute(v, "dp", [(at(z, x, c), at(z, x + 1, c)) for z, x, c in GRID])


def swap_c(v):
    return lax.ppermute(v, "dp", [(at(z, x, c), at(z, x, c + 1)) for z, x, c in GRID])


def swap_y(v):
    return lax.ppermute(v, "tensor", [(0, 1), (1, 0)])


def gather_y(v):
    other = swap_y(v)
    first = lax.axis_index("tensor") == 0
    return jnp.concatenate([jnp.where(first, v, other), jnp.where(first, other, v)])


def scatter_y(v):
    a, b = jnp.split(v, 2)
    first = lax.axis_index("tensor") == 0
    kept, sent = jnp.where(first, a, b), jnp.where(first, b, a)
    return kept.astype(F32) + swap_y(sent.astype(BF)).astype(F32)


def gather_z(v, way):
    one, three = shift_z(v, 1), shift_z(v, -1)
    two = shift_z(one, 1) if way > 0 else shift_z(three, -1)
    return jnp.stack([v, one, two, three])


def add2(a, b):
    return (a.astype(F32) + b.astype(F32)).astype(BF)


def reduce_z(v, way, two=None):
    two = shift_z(v[2], -way) if two is None else two
    if way > 0:
        one = shift_z(add2(v[1], two), -1)
        three = shift_z(v[3], 1)
    else:
        three = shift_z(add2(v[3], two), 1)
        one = shift_z(v[1], -1)
    return (v[0].astype(F32) + one.astype(F32) + three.astype(F32)).astype(BF)


def tied(v, w):
    return lax.optimization_barrier((v, w))


def gather_rel(v1, v2, v5, v6, plan, aside):
    w5 = jnp.stack([v5, swap_x(v5)])
    w6 = jnp.stack([v6, swap_y(v6)])
    s1 = gather_z(v1, 1)
    s2 = gather_z(v2, -1)
    w5 = jnp.stack([w5, swap_y(w5)])
    w6 = jnp.stack([w6, swap_x(w6)])
    s1, s2, w5, w6 = lax.optimization_barrier((s1, s2, w5, w6))
    s1x, s2y = swap_x(s1), swap_y(s2)
    five = [shift_z(w5, 1), shift_z(w5, -1)]
    six = [shift_z(w6, 1), shift_z(w6, -1)]
    (five, six), (s1x, s2y), plan = lax.optimization_barrier(((five, six), (s1x, s2y), plan))
    s1 = jnp.stack([s1, s1x])
    s2 = jnp.stack([s2, s2y])
    s1y, s2x = swap_y(s1), swap_x(s2)
    five.append(shift_z(five[0], 1))
    six.append(shift_z(six[1], -1))
    plan, (five, six) = tied(plan, (five, six))
    o5 = jnp.stack([w5, five[0], five[2], five[1]])
    o6 = jnp.stack([w6, six[0], six[2], six[1]])
    (s1y, s2x), done = tied((s1y, s2x), aside(plan))
    first = (s1, s1y, s2, s2x, o5, o6)
    return first, tuple(swap_c(v) for v in first), plan, done


def scatter_core(near, far):
    p5, p6, p1, p2 = [add2(near[i], swap_c(far[i])) for i in (2, 3, 0, 1)]
    return lax.optimization_barrier((p1, p2, p5, p6))


def scatter_first(p1, p2, p5, p6, aside=None):
    two5, two6 = shift_z(p5[2], -1), shift_z(p6[2], 1)
    (two5, two6), aside = tied((two5, two6), aside)
    p5 = reduce_z(p5, 1, two5)
    p6 = reduce_z(p6, -1, two6)
    p1 = add2(p1[0], swap_y(p1[1]))
    p2 = add2(p2[0], swap_x(p2[1]))
    return (p1, p2, p5, p6), aside


def scatter_second(p1, p2, p5, p6):
    p5 = add2(p5[0], swap_y(p5[1]))
    p6 = add2(p6[0], swap_x(p6[1]))
    p1 = add2(p1[0], swap_x(p1[1]))
    p2 = add2(p2[0], swap_y(p2[1]))
    return p1, p2, p5, p6


def scatter_last(p1, p2, p5, p6):
    p5 = add2(p5[0], swap_x(p5[1]))
    p6 = add2(p6[0], swap_y(p6[1]))
    return reduce_z(p1, 1), reduce_z(p2, -1), p5, p6


def scatter_rows_core(near, far):
    return [add2(n, swap_c(f)) for n, f in zip(near, far)]


def scatter_rows(a, b):
    b = reduce_z(b, -1)
    a = add2(a[0], swap_x(a[1]))
    b = add2(b[0], swap_x(b[1]))
    return jnp.concatenate([reduce_z(a, 1), b], axis=1)


def scatter_blocks(v):
    d = jnp.arange(16)
    v = jnp.take(v, sequence_at(d // 8, d // 2 % 4, d % 2), axis=0)
    v = (v[:8] + swap_c(v[8:])).reshape(4, 2, *v.shape[1:])
    v = v[:, 0] + swap_x(v[:, 1])
    one = shift_z(v[1] + shift_z(v[2], -1), -1)
    return v[0] + one + shift_z(v[3], 1)


def sequence_at(dc, dz, dx):
    at = lax.axis_index("dp")
    return (at // 4 - dz) % 4 * 4 + (at // 2 % 2 + dx) % 2 * 2 + (at % 2 + dc) % 2


def nn(a, b):
    return lax.dot_general(a, b, (((1,), (0,)), ((), ())), preferred_element_type=F32)


def nt(a, b):
    return lax.dot_general(a, b, (((1,), (1,)), ((), ())), preferred_element_type=F32)


def pick_rows(rank, slots):
    at_slot = lax.broadcasted_iota(jnp.int32, (slots, rank.shape[1]), 0).astype(F32)
    return jnp.concatenate(
        [(rank[e : e + 1, :] == at_slot).astype(F32).astype(BF) for e in range(rank.shape[0])],
        axis=0,
    )


def pick_cols(rank, slots):
    at_slot = lax.broadcasted_iota(jnp.int32, (rank.shape[0], slots), 1).astype(F32)
    return jnp.concatenate(
        [(rank[:, e : e + 1] == at_slot).astype(F32).astype(BF) for e in range(rank.shape[1])],
        axis=1,
    )


def cot_kernel(where, rank, cot_a, cot_b, down, cots, d_act):
    slots = cots.shape[2] // 2
    for dx, cot in enumerate((cot_a, cot_b)):
        both = nn(pick_rows(rank[dx], slots), cot[0]).astype(BF)
        for e in range(2):
            cots[e, 0, dx * slots : (dx + 1) * slots, :] = both[e * slots : (e + 1) * slots]
    for e in range(2):
        d_act[e, 0] = nt(cots[e, 0], down[e])


def expert_kernel(
    rank, rank_t, cols, d_act, x1a, x1b, x2a, x2b, x5, x6, w_gate, w_up,
    rows, scaled, d_g, d_u, t1, t2, t5, t6, back,
):
    slots = rows.shape[2] // 2
    n = x1a.shape[2]
    gates = []
    for dx, x2 in enumerate((x2a, x2b)):
        pick = pick_rows(rank[dx], slots)
        low, high = pick[:, :n], pick[:, n:]
        block1 = nn(low, x1a[dx, 0]) + nn(high, x1b[dx, 0])
        block2 = nn(low, x2[0, 0]) + nn(high, x2[1, 0])
        block5 = nn(low, x5[0, 0, dx]) + nn(high, x5[0, 1, dx])
        block6 = nn(low, x6[0, dx, 0]) + nn(high, x6[0, dx, 1])
        low = dx * slots
        for e in range(2):
            part = slice(e * slots, (e + 1) * slots)
            rows[e, 0, low : low + slots, 0:768] = block1[part].astype(BF)
            rows[e, 0, low : low + slots, 768:1536] = block2[part].astype(BF)
            rows[e, 0, low : low + slots, 1536:1792] = block5[part, :256].astype(BF)
            rows[e, 0, low : low + slots, 1792:2048] = block6[part].astype(BF)
            both = cols[e, 0:1, :] + cols[e, 1:2, :]
            gates.append(jnp.sum(block5[part, 256:] * both, axis=1, keepdims=True))
    extras = []
    for e in range(2):
        gate = jnp.concatenate([gates[e], gates[2 + e]], axis=0)
        g = nn(rows[e, 0], w_gate[e])
        u = nn(rows[e, 0], w_up[e])
        da = d_act[e, 0]
        sig = 1.0 / (1.0 + jnp.exp(-g))
        silu = g * sig
        act = silu * u
        scaled[e, 0] = (act * gate).astype(BF)
        d_gate = jnp.sum(act * da, axis=1, keepdims=True)
        da = da * gate
        dg = (da * u * sig * (1.0 + g * (1.0 - sig))).astype(BF)
        du = (da * silu).astype(BF)
        d_g[e, 0] = dg
        d_u[e, 0] = du
        high = d_gate.astype(BF).astype(F32)
        extras.append(high * cols[e, 0:1, :] + (d_gate - high) * cols[e, 1:2, :])
        dr = (nt(dg, w_gate[e]) + nt(du, w_up[e])).astype(BF)
        for dx in range(2):
            back[dx, e * slots : (e + 1) * slots, :] = dr[dx * slots : (dx + 1) * slots]
    extra = [
        jnp.concatenate([extras[e][dx * slots : (dx + 1) * slots] for e in range(2)], axis=0)
        for dx in range(2)
    ]
    put_back(rank_t, back, t1, t2, t5, t6, slots, extra)


def put_back(rank_t, back, t1, t2, t5, t6, slots, extra=None):
    for dx in range(2):
        pick_t = pick_cols(rank_t[dx], slots)
        n = pick_t.shape[0] // 2
        p1, p2, p5, p6 = [
            nn(pick_t, back[dx, :, a:b]).astype(BF) for a, b in zip(SPLIT[:-1], SPLIT[1:])
        ]
        for dy in range(2):
            half = slice(dy * n, (dy + 1) * n)
            t1[dy, dx, 0] = p1[half]
            t2[dx, dy, 0] = p2[half]
            t5[0, dy, dx, :, 0:256] = p5[half]
            t6[0, dx, dy] = p6[half]
        if extra is not None:
            p7 = nn(pick_t, extra[dx].astype(BF)).astype(BF)
            for dy in range(2):
                t5[0, dy, dx, :, 256:] = p7[dy * n : (dy + 1) * n]


def out_kernel(rank_t, scaled, down, t1, t2, t5, t6, back):
    slots = scaled.shape[2] // 2
    for e in range(2):
        y = nn(scaled[e, 0], down[e]).astype(BF)
        for dx in range(2):
            back[dx, e * slots : (e + 1) * slots, :] = y[dx * slots : (dx + 1) * slots]
    put_back(rank_t, back, t1, t2, t5, t6, slots)


def grad_kernel(where, left, right, a, b):
    both = lax.dot_general(
        left[...], right[...], (((0,), (0,)), ((), ())), preferred_element_type=F32
    ).astype(BF)
    width = a.shape[-1]
    a[0, 0] = both[:, :width]
    b[0, 0] = both[:, width:]


def run_grad(where, left, right):
    count, columns = right.shape
    width = columns * 9 // 16 // 128 * 128
    shard = left.shape[1] // 16
    return pl.pallas_call(
        grad_kernel,
        grid_spec=pltpu.PrefetchScalarGridSpec(
            num_scalar_prefetch=1,
            grid=(2, 4),
            in_specs=[
                pl.BlockSpec((count, shard), lambda dx, dz, w: (0, w[2 * dz + dx])),
                pl.BlockSpec((count, columns), lambda dx, dz, w: (0, 0)),
            ],
            out_specs=[
                pl.BlockSpec((1, 1, shard, width), lambda dx, dz, w: (dx, dz, 0, 0)),
                pl.BlockSpec((1, 1, shard, columns - width), lambda dx, dz, w: (dz, dx, 0, 0)),
            ],
        ),
        out_shape=[
            shaped((2, 4, shard, width), BF),
            shaped((4, 2, shard, columns - width), BF),
        ],
        compiler_params=LIMIT,
        name="grad",
    )(where, left, right)


def pair(*tail):
    return pl.BlockSpec((2, *tail), lambda i, *_: (i,) + (0,) * len(tail))


def z_last(*lead):
    def spec(rows, columns):
        return pl.BlockSpec(
            (*lead, 1, rows, columns), lambda i, *_: (0,) * len(lead) + (i, 0, 0)
        )

    return spec


def z_first(rows, columns):
    return pl.BlockSpec((1, 2, 2, rows, columns), lambda i, *_: (i, 0, 0, 0, 0))


def block_specs(n, extra):
    return [z_last(2, 2)(n, 768), z_last(2, 2)(n, 768), z_first(n, 256 + extra), z_first(n, 256)]


def block_shapes(n, extra):
    shapes = [(2, 2, 4, n, 768), (2, 2, 4, n, 768), (4, 2, 2, n, 256 + extra), (4, 2, 2, n, 256)]
    return [shaped(v, BF) for v in shapes]


def by_expert(*tail):
    return pl.BlockSpec((2, 1, *tail), lambda i, *_: (0, i) + (0,) * len(tail))


def fixed(*shape):
    return pl.BlockSpec(
        shape, lambda i, *_: (0,) * len(shape), pipeline_mode=pl.Buffered(1)
    )


def shaped(shape, kind):
    return jax.ShapeDtypeStruct(shape, kind)


LIMIT = pltpu.CompilerParams(vmem_limit_bytes=60000 * 1024)


def run_cots(where, rank, cot_all, down, slots):
    seq, width = cot_all.shape[1:]
    ff = down.shape[1]
    return pl.pallas_call(
        cot_kernel,
        grid_spec=pltpu.PrefetchScalarGridSpec(
            num_scalar_prefetch=1,
            grid=(4,),
            in_specs=[
                pair(2, seq),
                pl.BlockSpec((1, seq, width), lambda i, w: (w[2 * i], 0, 0)),
                pl.BlockSpec((1, seq, width), lambda i, w: (w[2 * i + 1], 0, 0)),
                fixed(2, ff, width),
            ],
            out_specs=[by_expert(2 * slots, width), by_expert(2 * slots, ff)],
        ),
        out_shape=[shaped((2, 4, 2 * slots, width), BF), shaped((2, 4, 2 * slots, ff), F32)],
        compiler_params=LIMIT,
        name="cots",
    )(where, rank, cot_all, cot_all, down)


def run_experts(rank, rank_t, cols, d_act, parts, w_gate, w_up, slots):
    s1, s1y, s2, s2x, o5, o6 = parts
    n = s1.shape[2]
    seq, width, ff = 2 * n, w_gate.shape[1], w_gate.shape[2]
    return pl.pallas_call(
        expert_kernel,
        grid=(4,),
        in_specs=[
            pair(2, seq),
            pair(seq, 2),
            fixed(*cols.shape),
            by_expert(2 * slots, ff),
            z_last(2)(n, 768),
            z_last(2)(n, 768),
            z_last(2)(n, 768),
            z_last(2)(n, 768),
            z_first(n, 384),
            z_first(n, 256),
            fixed(2, width, ff),
            fixed(2, width, ff),
        ],
        out_specs=[
            by_expert(2 * slots, width),
            by_expert(2 * slots, ff),
            by_expert(2 * slots, ff),
            by_expert(2 * slots, ff),
        ]
        + block_specs(n, 128),
        out_shape=[
            shaped((2, 4, 2 * slots, width), BF),
            shaped((2, 4, 2 * slots, ff), BF),
            shaped((2, 4, 2 * slots, ff), BF),
            shaped((2, 4, 2 * slots, ff), BF),
        ]
        + block_shapes(n, 128),
        scratch_shapes=[pltpu.VMEM((2, 2 * slots, width), BF)],
        compiler_params=LIMIT,
        name="experts",
    )(
        rank, rank_t, cols, d_act, s1, s1y, s2, s2x, o5, o6, w_gate, w_up,
    )


def run_outs(rank_t, scaled, down, slots):
    seq, ff, width = rank_t.shape[1], down.shape[1], down.shape[2]
    return pl.pallas_call(
        out_kernel,
        grid=(4,),
        in_specs=[pair(seq, 2), by_expert(2 * slots, ff), fixed(2, ff, width)],
        out_specs=block_specs(seq // 2, 0),
        out_shape=block_shapes(seq // 2, 0),
        scratch_shapes=[pltpu.VMEM((2, 2 * slots, width), BF)],
        compiler_params=LIMIT,
        name="outs",
    )(rank_t, scaled, down)


def flip(v, axis, y):
    a, b = jnp.split(v, 2, axis=axis)
    return jnp.where(y == 0, v, jnp.concatenate([b, a], axis=axis))


def slot_plan(ids_all, experts):
    y = lax.axis_index("tensor")
    seq = ids_all.shape[1]
    mine = lax.axis_index("dp") * 2 + jnp.arange(2, dtype=jnp.int32)
    mask = jnp.any(ids_all[:, None, :, :] == mine[None, :, None, None], axis=3)
    before = (jnp.arange(seq)[:, None] < jnp.arange(seq)[None, :]).astype(BF)
    rank = jnp.einsum("gea,ab->geb", mask.astype(BF), before, preferred_element_type=F32)
    rank = jnp.where(mask, rank, -1.0)
    d = jnp.arange(16)
    where = sequence_at(d // 8, d // 2 % 4, d % 2)
    rank = jnp.take(rank, where, axis=0)
    rank_rel = flip(rank, 2, y)
    rank_t = jnp.swapaxes(rank_rel, 1, 2)
    column = jnp.arange(128)
    cols = (
        column[None, None, :] == (mine[:, None] + jnp.array([[0, experts]]))[:, :, None]
    ).astype(F32)
    halves = lambda v: (v[:8], v[8:])
    return halves(where.astype(jnp.int32)), halves(rank), halves(rank_rel), halves(rank_t), cols


def moe_small(plan, cot_all, ffn_in, gate_x, gate_weight, up_weight, down_weight, slots):

    def cot_rows(plan):
        return [run_cots(plan[0][k], plan[1][k], cot_all, down_weight, slots) for k in (0, 1)]

    v1, v2, v5, v6 = [ffn_in[:, a:b] for a, b in zip(SPLIT[:-1], SPLIT[1:])]
    v5 = jnp.concatenate([v5, gate_x], axis=1)
    *parts, plan, both = gather_rel(v1, v2, v5, v6, plan, cot_rows)
    rank_rel, rank_t, cols = plan[2:]
    cots, d_act = zip(*both)
    far, near = [
        run_experts(
            rank_rel[k], rank_t[k], cols, d_act[k], parts[k], gate_weight, up_weight, slots
        )
        for k in (1, 0)
    ]
    step = scatter_core(near[4:], far[4:])
    step, (near, far, cots) = scatter_first(*step, (near[:4], far[:4], cots))
    kept = lambda i: (near[i], far[i])
    outs = [run_outs(rank_t[k], kept(1)[k], down_weight, slots) for k in (0, 1)]
    total = lambda spec, a, b: jnp.einsum(spec, a[0], b[0], preferred_element_type=F32) + jnp.einsum(
        spec, a[1], b[1], preferred_element_type=F32
    )
    down_grad = total("egsf,egsd->efd", kept(1), cots)
    step, (outs, down_grad) = tied(step, (outs, down_grad))
    d1, d2, d5, d6 = scatter_last(*scatter_second(*step))
    outs = scatter_core(*outs)
    d_sum = jnp.concatenate([d1, d2, d5[:, :256], d6, d5[:, 256:]], axis=1)
    d_sum, y_sum = tied(d_sum, outs)
    d_sum = d_sum.astype(F32)

    def later(aside):
        (rows, d_g, d_u), aside = tied((kept(0), kept(2), kept(3)), aside)
        return total("egsd,egsf->edf", rows, d_g), total("egsd,egsf->edf", rows, d_u), aside

    return d_sum, y_sum, later, down_grad


def moe_large(
    ids_all, cotangent, ffn_in, gate_x, gate_weight, up_weight, down_weight, experts, slots
):
    dp, seq = ids_all.shape[:2]
    local = gate_weight.shape[0]
    dp_at = lax.axis_index("dp")
    mine = dp_at * local + jnp.arange(local, dtype=jnp.int32)
    mask = jnp.any(ids_all[:, :, None, :] == mine[None, None, :, None], axis=3).astype(BF)
    gate_all = gather_all(gate_x).reshape(dp, seq, -1)
    before = (jnp.arange(seq)[:, None] > jnp.arange(seq)[None, :]).astype(BF)
    rank = jnp.einsum("ab,gbe->gea", before, mask, preferred_element_type=F32)
    rank = jnp.where(jnp.swapaxes(mask, 1, 2) > 0, rank, -1.0)
    pick = (rank[:, :, None, :] == jnp.arange(slots, dtype=F32)[None, None, :, None]).astype(BF)

    cots = dispatch(pick, cotangent, dp, seq, None)
    rows = dispatch(pick, ffn_in, dp, seq, cots)
    gate_tok = lax.dynamic_slice_in_dim(gate_all, dp_at * local, local, 2).astype(
        F32
    ) + lax.dynamic_slice_in_dim(gate_all, experts + dp_at * local, local, 2).astype(F32)
    gate_slot = jnp.sum(pick.astype(F32) * jnp.swapaxes(gate_tok, 1, 2)[:, :, None, :], axis=3)

    g_proj = jnp.einsum("gesd,edf->gesf", rows, gate_weight, preferred_element_type=F32)
    u_proj = jnp.einsum("gesd,edf->gesf", rows, up_weight, preferred_element_type=F32)
    d_act = jnp.einsum("gesd,efd->gesf", cots, down_weight, preferred_element_type=F32)
    sig = 1.0 / (1.0 + jnp.exp(-g_proj))
    silu = g_proj * sig
    act = silu * u_proj
    scaled = (act * gate_slot[..., None]).astype(BF)
    d_gate_slot = jnp.sum(act * d_act, axis=3)
    d_act = d_act * gate_slot[..., None]
    d_g = (d_act * u_proj * sig * (1.0 + g_proj * (1.0 - sig))).astype(BF)
    d_u = (d_act * silu).astype(BF)
    d_rows = (
        jnp.einsum("gesf,edf->gesd", d_g, gate_weight, preferred_element_type=F32)
        + jnp.einsum("gesf,edf->gesd", d_u, up_weight, preferred_element_type=F32)
    ).astype(BF)
    dg_high, dg_low = split2(d_gate_slot)
    column = jnp.arange(lanes(2 * experts))
    high_col = (column[None, :] == mine[:, None])[None, :, None, :]
    low_col = (column[None, :] == experts + mine[:, None])[None, :, None, :]
    extra = jnp.where(high_col, dg_high[..., None], jnp.where(low_col, dg_low[..., None], 0.0))
    d_rows = jnp.concatenate([d_rows, extra.astype(BF)], axis=3)
    d_sum = combine(pick, d_rows, dp, seq, None)

    y_rows = jnp.einsum("gesf,efd->gesd", scaled, down_weight, preferred_element_type=F32)
    y_sum = combine(pick, y_rows.astype(BF), dp, seq, d_sum)
    down_grad = jnp.einsum("gesf,gesd->efd", scaled, cots, preferred_element_type=F32)
    gate_grad = jnp.einsum("gesd,gesf->edf", rows, d_g, preferred_element_type=F32)
    up_grad = jnp.einsum("gesd,gesf->edf", rows, d_u, preferred_element_type=F32)

    return d_sum, y_sum, gate_grad, up_grad, down_grad


def pad_to(v, width):
    return jnp.pad(v, ((0, 0), (0, width - v.shape[1])))


def lanes(count):
    return -(-count // 128) * 128


def on_device(
    tokens,
    attn_gain,
    q_weight,
    key_matrix,
    value_matrix,
    o_weight,
    query_norm_gain,
    k_gain,
    ffn_gain,
    router_weight,
    gate_weight,
    up_weight,
    down_weight,
    expert_ids,
    cotangent,
):
    dp = lax.axis_size("dp")
    tensor = lax.axis_size("tensor")
    dp_at = lax.axis_index("dp")
    own, width = tokens.shape
    seq = expert_ids.shape[0]
    begin = lax.axis_index("tensor") * own
    local = gate_weight.shape[0]
    experts = local * dp
    slots = 10 * seq * expert_ids.shape[1] // (8 * experts)
    slots = -(-slots // 16) * 16
    shard = q_weight.shape[0]
    gshard = query_norm_gain.shape[0]
    hq = q_weight.shape[1] // HEAD
    hk = key_matrix.shape[1] // HEAD
    group = hq // hk
    qkv_width = (hq + 2 * hk) * HEAD
    top = expert_ids.shape[1]
    fast = (dp, tensor, local, seq, width) == (16, 2, 2, 384, 2048)

    arange_e = jnp.arange(experts, dtype=jnp.int32)
    own_ids = lax.dynamic_slice_in_dim(expert_ids, begin, own, 0)
    own_mask = jnp.any(own_ids[:, :, None] == arange_e[None, None, :], axis=1)

    gain_rows = jnp.stack(
        [
            attn_gain,
            ffn_gain,
            jnp.pad(query_norm_gain, (0, shard - gshard)),
            jnp.pad(k_gain, (0, shard - gshard)),
        ],
        axis=1,
    )
    ids_rows = expert_ids.reshape(shard, -1).astype(BF)
    small = jnp.concatenate([router_weight, gain_rows, ids_rows], axis=1)
    small = pad_to(small, lanes(small.shape[1]))
    small_end = qkv_width + small.shape[1]
    all_in = gather_dp(
        jnp.concatenate([q_weight, key_matrix, value_matrix, small, o_weight.T], axis=1)
    )
    layer_in = gather_y(tokens)
    o_t = all_in[:, small_end:]
    if fast:
        cot_all = gather_dp(gather_y(cotangent)).reshape(dp, seq, width)

    w_qkv = all_in[:, :qkv_width]
    router = all_in[:, qkv_width : qkv_width + experts]
    gains = all_in[:, qkv_width + experts : qkv_width + experts + 4].astype(F32)
    ids_all = all_in[:, qkv_width + experts + 4 :][:, : seq * top // shard]
    ids_all = ids_all.astype(jnp.int32).reshape(dp, seq, top)
    attn_gain32 = gains[:, 0]
    ffn_gain32 = gains[:, 1]
    q_gain32 = gains[:, 2].reshape(dp, shard)[:, :gshard].reshape(-1)
    k_gain32 = gains[:, 3].reshape(dp, shard)[:, :gshard].reshape(-1)

    residual = layer_in.astype(F32)
    normed = rms(residual, attn_gain32).astype(BF)
    qkv = dot(normed, w_qkv, 1, 0)
    cos, sin = rope_tables(seq)
    q_raw = qkv[:, : hq * HEAD].reshape(seq, hq, HEAD)
    k_raw = qkv[:, hq * HEAD : (hq + hk) * HEAD].reshape(seq, hk, HEAD)
    v_low = qkv[:, (hq + hk) * HEAD :].astype(BF).reshape(seq, hk, HEAD)
    q_low = rope(rms(q_raw, q_gain32), cos, sin).astype(BF).reshape(seq, hk, group, HEAD)
    k_low = rope(rms(k_raw, k_gain32), cos, sin).astype(BF)
    causal = jnp.arange(seq)[:, None] >= jnp.arange(seq)[None, :]
    scale = HEAD ** (-0.5)
    scores = jnp.einsum("qhgd,khd->hgqk", q_low, k_low, preferred_element_type=F32) * scale
    expo = jnp.where(causal, jnp.exp(scores), 0.0)
    total = jnp.sum(expo, axis=-1, keepdims=True)
    probs = expo / total
    context = jnp.einsum("hgqk,khd->qhgd", probs.astype(BF), v_low, preferred_element_type=F32)
    context = context.reshape(seq, hq * HEAD).astype(BF)
    if fast:
        plan = slot_plan(ids_all, experts)
    hidden = tokens.astype(F32) + scatter_y(dot(context, o_t, 1, 1))

    ffn_in = rms(hidden, ffn_gain32).astype(BF)
    logits = dot(ffn_in, router, 1, 0)
    chosen = jnp.where(own_mask, jnp.exp(logits), 0.0)
    gates = chosen / jnp.sum(chosen, axis=1, keepdims=True)
    gate_high, gate_low = split2(gates)
    gate_x = pad_to(jnp.concatenate([gate_high, gate_low], axis=1), lanes(2 * experts))
    args = (gate_weight, up_weight, down_weight)
    if fast:
        d_sum, y_sum, later, down_grad = moe_small(
            plan, cot_all, ffn_in, gate_x, *args, slots
        )
    else:
        d_sum, y_sum, gate_grad, up_grad, down_grad = moe_large(
            ids_all, cotangent, ffn_in, gate_x, *args, experts, slots
        )
    d_gates = d_sum[:, width : width + experts] + d_sum[:, width + experts : width + 2 * experts]
    d_logits = gates * (d_gates - jnp.sum(gates * d_gates, axis=1, keepdims=True))
    d_high, d_low = split2(d_logits)
    d_ffn = d_sum[:, :width] + dot(d_high, router, 1, 1) + dot(d_low, router, 1, 1)
    router_part = dot(ffn_in, d_high, 0, 0) + dot(ffn_in, d_low, 0, 0)
    d_hidden, ffn_gain_rows = rms_back(hidden, ffn_gain32, d_ffn)
    ffn_gain_part = jnp.sum(ffn_gain_rows, axis=0)
    d_hidden = d_hidden + cotangent.astype(F32)
    d_attn = gather_y(d_hidden.astype(BF))

    o_part = dot(d_attn, context, 0, 0).astype(BF)
    d_attn, o_part = tied(d_attn, o_part)
    o_sum = scatter_dp(o_part).astype(F32)
    if fast:
        y_sum = scatter_first(*y_sum)[0]
    d_context = dot(d_attn, o_t, 1, 0).astype(BF).reshape(seq, hk, group, HEAD)
    d_probs = jnp.einsum("qhgd,khd->hgqk", d_context, v_low, preferred_element_type=F32)
    d_values = jnp.einsum("hgqk,qhgd->khd", probs.astype(BF), d_context, preferred_element_type=F32)
    if fast:
        d_probs, y_sum = tied(d_probs, y_sum)
        y_sum = scatter_second(*y_sum)
    d_scores = probs * (d_probs - jnp.sum(probs * d_probs, axis=-1, keepdims=True))
    d_scores = d_scores.astype(BF)
    if fast:
        d_scores, y_sum = tied(d_scores, y_sum)
        y_sum = scatter_last(*y_sum)
    d_q = jnp.einsum("hgqk,khd->qhgd", d_scores, k_low, preferred_element_type=F32) * scale
    d_k = jnp.einsum("hgqk,qhgd->khd", d_scores, q_low, preferred_element_type=F32) * scale
    d_q_raw, q_gain_rows = rms_back(q_raw, q_gain32, rope_back(d_q.reshape(seq, hq, HEAD), cos, sin))
    d_k_raw, k_gain_rows = rms_back(k_raw, k_gain32, rope_back(d_k, cos, sin))
    d_qkv = jnp.concatenate(
        [
            d_q_raw.reshape(seq, hq * HEAD).astype(BF),
            d_k_raw.reshape(seq, hk * HEAD).astype(BF),
            d_values.reshape(seq, hk * HEAD).astype(BF),
        ],
        axis=1,
    )
    if fast:
        d_qkv, y_sum = tied(d_qkv, y_sum)
        far, near = [run_grad(plan[0][k], normed, d_qkv) for k in (1, 0)]
        a, b = scatter_rows_core(near, far)
        d_qkv, (a, b) = tied(d_qkv, (a, b))
        gate_grad, up_grad, (a, b) = later((a, b))
        qkv_sum = scatter_rows(a, b).astype(F32)
        y_sum = jnp.concatenate(y_sum, axis=1).astype(F32)
    else:
        qkv_sum = scatter_dp(dot(normed, d_qkv, 0, 0).astype(BF)).astype(F32)
    output = (hidden + y_sum).astype(BF)
    d_normed = scatter_y(dot(d_qkv, w_qkv, 1, 1))
    d_tokens, attn_gain_rows = rms_back(tokens.astype(F32), attn_gain32, d_normed)
    tokens_grad = d_tokens + d_hidden

    spread = lambda v: jnp.pad(v.reshape(dp, gshard), ((0, 0), (0, shard - gshard))).reshape(-1)
    small_part = jnp.concatenate(
        [
            router_part,
            jnp.stack(
                [
                    jnp.sum(attn_gain_rows, axis=0),
                    ffn_gain_part,
                    spread(jnp.sum(q_gain_rows, axis=(0, 1))),
                    spread(jnp.sum(k_gain_rows, axis=(0, 1))),
                ],
                axis=1,
            ),
        ],
        axis=1,
    )
    small_part = pad_to(small_part, lanes(experts + 4))
    if fast:
        small_sum = scatter_blocks(small_part.reshape(dp, shard, -1))
    else:
        small_sum = scatter_dp(small_part)
    small_sum = small_sum + swap_y(small_sum)
    return (
        output,
        tokens_grad,
        small_sum[:, experts],
        qkv_sum[:, : hq * HEAD],
        qkv_sum[:, hq * HEAD : (hq + hk) * HEAD],
        qkv_sum[:, (hq + hk) * HEAD :],
        o_sum.T,
        small_sum[:gshard, experts + 2],
        small_sum[:gshard, experts + 3],
        small_sum[:, experts + 1],
        small_sum[:, :experts],
        gate_grad,
        up_grad,
        down_grad,
    )


def solution(mesh):
    rows = P(("dp", "tensor"), None)
    both = P("dp", "tensor")
    return jax.shard_map(
        on_device,
        mesh=mesh,
        in_specs=(
            rows,
            P("dp"),
            both,
            both,
            both,
            P("tensor", "dp"),
            P("dp"),
            P("dp"),
            P("dp"),
            P("dp", None),
            P("dp", None, "tensor"),
            P("dp", None, "tensor"),
            P("dp", "tensor", None),
            P("dp", None),
            rows,
        ),
        out_specs=(
            rows,
            rows,
            P("dp"),
            both,
            both,
            both,
            P("tensor", "dp"),
            P("dp"),
            P("dp"),
            P("dp"),
            P("dp", None),
            P("dp", None, "tensor"),
            P("dp", None, "tensor"),
            P("dp", "tensor", None),
        ),
        check_vma=False,
    )
```

```python
import jax
import jax.numpy as jnp
from jax import lax
from jax.experimental import pallas as pl
from jax.experimental.pallas import tpu as pltpu
from jax.sharding import PartitionSpec as P

HEAD = 128
EPS = 1e-06
THETA = 1000000.0
BF = jnp.bfloat16
F32 = jnp.float32


def dot(a, b, ca, cb):
    return lax.dot_general(a, b, (((ca,), (cb,)), ((), ())), preferred_element_type=F32)


def rms(v, gain):
    return v * lax.rsqrt(jnp.mean(v * v, axis=-1, keepdims=True) + EPS) * gain


def rms_back(v, gain, u):
    inv = lax.rsqrt(jnp.mean(v * v, axis=-1, keepdims=True) + EPS)
    ug = u * gain
    grad = ug * inv - v * (jnp.mean(ug * v, axis=-1, keepdims=True) * inv * inv * inv)
    return grad, u * v * inv


def rope_tables(count):
    inverse = THETA ** (-(jnp.arange(HEAD // 2, dtype=F32) * 2.0 / HEAD))
    angles = jnp.arange(count, dtype=F32)[:, None] * inverse[None, :]
    cos, sin = jnp.cos(angles), jnp.sin(angles)
    return jnp.concatenate([cos, cos], axis=1), jnp.concatenate([-sin, sin], axis=1)


def half_turn(v):
    return pltpu.roll(v, HEAD // 2, 1)


def turned(raw, gain, cos, sin):
    v = rms(raw, gain)
    return (v * cos + half_turn(v) * sin).astype(BF)


def soft(q, k):
    scores = lax.dot_general(q, k, (((1,), (1,)), ((), ())), preferred_element_type=F32)
    scores = scores * HEAD ** (-0.5)
    row = lax.broadcasted_iota(jnp.int32, scores.shape, 0)
    column = lax.broadcasted_iota(jnp.int32, scores.shape, 1)
    e = jnp.where(row >= column, jnp.exp(scores), 0.0)
    return e * (1.0 / jnp.sum(e, axis=1, keepdims=True))


def attend_kernel(q_raw, k_raw, v_raw, gains, cos, sin, context, keys):
    @pl.when(pl.program_id(1) == 0)
    def _():
        keys[...] = turned(k_raw[...], gains[1:2], cos[...], sin[...])

    v = v_raw[...].astype(BF)
    for h in range(2):
        part = slice(h * HEAD, (h + 1) * HEAD)
        q = turned(q_raw[:, part], gains[0:1], cos[...], sin[...])
        p = soft(q, keys[...]).astype(BF)
        context[:, part] = lax.dot_general(
            p, v, (((1,), (0,)), ((), ())), preferred_element_type=F32
        ).astype(BF)


def attend_back_kernel(
    q_raw, k_raw, v_raw, d_context, gains, cos, sin, d_q, d_k, d_v, d_gains, keys, k_sum, v_sum
):
    at = pl.program_id(0)

    @pl.when(at == 0)
    def _():
        keys[...] = turned(k_raw[...], gains[1:2], cos[...], sin[...])
        k_sum[...] = jnp.zeros_like(k_sum)
        v_sum[...] = jnp.zeros_like(v_sum)
        d_gains[...] = jnp.zeros_like(d_gains)

    def back(raw, gain, u):
        return rms_back(raw, gain, u * cos[...] - half_turn(u) * sin[...])

    v = v_raw[...].astype(BF)
    scale = HEAD ** (-0.5)
    for h in range(2):
        part = slice(h * HEAD, (h + 1) * HEAD)
        raw = q_raw[:, part]
        q = turned(raw, gains[0:1], cos[...], sin[...])
        p = soft(q, keys[...])
        dc = d_context[:, part]
        dp = lax.dot_general(dc, v, (((1,), (1,)), ((), ())), preferred_element_type=F32)
        v_sum[...] += lax.dot_general(
            p.astype(BF), dc, (((0,), (0,)), ((), ())), preferred_element_type=F32
        )
        ds = (p * (dp - jnp.sum(p * dp, axis=1, keepdims=True))).astype(BF)
        dq = lax.dot_general(
            ds, keys[...], (((1,), (0,)), ((), ())), preferred_element_type=F32
        )
        k_sum[...] += lax.dot_general(ds, q, (((0,), (0,)), ((), ())), preferred_element_type=F32)
        grad, gain_rows = back(raw, gains[0:1], dq * scale)
        d_q[:, part] = grad.astype(BF)
        d_gains[0:1, :] += jnp.sum(gain_rows, axis=0, keepdims=True)

    @pl.when(at == pl.num_programs(0) - 1)
    def _():
        grad, gain_rows = back(k_raw[...], gains[1:2], k_sum[...] * scale)
        d_k[...] = grad.astype(BF)
        d_v[...] = v_sum[...].astype(BF)
        d_gains[1:2, :] += jnp.sum(gain_rows, axis=0, keepdims=True)


def run_attend(qkv, gains, cos, sin, hq, hk):
    seq = qkv.shape[0]
    pairs = hq // hk // 2
    block = lambda width, index: pl.BlockSpec((seq, width * HEAD), index)
    whole = lambda rows: pl.BlockSpec((rows, HEAD), lambda i, j: (0, 0))
    return pl.pallas_call(
        attend_kernel,
        grid=(hk, pairs),
        in_specs=[
            block(2, lambda i, j: (0, i * pairs + j)),
            block(1, lambda i, j: (0, hq + i)),
            block(1, lambda i, j: (0, hq + hk + i)),
            whole(8),
            whole(seq),
            whole(seq),
        ],
        out_specs=block(2, lambda i, j: (0, i * pairs + j)),
        out_shape=jax.ShapeDtypeStruct((seq, hq * HEAD), BF),
        scratch_shapes=[pltpu.VMEM((seq, HEAD), BF)],
        name="attend",
    )(qkv, qkv, qkv, gains, cos, sin)


def run_attend_back(head, qkv, d_context, gains, cos, sin, hq, hk):
    seq = qkv.shape[0]
    pairs = hq // hk // 2
    block = lambda width, index: pl.BlockSpec((seq, width * HEAD), index)
    whole = lambda rows: pl.BlockSpec((rows, HEAD), lambda j: (0, 0))
    return pl.pallas_call(
        attend_back_kernel,
        grid=(pairs,),
        in_specs=[
            block(2, lambda j: (0, head * pairs + j)),
            block(1, lambda j: (0, hq + head)),
            block(1, lambda j: (0, hq + hk + head)),
            block(2, lambda j: (0, head * pairs + j)),
            whole(8),
            whole(seq),
            whole(seq),
        ],
        out_specs=[block(2, lambda j: (0, j)), whole(seq), whole(seq), whole(8)],
        out_shape=[
            jax.ShapeDtypeStruct((seq, 2 * pairs * HEAD), BF),
            jax.ShapeDtypeStruct((seq, HEAD), BF),
            jax.ShapeDtypeStruct((seq, HEAD), BF),
            jax.ShapeDtypeStruct((8, HEAD), F32),
        ],
        scratch_shapes=[
            pltpu.VMEM((seq, HEAD), BF),
            pltpu.VMEM((seq, HEAD), F32),
            pltpu.VMEM((seq, HEAD), F32),
        ],
        name="attend_back",
    )(qkv, qkv, qkv, d_context, gains, cos, sin)


def split2(v):
    high = v.astype(BF)
    return high, (v - high.astype(F32)).astype(BF)


def gather_dp(v):
    return lax.all_gather(v, "dp", axis=0, tiled=True)


def gather_all(v):
    return lax.all_gather(v, ("dp", "tensor"), axis=0, tiled=True)


def scatter_all(v):
    return lax.psum_scatter(v, ("dp", "tensor"), scatter_dimension=0, tiled=True)


def scatter_dp(v):
    return lax.psum_scatter(v, "dp", scatter_dimension=0, tiled=True)


def pieces(width, dp, seq):
    count = 1 if dp * seq <= 8192 else 4
    step = width // count // 128 * 128
    edges = [step * i for i in range(count)] + [width]
    return list(zip(edges[:-1], edges[1:]))


def after(v, earlier):
    return v if earlier is None else lax.optimization_barrier((v, earlier))[0]


def dispatch(pick, own, dp, seq, earlier):
    blocks = []
    for low, high in pieces(own.shape[1], dp, seq):
        every = gather_all(after(own[:, low:high], earlier)).reshape(dp, seq, high - low)
        block = jnp.einsum("gest,gtd->gesd", pick, every, preferred_element_type=F32).astype(BF)
        blocks.append(block)
        earlier = block if len(pieces(own.shape[1], dp, seq)) > 1 else None
    return jnp.concatenate(blocks, axis=3)


def combine(pick, rows, dp, seq, earlier):
    blocks = []
    for low, high in pieces(rows.shape[3], dp, seq):
        tok = jnp.einsum(
            "gest,gesd->gtd",
            pick,
            after(rows[:, :, :, low:high], earlier),
            preferred_element_type=F32,
        ).astype(BF)
        blocks.append(scatter_all(tok.reshape(dp * seq, high - low)))
        earlier = blocks[-1] if len(pieces(rows.shape[3], dp, seq)) > 1 else None
    return jnp.concatenate(blocks, axis=1).astype(F32)


GRID = [(z, x, c) for z in range(4) for x in range(2) for c in range(2)]
SPLIT = (0, 768, 1536, 1792, 2048)


def at(z, x, c):
    return z % 4 * 4 + x % 2 * 2 + c % 2


def shift_z(v, k):
    return lax.ppermute(v, "dp", [(at(z, x, c), at(z + k, x, c)) for z, x, c in GRID])


def swap_x(v):
    return lax.ppermute(v, "dp", [(at(z, x, c), at(z, x + 1, c)) for z, x, c in GRID])


def swap_c(v):
    return lax.ppermute(v, "dp", [(at(z, x, c), at(z, x, c + 1)) for z, x, c in GRID])


def swap_y(v):
    return lax.ppermute(v, "tensor", [(0, 1), (1, 0)])


def gather_y(v):
    other = swap_y(v)
    first = lax.axis_index("tensor") == 0
    return jnp.concatenate([jnp.where(first, v, other), jnp.where(first, other, v)])


def scatter_y(v):
    a, b = jnp.split(v, 2)
    first = lax.axis_index("tensor") == 0
    kept, sent = jnp.where(first, a, b), jnp.where(first, b, a)
    return kept.astype(F32) + swap_y(sent.astype(BF)).astype(F32)


def gather_z(v, way):
    one, three = shift_z(v, 1), shift_z(v, -1)
    two = shift_z(one, 1) if way > 0 else shift_z(three, -1)
    return jnp.stack([v, one, two, three])


def add2(a, b):
    return (a.astype(F32) + b.astype(F32)).astype(BF)


def reduce_z(v, way, two=None):
    two = shift_z(v[2], -way) if two is None else two
    if way > 0:
        one = shift_z(add2(v[1], two), -1)
        three = shift_z(v[3], 1)
    else:
        three = shift_z(add2(v[3], two), 1)
        one = shift_z(v[1], -1)
    return (v[0].astype(F32) + one.astype(F32) + three.astype(F32)).astype(BF)


def tied(v, w):
    return lax.optimization_barrier((v, w))


def gather_rel(v1, v2, v5, v6, plan, aside):
    w5 = jnp.stack([v5, swap_x(v5)])
    w6 = jnp.stack([v6, swap_y(v6)])
    s1 = gather_z(v1, 1)
    s2 = gather_z(v2, -1)
    w5 = jnp.stack([w5, swap_y(w5)])
    w6 = jnp.stack([w6, swap_x(w6)])
    s1, s2, w5, w6 = lax.optimization_barrier((s1, s2, w5, w6))
    s1x, s2y = swap_x(s1), swap_y(s2)
    five = [shift_z(w5, 1), shift_z(w5, -1)]
    six = [shift_z(w6, 1), shift_z(w6, -1)]
    (five, six), (s1x, s2y), plan = lax.optimization_barrier(((five, six), (s1x, s2y), plan))
    s1 = jnp.stack([s1, s1x])
    s2 = jnp.stack([s2, s2y])
    s1y, s2x = swap_y(s1), swap_x(s2)
    five.append(shift_z(five[0], 1))
    six.append(shift_z(six[1], -1))
    plan, (five, six) = tied(plan, (five, six))
    o5 = jnp.stack([w5, five[0], five[2], five[1]])
    o6 = jnp.stack([w6, six[0], six[2], six[1]])
    (s1y, s2x), done = tied((s1y, s2x), aside(plan))
    first = (s1, s1y, s2, s2x, o5, o6)
    return first, tuple(swap_c(v) for v in first), plan, done


def scatter_core(near, far):
    p5, p6, p1, p2 = [add2(near[i], swap_c(far[i])) for i in (2, 3, 0, 1)]
    return lax.optimization_barrier((p1, p2, p5, p6))


def scatter_first(p1, p2, p5, p6, aside=None):
    two5, two6 = shift_z(p5[2], -1), shift_z(p6[2], 1)
    (two5, two6), aside = tied((two5, two6), aside)
    p5 = reduce_z(p5, 1, two5)
    p6 = reduce_z(p6, -1, two6)
    p1 = add2(p1[0], swap_y(p1[1]))
    p2 = add2(p2[0], swap_x(p2[1]))
    return (p1, p2, p5, p6), aside


def scatter_second(p1, p2, p5, p6):
    p5 = add2(p5[0], swap_y(p5[1]))
    p6 = add2(p6[0], swap_x(p6[1]))
    p1 = add2(p1[0], swap_x(p1[1]))
    p2 = add2(p2[0], swap_y(p2[1]))
    return p1, p2, p5, p6


def scatter_last(p1, p2, p5, p6):
    p5 = add2(p5[0], swap_x(p5[1]))
    p6 = add2(p6[0], swap_y(p6[1]))
    return reduce_z(p1, 1), reduce_z(p2, -1), p5, p6


def scatter_rows_core(near, far):
    return [add2(n, swap_c(f)) for n, f in zip(near, far)]


def scatter_rows(a, b):
    b = reduce_z(b, -1)
    a = add2(a[0], swap_x(a[1]))
    b = add2(b[0], swap_x(b[1]))
    return jnp.concatenate([reduce_z(a, 1), b], axis=1)


def scatter_blocks(v):
    d = jnp.arange(16)
    v = jnp.take(v, sequence_at(d // 8, d // 2 % 4, d % 2), axis=0)
    v = (v[:8] + swap_c(v[8:])).reshape(4, 2, *v.shape[1:])
    v = v[:, 0] + swap_x(v[:, 1])
    one = shift_z(v[1] + shift_z(v[2], -1), -1)
    return v[0] + one + shift_z(v[3], 1)


def sequence_at(dc, dz, dx):
    at = lax.axis_index("dp")
    return (at // 4 - dz) % 4 * 4 + (at // 2 % 2 + dx) % 2 * 2 + (at % 2 + dc) % 2


def nn(a, b):
    return lax.dot_general(a, b, (((1,), (0,)), ((), ())), preferred_element_type=F32)


def nt(a, b):
    return lax.dot_general(a, b, (((1,), (1,)), ((), ())), preferred_element_type=F32)


def pick_rows(rank, slots):
    at_slot = lax.broadcasted_iota(jnp.int32, (slots, rank.shape[1]), 0).astype(F32)
    return jnp.concatenate(
        [(rank[e : e + 1, :] == at_slot).astype(F32).astype(BF) for e in range(rank.shape[0])],
        axis=0,
    )


def pick_cols(rank, slots):
    at_slot = lax.broadcasted_iota(jnp.int32, (rank.shape[0], slots), 1).astype(F32)
    return jnp.concatenate(
        [(rank[:, e : e + 1] == at_slot).astype(F32).astype(BF) for e in range(rank.shape[1])],
        axis=1,
    )


def cot_kernel(where, rank, cot_a, cot_b, down, cots, d_act):
    slots = cots.shape[2] // 2
    for dx, cot in enumerate((cot_a, cot_b)):
        both = nn(pick_rows(rank[dx], slots), cot[0]).astype(BF)
        for e in range(2):
            cots[e, 0, dx * slots : (dx + 1) * slots, :] = both[e * slots : (e + 1) * slots]
    for e in range(2):
        d_act[e, 0] = nt(cots[e, 0], down[e])


def expert_kernel(
    rank, rank_t, cols, d_act, x1a, x1b, x2a, x2b, x5, x6, w_gate, w_up,
    rows, scaled, d_g, d_u, t1, t2, t5, t6, back,
):
    slots = rows.shape[2] // 2
    n = x1a.shape[2]
    gates = []
    for dx, x2 in enumerate((x2a, x2b)):
        pick = pick_rows(rank[dx], slots)
        low, high = pick[:, :n], pick[:, n:]
        block1 = nn(low, x1a[dx, 0]) + nn(high, x1b[dx, 0])
        block2 = nn(low, x2[0, 0]) + nn(high, x2[1, 0])
        block5 = nn(low, x5[0, 0, dx]) + nn(high, x5[0, 1, dx])
        block6 = nn(low, x6[0, dx, 0]) + nn(high, x6[0, dx, 1])
        low = dx * slots
        for e in range(2):
            part = slice(e * slots, (e + 1) * slots)
            rows[e, 0, low : low + slots, 0:768] = block1[part].astype(BF)
            rows[e, 0, low : low + slots, 768:1536] = block2[part].astype(BF)
            rows[e, 0, low : low + slots, 1536:1792] = block5[part, :256].astype(BF)
            rows[e, 0, low : low + slots, 1792:2048] = block6[part].astype(BF)
            both = cols[e, 0:1, :] + cols[e, 1:2, :]
            gates.append(jnp.sum(block5[part, 256:] * both, axis=1, keepdims=True))
    extras = []
    for e in range(2):
        gate = jnp.concatenate([gates[e], gates[2 + e]], axis=0)
        g = nn(rows[e, 0], w_gate[e])
        u = nn(rows[e, 0], w_up[e])
        da = d_act[e, 0]
        sig = 1.0 / (1.0 + jnp.exp(-g))
        silu = g * sig
        act = silu * u
        scaled[e, 0] = (act * gate).astype(BF)
        d_gate = jnp.sum(act * da, axis=1, keepdims=True)
        da = da * gate
        dg = (da * u * sig * (1.0 + g * (1.0 - sig))).astype(BF)
        du = (da * silu).astype(BF)
        d_g[e, 0] = dg
        d_u[e, 0] = du
        high = d_gate.astype(BF).astype(F32)
        extras.append(high * cols[e, 0:1, :] + (d_gate - high) * cols[e, 1:2, :])
        dr = (nt(dg, w_gate[e]) + nt(du, w_up[e])).astype(BF)
        for dx in range(2):
            back[dx, e * slots : (e + 1) * slots, :] = dr[dx * slots : (dx + 1) * slots]
    extra = [
        jnp.concatenate([extras[e][dx * slots : (dx + 1) * slots] for e in range(2)], axis=0)
        for dx in range(2)
    ]
    put_back(rank_t, back, t1, t2, t5, t6, slots, extra)


def put_back(rank_t, back, t1, t2, t5, t6, slots, extra=None):
    for dx in range(2):
        pick_t = pick_cols(rank_t[dx], slots)
        n = pick_t.shape[0] // 2
        p1, p2, p5, p6 = [
            nn(pick_t, back[dx, :, a:b]).astype(BF) for a, b in zip(SPLIT[:-1], SPLIT[1:])
        ]
        for dy in range(2):
            half = slice(dy * n, (dy + 1) * n)
            t1[dy, dx, 0] = p1[half]
            t2[dx, dy, 0] = p2[half]
            t5[0, dy, dx, :, 0:256] = p5[half]
            t6[0, dx, dy] = p6[half]
        if extra is not None:
            p7 = nn(pick_t, extra[dx].astype(BF)).astype(BF)
            for dy in range(2):
                t5[0, dy, dx, :, 256:] = p7[dy * n : (dy + 1) * n]


def out_kernel(rank_t, scaled, down, t1, t2, t5, t6, back):
    slots = scaled.shape[2] // 2
    for e in range(2):
        y = nn(scaled[e, 0], down[e]).astype(BF)
        for dx in range(2):
            back[dx, e * slots : (e + 1) * slots, :] = y[dx * slots : (dx + 1) * slots]
    put_back(rank_t, back, t1, t2, t5, t6, slots)


def grad_kernel(where, left, right, a, b):
    both = lax.dot_general(
        left[...], right[...], (((0,), (0,)), ((), ())), preferred_element_type=F32
    ).astype(BF)
    width = a.shape[-1]
    a[0, 0] = both[:, :width]
    b[0, 0] = both[:, width:]


def run_grad(where, left, right):
    count, columns = right.shape
    width = columns * 9 // 16 // 128 * 128
    shard = left.shape[1] // 16
    return pl.pallas_call(
        grad_kernel,
        grid_spec=pltpu.PrefetchScalarGridSpec(
            num_scalar_prefetch=1,
            grid=(2, 4),
            in_specs=[
                pl.BlockSpec((count, shard), lambda dx, dz, w: (0, w[2 * dz + dx])),
                pl.BlockSpec((count, columns), lambda dx, dz, w: (0, 0)),
            ],
            out_specs=[
                pl.BlockSpec((1, 1, shard, width), lambda dx, dz, w: (dx, dz, 0, 0)),
                pl.BlockSpec((1, 1, shard, columns - width), lambda dx, dz, w: (dz, dx, 0, 0)),
            ],
        ),
        out_shape=[
            shaped((2, 4, shard, width), BF),
            shaped((4, 2, shard, columns - width), BF),
        ],
        compiler_params=LIMIT,
        name="grad",
    )(where, left, right)


def pair(*tail):
    return pl.BlockSpec((2, *tail), lambda i, *_: (i,) + (0,) * len(tail))


def z_last(*lead):
    def spec(rows, columns):
        return pl.BlockSpec(
            (*lead, 1, rows, columns), lambda i, *_: (0,) * len(lead) + (i, 0, 0)
        )

    return spec


def z_first(rows, columns):
    return pl.BlockSpec((1, 2, 2, rows, columns), lambda i, *_: (i, 0, 0, 0, 0))


def block_specs(n, extra):
    return [z_last(2, 2)(n, 768), z_last(2, 2)(n, 768), z_first(n, 256 + extra), z_first(n, 256)]


def block_shapes(n, extra):
    shapes = [(2, 2, 4, n, 768), (2, 2, 4, n, 768), (4, 2, 2, n, 256 + extra), (4, 2, 2, n, 256)]
    return [shaped(v, BF) for v in shapes]


def by_expert(*tail):
    return pl.BlockSpec((2, 1, *tail), lambda i, *_: (0, i) + (0,) * len(tail))


def fixed(*shape):
    return pl.BlockSpec(
        shape, lambda i, *_: (0,) * len(shape), pipeline_mode=pl.Buffered(1)
    )


def shaped(shape, kind):
    return jax.ShapeDtypeStruct(shape, kind)


LIMIT = pltpu.CompilerParams(vmem_limit_bytes=60000 * 1024)


def run_cots(where, rank, cot_all, down, slots):
    seq, width = cot_all.shape[1:]
    ff = down.shape[1]
    return pl.pallas_call(
        cot_kernel,
        grid_spec=pltpu.PrefetchScalarGridSpec(
            num_scalar_prefetch=1,
            grid=(4,),
            in_specs=[
                pair(2, seq),
                pl.BlockSpec((1, seq, width), lambda i, w: (w[2 * i], 0, 0)),
                pl.BlockSpec((1, seq, width), lambda i, w: (w[2 * i + 1], 0, 0)),
                fixed(2, ff, width),
            ],
            out_specs=[by_expert(2 * slots, width), by_expert(2 * slots, ff)],
        ),
        out_shape=[shaped((2, 4, 2 * slots, width), BF), shaped((2, 4, 2 * slots, ff), F32)],
        compiler_params=LIMIT,
        name="cots",
    )(where, rank, cot_all, cot_all, down)


def run_experts(rank, rank_t, cols, d_act, parts, w_gate, w_up, slots):
    s1, s1y, s2, s2x, o5, o6 = parts
    n = s1.shape[2]
    seq, width, ff = 2 * n, w_gate.shape[1], w_gate.shape[2]
    return pl.pallas_call(
        expert_kernel,
        grid=(4,),
        in_specs=[
            pair(2, seq),
            pair(seq, 2),
            fixed(*cols.shape),
            by_expert(2 * slots, ff),
            z_last(2)(n, 768),
            z_last(2)(n, 768),
            z_last(2)(n, 768),
            z_last(2)(n, 768),
            z_first(n, 384),
            z_first(n, 256),
            fixed(2, width, ff),
            fixed(2, width, ff),
        ],
        out_specs=[
            by_expert(2 * slots, width),
            by_expert(2 * slots, ff),
            by_expert(2 * slots, ff),
            by_expert(2 * slots, ff),
        ]
        + block_specs(n, 128),
        out_shape=[
            shaped((2, 4, 2 * slots, width), BF),
            shaped((2, 4, 2 * slots, ff), BF),
            shaped((2, 4, 2 * slots, ff), BF),
            shaped((2, 4, 2 * slots, ff), BF),
        ]
        + block_shapes(n, 128),
        scratch_shapes=[pltpu.VMEM((2, 2 * slots, width), BF)],
        compiler_params=LIMIT,
        name="experts",
    )(
        rank, rank_t, cols, d_act, s1, s1y, s2, s2x, o5, o6, w_gate, w_up,
    )


def run_outs(rank_t, scaled, down, slots):
    seq, ff, width = rank_t.shape[1], down.shape[1], down.shape[2]
    return pl.pallas_call(
        out_kernel,
        grid=(4,),
        in_specs=[pair(seq, 2), by_expert(2 * slots, ff), fixed(2, ff, width)],
        out_specs=block_specs(seq // 2, 0),
        out_shape=block_shapes(seq // 2, 0),
        scratch_shapes=[pltpu.VMEM((2, 2 * slots, width), BF)],
        compiler_params=LIMIT,
        name="outs",
    )(rank_t, scaled, down)


def flip(v, axis, y):
    a, b = jnp.split(v, 2, axis=axis)
    return jnp.where(y == 0, v, jnp.concatenate([b, a], axis=axis))


def slot_plan(ids_all, experts):
    y = lax.axis_index("tensor")
    seq = ids_all.shape[1]
    mine = lax.axis_index("dp") * 2 + jnp.arange(2, dtype=jnp.int32)
    mask = jnp.any(ids_all[:, None, :, :] == mine[None, :, None, None], axis=3)
    before = (jnp.arange(seq)[:, None] < jnp.arange(seq)[None, :]).astype(BF)
    rank = jnp.einsum("gea,ab->geb", mask.astype(BF), before, preferred_element_type=F32)
    rank = jnp.where(mask, rank, -1.0)
    d = jnp.arange(16)
    where = sequence_at(d // 8, d // 2 % 4, d % 2)
    rank = jnp.take(rank, where, axis=0)
    rank_rel = flip(rank, 2, y)
    rank_t = jnp.swapaxes(rank_rel, 1, 2)
    column = jnp.arange(128)
    cols = (
        column[None, None, :] == (mine[:, None] + jnp.array([[0, experts]]))[:, :, None]
    ).astype(F32)
    halves = lambda v: (v[:8], v[8:])
    return halves(where.astype(jnp.int32)), halves(rank), halves(rank_rel), halves(rank_t), cols


def moe_small(plan, cot_all, ffn_in, gate_x, gate_weight, up_weight, down_weight, slots):

    def cot_rows(plan):
        return [run_cots(plan[0][k], plan[1][k], cot_all, down_weight, slots) for k in (0, 1)]

    v1, v2, v5, v6 = [ffn_in[:, a:b] for a, b in zip(SPLIT[:-1], SPLIT[1:])]
    v5 = jnp.concatenate([v5, gate_x], axis=1)
    *parts, plan, both = gather_rel(v1, v2, v5, v6, plan, cot_rows)
    rank_rel, rank_t, cols = plan[2:]
    cots, d_act = zip(*both)
    far, near = [
        run_experts(
            rank_rel[k], rank_t[k], cols, d_act[k], parts[k], gate_weight, up_weight, slots
        )
        for k in (1, 0)
    ]
    step = scatter_core(near[4:], far[4:])
    step, (near, far, cots) = scatter_first(*step, (near[:4], far[:4], cots))
    kept = lambda i: (near[i], far[i])
    outs = [run_outs(rank_t[k], kept(1)[k], down_weight, slots) for k in (0, 1)]
    total = lambda spec, a, b: jnp.einsum(spec, a[0], b[0], preferred_element_type=F32) + jnp.einsum(
        spec, a[1], b[1], preferred_element_type=F32
    )
    down_grad = total("egsf,egsd->efd", kept(1), cots)
    step, (outs, down_grad) = tied(step, (outs, down_grad))
    step, (p1, p2, p5, p6) = tied(scatter_second(*step), scatter_core(*outs))
    d1, d2, d5, d6 = scatter_last(*step)
    p1 = add2(p1[0], swap_y(p1[1]))
    p2 = add2(p2[0], swap_x(p2[1]))
    d_sum = jnp.concatenate([d1, d2, d5[:, :256], d6, d5[:, 256:]], axis=1)
    d_sum, (p5, p6) = tied(d_sum, (p5, p6))
    d_sum = d_sum.astype(F32)

    def later(i, aside):
        (rows, grads), aside = tied((kept(0), kept(i)), aside)
        return total("egsd,egsf->edf", rows, grads), aside

    return d_sum, (p1, p2, p5, p6), later, down_grad


def moe_large(
    ids_all, cotangent, ffn_in, gate_x, gate_weight, up_weight, down_weight, experts, slots
):
    dp, seq = ids_all.shape[:2]
    local = gate_weight.shape[0]
    dp_at = lax.axis_index("dp")
    mine = dp_at * local + jnp.arange(local, dtype=jnp.int32)
    mask = jnp.any(ids_all[:, :, None, :] == mine[None, None, :, None], axis=3).astype(BF)
    gate_all = gather_all(gate_x).reshape(dp, seq, -1)
    before = (jnp.arange(seq)[:, None] > jnp.arange(seq)[None, :]).astype(BF)
    rank = jnp.einsum("ab,gbe->gea", before, mask, preferred_element_type=F32)
    rank = jnp.where(jnp.swapaxes(mask, 1, 2) > 0, rank, -1.0)
    pick = (rank[:, :, None, :] == jnp.arange(slots, dtype=F32)[None, None, :, None]).astype(BF)

    cots = dispatch(pick, cotangent, dp, seq, None)
    rows = dispatch(pick, ffn_in, dp, seq, cots)
    gate_tok = lax.dynamic_slice_in_dim(gate_all, dp_at * local, local, 2).astype(
        F32
    ) + lax.dynamic_slice_in_dim(gate_all, experts + dp_at * local, local, 2).astype(F32)
    gate_slot = jnp.sum(pick.astype(F32) * jnp.swapaxes(gate_tok, 1, 2)[:, :, None, :], axis=3)

    g_proj = jnp.einsum("gesd,edf->gesf", rows, gate_weight, preferred_element_type=F32)
    u_proj = jnp.einsum("gesd,edf->gesf", rows, up_weight, preferred_element_type=F32)
    d_act = jnp.einsum("gesd,efd->gesf", cots, down_weight, preferred_element_type=F32)
    sig = 1.0 / (1.0 + jnp.exp(-g_proj))
    silu = g_proj * sig
    act = silu * u_proj
    scaled = (act * gate_slot[..., None]).astype(BF)
    d_gate_slot = jnp.sum(act * d_act, axis=3)
    d_act = d_act * gate_slot[..., None]
    d_g = (d_act * u_proj * sig * (1.0 + g_proj * (1.0 - sig))).astype(BF)
    d_u = (d_act * silu).astype(BF)
    d_rows = (
        jnp.einsum("gesf,edf->gesd", d_g, gate_weight, preferred_element_type=F32)
        + jnp.einsum("gesf,edf->gesd", d_u, up_weight, preferred_element_type=F32)
    ).astype(BF)
    dg_high, dg_low = split2(d_gate_slot)
    column = jnp.arange(lanes(2 * experts))
    high_col = (column[None, :] == mine[:, None])[None, :, None, :]
    low_col = (column[None, :] == experts + mine[:, None])[None, :, None, :]
    extra = jnp.where(high_col, dg_high[..., None], jnp.where(low_col, dg_low[..., None], 0.0))
    d_rows = jnp.concatenate([d_rows, extra.astype(BF)], axis=3)
    d_sum = combine(pick, d_rows, dp, seq, None)

    y_rows = jnp.einsum("gesf,efd->gesd", scaled, down_weight, preferred_element_type=F32)
    y_sum = combine(pick, y_rows.astype(BF), dp, seq, d_sum)
    down_grad = jnp.einsum("gesf,gesd->efd", scaled, cots, preferred_element_type=F32)
    gate_grad = jnp.einsum("gesd,gesf->edf", rows, d_g, preferred_element_type=F32)
    up_grad = jnp.einsum("gesd,gesf->edf", rows, d_u, preferred_element_type=F32)

    return d_sum, y_sum, gate_grad, up_grad, down_grad


def pad_to(v, width):
    return jnp.pad(v, ((0, 0), (0, width - v.shape[1])))


def lanes(count):
    return -(-count // 128) * 128


def on_device(
    tokens,
    attn_gain,
    q_weight,
    key_matrix,
    value_matrix,
    o_weight,
    query_norm_gain,
    k_gain,
    ffn_gain,
    router_weight,
    gate_weight,
    up_weight,
    down_weight,
    expert_ids,
    cotangent,
):
    dp = lax.axis_size("dp")
    tensor = lax.axis_size("tensor")
    dp_at = lax.axis_index("dp")
    own, width = tokens.shape
    seq = expert_ids.shape[0]
    begin = lax.axis_index("tensor") * own
    local = gate_weight.shape[0]
    experts = local * dp
    slots = 10 * seq * expert_ids.shape[1] // (8 * experts)
    slots = -(-slots // 16) * 16
    shard = q_weight.shape[0]
    gshard = query_norm_gain.shape[0]
    hq = q_weight.shape[1] // HEAD
    hk = key_matrix.shape[1] // HEAD
    qkv_width = (hq + 2 * hk) * HEAD
    top = expert_ids.shape[1]
    fast = (dp, tensor, local, seq, width) == (16, 2, 2, 384, 2048)

    arange_e = jnp.arange(experts, dtype=jnp.int32)
    own_ids = lax.dynamic_slice_in_dim(expert_ids, begin, own, 0)
    own_mask = jnp.any(own_ids[:, :, None] == arange_e[None, None, :], axis=1)

    gain_rows = jnp.stack(
        [
            attn_gain,
            ffn_gain,
            jnp.pad(query_norm_gain, (0, shard - gshard)),
            jnp.pad(k_gain, (0, shard - gshard)),
        ],
        axis=1,
    )
    ids_rows = expert_ids.reshape(shard, -1).astype(BF)
    small = jnp.concatenate([router_weight, gain_rows, ids_rows], axis=1)
    small = pad_to(small, lanes(small.shape[1]))
    small_end = qkv_width + small.shape[1]
    all_in = gather_dp(
        jnp.concatenate([q_weight, key_matrix, value_matrix, small, o_weight.T], axis=1)
    )
    layer_in = gather_y(tokens)
    o_t = all_in[:, small_end:]
    if fast:
        cot_all = gather_dp(gather_y(cotangent)).reshape(dp, seq, width)

    w_qkv = all_in[:, :qkv_width]
    router = all_in[:, qkv_width : qkv_width + experts]
    gains = all_in[:, qkv_width + experts : qkv_width + experts + 4].astype(F32)
    ids_all = all_in[:, qkv_width + experts + 4 :][:, : seq * top // shard]
    ids_all = ids_all.astype(jnp.int32).reshape(dp, seq, top)
    attn_gain32 = gains[:, 0]
    ffn_gain32 = gains[:, 1]
    q_gain32 = gains[:, 2].reshape(dp, shard)[:, :gshard].reshape(-1)
    k_gain32 = gains[:, 3].reshape(dp, shard)[:, :gshard].reshape(-1)

    residual = layer_in.astype(F32)
    normed = rms(residual, attn_gain32).astype(BF)
    qkv = dot(normed, w_qkv, 1, 0)
    cos, sin = rope_tables(seq)
    head_gains = jnp.pad(jnp.stack([q_gain32, k_gain32]), ((0, 6), (0, 0)))
    context = run_attend(qkv, head_gains, cos, sin, hq, hk)
    if fast:
        plan = slot_plan(ids_all, experts)
    hidden = tokens.astype(F32) + scatter_y(dot(context, o_t, 1, 1))

    ffn_in = rms(hidden, ffn_gain32).astype(BF)
    logits = dot(ffn_in, router, 1, 0)
    chosen = jnp.where(own_mask, jnp.exp(logits), 0.0)
    gates = chosen / jnp.sum(chosen, axis=1, keepdims=True)
    gate_high, gate_low = split2(gates)
    gate_x = pad_to(jnp.concatenate([gate_high, gate_low], axis=1), lanes(2 * experts))
    args = (gate_weight, up_weight, down_weight)
    if fast:
        d_sum, y_sum, later, down_grad = moe_small(
            plan, cot_all, ffn_in, gate_x, *args, slots
        )
    else:
        d_sum, y_sum, gate_grad, up_grad, down_grad = moe_large(
            ids_all, cotangent, ffn_in, gate_x, *args, experts, slots
        )
    d_gates = d_sum[:, width : width + experts] + d_sum[:, width + experts : width + 2 * experts]
    d_logits = gates * (d_gates - jnp.sum(gates * d_gates, axis=1, keepdims=True))
    d_high, d_low = split2(d_logits)
    d_ffn = d_sum[:, :width] + dot(d_high, router, 1, 1) + dot(d_low, router, 1, 1)
    router_part = dot(ffn_in, d_high, 0, 0) + dot(ffn_in, d_low, 0, 0)
    d_hidden, ffn_gain_rows = rms_back(hidden, ffn_gain32, d_ffn)
    ffn_gain_part = jnp.sum(ffn_gain_rows, axis=0)
    d_hidden = d_hidden + cotangent.astype(F32)
    d_attn = d_hidden.astype(BF)
    if fast:
        p1, p2, p5, p6 = y_sum
        d_attn, (p1, p2) = tied(d_attn, (p1, p2))
    d_attn = gather_y(d_attn)

    o_part = dot(d_attn, context, 0, 0).astype(BF)
    d_attn, o_part = tied(d_attn, o_part)
    o_sum = scatter_dp(o_part).astype(F32)
    if fast:
        two5, two6 = shift_z(p5[2], -1), shift_z(p6[2], 1)
        p1 = add2(p1[0], swap_x(p1[1]))
        p2 = add2(p2[0], swap_y(p2[1]))
        gate_grad, d_attn = later(2, d_attn)
    d_context = dot(d_attn, o_t, 1, 0).astype(BF)
    heads = []
    for head in range(hk):
        heads.append(run_attend_back(head, qkv, d_context, head_gains, cos, sin, hq, hk))
        if fast and head == 0:
            aside = (p1, p2, two5, two6, gate_grad)
            d_context, heads, aside = lax.optimization_barrier((d_context, heads, aside))
            p1, p2, two5, two6, gate_grad = aside
            p5, p6 = reduce_z(p5, 1, two5), reduce_z(p6, -1, two6)
    d_qkv = jnp.concatenate([h[k] for k in range(3) for h in heads], axis=1)
    q_gain_part = sum(h[3][0] for h in heads)
    k_gain_part = sum(h[3][1] for h in heads)
    if fast:
        d_qkv, (p5, p6) = tied(d_qkv, (p5, p6))
        p5 = add2(p5[0], swap_y(p5[1]))
        p6 = add2(p6[0], swap_x(p6[1]))
        far, near = [run_grad(plan[0][k], normed, d_qkv) for k in (1, 0)]
        y_sum = scatter_last(p1, p2, p5, p6)
        (a, b), y_sum = tied(scatter_rows_core(near, far), y_sum)
        d_qkv, (a, b) = tied(d_qkv, (a, b))
        up_grad, (a, b) = later(3, (a, b))
        qkv_sum = scatter_rows(a, b).astype(F32)
        y_sum = jnp.concatenate(y_sum, axis=1).astype(F32)
    else:
        qkv_sum = scatter_dp(dot(normed, d_qkv, 0, 0).astype(BF)).astype(F32)
    output = (hidden + y_sum).astype(BF)
    d_normed = scatter_y(dot(d_qkv, w_qkv, 1, 1))
    d_tokens, attn_gain_rows = rms_back(tokens.astype(F32), attn_gain32, d_normed)
    tokens_grad = d_tokens + d_hidden

    spread = lambda v: jnp.pad(v.reshape(dp, gshard), ((0, 0), (0, shard - gshard))).reshape(-1)
    small_part = jnp.concatenate(
        [
            router_part,
            jnp.stack(
                [
                    jnp.sum(attn_gain_rows, axis=0),
                    ffn_gain_part,
                    spread(q_gain_part),
                    spread(k_gain_part),
                ],
                axis=1,
            ),
        ],
        axis=1,
    )
    small_part = pad_to(small_part, lanes(experts + 4))
    if fast:
        small_sum = scatter_blocks(small_part.reshape(dp, shard, -1))
    else:
        small_sum = scatter_dp(small_part)
    small_sum = small_sum + swap_y(small_sum)
    return (
        output,
        tokens_grad,
        small_sum[:, experts],
        qkv_sum[:, : hq * HEAD],
        qkv_sum[:, hq * HEAD : (hq + hk) * HEAD],
        qkv_sum[:, (hq + hk) * HEAD :],
        o_sum.T,
        small_sum[:gshard, experts + 2],
        small_sum[:gshard, experts + 3],
        small_sum[:, experts + 1],
        small_sum[:, :experts],
        gate_grad,
        up_grad,
        down_grad,
    )


def solution(mesh):
    rows = P(("dp", "tensor"), None)
    both = P("dp", "tensor")
    return jax.shard_map(
        on_device,
        mesh=mesh,
        in_specs=(
            rows,
            P("dp"),
            both,
            both,
            both,
            P("tensor", "dp"),
            P("dp"),
            P("dp"),
            P("dp"),
            P("dp", None),
            P("dp", None, "tensor"),
            P("dp", None, "tensor"),
            P("dp", "tensor", None),
            P("dp", None),
            rows,
        ),
        out_specs=(
            rows,
            rows,
            P("dp"),
            both,
            both,
            both,
            P("tensor", "dp"),
            P("dp"),
            P("dp"),
            P("dp"),
            P("dp", None),
            P("dp", None, "tensor"),
            P("dp", None, "tensor"),
            P("dp", "tensor", None),
        ),
        check_vma=False,
    )
```

```python
import jax
import jax.numpy as jnp
from jax import lax
from jax.experimental import pallas as pl
from jax.experimental.pallas import tpu as pltpu
from jax.sharding import PartitionSpec as P


HEAD = 128
EPS = 1e-06
THETA = 1000000.0
BF = jnp.bfloat16
F32 = jnp.float32


def dot(a, b, ca, cb):
    return lax.dot_general(a, b, (((ca,), (cb,)), ((), ())), preferred_element_type=F32)


def rms(v, gain):
    return v * lax.rsqrt(jnp.mean(v * v, axis=-1, keepdims=True) + EPS) * gain


def rms_back(v, gain, u):
    inv = lax.rsqrt(jnp.mean(v * v, axis=-1, keepdims=True) + EPS)
    ug = u * gain
    grad = ug * inv - v * (jnp.mean(ug * v, axis=-1, keepdims=True) * inv * inv * inv)
    return grad, u * v * inv


def rope_tables(count):
    inverse = THETA ** (-(jnp.arange(HEAD // 2, dtype=F32) * 2.0 / HEAD))
    angles = jnp.arange(count, dtype=F32)[:, None] * inverse[None, :]
    cos, sin = jnp.cos(angles), jnp.sin(angles)
    return jnp.concatenate([cos, cos], axis=1), jnp.concatenate([-sin, sin], axis=1)


def half_turn(v):
    return pltpu.roll(v, HEAD // 2, 1)


def turned(raw, gain, cos, sin):
    v = rms(raw, gain)
    return (v * cos + half_turn(v) * sin).astype(BF)


def soft(q, k):
    scores = lax.dot_general(q, k, (((1,), (1,)), ((), ())), preferred_element_type=F32)
    scores = scores * HEAD ** (-0.5)
    row = lax.broadcasted_iota(jnp.int32, scores.shape, 0)
    column = lax.broadcasted_iota(jnp.int32, scores.shape, 1)
    e = jnp.where(row >= column, jnp.exp(scores), 0.0)
    return e * (1.0 / jnp.sum(e, axis=1, keepdims=True))


def attend_kernel(q_raw, k_raw, v_raw, gains, cos, sin, context, keys):
    @pl.when(pl.program_id(1) == 0)
    def _():
        keys[...] = turned(k_raw[...], gains[1:2], cos[...], sin[...])

    v = v_raw[...].astype(BF)
    for h in range(2):
        part = slice(h * HEAD, (h + 1) * HEAD)
        q = turned(q_raw[:, part], gains[0:1], cos[...], sin[...])
        p = soft(q, keys[...]).astype(BF)
        context[:, part] = lax.dot_general(
            p, v, (((1,), (0,)), ((), ())), preferred_element_type=F32
        ).astype(BF)


def attend_back_kernel(
    q_raw, k_raw, v_raw, d_context, gains, cos, sin, d_q, d_k, d_v, d_gains, keys, k_sum, v_sum
):
    at = pl.program_id(0)

    @pl.when(at == 0)
    def _():
        keys[...] = turned(k_raw[...], gains[1:2], cos[...], sin[...])
        k_sum[...] = jnp.zeros_like(k_sum)
        v_sum[...] = jnp.zeros_like(v_sum)
        d_gains[...] = jnp.zeros_like(d_gains)

    def back(raw, gain, u):
        return rms_back(raw, gain, u * cos[...] - half_turn(u) * sin[...])

    v = v_raw[...].astype(BF)
    scale = HEAD ** (-0.5)
    for h in range(2):
        part = slice(h * HEAD, (h + 1) * HEAD)
        raw = q_raw[:, part]
        q = turned(raw, gains[0:1], cos[...], sin[...])
        p = soft(q, keys[...])
        dc = d_context[:, part]
        dp = lax.dot_general(dc, v, (((1,), (1,)), ((), ())), preferred_element_type=F32)
        v_sum[...] += lax.dot_general(
            p.astype(BF), dc, (((0,), (0,)), ((), ())), preferred_element_type=F32
        )
        ds = (p * (dp - jnp.sum(p * dp, axis=1, keepdims=True))).astype(BF)
        dq = lax.dot_general(
            ds, keys[...], (((1,), (0,)), ((), ())), preferred_element_type=F32
        )
        k_sum[...] += lax.dot_general(ds, q, (((0,), (0,)), ((), ())), preferred_element_type=F32)
        grad, gain_rows = back(raw, gains[0:1], dq * scale)
        d_q[:, part] = grad.astype(BF)
        d_gains[0:1, :] += jnp.sum(gain_rows, axis=0, keepdims=True)

    @pl.when(at == pl.num_programs(0) - 1)
    def _():
        grad, gain_rows = back(k_raw[...], gains[1:2], k_sum[...] * scale)
        d_k[...] = grad.astype(BF)
        d_v[...] = v_sum[...].astype(BF)
        d_gains[1:2, :] += jnp.sum(gain_rows, axis=0, keepdims=True)


def run_attend(qkv, gains, cos, sin, hq, hk):
    seq = qkv.shape[0]
    pairs = hq // hk // 2
    block = lambda width, index: pl.BlockSpec((seq, width * HEAD), index)
    whole = lambda rows: pl.BlockSpec((rows, HEAD), lambda i, j: (0, 0))
    return pl.pallas_call(
        attend_kernel,
        grid=(hk, pairs),
        in_specs=[
            block(2, lambda i, j: (0, i * pairs + j)),
            block(1, lambda i, j: (0, hq + i)),
            block(1, lambda i, j: (0, hq + hk + i)),
            whole(8),
            whole(seq),
            whole(seq),
        ],
        out_specs=block(2, lambda i, j: (0, i * pairs + j)),
        out_shape=jax.ShapeDtypeStruct((seq, hq * HEAD), BF),
        scratch_shapes=[pltpu.VMEM((seq, HEAD), BF)],
        name="attend",
    )(qkv, qkv, qkv, gains, cos, sin)


def run_attend_back(head, qkv, d_context, gains, cos, sin, hq, hk):
    seq = qkv.shape[0]
    pairs = hq // hk // 2
    block = lambda width, index: pl.BlockSpec((seq, width * HEAD), index)
    whole = lambda rows: pl.BlockSpec((rows, HEAD), lambda j: (0, 0))
    return pl.pallas_call(
        attend_back_kernel,
        grid=(pairs,),
        in_specs=[
            block(2, lambda j: (0, head * pairs + j)),
            block(1, lambda j: (0, hq + head)),
            block(1, lambda j: (0, hq + hk + head)),
            block(2, lambda j: (0, head * pairs + j)),
            whole(8),
            whole(seq),
            whole(seq),
        ],
        out_specs=[block(2, lambda j: (0, j)), whole(seq), whole(seq), whole(8)],
        out_shape=[
            jax.ShapeDtypeStruct((seq, 2 * pairs * HEAD), BF),
            jax.ShapeDtypeStruct((seq, HEAD), BF),
            jax.ShapeDtypeStruct((seq, HEAD), BF),
            jax.ShapeDtypeStruct((8, HEAD), F32),
        ],
        scratch_shapes=[
            pltpu.VMEM((seq, HEAD), BF),
            pltpu.VMEM((seq, HEAD), F32),
            pltpu.VMEM((seq, HEAD), F32),
        ],
        name="attend_back",
    )(qkv, qkv, qkv, d_context, gains, cos, sin)


def split2(v):
    high = v.astype(BF)
    return high, (v - high.astype(F32)).astype(BF)


def gather_dp(v):
    return lax.all_gather(v, "dp", axis=0, tiled=True)


def gather_all(v):
    return lax.all_gather(v, ("dp", "tensor"), axis=0, tiled=True)


def scatter_all(v):
    return lax.psum_scatter(v, ("dp", "tensor"), scatter_dimension=0, tiled=True)


def scatter_dp(v):
    return lax.psum_scatter(v, "dp", scatter_dimension=0, tiled=True)


def pieces(width, dp, seq):
    count = 1 if dp * seq <= 8192 else 4
    step = width // count // 128 * 128
    edges = [step * i for i in range(count)] + [width]
    return list(zip(edges[:-1], edges[1:]))


def after(v, earlier):
    return v if earlier is None else lax.optimization_barrier((v, earlier))[0]


def dispatch(pick, own, dp, seq, earlier):
    blocks = []
    for low, high in pieces(own.shape[1], dp, seq):
        every = gather_all(after(own[:, low:high], earlier)).reshape(dp, seq, high - low)
        block = jnp.einsum("gest,gtd->gesd", pick, every, preferred_element_type=F32).astype(BF)
        blocks.append(block)
        earlier = block if len(pieces(own.shape[1], dp, seq)) > 1 else None
    return jnp.concatenate(blocks, axis=3)


def combine(pick, rows, dp, seq, earlier):
    blocks = []
    for low, high in pieces(rows.shape[3], dp, seq):
        tok = jnp.einsum(
            "gest,gesd->gtd",
            pick,
            after(rows[:, :, :, low:high], earlier),
            preferred_element_type=F32,
        ).astype(BF)
        blocks.append(scatter_all(tok.reshape(dp * seq, high - low)))
        earlier = blocks[-1] if len(pieces(rows.shape[3], dp, seq)) > 1 else None
    return jnp.concatenate(blocks, axis=1).astype(F32)


GRID = [(z, x, c) for z in range(4) for x in range(2) for c in range(2)]
SPLIT = (0, 768, 1536, 1792, 2048)


def at(z, x, c):
    return z % 4 * 4 + x % 2 * 2 + c % 2


def shift_z(v, k):
    return lax.ppermute(v, "dp", [(at(z, x, c), at(z + k, x, c)) for z, x, c in GRID])


def swap_x(v):
    return lax.ppermute(v, "dp", [(at(z, x, c), at(z, x + 1, c)) for z, x, c in GRID])


def swap_c(v):
    return lax.ppermute(v, "dp", [(at(z, x, c), at(z, x, c + 1)) for z, x, c in GRID])


def swap_y(v):
    return lax.ppermute(v, "tensor", [(0, 1), (1, 0)])


def gather_y(v):
    other = swap_y(v)
    first = lax.axis_index("tensor") == 0
    return jnp.concatenate([jnp.where(first, v, other), jnp.where(first, other, v)])


def scatter_y(v):
    a, b = jnp.split(v, 2)
    first = lax.axis_index("tensor") == 0
    kept, sent = jnp.where(first, a, b), jnp.where(first, b, a)
    return kept.astype(F32) + swap_y(sent.astype(BF)).astype(F32)


def gather_z(v, way):
    one, three = shift_z(v, 1), shift_z(v, -1)
    two = shift_z(one, 1) if way > 0 else shift_z(three, -1)
    return jnp.stack([v, one, two, three])


def add2(a, b):
    return (a.astype(F32) + b.astype(F32)).astype(BF)


def reduce_z(v, way, two=None):
    two = shift_z(v[2], -way) if two is None else two
    if way > 0:
        one = shift_z(add2(v[1], two), -1)
        three = shift_z(v[3], 1)
    else:
        three = shift_z(add2(v[3], two), 1)
        one = shift_z(v[1], -1)
    return (v[0].astype(F32) + one.astype(F32) + three.astype(F32)).astype(BF)


def tied(v, w):
    return lax.optimization_barrier((v, w))


def gather_rel(v1, v2, v5, v6, plan, aside):
    w5 = jnp.stack([v5, swap_x(v5)])
    w6 = jnp.stack([v6, swap_y(v6)])
    s1 = gather_z(v1, 1)
    s2 = gather_z(v2, -1)
    w5 = jnp.stack([w5, swap_y(w5)])
    w6 = jnp.stack([w6, swap_x(w6)])
    s1, s2, w5, w6, plan = lax.optimization_barrier((s1, s2, w5, w6, plan))
    s1x, s2y = swap_x(s1), swap_y(s2)
    five = [shift_z(w5, 1), shift_z(w5, -1)]
    six = [shift_z(w6, 1), shift_z(w6, -1)]
    far = aside(1, plan)
    five, six, s1x, s2y, far = lax.optimization_barrier((five, six, s1x, s2y, far))
    s1 = jnp.stack([s1, s1x])
    s2 = jnp.stack([s2, s2y])
    s1y, s2x = swap_y(s1), swap_x(s2)
    five.append(shift_z(five[0], 1))
    six.append(shift_z(six[1], -1))
    plan, (five, six) = tied(plan, (five, six))
    o5 = jnp.stack([w5, five[0], five[2], five[1]])
    o6 = jnp.stack([w6, six[0], six[2], six[1]])
    (s1y, s2x), near = tied((s1y, s2x), aside(0, plan))
    first = (s1, s1y, s2, s2x, o5, o6)
    return first, tuple(swap_c(v) for v in first), plan, (near, far)


def scatter_core(near, far):
    p5, p6, p1, p2 = [add2(near[i], swap_c(far[i])) for i in (2, 3, 0, 1)]
    return lax.optimization_barrier((p1, p2, p5, p6))


def scatter_first(p1, p2, p5, p6, aside=None):
    two5, two6 = shift_z(p5[2], -1), shift_z(p6[2], 1)
    (two5, two6), aside = tied((two5, two6), aside)
    p5 = reduce_z(p5, 1, two5)
    p6 = reduce_z(p6, -1, two6)
    p1 = add2(p1[0], swap_y(p1[1]))
    p2 = add2(p2[0], swap_x(p2[1]))
    return (p1, p2, p5, p6), aside


def scatter_second(p1, p2, p5, p6):
    p5 = add2(p5[0], swap_y(p5[1]))
    p6 = add2(p6[0], swap_x(p6[1]))
    p1 = add2(p1[0], swap_x(p1[1]))
    p2 = add2(p2[0], swap_y(p2[1]))
    return p1, p2, p5, p6


def scatter_last(p1, p2, p5, p6):
    p5 = add2(p5[0], swap_x(p5[1]))
    p6 = add2(p6[0], swap_y(p6[1]))
    return reduce_z(p1, 1), reduce_z(p2, -1), p5, p6


def scatter_rows_core(near, far):
    a = swap_c(far[0])
    b = swap_c(far[1])
    return add2(near[0], a), add2(near[1], b)


def scatter_rows(a, b):
    b = reduce_z(b, -1)
    a = add2(a[0], swap_x(a[1]))
    b = add2(b[0], swap_x(b[1]))
    return jnp.concatenate([reduce_z(a, 1), b], axis=1)


def sequence_at(dc, dz, dx):
    at = lax.axis_index("dp")
    return (at // 4 - dz) % 4 * 4 + (at // 2 % 2 + dx) % 2 * 2 + (at % 2 + dc) % 2


def nn(a, b):
    return lax.dot_general(a, b, (((1,), (0,)), ((), ())), preferred_element_type=F32)


def nt(a, b):
    return lax.dot_general(a, b, (((1,), (1,)), ((), ())), preferred_element_type=F32)


def pick_rows(rank, slots):
    at_slot = lax.broadcasted_iota(jnp.int32, (slots, rank.shape[1]), 0).astype(F32)
    return jnp.concatenate(
        [(rank[e : e + 1, :] == at_slot).astype(F32).astype(BF) for e in range(rank.shape[0])],
        axis=0,
    )


def pick_cols(rank, slots):
    at_slot = lax.broadcasted_iota(jnp.int32, (rank.shape[0], slots), 1).astype(F32)
    return jnp.concatenate(
        [(rank[:, e : e + 1] == at_slot).astype(F32).astype(BF) for e in range(rank.shape[1])],
        axis=1,
    )


def cot_kernel(where, rank, cot_a, cot_b, down, cots, d_act):
    slots = cots.shape[2] // 2
    for dx, cot in enumerate((cot_a, cot_b)):
        both = nn(pick_rows(rank[dx], slots), cot[0]).astype(BF)
        for e in range(2):
            cots[e, 0, dx * slots : (dx + 1) * slots, :] = both[e * slots : (e + 1) * slots]
    for e in range(2):
        d_act[e, 0] = nt(cots[e, 0], down[e])


def expert_kernel(
    rank, rank_t, cols, d_act, x1a, x1b, x2a, x2b, x5, x6, weights,
    rows, scaled, d_g, d_u, t1, t2, t5, t6, back,
):
    slots = rows.shape[2] // 2
    n = x1a.shape[2]
    gates = []
    for dx, x2 in enumerate((x2a, x2b)):
        pick = pick_rows(rank[dx], slots)
        low, high = pick[:, :n], pick[:, n:]
        block1 = nn(low, x1a[dx, 0]) + nn(high, x1b[dx, 0])
        block2 = nn(low, x2[0, 0]) + nn(high, x2[1, 0])
        block5 = nn(low, x5[0, 0, dx]) + nn(high, x5[0, 1, dx])
        block6 = nn(low, x6[0, dx, 0]) + nn(high, x6[0, dx, 1])
        low = dx * slots
        for e in range(2):
            part = slice(e * slots, (e + 1) * slots)
            rows[e, 0, low : low + slots, 0:768] = block1[part].astype(BF)
            rows[e, 0, low : low + slots, 768:1536] = block2[part].astype(BF)
            rows[e, 0, low : low + slots, 1536:1792] = block5[part, :256].astype(BF)
            rows[e, 0, low : low + slots, 1792:2048] = block6[part].astype(BF)
            both = cols[e, 0:1, :] + cols[e, 1:2, :]
            gates.append(jnp.sum(block5[part, 256:] * both, axis=1, keepdims=True))
    extras = []
    for e in range(2):
        gate = jnp.concatenate([gates[e], gates[2 + e]], axis=0)
        g = nn(rows[e, 0], weights[e])
        g, u = jnp.split(g, 2, axis=1)
        da = d_act[e, 0]
        sig = 1.0 / (1.0 + jnp.exp(-g))
        silu = g * sig
        act = silu * u
        scaled[e, 0] = (act * gate).astype(BF)
        d_gate = jnp.sum(act * da, axis=1, keepdims=True)
        da = da * gate
        dg = (da * u * sig * (1.0 + g * (1.0 - sig))).astype(BF)
        du = (da * silu).astype(BF)
        d_g[e, 0] = dg
        d_u[e, 0] = du
        high = d_gate.astype(BF).astype(F32)
        extras.append(high * cols[e, 0:1, :] + (d_gate - high) * cols[e, 1:2, :])
        dr = nt(jnp.concatenate([dg, du], axis=1), weights[e]).astype(BF)
        for dx in range(2):
            back[dx, e * slots : (e + 1) * slots, :] = dr[dx * slots : (dx + 1) * slots]
    extra = [
        jnp.concatenate([extras[e][dx * slots : (dx + 1) * slots] for e in range(2)], axis=0)
        for dx in range(2)
    ]
    put_back(rank_t, back, t1, t2, t5, t6, slots, extra)


def put_back(rank_t, back, t1, t2, t5, t6, slots, extra=None):
    for dx in range(2):
        pick_t = pick_cols(rank_t[dx], slots)
        n = pick_t.shape[0] // 2
        p1, p2, p5, p6 = [
            nn(pick_t, back[dx, :, a:b]).astype(BF) for a, b in zip(SPLIT[:-1], SPLIT[1:])
        ]
        for dy in range(2):
            half = slice(dy * n, (dy + 1) * n)
            t1[dy, dx, 0] = p1[half]
            t2[dx, dy, 0] = p2[half]
            t5[0, dy, dx, :, 0:256] = p5[half]
            t6[0, dx, dy] = p6[half]
        if extra is not None:
            p7 = nn(pick_t, extra[dx].astype(BF)).astype(BF)
            for dy in range(2):
                t5[0, dy, dx, :, 256:] = p7[dy * n : (dy + 1) * n]


def out_kernel(rank_t, scaled, down, t1, t2, t5, t6, back):
    slots = scaled.shape[2] // 2
    for e in range(2):
        y = nn(scaled[e, 0], down[e]).astype(BF)
        for dx in range(2):
            back[dx, e * slots : (e + 1) * slots, :] = y[dx * slots : (dx + 1) * slots]
    put_back(rank_t, back, t1, t2, t5, t6, slots)


def grad_kernel(where, left, right, small, a, b):
    both = lax.dot_general(
        left[...], right[...], (((0,), (0,)), ((), ())), preferred_element_type=F32
    ).astype(BF)
    width = a.shape[-1]
    a[0, 0] = both[:, :width]
    b[0, 0, :, : both.shape[1] - width] = both[:, width:]
    b[0, 0, :, both.shape[1] - width :] = small[...].astype(BF)


def run_grad(where, left, right, small):
    count, columns = right.shape
    rest = small.shape[1]
    width = columns * 9 // 16 // 128 * 128
    shard = left.shape[1] // 16
    return pl.pallas_call(
        grad_kernel,
        grid_spec=pltpu.PrefetchScalarGridSpec(
            num_scalar_prefetch=1,
            grid=(2, 4),
            in_specs=[
                pl.BlockSpec((count, shard), lambda dx, dz, w: (0, w[2 * dz + dx])),
                pl.BlockSpec((count, columns), lambda dx, dz, w: (0, 0)),
                pl.BlockSpec((shard, rest), lambda dx, dz, w: (w[2 * dz + dx], 0)),
            ],
            out_specs=[
                pl.BlockSpec((1, 1, shard, width), lambda dx, dz, w: (dx, dz, 0, 0)),
                pl.BlockSpec((1, 1, shard, columns - width + rest), lambda dx, dz, w: (dz, dx, 0, 0)),
            ],
        ),
        out_shape=[
            shaped((2, 4, shard, width), BF),
            shaped((4, 2, shard, columns - width + rest), BF),
        ],
        compiler_params=LIMIT,
        name="grad",
    )(where, left, right, small)


def pair(*tail):
    return pl.BlockSpec((2, *tail), lambda i, *_: (i,) + (0,) * len(tail))


def z_last(*lead):
    def spec(rows, columns):
        return pl.BlockSpec(
            (*lead, 1, rows, columns), lambda i, *_: (0,) * len(lead) + (i, 0, 0)
        )

    return spec


def z_first(rows, columns):
    return pl.BlockSpec((1, 2, 2, rows, columns), lambda i, *_: (i, 0, 0, 0, 0))


def block_specs(n, extra):
    return [z_last(2, 2)(n, 768), z_last(2, 2)(n, 768), z_first(n, 256 + extra), z_first(n, 256)]


def block_shapes(n, extra):
    shapes = [(2, 2, 4, n, 768), (2, 2, 4, n, 768), (4, 2, 2, n, 256 + extra), (4, 2, 2, n, 256)]
    return [shaped(v, BF) for v in shapes]


def by_expert(*tail):
    return pl.BlockSpec((2, 1, *tail), lambda i, *_: (0, i) + (0,) * len(tail))


def fixed(*shape):
    return pl.BlockSpec(
        shape, lambda i, *_: (0,) * len(shape), pipeline_mode=pl.Buffered(1)
    )


def shaped(shape, kind):
    return jax.ShapeDtypeStruct(shape, kind)


LIMIT = pltpu.CompilerParams(vmem_limit_bytes=58 * 1024 * 1024)


def run_cots(where, rank, cot_all, down, slots):
    seq, width = cot_all.shape[1:]
    ff = down.shape[1]
    return pl.pallas_call(
        cot_kernel,
        grid_spec=pltpu.PrefetchScalarGridSpec(
            num_scalar_prefetch=1,
            grid=(4,),
            in_specs=[
                pair(2, seq),
                pl.BlockSpec((1, seq, width), lambda i, w: (w[2 * i], 0, 0)),
                pl.BlockSpec((1, seq, width), lambda i, w: (w[2 * i + 1], 0, 0)),
                fixed(2, ff, width),
            ],
            out_specs=[by_expert(2 * slots, width), by_expert(2 * slots, ff)],
        ),
        out_shape=[shaped((2, 4, 2 * slots, width), BF), shaped((2, 4, 2 * slots, ff), F32)],
        compiler_params=LIMIT,
        name="cots",
    )(where, rank, cot_all, cot_all, down)


def run_experts(rank, rank_t, cols, d_act, parts, weights, slots):
    s1, s1y, s2, s2x, o5, o6 = parts
    n = s1.shape[2]
    seq, width, ff = 2 * n, weights.shape[1], weights.shape[2] // 2
    return pl.pallas_call(
        expert_kernel,
        grid=(4,),
        in_specs=[
            pair(2, seq),
            pair(seq, 2),
            fixed(*cols.shape),
            by_expert(2 * slots, ff),
            z_last(2)(n, 768),
            z_last(2)(n, 768),
            z_last(2)(n, 768),
            z_last(2)(n, 768),
            z_first(n, 384),
            z_first(n, 256),
            fixed(2, width, 2 * ff),
        ],
        out_specs=[
            by_expert(2 * slots, width),
            by_expert(2 * slots, ff),
            by_expert(2 * slots, ff),
            by_expert(2 * slots, ff),
        ]
        + block_specs(n, 128),
        out_shape=[
            shaped((2, 4, 2 * slots, width), BF),
            shaped((2, 4, 2 * slots, ff), BF),
            shaped((2, 4, 2 * slots, ff), BF),
            shaped((2, 4, 2 * slots, ff), BF),
        ]
        + block_shapes(n, 128),
        scratch_shapes=[pltpu.VMEM((2, 2 * slots, width), BF)],
        compiler_params=LIMIT,
        name="experts",
    )(
        rank, rank_t, cols, d_act, s1, s1y, s2, s2x, o5, o6, weights,
    )


def run_outs(rank_t, scaled, down, slots):
    seq, ff, width = rank_t.shape[1], down.shape[1], down.shape[2]
    return pl.pallas_call(
        out_kernel,
        grid=(4,),
        in_specs=[pair(seq, 2), by_expert(2 * slots, ff), fixed(2, ff, width)],
        out_specs=block_specs(seq // 2, 0),
        out_shape=block_shapes(seq // 2, 0),
        scratch_shapes=[pltpu.VMEM((2, 2 * slots, width), BF)],
        compiler_params=LIMIT,
        name="outs",
    )(rank_t, scaled, down)


def flip(v, axis, y):
    a, b = jnp.split(v, 2, axis=axis)
    return jnp.where(y == 0, v, jnp.concatenate([b, a], axis=axis))


def slot_plan(ids_all, experts):
    y = lax.axis_index("tensor")
    seq = ids_all.shape[1]
    mine = lax.axis_index("dp") * 2 + jnp.arange(2, dtype=jnp.int32)
    mask = jnp.any(ids_all[:, None, :, :] == mine[None, :, None, None], axis=3)
    before = (jnp.arange(seq)[:, None] < jnp.arange(seq)[None, :]).astype(BF)
    rank = jnp.einsum("gea,ab->geb", mask.astype(BF), before, preferred_element_type=F32)
    rank = jnp.where(mask, rank, -1.0)
    d = jnp.arange(16)
    where = sequence_at(d // 8, d // 2 % 4, d % 2)
    rank = jnp.take(rank, where, axis=0)
    rank_rel = flip(rank, 2, y)
    rank_t = jnp.swapaxes(rank_rel, 1, 2)
    column = jnp.arange(128)
    cols = (
        column[None, None, :] == (mine[:, None] + jnp.array([[0, experts]]))[:, :, None]
    ).astype(F32)
    halves = lambda v: (v[:8], v[8:])
    return halves(where.astype(jnp.int32)), halves(rank), halves(rank_rel), halves(rank_t), cols


def moe_small(plan, cot_all, ffn_in, gate_x, weights, down_weight, slots):

    def cot_rows(k, plan):
        return run_cots(plan[0][k], plan[1][k], cot_all, down_weight, slots)

    v1, v2, v5, v6 = [ffn_in[:, a:b] for a, b in zip(SPLIT[:-1], SPLIT[1:])]
    v5 = jnp.concatenate([v5, gate_x], axis=1)
    *parts, plan, both = gather_rel(v1, v2, v5, v6, plan, cot_rows)
    rank_rel, rank_t, cols = plan[2:]
    cots, d_act = zip(*both)
    far, near = [
        run_experts(rank_rel[k], rank_t[k], cols, d_act[k], parts[k], weights, slots)
        for k in (1, 0)
    ]
    step = scatter_core(near[4:], far[4:])
    step, (near, far, cots) = scatter_first(*step, (near[:4], far[:4], cots))
    kept = lambda i: (near[i], far[i])
    outs = [run_outs(rank_t[k], kept(1)[k], down_weight, slots) for k in (0, 1)]
    total = lambda spec, a, b: jnp.einsum(spec, a[0], b[0], preferred_element_type=F32) + jnp.einsum(
        spec, a[1], b[1], preferred_element_type=F32
    )
    down_grad = total("egsf,egsd->efd", kept(1), cots)
    step, (outs, down_grad) = tied(step, (outs, down_grad))
    step, (p1, p2, p5, p6) = tied(scatter_second(*step), scatter_core(*outs))
    d5 = add2(step[2][0], swap_x(step[2][1]))
    d6 = add2(step[3][0], swap_y(step[3][1]))
    p2, (d5, d6) = tied(p2, (d5, d6))
    d1 = reduce_z(step[0], 1)
    d2 = reduce_z(step[1], -1)
    p2 = add2(p2[0], swap_x(p2[1]))
    d_sum = jnp.concatenate([d1, d2, d5[:, :256], d6, d5[:, 256:]], axis=1)
    d_sum, (p1, p5, p6) = tied(d_sum, (p1, p5, p6))
    d_sum = d_sum.astype(F32)

    def later(i, aside):
        (rows, grads), aside = tied((kept(0), kept(i)), aside)
        return total("egsd,egsf->edf", rows, grads), aside

    return d_sum, (p1, p2, p5, p6), later, down_grad


def moe_large(
    ids_all, cotangent, ffn_in, gate_x, gate_weight, up_weight, down_weight, experts, slots
):
    dp, seq = ids_all.shape[:2]
    local = gate_weight.shape[0]
    dp_at = lax.axis_index("dp")
    mine = dp_at * local + jnp.arange(local, dtype=jnp.int32)
    mask = jnp.any(ids_all[:, :, None, :] == mine[None, None, :, None], axis=3).astype(BF)
    gate_all = gather_all(gate_x).reshape(dp, seq, -1)
    before = (jnp.arange(seq)[:, None] > jnp.arange(seq)[None, :]).astype(BF)
    rank = jnp.einsum("ab,gbe->gea", before, mask, preferred_element_type=F32)
    rank = jnp.where(jnp.swapaxes(mask, 1, 2) > 0, rank, -1.0)
    pick = (rank[:, :, None, :] == jnp.arange(slots, dtype=F32)[None, None, :, None]).astype(BF)

    cots = dispatch(pick, cotangent, dp, seq, None)
    rows = dispatch(pick, ffn_in, dp, seq, cots)
    gate_tok = lax.dynamic_slice_in_dim(gate_all, dp_at * local, local, 2).astype(
        F32
    ) + lax.dynamic_slice_in_dim(gate_all, experts + dp_at * local, local, 2).astype(F32)
    gate_slot = jnp.sum(pick.astype(F32) * jnp.swapaxes(gate_tok, 1, 2)[:, :, None, :], axis=3)

    g_proj = jnp.einsum("gesd,edf->gesf", rows, gate_weight, preferred_element_type=F32)
    u_proj = jnp.einsum("gesd,edf->gesf", rows, up_weight, preferred_element_type=F32)
    d_act = jnp.einsum("gesd,efd->gesf", cots, down_weight, preferred_element_type=F32)
    sig = 1.0 / (1.0 + jnp.exp(-g_proj))
    silu = g_proj * sig
    act = silu * u_proj
    scaled = (act * gate_slot[..., None]).astype(BF)
    d_gate_slot = jnp.sum(act * d_act, axis=3)
    d_act = d_act * gate_slot[..., None]
    d_g = (d_act * u_proj * sig * (1.0 + g_proj * (1.0 - sig))).astype(BF)
    d_u = (d_act * silu).astype(BF)
    d_rows = (
        jnp.einsum("gesf,edf->gesd", d_g, gate_weight, preferred_element_type=F32)
        + jnp.einsum("gesf,edf->gesd", d_u, up_weight, preferred_element_type=F32)
    ).astype(BF)
    dg_high, dg_low = split2(d_gate_slot)
    column = jnp.arange(lanes(2 * experts))
    high_col = (column[None, :] == mine[:, None])[None, :, None, :]
    low_col = (column[None, :] == experts + mine[:, None])[None, :, None, :]
    extra = jnp.where(high_col, dg_high[..., None], jnp.where(low_col, dg_low[..., None], 0.0))
    d_rows = jnp.concatenate([d_rows, extra.astype(BF)], axis=3)
    d_sum = combine(pick, d_rows, dp, seq, None)

    y_rows = jnp.einsum("gesf,efd->gesd", scaled, down_weight, preferred_element_type=F32)
    y_sum = combine(pick, y_rows.astype(BF), dp, seq, d_sum)
    down_grad = jnp.einsum("gesf,gesd->efd", scaled, cots, preferred_element_type=F32)
    gate_grad = jnp.einsum("gesd,gesf->edf", rows, d_g, preferred_element_type=F32)
    up_grad = jnp.einsum("gesd,gesf->edf", rows, d_u, preferred_element_type=F32)

    return d_sum, y_sum, gate_grad, up_grad, down_grad


def pad_to(v, width):
    return jnp.pad(v, ((0, 0), (0, width - v.shape[1])))


def lanes(count):
    return -(-count // 128) * 128


def on_device(
    tokens,
    attn_gain,
    q_weight,
    key_matrix,
    value_matrix,
    o_weight,
    query_norm_gain,
    k_gain,
    ffn_gain,
    router_weight,
    gate_weight,
    up_weight,
    down_weight,
    expert_ids,
    cotangent,
):
    dp = lax.axis_size("dp")
    tensor = lax.axis_size("tensor")
    own, width = tokens.shape
    seq = expert_ids.shape[0]
    begin = lax.axis_index("tensor") * own
    local = gate_weight.shape[0]
    experts = local * dp
    slots = 10 * seq * expert_ids.shape[1] // (8 * experts)
    slots = -(-slots // 16) * 16
    shard = q_weight.shape[0]
    gshard = query_norm_gain.shape[0]
    hq = q_weight.shape[1] // HEAD
    hk = key_matrix.shape[1] // HEAD
    qkv_width = (hq + 2 * hk) * HEAD
    top = expert_ids.shape[1]
    fast = (dp, tensor, local, seq, width) == (16, 2, 2, 384, 2048)

    arange_e = jnp.arange(experts, dtype=jnp.int32)
    own_ids = lax.dynamic_slice_in_dim(expert_ids, begin, own, 0)
    own_mask = jnp.any(own_ids[:, :, None] == arange_e[None, None, :], axis=1)

    gain_rows = jnp.stack(
        [
            attn_gain,
            ffn_gain,
            jnp.pad(query_norm_gain, (0, shard - gshard)),
            jnp.pad(k_gain, (0, shard - gshard)),
        ],
        axis=1,
    )
    ids_rows = expert_ids.reshape(shard, -1).astype(BF)
    small = jnp.concatenate([router_weight, gain_rows, ids_rows], axis=1)
    small = pad_to(small, lanes(small.shape[1]))
    small_end = qkv_width + small.shape[1]
    all_in = gather_dp(
        jnp.concatenate([q_weight, key_matrix, value_matrix, small, o_weight.T], axis=1)
    )
    layer_in = gather_y(tokens)
    if fast:
        weights = jnp.concatenate([gate_weight, up_weight], axis=2)
        layer_in, weights = tied(layer_in, weights)
    o_t = all_in[:, small_end:]
    if fast:
        cot_all = gather_dp(gather_y(cotangent)).reshape(dp, seq, width)

    w_qkv = all_in[:, :qkv_width]
    router = all_in[:, qkv_width : qkv_width + experts]
    gains = all_in[:, qkv_width + experts : qkv_width + experts + 4].astype(F32)
    ids_all = all_in[:, qkv_width + experts + 4 :][:, : seq * top // shard]
    ids_all = ids_all.astype(jnp.int32).reshape(dp, seq, top)
    attn_gain32 = gains[:, 0]
    ffn_gain32 = gains[:, 1]
    q_gain32 = gains[:, 2].reshape(dp, shard)[:, :gshard].reshape(-1)
    k_gain32 = gains[:, 3].reshape(dp, shard)[:, :gshard].reshape(-1)

    residual = layer_in.astype(F32)
    normed = rms(residual, attn_gain32).astype(BF)
    qkv = dot(normed, w_qkv, 1, 0)
    cos, sin = rope_tables(seq)
    head_gains = jnp.pad(jnp.stack([q_gain32, k_gain32]), ((0, 6), (0, 0)))
    context = run_attend(qkv, head_gains, cos, sin, hq, hk)
    attn_part = dot(context, o_t, 1, 1)
    if fast:
        attn_part, ids_all = tied(attn_part, ids_all)
        plan = slot_plan(ids_all, experts)
    hidden = tokens.astype(F32) + scatter_y(attn_part)

    ffn_in = rms(hidden, ffn_gain32).astype(BF)
    logits = dot(ffn_in, router, 1, 0)
    chosen = jnp.where(own_mask, jnp.exp(logits), 0.0)
    gates = chosen / jnp.sum(chosen, axis=1, keepdims=True)
    gate_high, gate_low = split2(gates)
    gate_x = pad_to(jnp.concatenate([gate_high, gate_low], axis=1), lanes(2 * experts))
    args = (gate_weight, up_weight, down_weight)
    if fast:
        d_sum, y_sum, later, down_grad = moe_small(
            plan, cot_all, ffn_in, gate_x, weights, down_weight, slots
        )
    else:
        d_sum, y_sum, gate_grad, up_grad, down_grad = moe_large(
            ids_all, cotangent, ffn_in, gate_x, *args, experts, slots
        )
    d_gates = d_sum[:, width : width + experts] + d_sum[:, width + experts : width + 2 * experts]
    d_logits = gates * (d_gates - jnp.sum(gates * d_gates, axis=1, keepdims=True))
    d_high, d_low = split2(d_logits)
    d_ffn = d_sum[:, :width] + dot(d_high, router, 1, 1) + dot(d_low, router, 1, 1)
    router_part = dot(ffn_in, d_high, 0, 0) + dot(ffn_in, d_low, 0, 0)
    d_hidden, ffn_gain_rows = rms_back(hidden, ffn_gain32, d_ffn)
    ffn_gain_part = jnp.sum(ffn_gain_rows, axis=0)
    d_hidden = d_hidden + cotangent.astype(F32)
    d_attn = gather_y(d_hidden.astype(BF))

    o_part = dot(d_attn, context, 0, 0).astype(BF)
    d_attn, o_part = tied(d_attn, o_part)
    o_sum = scatter_dp(o_part).astype(F32)
    if fast:
        p1, p2, p5, p6 = y_sum
        d_attn, p1 = tied(d_attn, p1)
        p1 = add2(p1[0], swap_y(p1[1]))
        two5, two6 = shift_z(p5[2], -1), shift_z(p6[2], 1)
        gate_grad, d_attn = later(2, d_attn)
    d_context = dot(d_attn, o_t, 1, 0).astype(BF)
    heads = []
    for head in range(hk):
        heads.append(run_attend_back(head, qkv, d_context, head_gains, cos, sin, hq, hk))
        if fast and head == 0:
            aside = (p1, p2, two5, two6, gate_grad)
            d_context, heads, aside = lax.optimization_barrier((d_context, heads, aside))
            p1, p2, two5, two6, gate_grad = aside
            p1 = add2(p1[0], swap_x(p1[1]))
            p2 = add2(p2[0], swap_y(p2[1]))
            p5 = reduce_z(p5, 1, two5)
            p6 = reduce_z(p6, -1, two6)
    d_qkv = jnp.concatenate([h[k] for k in range(3) for h in heads], axis=1)
    spread = lambda v: jnp.pad(v.reshape(dp, gshard), ((0, 0), (0, shard - gshard))).reshape(-1)
    small_part = jnp.concatenate(
        [
            router_part,
            jnp.stack(
                [
                    ffn_gain_part,
                    spread(sum(h[3][0] for h in heads)),
                    spread(sum(h[3][1] for h in heads)),
                ],
                axis=1,
            ),
        ],
        axis=1,
    )
    small_part = pad_to(small_part, lanes(experts + 3))
    if fast:
        d_qkv, (p1, p2, p5, p6) = tied(d_qkv, (p1, p2, p5, p6))
        p5 = add2(p5[0], swap_y(p5[1]))
        p6 = add2(p6[0], swap_x(p6[1]))
        far = run_grad(plan[0][1], normed, d_qkv, small_part)
        near = run_grad(plan[0][0], normed, d_qkv, small_part)
        y_sum = scatter_last(p1, p2, p5, p6)
        (a, b), y_sum = tied(scatter_rows_core(near, far), y_sum)
        d_qkv, (a, b) = tied(d_qkv, (a, b))
        up_grad, (a, b) = later(3, (a, b))
        qkv_sum = scatter_rows(a, b).astype(F32)
        qkv_sum, small_sum = qkv_sum[:, :qkv_width], qkv_sum[:, qkv_width:]
        y_sum = jnp.concatenate(y_sum, axis=1).astype(F32)
    else:
        qkv_sum = scatter_dp(dot(normed, d_qkv, 0, 0).astype(BF)).astype(F32)
        small_sum = scatter_dp(small_part)
    output = (hidden + y_sum).astype(BF)
    d_normed = dot(d_qkv, w_qkv, 1, 1)
    d_normed = scatter_y(d_normed)
    d_tokens, _ = rms_back(tokens.astype(F32), attn_gain32, d_normed)
    tokens_grad = d_tokens + d_hidden

    weights = jnp.concatenate([q_weight, key_matrix, value_matrix], axis=1).astype(F32)
    gain_part = jnp.sum(weights * qkv_sum, axis=1) / attn_gain.astype(F32)
    small_sum = jnp.concatenate([small_sum, gain_part[:, None]], axis=1)
    small_sum = small_sum + swap_y(small_sum)
    return (
        output,
        tokens_grad,
        small_sum[:, -1],
        qkv_sum[:, : hq * HEAD],
        qkv_sum[:, hq * HEAD : (hq + hk) * HEAD],
        qkv_sum[:, (hq + hk) * HEAD :],
        o_sum.T,
        small_sum[:gshard, experts + 1],
        small_sum[:gshard, experts + 2],
        small_sum[:, experts],
        small_sum[:, :experts],
        gate_grad,
        up_grad,
        down_grad,
    )


def solution(mesh):
    rows = P(("dp", "tensor"), None)
    both = P("dp", "tensor")
    return jax.shard_map(
        on_device,
        mesh=mesh,
        in_specs=(
            rows,
            P("dp"),
            both,
            both,
            both,
            P("tensor", "dp"),
            P("dp"),
            P("dp"),
            P("dp"),
            P("dp", None),
            P("dp", None, "tensor"),
            P("dp", None, "tensor"),
            P("dp", "tensor", None),
            P("dp", None),
            rows,
        ),
        out_specs=(
            rows,
            rows,
            P("dp"),
            both,
            both,
            both,
            P("tensor", "dp"),
            P("dp"),
            P("dp"),
            P("dp"),
            P("dp", None),
            P("dp", None, "tensor"),
            P("dp", None, "tensor"),
            P("dp", "tensor", None),
        ),
        check_vma=False,
    )
```

```python
import jax
import jax.numpy as jnp
from jax import lax
from jax.experimental import pallas as pl
from jax.experimental.pallas import tpu as pltpu
from jax.sharding import PartitionSpec as P


HEAD = 128
EPS = 1e-06
THETA = 1000000.0
BF = jnp.bfloat16
F32 = jnp.float32


def dot(a, b, ca, cb):
    return lax.dot_general(a, b, (((ca,), (cb,)), ((), ())), preferred_element_type=F32)


def rms(v, gain):
    return v * lax.rsqrt(jnp.mean(v * v, axis=-1, keepdims=True) + EPS) * gain


def rms_back(v, gain, u):
    inv = lax.rsqrt(jnp.mean(v * v, axis=-1, keepdims=True) + EPS)
    ug = u * gain
    grad = ug * inv - v * (jnp.mean(ug * v, axis=-1, keepdims=True) * inv * inv * inv)
    return grad, u * v * inv


def rope_tables(count):
    inverse = THETA ** (-(jnp.arange(HEAD // 2, dtype=F32) * 2.0 / HEAD))
    angles = jnp.arange(count, dtype=F32)[:, None] * inverse[None, :]
    cos, sin = jnp.cos(angles), jnp.sin(angles)
    return jnp.concatenate([cos, cos], axis=1), jnp.concatenate([-sin, sin], axis=1)


def half_turn(v):
    return pltpu.roll(v, HEAD // 2, 1)


def turned(raw, gain, cos, sin):
    v = rms(raw, gain)
    return (v * cos + half_turn(v) * sin).astype(BF)


def soft(q, k):
    scores = lax.dot_general(q, k, (((1,), (1,)), ((), ())), preferred_element_type=F32)
    scores = scores * HEAD ** (-0.5)
    row = lax.broadcasted_iota(jnp.int32, scores.shape, 0)
    column = lax.broadcasted_iota(jnp.int32, scores.shape, 1)
    e = jnp.where(row >= column, jnp.exp(scores), 0.0)
    return e * (1.0 / jnp.sum(e, axis=1, keepdims=True))


def attend_kernel(q_raw, k_raw, v_raw, gains, cos, sin, context, keys):
    @pl.when(pl.program_id(1) == 0)
    def _():
        keys[...] = turned(k_raw[...], gains[1:2], cos[...], sin[...])

    v = v_raw[...].astype(BF)
    for h in range(2):
        part = slice(h * HEAD, (h + 1) * HEAD)
        q = turned(q_raw[:, part], gains[0:1], cos[...], sin[...])
        p = soft(q, keys[...]).astype(BF)
        context[:, part] = lax.dot_general(
            p, v, (((1,), (0,)), ((), ())), preferred_element_type=F32
        ).astype(BF)


def attend_back_kernel(
    q_raw, k_raw, v_raw, d_context, gains, cos, sin, d_q, d_k, d_v, d_gains, keys, k_sum, v_sum
):
    at = pl.program_id(0)

    @pl.when(at == 0)
    def _():
        keys[...] = turned(k_raw[...], gains[1:2], cos[...], sin[...])
        k_sum[...] = jnp.zeros_like(k_sum)
        v_sum[...] = jnp.zeros_like(v_sum)
        d_gains[...] = jnp.zeros_like(d_gains)

    def back(raw, gain, u):
        return rms_back(raw, gain, u * cos[...] - half_turn(u) * sin[...])

    v = v_raw[...].astype(BF)
    scale = HEAD ** (-0.5)
    for h in range(2):
        part = slice(h * HEAD, (h + 1) * HEAD)
        raw = q_raw[:, part]
        q = turned(raw, gains[0:1], cos[...], sin[...])
        p = soft(q, keys[...])
        dc = d_context[:, part]
        dp = lax.dot_general(dc, v, (((1,), (1,)), ((), ())), preferred_element_type=F32)
        v_sum[...] += lax.dot_general(
            p.astype(BF), dc, (((0,), (0,)), ((), ())), preferred_element_type=F32
        )
        ds = (p * (dp - jnp.sum(p * dp, axis=1, keepdims=True))).astype(BF)
        dq = lax.dot_general(
            ds, keys[...], (((1,), (0,)), ((), ())), preferred_element_type=F32
        )
        k_sum[...] += lax.dot_general(ds, q, (((0,), (0,)), ((), ())), preferred_element_type=F32)
        grad, gain_rows = back(raw, gains[0:1], dq * scale)
        d_q[:, part] = grad.astype(BF)
        d_gains[0:1, :] += jnp.sum(gain_rows, axis=0, keepdims=True)

    @pl.when(at == pl.num_programs(0) - 1)
    def _():
        grad, gain_rows = back(k_raw[...], gains[1:2], k_sum[...] * scale)
        d_k[...] = grad.astype(BF)
        d_v[...] = v_sum[...].astype(BF)
        d_gains[1:2, :] += jnp.sum(gain_rows, axis=0, keepdims=True)


def run_attend(qkv, gains, cos, sin, hq, hk):
    seq = qkv.shape[0]
    pairs = hq // hk // 2
    block = lambda width, index: pl.BlockSpec((seq, width * HEAD), index)
    whole = lambda rows: pl.BlockSpec((rows, HEAD), lambda i, j: (0, 0))
    return pl.pallas_call(
        attend_kernel,
        grid=(hk, pairs),
        in_specs=[
            block(2, lambda i, j: (0, i * pairs + j)),
            block(1, lambda i, j: (0, hq + i)),
            block(1, lambda i, j: (0, hq + hk + i)),
            whole(8),
            whole(seq),
            whole(seq),
        ],
        out_specs=block(2, lambda i, j: (0, i * pairs + j)),
        out_shape=jax.ShapeDtypeStruct((seq, hq * HEAD), BF),
        scratch_shapes=[pltpu.VMEM((seq, HEAD), BF)],
        name="attend",
    )(qkv, qkv, qkv, gains, cos, sin)


def run_attend_back(head, qkv, d_context, gains, cos, sin, hq, hk):
    seq = qkv.shape[0]
    pairs = hq // hk // 2
    block = lambda width, index: pl.BlockSpec((seq, width * HEAD), index)
    whole = lambda rows: pl.BlockSpec((rows, HEAD), lambda j: (0, 0))
    return pl.pallas_call(
        attend_back_kernel,
        grid=(pairs,),
        in_specs=[
            block(2, lambda j: (0, head * pairs + j)),
            block(1, lambda j: (0, hq + head)),
            block(1, lambda j: (0, hq + hk + head)),
            block(2, lambda j: (0, head * pairs + j)),
            whole(8),
            whole(seq),
            whole(seq),
        ],
        out_specs=[block(2, lambda j: (0, j)), whole(seq), whole(seq), whole(8)],
        out_shape=[
            jax.ShapeDtypeStruct((seq, 2 * pairs * HEAD), BF),
            jax.ShapeDtypeStruct((seq, HEAD), BF),
            jax.ShapeDtypeStruct((seq, HEAD), BF),
            jax.ShapeDtypeStruct((8, HEAD), F32),
        ],
        scratch_shapes=[
            pltpu.VMEM((seq, HEAD), BF),
            pltpu.VMEM((seq, HEAD), F32),
            pltpu.VMEM((seq, HEAD), F32),
        ],
        name="attend_back",
    )(qkv, qkv, qkv, d_context, gains, cos, sin)


def split2(v):
    high = v.astype(BF)
    return high, (v - high.astype(F32)).astype(BF)


def gather_dp(v):
    return lax.all_gather(v, "dp", axis=0, tiled=True)


def gather_all(v):
    return lax.all_gather(v, ("dp", "tensor"), axis=0, tiled=True)


def scatter_all(v):
    return lax.psum_scatter(v, ("dp", "tensor"), scatter_dimension=0, tiled=True)


def scatter_dp(v):
    return lax.psum_scatter(v, "dp", scatter_dimension=0, tiled=True)


def pieces(width, dp, seq):
    count = 1 if dp * seq <= 8192 else 4
    step = width // count // 128 * 128
    edges = [step * i for i in range(count)] + [width]
    return list(zip(edges[:-1], edges[1:]))


def after(v, earlier):
    return v if earlier is None else lax.optimization_barrier((v, earlier))[0]


def dispatch(pick, own, dp, seq, earlier):
    blocks = []
    for low, high in pieces(own.shape[1], dp, seq):
        every = gather_all(after(own[:, low:high], earlier)).reshape(dp, seq, high - low)
        block = jnp.einsum("gest,gtd->gesd", pick, every, preferred_element_type=F32).astype(BF)
        blocks.append(block)
        earlier = block if len(pieces(own.shape[1], dp, seq)) > 1 else None
    return jnp.concatenate(blocks, axis=3)


def combine(pick, rows, dp, seq, earlier):
    blocks = []
    for low, high in pieces(rows.shape[3], dp, seq):
        tok = jnp.einsum(
            "gest,gesd->gtd",
            pick,
            after(rows[:, :, :, low:high], earlier),
            preferred_element_type=F32,
        ).astype(BF)
        blocks.append(scatter_all(tok.reshape(dp * seq, high - low)))
        earlier = blocks[-1] if len(pieces(rows.shape[3], dp, seq)) > 1 else None
    return jnp.concatenate(blocks, axis=1).astype(F32)


GRID = [(z, x, c) for z in range(4) for x in range(2) for c in range(2)]
SPLIT = (0, 768, 1536, 1792, 2048)


def at(z, x, c):
    return z % 4 * 4 + x % 2 * 2 + c % 2


def shift_z(v, k):
    return lax.ppermute(v, "dp", [(at(z, x, c), at(z + k, x, c)) for z, x, c in GRID])


def swap_x(v):
    return lax.ppermute(v, "dp", [(at(z, x, c), at(z, x + 1, c)) for z, x, c in GRID])


def swap_c(v):
    return lax.ppermute(v, "dp", [(at(z, x, c), at(z, x, c + 1)) for z, x, c in GRID])


def swap_y(v):
    return lax.ppermute(v, "tensor", [(0, 1), (1, 0)])


def gather_y(v):
    other = swap_y(v)
    first = lax.axis_index("tensor") == 0
    return jnp.concatenate([jnp.where(first, v, other), jnp.where(first, other, v)])


def scatter_y(v):
    a, b = jnp.split(v, 2)
    first = lax.axis_index("tensor") == 0
    kept, sent = jnp.where(first, a, b), jnp.where(first, b, a)
    other = swap_y(sent.astype(BF))
    return kept.astype(F32) + other.astype(F32)


def gather_z(v, way):
    one, three = shift_z(v, 1), shift_z(v, -1)
    two = shift_z(one, 1) if way > 0 else shift_z(three, -1)
    return jnp.stack([v, one, two, three])


def add2(a, b):
    return (a.astype(F32) + b.astype(F32)).astype(BF)


def reduce_z(v, way, two=None):
    if two is None:
        two = first_hop(v, way)
    side = shift_z(v[3 if way > 0 else 1], way)
    relay = shift_z(add2(v[1 if way > 0 else 3], two), -way)
    return (v[0].astype(F32) + side.astype(F32) + relay.astype(F32)).astype(BF)


def first_hop(v, way):
    return shift_z(v[2], -way)


def tied(v, w):
    return lax.optimization_barrier((v, w))


def gather_rel(v1, v2, v5, v6, plan, aside):
    w5 = jnp.stack([v5, swap_x(v5)])
    w6 = jnp.stack([v6, swap_y(v6)])
    s1 = gather_z(v1, 1)
    s2 = gather_z(v2, -1)
    w5 = jnp.stack([w5, swap_y(w5)])
    w6 = jnp.stack([w6, swap_x(w6)])
    s1, s2, w5, w6, plan = lax.optimization_barrier((s1, s2, w5, w6, plan))
    s1x, s2y = swap_x(s1), swap_y(s2)
    five = [shift_z(w5, 1), shift_z(w5, -1)]
    six = [shift_z(w6, 1), shift_z(w6, -1)]
    far = aside(1, plan)
    five, six, s1x, s2y, far = lax.optimization_barrier((five, six, s1x, s2y, far))
    s1 = jnp.stack([s1, s1x])
    s2 = jnp.stack([s2, s2y])
    s1y, s2x = swap_y(s1), swap_x(s2)
    five.append(shift_z(five[0], 1))
    six.append(shift_z(six[1], -1))
    plan, (five, six) = tied(plan, (five, six))
    o5 = jnp.stack([w5, five[0], five[2], five[1]])
    o6 = jnp.stack([w6, six[0], six[2], six[1]])
    (s1y, s2x), near = tied((s1y, s2x), aside(0, plan))
    first = (s1, s1y, s2, s2x, o5, o6)
    return first, tuple(swap_c(v) for v in first), plan, (near, far)


def scatter_core(near, far):
    p5, p6, p1, p2 = [add2(near[i], swap_c(far[i])) for i in (2, 3, 0, 1)]
    return p1, p2, p5, p6


def step_x(v):
    other = swap_x(v[1])
    return add2(v[0], other)


def step_y(v):
    other = swap_y(v[1])
    return add2(v[0], other)


def scatter_rows_core(near, far):
    a = swap_c(far[0])
    b = swap_c(far[1])
    return add2(near[0], a), add2(near[1], b)


def scatter_rows(a, b):
    b = reduce_z(b, -1)
    a = step_x(a)
    b = step_x(b)
    return jnp.concatenate([reduce_z(a, 1), b], axis=1)


def sequence_at(dc, dz, dx):
    at = lax.axis_index("dp")
    return (at // 4 - dz) % 4 * 4 + (at // 2 % 2 + dx) % 2 * 2 + (at % 2 + dc) % 2


def nn(a, b):
    return lax.dot_general(a, b, (((1,), (0,)), ((), ())), preferred_element_type=F32)


def nt(a, b):
    return lax.dot_general(a, b, (((1,), (1,)), ((), ())), preferred_element_type=F32)


def pick_rows(rank, slots):
    at_slot = lax.broadcasted_iota(jnp.int32, (slots, rank.shape[1]), 0).astype(F32)
    return jnp.concatenate(
        [(rank[e : e + 1, :] == at_slot).astype(F32).astype(BF) for e in range(rank.shape[0])],
        axis=0,
    )


def pick_cols(rank, slots):
    at_slot = lax.broadcasted_iota(jnp.int32, (rank.shape[0], slots), 1).astype(F32)
    return jnp.concatenate(
        [(rank[:, e : e + 1] == at_slot).astype(F32).astype(BF) for e in range(rank.shape[1])],
        axis=1,
    )


def cot_kernel(where, rank, cot_a, cot_b, down, cots, d_act):
    slots = cots.shape[2] // 2
    for dx, cot in enumerate((cot_a, cot_b)):
        both = nn(pick_rows(rank[dx], slots), cot[0]).astype(BF)
        for e in range(2):
            cots[e, 0, dx * slots : (dx + 1) * slots, :] = both[e * slots : (e + 1) * slots]
    for e in range(2):
        d_act[e, 0] = nt(cots[e, 0], down[e])


def expert_kernel(
    rank, rank_t, cols, d_act, x1a, x1b, x2a, x2b, x5, x6, weights,
    rows, scaled, d_g, d_u, t1, t2, t5, t6, back,
):
    slots = rows.shape[2] // 2
    n = x1a.shape[2]
    gates = []
    for dx, x2 in enumerate((x2a, x2b)):
        pick = pick_rows(rank[dx], slots)
        low, high = pick[:, :n], pick[:, n:]
        block1 = nn(low, x1a[dx, 0]) + nn(high, x1b[dx, 0])
        block2 = nn(low, x2[0, 0]) + nn(high, x2[1, 0])
        block5 = nn(low, x5[0, 0, dx]) + nn(high, x5[0, 1, dx])
        block6 = nn(low, x6[0, dx, 0]) + nn(high, x6[0, dx, 1])
        low = dx * slots
        for e in range(2):
            part = slice(e * slots, (e + 1) * slots)
            rows[e, 0, low : low + slots, 0:768] = block1[part].astype(BF)
            rows[e, 0, low : low + slots, 768:1536] = block2[part].astype(BF)
            rows[e, 0, low : low + slots, 1536:1792] = block5[part, :256].astype(BF)
            rows[e, 0, low : low + slots, 1792:2048] = block6[part].astype(BF)
            both = cols[e, 0:1, :] + cols[e, 1:2, :]
            gates.append(jnp.sum(block5[part, 256:] * both, axis=1, keepdims=True))
    extras = []
    for e in range(2):
        gate = jnp.concatenate([gates[e], gates[2 + e]], axis=0)
        g = nn(rows[e, 0], weights[e])
        g, u = jnp.split(g, 2, axis=1)
        da = d_act[e, 0]
        sig = 1.0 / (1.0 + jnp.exp(-g))
        silu = g * sig
        act = silu * u
        scaled[e, 0] = (act * gate).astype(BF)
        d_gate = jnp.sum(act * da, axis=1, keepdims=True)
        da = da * gate
        dg = (da * u * sig * (1.0 + g * (1.0 - sig))).astype(BF)
        du = (da * silu).astype(BF)
        d_g[e, 0] = dg
        d_u[e, 0] = du
        high = d_gate.astype(BF).astype(F32)
        extras.append(high * cols[e, 0:1, :] + (d_gate - high) * cols[e, 1:2, :])
        dr = nt(jnp.concatenate([dg, du], axis=1), weights[e]).astype(BF)
        for dx in range(2):
            back[dx, e * slots : (e + 1) * slots, :] = dr[dx * slots : (dx + 1) * slots]
    extra = [
        jnp.concatenate([extras[e][dx * slots : (dx + 1) * slots] for e in range(2)], axis=0)
        for dx in range(2)
    ]
    put_back(rank_t, back, t1, t2, t5, t6, slots, extra)


def put_back(rank_t, back, t1, t2, t5, t6, slots, extra=None):
    for dx in range(2):
        pick_t = pick_cols(rank_t[dx], slots)
        n = pick_t.shape[0] // 2
        p1, p2, p5, p6 = [
            nn(pick_t, back[dx, :, a:b]).astype(BF) for a, b in zip(SPLIT[:-1], SPLIT[1:])
        ]
        for dy in range(2):
            half = slice(dy * n, (dy + 1) * n)
            t1[dy, dx, 0] = p1[half]
            t2[dx, dy, 0] = p2[half]
            t5[0, dy, dx, :, 0:256] = p5[half]
            t6[0, dx, dy] = p6[half]
        if extra is not None:
            p7 = nn(pick_t, extra[dx].astype(BF)).astype(BF)
            for dy in range(2):
                t5[0, dy, dx, :, 256:] = p7[dy * n : (dy + 1) * n]


def out_kernel(rank_t, scaled, down, t1, t2, t5, t6, back):
    slots = scaled.shape[2] // 2
    for e in range(2):
        y = nn(scaled[e, 0], down[e]).astype(BF)
        for dx in range(2):
            back[dx, e * slots : (e + 1) * slots, :] = y[dx * slots : (dx + 1) * slots]
    put_back(rank_t, back, t1, t2, t5, t6, slots)


def grad_kernel(where, left, right, small, heads, a, b):
    both = lax.dot_general(
        left[...], right[...], (((0,), (0,)), ((), ())), preferred_element_type=F32
    ).astype(BF)
    width = a.shape[-1]
    a[0, 0] = both[:, :width]
    b[0, 0, :, : both.shape[1] - width] = both[:, width:]
    rest = jnp.zeros((small.shape[0] - heads.shape[0], small.shape[1]), F32)
    both_small = small[...] + jnp.concatenate([heads[...], rest], axis=0)
    b[0, 0, :, both.shape[1] - width :] = both_small.astype(BF)


def run_grad(where, left, right, small, heads):
    count, columns = right.shape
    rest = small.shape[1]
    width = columns * 9 // 16 // 128 * 128
    shard = left.shape[1] // 16
    return pl.pallas_call(
        grad_kernel,
        grid_spec=pltpu.PrefetchScalarGridSpec(
            num_scalar_prefetch=1,
            grid=(2, 4),
            in_specs=[
                pl.BlockSpec((count, shard), lambda dx, dz, w: (0, w[2 * dz + dx])),
                pl.BlockSpec((count, columns), lambda dx, dz, w: (0, 0)),
                pl.BlockSpec((shard, rest), lambda dx, dz, w: (w[2 * dz + dx], 0)),
                pl.BlockSpec((HEAD // 16, rest), lambda dx, dz, w: (w[2 * dz + dx], 0)),
            ],
            out_specs=[
                pl.BlockSpec((1, 1, shard, width), lambda dx, dz, w: (dx, dz, 0, 0)),
                pl.BlockSpec((1, 1, shard, columns - width + rest), lambda dx, dz, w: (dz, dx, 0, 0)),
            ],
        ),
        out_shape=[
            shaped((2, 4, shard, width), BF),
            shaped((4, 2, shard, columns - width + rest), BF),
        ],
        compiler_params=LIMIT,
        name="grad",
    )(where, left, right, small, heads)


def pair(*tail):
    return pl.BlockSpec((2, *tail), lambda i, *_: (i,) + (0,) * len(tail))


def z_last(*lead):
    def spec(rows, columns):
        return pl.BlockSpec(
            (*lead, 1, rows, columns), lambda i, *_: (0,) * len(lead) + (i, 0, 0)
        )

    return spec


def z_first(rows, columns):
    return pl.BlockSpec((1, 2, 2, rows, columns), lambda i, *_: (i, 0, 0, 0, 0))


def block_specs(n, extra):
    return [z_last(2, 2)(n, 768), z_last(2, 2)(n, 768), z_first(n, 256 + extra), z_first(n, 256)]


def block_shapes(n, extra):
    shapes = [(2, 2, 4, n, 768), (2, 2, 4, n, 768), (4, 2, 2, n, 256 + extra), (4, 2, 2, n, 256)]
    return [shaped(v, BF) for v in shapes]


def by_expert(*tail):
    return pl.BlockSpec((2, 1, *tail), lambda i, *_: (0, i) + (0,) * len(tail))


def fixed(*shape):
    return pl.BlockSpec(
        shape, lambda i, *_: (0,) * len(shape), pipeline_mode=pl.Buffered(1)
    )


def shaped(shape, kind):
    return jax.ShapeDtypeStruct(shape, kind)


LIMIT = pltpu.CompilerParams(vmem_limit_bytes=58 * 1024 * 1024)


def run_cots(where, rank, cot_all, down, slots):
    seq, width = cot_all.shape[1:]
    ff = down.shape[1]
    return pl.pallas_call(
        cot_kernel,
        grid_spec=pltpu.PrefetchScalarGridSpec(
            num_scalar_prefetch=1,
            grid=(4,),
            in_specs=[
                pair(2, seq),
                pl.BlockSpec((1, seq, width), lambda i, w: (w[2 * i], 0, 0)),
                pl.BlockSpec((1, seq, width), lambda i, w: (w[2 * i + 1], 0, 0)),
                fixed(2, ff, width),
            ],
            out_specs=[by_expert(2 * slots, width), by_expert(2 * slots, ff)],
        ),
        out_shape=[shaped((2, 4, 2 * slots, width), BF), shaped((2, 4, 2 * slots, ff), F32)],
        compiler_params=LIMIT,
        name="cots",
    )(where, rank, cot_all, cot_all, down)


def run_experts(rank, rank_t, cols, d_act, parts, weights, slots):
    s1, s1y, s2, s2x, o5, o6 = parts
    n = s1.shape[2]
    seq, width, ff = 2 * n, weights.shape[1], weights.shape[2] // 2
    return pl.pallas_call(
        expert_kernel,
        grid=(4,),
        in_specs=[
            pair(2, seq),
            pair(seq, 2),
            fixed(*cols.shape),
            by_expert(2 * slots, ff),
            z_last(2)(n, 768),
            z_last(2)(n, 768),
            z_last(2)(n, 768),
            z_last(2)(n, 768),
            z_first(n, 384),
            z_first(n, 256),
            fixed(2, width, 2 * ff),
        ],
        out_specs=[
            by_expert(2 * slots, width),
            by_expert(2 * slots, ff),
            by_expert(2 * slots, ff),
            by_expert(2 * slots, ff),
        ]
        + block_specs(n, 128),
        out_shape=[
            shaped((2, 4, 2 * slots, width), BF),
            shaped((2, 4, 2 * slots, ff), BF),
            shaped((2, 4, 2 * slots, ff), BF),
            shaped((2, 4, 2 * slots, ff), BF),
        ]
        + block_shapes(n, 128),
        scratch_shapes=[pltpu.VMEM((2, 2 * slots, width), BF)],
        compiler_params=LIMIT,
        name="experts",
    )(
        rank, rank_t, cols, d_act, s1, s1y, s2, s2x, o5, o6, weights,
    )


def run_outs(rank_t, scaled, down, slots):
    seq, ff, width = rank_t.shape[1], down.shape[1], down.shape[2]
    return pl.pallas_call(
        out_kernel,
        grid=(4,),
        in_specs=[pair(seq, 2), by_expert(2 * slots, ff), fixed(2, ff, width)],
        out_specs=block_specs(seq // 2, 0),
        out_shape=block_shapes(seq // 2, 0),
        scratch_shapes=[pltpu.VMEM((2, 2 * slots, width), BF)],
        compiler_params=LIMIT,
        name="outs",
    )(rank_t, scaled, down)


def flip(v, axis, y):
    a, b = jnp.split(v, 2, axis=axis)
    return jnp.where(y == 0, v, jnp.concatenate([b, a], axis=axis))


def slot_plan(ids_all, experts):
    y = lax.axis_index("tensor")
    seq = ids_all.shape[1]
    mine = lax.axis_index("dp") * 2 + jnp.arange(2, dtype=jnp.int32)
    mask = jnp.any(ids_all[:, None, :, :] == mine[None, :, None, None], axis=3)
    before = (jnp.arange(seq)[:, None] < jnp.arange(seq)[None, :]).astype(BF)
    rank = jnp.einsum("gea,ab->geb", mask.astype(BF), before, preferred_element_type=F32)
    rank = jnp.where(mask, rank, -1.0)
    d = jnp.arange(16)
    where = sequence_at(d // 8, d // 2 % 4, d % 2)
    rank = jnp.take(rank, where, axis=0)
    rank_rel = flip(rank, 2, y)
    rank_t = jnp.swapaxes(rank_rel, 1, 2)
    column = jnp.arange(128)
    cols = (
        column[None, None, :] == (mine[:, None] + jnp.array([[0, experts]]))[:, :, None]
    ).astype(F32)
    halves = lambda v: (v[:8], v[8:])
    return halves(where.astype(jnp.int32)), halves(rank), halves(rank_rel), halves(rank_t), cols


def moe_small(plan, cot_all, ffn_in, gate_x, weights, down_weight, slots):

    def cot_rows(k, plan):
        return run_cots(plan[0][k], plan[1][k], cot_all, down_weight, slots)

    v1, v2, v5, v6 = [ffn_in[:, a:b] for a, b in zip(SPLIT[:-1], SPLIT[1:])]
    v5 = jnp.concatenate([v5, gate_x], axis=1)
    *parts, plan, both = gather_rel(v1, v2, v5, v6, plan, cot_rows)
    rank_rel, rank_t, cols = plan[2:]
    cots, d_act = zip(*both)
    far, near = [
        run_experts(rank_rel[k], rank_t[k], cols, d_act[k], parts[k], weights, slots)
        for k in (1, 0)
    ]
    p1, p2, p5, p6 = scatter_core(near[4:], far[4:])
    kept = lambda i: (near[i], far[i])
    total = lambda spec, a, b: jnp.einsum(spec, a[0], b[0], preferred_element_type=F32) + jnp.einsum(
        spec, a[1], b[1], preferred_element_type=F32
    )
    p5 = reduce_z(p5, 1)
    p6 = reduce_z(p6, -1)
    p1 = step_y(p1)
    p2 = step_x(p2)
    down_grad = total("egsf,egsd->efd", kept(1), cots)
    outs = []
    for k in (0, 1):
        outs.append(run_outs(rank_t[k], kept(1)[k], down_weight, slots))
    (p1, p2, p5, p6), (outs, down_grad) = tied((p1, p2, p5, p6), (outs, down_grad))
    p5 = step_y(p5)
    p6 = step_x(p6)
    p1 = step_x(p1)
    p2 = step_y(p2)
    up_grad = total("egsd,egsf->edf", kept(0), kept(3))
    (p1, p2, p5, p6), up_grad = tied((p1, p2, p5, p6), up_grad)
    d5 = step_x(p5)
    d6 = step_y(p6)
    d1 = reduce_z(p1, 1)
    d2 = reduce_z(p2, -1)
    p1, p2, p5, p6 = scatter_core(*outs)
    p2, (d5, d6) = tied(p2, (d5, d6))
    p2 = step_x(p2)
    d_sum = jnp.concatenate([d1, d2, d5[:, :256], d6, d5[:, 256:]], axis=1)
    d_sum, (p1, p5, p6) = tied(d_sum, (p1, p5, p6))
    d_sum = d_sum.astype(F32)

    def gate_later(aside):
        (rows, grads), aside = tied((kept(0), kept(2)), aside)
        return total("egsd,egsf->edf", rows, grads), aside

    return d_sum, (p1, p2, p5, p6), gate_later, up_grad, down_grad


def moe_large(
    ids_all, cotangent, ffn_in, gate_x, gate_weight, up_weight, down_weight, experts, slots
):
    dp, seq = ids_all.shape[:2]
    local = gate_weight.shape[0]
    dp_at = lax.axis_index("dp")
    mine = dp_at * local + jnp.arange(local, dtype=jnp.int32)
    mask = jnp.any(ids_all[:, :, None, :] == mine[None, None, :, None], axis=3).astype(BF)
    gate_all = gather_all(gate_x).reshape(dp, seq, -1)
    before = (jnp.arange(seq)[:, None] > jnp.arange(seq)[None, :]).astype(BF)
    rank = jnp.einsum("ab,gbe->gea", before, mask, preferred_element_type=F32)
    rank = jnp.where(jnp.swapaxes(mask, 1, 2) > 0, rank, -1.0)
    pick = (rank[:, :, None, :] == jnp.arange(slots, dtype=F32)[None, None, :, None]).astype(BF)

    cots = dispatch(pick, cotangent, dp, seq, None)
    rows = dispatch(pick, ffn_in, dp, seq, cots)
    gate_tok = lax.dynamic_slice_in_dim(gate_all, dp_at * local, local, 2).astype(
        F32
    ) + lax.dynamic_slice_in_dim(gate_all, experts + dp_at * local, local, 2).astype(F32)
    gate_slot = jnp.sum(pick.astype(F32) * jnp.swapaxes(gate_tok, 1, 2)[:, :, None, :], axis=3)

    g_proj = jnp.einsum("gesd,edf->gesf", rows, gate_weight, preferred_element_type=F32)
    u_proj = jnp.einsum("gesd,edf->gesf", rows, up_weight, preferred_element_type=F32)
    d_act = jnp.einsum("gesd,efd->gesf", cots, down_weight, preferred_element_type=F32)
    sig = 1.0 / (1.0 + jnp.exp(-g_proj))
    silu = g_proj * sig
    act = silu * u_proj
    scaled = (act * gate_slot[..., None]).astype(BF)
    d_gate_slot = jnp.sum(act * d_act, axis=3)
    d_act = d_act * gate_slot[..., None]
    d_g = (d_act * u_proj * sig * (1.0 + g_proj * (1.0 - sig))).astype(BF)
    d_u = (d_act * silu).astype(BF)
    d_rows = (
        jnp.einsum("gesf,edf->gesd", d_g, gate_weight, preferred_element_type=F32)
        + jnp.einsum("gesf,edf->gesd", d_u, up_weight, preferred_element_type=F32)
    ).astype(BF)
    dg_high, dg_low = split2(d_gate_slot)
    column = jnp.arange(lanes(2 * experts))
    high_col = (column[None, :] == mine[:, None])[None, :, None, :]
    low_col = (column[None, :] == experts + mine[:, None])[None, :, None, :]
    extra = jnp.where(high_col, dg_high[..., None], jnp.where(low_col, dg_low[..., None], 0.0))
    d_rows = jnp.concatenate([d_rows, extra.astype(BF)], axis=3)
    d_sum = combine(pick, d_rows, dp, seq, None)

    y_rows = jnp.einsum("gesf,efd->gesd", scaled, down_weight, preferred_element_type=F32)
    y_sum = combine(pick, y_rows.astype(BF), dp, seq, d_sum)
    down_grad = jnp.einsum("gesf,gesd->efd", scaled, cots, preferred_element_type=F32)
    gate_grad = jnp.einsum("gesd,gesf->edf", rows, d_g, preferred_element_type=F32)
    up_grad = jnp.einsum("gesd,gesf->edf", rows, d_u, preferred_element_type=F32)

    return d_sum, y_sum, gate_grad, up_grad, down_grad


def pad_to(v, width):
    return jnp.pad(v, ((0, 0), (0, width - v.shape[1])))


def lanes(count):
    return -(-count // 128) * 128


def on_device(
    tokens,
    attn_gain,
    q_weight,
    key_matrix,
    value_matrix,
    o_weight,
    query_norm_gain,
    k_gain,
    ffn_gain,
    router_weight,
    gate_weight,
    up_weight,
    down_weight,
    expert_ids,
    cotangent,
):
    dp = lax.axis_size("dp")
    tensor = lax.axis_size("tensor")
    own, width = tokens.shape
    seq = expert_ids.shape[0]
    begin = lax.axis_index("tensor") * own
    local = gate_weight.shape[0]
    experts = local * dp
    slots = 10 * seq * expert_ids.shape[1] // (8 * experts)
    slots = -(-slots // 16) * 16
    shard = q_weight.shape[0]
    gshard = query_norm_gain.shape[0]
    hq = q_weight.shape[1] // HEAD
    hk = key_matrix.shape[1] // HEAD
    qkv_width = (hq + 2 * hk) * HEAD
    top = expert_ids.shape[1]
    fast = (dp, tensor, local, seq, width) == (16, 2, 2, 384, 2048)

    arange_e = jnp.arange(experts, dtype=jnp.int32)
    own_ids = lax.dynamic_slice_in_dim(expert_ids, begin, own, 0)
    own_mask = jnp.any(own_ids[:, :, None] == arange_e[None, None, :], axis=1)

    gain_rows = jnp.stack(
        [
            attn_gain,
            ffn_gain,
            jnp.pad(query_norm_gain, (0, shard - gshard)),
            jnp.pad(k_gain, (0, shard - gshard)),
        ],
        axis=1,
    )
    ids_rows = expert_ids.reshape(shard, -1).astype(BF)
    small = jnp.concatenate([router_weight, gain_rows, ids_rows], axis=1)
    small = pad_to(small, lanes(small.shape[1]))
    small_end = qkv_width + small.shape[1]
    all_in = gather_dp(
        jnp.concatenate([q_weight, key_matrix, value_matrix, small, o_weight.T], axis=1)
    )
    layer_in = gather_y(tokens)
    if fast:
        weights = jnp.concatenate([gate_weight, up_weight], axis=2)
        layer_in, weights = tied(layer_in, weights)
    o_t = all_in[:, small_end:]
    if fast:
        cot_all = gather_dp(gather_y(cotangent)).reshape(dp, seq, width)

    w_qkv = all_in[:, :qkv_width]
    router = all_in[:, qkv_width : qkv_width + experts]
    gains = all_in[:, qkv_width + experts : qkv_width + experts + 4].astype(F32)
    ids_all = all_in[:, qkv_width + experts + 4 :][:, : seq * top // shard]
    ids_all = ids_all.astype(jnp.int32).reshape(dp, seq, top)
    attn_gain32 = gains[:, 0]
    ffn_gain32 = gains[:, 1]
    q_gain32 = gains[:, 2].reshape(dp, shard)[:, :gshard].reshape(-1)
    k_gain32 = gains[:, 3].reshape(dp, shard)[:, :gshard].reshape(-1)

    residual = layer_in.astype(F32)
    normed = rms(residual, attn_gain32).astype(BF)
    qkv = dot(normed, w_qkv, 1, 0)
    cos, sin = rope_tables(seq)
    head_gains = jnp.pad(jnp.stack([q_gain32, k_gain32]), ((0, 6), (0, 0)))
    context = run_attend(qkv, head_gains, cos, sin, hq, hk)
    attn_part = dot(context, o_t, 1, 1)
    if fast:
        attn_part, ids_all = tied(attn_part, ids_all)
        plan = slot_plan(ids_all, experts)
    hidden = tokens.astype(F32) + scatter_y(attn_part)

    ffn_in = rms(hidden, ffn_gain32).astype(BF)
    logits = dot(ffn_in, router, 1, 0)
    chosen = jnp.where(own_mask, jnp.exp(logits), 0.0)
    gates = chosen / jnp.sum(chosen, axis=1, keepdims=True)
    gate_high, gate_low = split2(gates)
    gate_x = pad_to(jnp.concatenate([gate_high, gate_low], axis=1), lanes(2 * experts))
    args = (gate_weight, up_weight, down_weight)
    if fast:
        d_sum, y_sum, gate_later, up_grad, down_grad = moe_small(
            plan, cot_all, ffn_in, gate_x, weights, down_weight, slots
        )
    else:
        d_sum, y_sum, gate_grad, up_grad, down_grad = moe_large(
            ids_all, cotangent, ffn_in, gate_x, *args, experts, slots
        )
    d_gates = d_sum[:, width : width + experts] + d_sum[:, width + experts : width + 2 * experts]
    d_logits = gates * (d_gates - jnp.sum(gates * d_gates, axis=1, keepdims=True))
    d_high, d_low = split2(d_logits)
    d_ffn = d_sum[:, :width] + dot(d_high, router, 1, 1) + dot(d_low, router, 1, 1)
    router_part = dot(ffn_in, d_high, 0, 0) + dot(ffn_in, d_low, 0, 0)
    d_hidden, ffn_gain_rows = rms_back(hidden, ffn_gain32, d_ffn)
    ffn_gain_part = jnp.sum(ffn_gain_rows, axis=0)
    d_hidden = d_hidden + cotangent.astype(F32)
    d_attn = gather_y(d_hidden.astype(BF))

    o_part = dot(d_attn, context, 0, 0).astype(BF)
    d_attn, o_part = tied(d_attn, o_part)
    o_sum = scatter_dp(o_part).astype(F32)
    if fast:
        p1, p2, p5, p6 = y_sum
        d_attn, p1 = tied(d_attn, p1)
        p1 = step_y(p1)
        two5, two6 = first_hop(p5, 1), first_hop(p6, -1)
        gate_grad, d_attn = gate_later(d_attn)
    d_context = dot(d_attn, o_t, 1, 0).astype(BF)
    heads = []
    for head in range(hk):
        heads.append(run_attend_back(head, qkv, d_context, head_gains, cos, sin, hq, hk))
        if fast and head == 0:
            aside = (p1, p2, two5, two6, gate_grad)
            d_context, heads, aside = lax.optimization_barrier((d_context, heads, aside))
            p1, p2, two5, two6, gate_grad = aside
            p1 = step_x(p1)
            p2 = step_y(p2)
            p5 = reduce_z(p5, 1, two5)
            p6 = reduce_z(p6, -1, two6)
    d_qkv = jnp.concatenate([h[k] for k in range(3) for h in heads], axis=1)
    small_part = jnp.concatenate([router_part, ffn_gain_part[:, None]], axis=1)
    small_part = pad_to(small_part, lanes(experts + 3))
    column = jnp.arange(small_part.shape[1])[None, :]
    head_part = sum(h[3][0] for h in heads)[:, None] * (column == experts + 1).astype(F32)
    head_part += sum(h[3][1] for h in heads)[:, None] * (column == experts + 2).astype(F32)
    if fast:
        d_qkv, (p1, p2, p5, p6) = tied(d_qkv, (p1, p2, p5, p6))
        y_sum = (reduce_z(p1, 1), reduce_z(p2, -1), step_x(step_y(p5)), step_y(step_x(p6)))
        far = run_grad(plan[0][1], normed, d_qkv, small_part, head_part)
        near = run_grad(plan[0][0], normed, d_qkv, small_part, head_part)
        a, b = scatter_rows_core(near, far)
        qkv_sum = scatter_rows(a, b).astype(F32)
        qkv_sum, small_sum = qkv_sum[:, :qkv_width], qkv_sum[:, qkv_width:]
        y_sum = jnp.concatenate(y_sum, axis=1).astype(F32)
    else:
        qkv_sum = scatter_dp(dot(normed, d_qkv, 0, 0).astype(BF)).astype(F32)
        head_part = jnp.pad(
            head_part.reshape(dp, gshard, -1), ((0, 0), (0, shard - gshard), (0, 0))
        )
        small_sum = scatter_dp(small_part + head_part.reshape(small_part.shape))
    output = (hidden + y_sum).astype(BF)
    d_normed = dot(d_qkv, w_qkv, 1, 1)
    d_normed = scatter_y(d_normed)
    d_tokens, _ = rms_back(tokens.astype(F32), attn_gain32, d_normed)
    tokens_grad = d_tokens + d_hidden

    weights = jnp.concatenate([q_weight, key_matrix, value_matrix], axis=1).astype(F32)
    gain_part = jnp.sum(weights * qkv_sum, axis=1) / attn_gain.astype(F32)
    small_sum = jnp.concatenate([small_sum, gain_part[:, None]], axis=1)
    small_sum = small_sum + swap_y(small_sum)
    return (
        output,
        tokens_grad,
        small_sum[:, -1],
        qkv_sum[:, : hq * HEAD],
        qkv_sum[:, hq * HEAD : (hq + hk) * HEAD],
        qkv_sum[:, (hq + hk) * HEAD :],
        o_sum.T,
        small_sum[:gshard, experts + 1],
        small_sum[:gshard, experts + 2],
        small_sum[:, experts],
        small_sum[:, :experts],
        gate_grad,
        up_grad,
        down_grad,
    )


def solution(mesh):
    rows = P(("dp", "tensor"), None)
    both = P("dp", "tensor")
    return jax.shard_map(
        on_device,
        mesh=mesh,
        in_specs=(
            rows,
            P("dp"),
            both,
            both,
            both,
            P("tensor", "dp"),
            P("dp"),
            P("dp"),
            P("dp"),
            P("dp", None),
            P("dp", None, "tensor"),
            P("dp", None, "tensor"),
            P("dp", "tensor", None),
            P("dp", None),
            rows,
        ),
        out_specs=(
            rows,
            rows,
            P("dp"),
            both,
            both,
            both,
            P("tensor", "dp"),
            P("dp"),
            P("dp"),
            P("dp"),
            P("dp", None),
            P("dp", None, "tensor"),
            P("dp", None, "tensor"),
            P("dp", "tensor", None),
        ),
        check_vma=False,
    )
```

```python
import jax
import jax.numpy as jnp
from jax import lax
from jax.experimental import pallas as pl
from jax.experimental.pallas import tpu as pltpu
from jax.sharding import PartitionSpec as P


HEAD = 128
EPS = 1e-06
THETA = 1000000.0
BF = jnp.bfloat16
F32 = jnp.float32


def dot(a, b, ca, cb):
    return lax.dot_general(a, b, (((ca,), (cb,)), ((), ())), preferred_element_type=F32)


def rms(v, gain):
    return v * lax.rsqrt(jnp.mean(v * v, axis=-1, keepdims=True) + EPS) * gain


def rms_back(v, gain, u):
    inv = lax.rsqrt(jnp.mean(v * v, axis=-1, keepdims=True) + EPS)
    ug = u * gain
    grad = ug * inv - v * (jnp.mean(ug * v, axis=-1, keepdims=True) * inv * inv * inv)
    return grad, u * v * inv


def rope_tables(count):
    inverse = THETA ** (-(jnp.arange(HEAD // 2, dtype=F32) * 2.0 / HEAD))
    angles = jnp.arange(count, dtype=F32)[:, None] * inverse[None, :]
    cos, sin = jnp.cos(angles), jnp.sin(angles)
    return jnp.concatenate([cos, cos], axis=1), jnp.concatenate([-sin, sin], axis=1)


def half_turn(v):
    return pltpu.roll(v, HEAD // 2, 1)


def turned(raw, gain, cos, sin):
    v = rms(raw, gain)
    return (v * cos + half_turn(v) * sin).astype(BF)


def soft(q, k):
    scores = lax.dot_general(q, k, (((1,), (1,)), ((), ())), preferred_element_type=F32)
    scores = scores * HEAD ** (-0.5)
    row = lax.broadcasted_iota(jnp.int32, scores.shape, 0)
    column = lax.broadcasted_iota(jnp.int32, scores.shape, 1)
    e = jnp.where(row >= column, jnp.exp(scores), 0.0)
    return e * (1.0 / jnp.sum(e, axis=1, keepdims=True))


def attend_kernel(q_raw, k_raw, v_raw, gains, cos, sin, context, keys):
    @pl.when(pl.program_id(1) == 0)
    def _():
        keys[...] = turned(k_raw[...], gains[1:2], cos[...], sin[...])

    v = v_raw[...].astype(BF)
    for h in range(2):
        part = slice(h * HEAD, (h + 1) * HEAD)
        q = turned(q_raw[:, part], gains[0:1], cos[...], sin[...])
        p = soft(q, keys[...]).astype(BF)
        context[:, part] = lax.dot_general(
            p, v, (((1,), (0,)), ((), ())), preferred_element_type=F32
        ).astype(BF)


def attend_back_kernel(
    q_raw, k_raw, v_raw, d_context, gains, cos, sin, d_q, d_k, d_v, d_gains, keys, k_sum, v_sum
):
    at = pl.program_id(0)

    @pl.when(at == 0)
    def _():
        keys[...] = turned(k_raw[...], gains[1:2], cos[...], sin[...])
        k_sum[...] = jnp.zeros_like(k_sum)
        v_sum[...] = jnp.zeros_like(v_sum)
        d_gains[...] = jnp.zeros_like(d_gains)

    def back(raw, gain, u):
        return rms_back(raw, gain, u * cos[...] - half_turn(u) * sin[...])

    v = v_raw[...].astype(BF)
    scale = HEAD ** (-0.5)
    for h in range(2):
        part = slice(h * HEAD, (h + 1) * HEAD)
        raw = q_raw[:, part]
        q = turned(raw, gains[0:1], cos[...], sin[...])
        p = soft(q, keys[...])
        dc = d_context[:, part]
        dp = lax.dot_general(dc, v, (((1,), (1,)), ((), ())), preferred_element_type=F32)
        v_sum[...] += lax.dot_general(
            p.astype(BF), dc, (((0,), (0,)), ((), ())), preferred_element_type=F32
        )
        ds = (p * (dp - jnp.sum(p * dp, axis=1, keepdims=True))).astype(BF)
        dq = lax.dot_general(
            ds, keys[...], (((1,), (0,)), ((), ())), preferred_element_type=F32
        )
        k_sum[...] += lax.dot_general(ds, q, (((0,), (0,)), ((), ())), preferred_element_type=F32)
        grad, gain_rows = back(raw, gains[0:1], dq * scale)
        d_q[:, part] = grad.astype(BF)
        d_gains[0:1, :] += jnp.sum(gain_rows, axis=0, keepdims=True)

    @pl.when(at == pl.num_programs(0) - 1)
    def _():
        grad, gain_rows = back(k_raw[...], gains[1:2], k_sum[...] * scale)
        d_k[...] = grad.astype(BF)
        d_v[...] = v_sum[...].astype(BF)
        d_gains[1:2, :] += jnp.sum(gain_rows, axis=0, keepdims=True)


def run_attend(qkv, gains, cos, sin, hq, hk):
    seq = qkv.shape[0]
    pairs = hq // hk // 2
    block = lambda width, index: pl.BlockSpec((seq, width * HEAD), index)
    whole = lambda rows: pl.BlockSpec((rows, HEAD), lambda i, j: (0, 0))
    return pl.pallas_call(
        attend_kernel,
        grid=(hk, pairs),
        in_specs=[
            block(2, lambda i, j: (0, i * pairs + j)),
            block(1, lambda i, j: (0, hq + i)),
            block(1, lambda i, j: (0, hq + hk + i)),
            whole(8),
            whole(seq),
            whole(seq),
        ],
        out_specs=block(2, lambda i, j: (0, i * pairs + j)),
        out_shape=jax.ShapeDtypeStruct((seq, hq * HEAD), BF),
        scratch_shapes=[pltpu.VMEM((seq, HEAD), BF)],
        name="attend",
    )(qkv, qkv, qkv, gains, cos, sin)


def run_attend_back(head, qkv, d_context, gains, cos, sin, hq, hk):
    seq = qkv.shape[0]
    pairs = hq // hk // 2
    block = lambda width, index: pl.BlockSpec((seq, width * HEAD), index)
    whole = lambda rows: pl.BlockSpec((rows, HEAD), lambda j: (0, 0))
    return pl.pallas_call(
        attend_back_kernel,
        grid=(pairs,),
        in_specs=[
            block(2, lambda j: (0, head * pairs + j)),
            block(1, lambda j: (0, hq + head)),
            block(1, lambda j: (0, hq + hk + head)),
            block(2, lambda j: (0, head * pairs + j)),
            whole(8),
            whole(seq),
            whole(seq),
        ],
        out_specs=[block(2, lambda j: (0, j)), whole(seq), whole(seq), whole(8)],
        out_shape=[
            jax.ShapeDtypeStruct((seq, 2 * pairs * HEAD), BF),
            jax.ShapeDtypeStruct((seq, HEAD), BF),
            jax.ShapeDtypeStruct((seq, HEAD), BF),
            jax.ShapeDtypeStruct((8, HEAD), F32),
        ],
        scratch_shapes=[
            pltpu.VMEM((seq, HEAD), BF),
            pltpu.VMEM((seq, HEAD), F32),
            pltpu.VMEM((seq, HEAD), F32),
        ],
        name="attend_back",
    )(qkv, qkv, qkv, d_context, gains, cos, sin)


def split2(v):
    high = v.astype(BF)
    return high, (v - high.astype(F32)).astype(BF)


def gather_dp(v):
    return lax.all_gather(v, "dp", axis=0, tiled=True)


def gather_all(v):
    return lax.all_gather(v, ("dp", "tensor"), axis=0, tiled=True)


def scatter_all(v):
    return lax.psum_scatter(v, ("dp", "tensor"), scatter_dimension=0, tiled=True)


def scatter_dp(v):
    return lax.psum_scatter(v, "dp", scatter_dimension=0, tiled=True)


def pieces(width, dp, seq):
    count = 1 if dp * seq <= 8192 else 4
    step = width // count // 128 * 128
    edges = [step * i for i in range(count)] + [width]
    return list(zip(edges[:-1], edges[1:]))


def after(v, earlier):
    return v if earlier is None else lax.optimization_barrier((v, earlier))[0]


def dispatch(pick, own, dp, seq, earlier):
    blocks = []
    for low, high in pieces(own.shape[1], dp, seq):
        every = gather_all(after(own[:, low:high], earlier)).reshape(dp, seq, high - low)
        block = jnp.einsum("gest,gtd->gesd", pick, every, preferred_element_type=F32).astype(BF)
        blocks.append(block)
        earlier = block if len(pieces(own.shape[1], dp, seq)) > 1 else None
    return jnp.concatenate(blocks, axis=3)


def combine(pick, rows, dp, seq, earlier):
    blocks = []
    for low, high in pieces(rows.shape[3], dp, seq):
        tok = jnp.einsum(
            "gest,gesd->gtd",
            pick,
            after(rows[:, :, :, low:high], earlier),
            preferred_element_type=F32,
        ).astype(BF)
        blocks.append(scatter_all(tok.reshape(dp * seq, high - low)))
        earlier = blocks[-1] if len(pieces(rows.shape[3], dp, seq)) > 1 else None
    return jnp.concatenate(blocks, axis=1).astype(F32)


GRID = [(z, x, c) for z in range(4) for x in range(2) for c in range(2)]
SPLIT = (0, 768, 1536, 1792, 2048)


def at(z, x, c):
    return z % 4 * 4 + x % 2 * 2 + c % 2


def shift_z(v, k):
    return lax.ppermute(v, "dp", [(at(z, x, c), at(z + k, x, c)) for z, x, c in GRID])


def swap_x(v):
    return lax.ppermute(v, "dp", [(at(z, x, c), at(z, x + 1, c)) for z, x, c in GRID])


def swap_c(v):
    return lax.ppermute(v, "dp", [(at(z, x, c), at(z, x, c + 1)) for z, x, c in GRID])


def swap_y(v):
    return lax.ppermute(v, "tensor", [(0, 1), (1, 0)])


def gather_y(v):
    other = swap_y(v)
    first = lax.axis_index("tensor") == 0
    return jnp.concatenate([jnp.where(first, v, other), jnp.where(first, other, v)])


def scatter_y(v):
    a, b = jnp.split(v, 2)
    first = lax.axis_index("tensor") == 0
    kept, sent = jnp.where(first, a, b), jnp.where(first, b, a)
    other = swap_y(sent.astype(BF))
    return kept.astype(F32) + other.astype(F32)


def add2(a, b):
    return (a.astype(F32) + b.astype(F32)).astype(BF)


def reduce_z(v, way, two=None):
    if two is None:
        two = first_hop(v, way)
    side = shift_z(v[3 if way > 0 else 1], way)
    relay = shift_z(add2(v[1 if way > 0 else 3], two), -way)
    return (v[0].astype(F32) + side.astype(F32) + relay.astype(F32)).astype(BF)


def first_hop(v, way):
    return shift_z(v[2], -way)


def tied(v, w):
    return lax.optimization_barrier((v, w))


def gather_a(v1, v2, v5, v6):
    x5, y6 = swap_x(v5), swap_y(v6)
    one1, three1 = shift_z(v1, 1), shift_z(v1, -1)
    one2, three2 = shift_z(v2, 1), shift_z(v2, -1)
    w5, w6 = jnp.stack([v5, x5]), jnp.stack([v6, y6])
    two1, two2 = shift_z(one1, 1), shift_z(three2, -1)
    y5, x6 = swap_y(w5), swap_x(w6)
    s1 = jnp.stack([v1, one1, two1, three1])
    s2 = jnp.stack([v2, one2, two2, three2])
    return lax.optimization_barrier((s1, s2, jnp.stack([w5, y5]), jnp.stack([w6, x6])))


def gather_c(s1, s2, w5, w6):
    s1x, s2y = swap_x(s1), swap_y(s2)
    five = (shift_z(w5, 1), shift_z(w5, -1))
    six = (shift_z(w6, 1), shift_z(w6, -1))
    return s1x, s2y, five, six


def gather_d(s1, s2, w5, w6, s1x, s2y, five, six):
    s1, s2 = jnp.stack([s1, s1x]), jnp.stack([s2, s2y])
    s1y, s2x = swap_y(s1), swap_x(s2)
    five2, six2 = shift_z(five[0], 1), shift_z(six[1], -1)
    o5 = jnp.stack([w5, five[0], five2, five[1]])
    o6 = jnp.stack([w6, six[0], six2, six[1]])
    return s1, s1y, s2, s2x, o5, o6


def split_columns(v):
    return [v[:, a:b] for a, b in zip(SPLIT[:-1], SPLIT[1:])]


def scatter_core(near, far):
    p5, p6, p1, p2 = [add2(near[i], swap_c(far[i])) for i in (2, 3, 0, 1)]
    return p1, p2, p5, p6


def step_x(v):
    other = swap_x(v[1])
    return add2(v[0], other)


def step_y(v):
    other = swap_y(v[1])
    return add2(v[0], other)


def scatter_rows_core(near, far):
    a = swap_c(far[0])
    b = swap_c(far[1])
    return add2(near[0], a), add2(near[1], b)


def scatter_rows(a, b):
    b = reduce_z(b, -1)
    a = step_x(a)
    b = step_x(b)
    return jnp.concatenate([reduce_z(a, 1), b], axis=1)


def sequence_at(dc, dz, dx):
    at = lax.axis_index("dp")
    return (at // 4 - dz) % 4 * 4 + (at // 2 % 2 + dx) % 2 * 2 + (at % 2 + dc) % 2


def nn(a, b):
    return lax.dot_general(a, b, (((1,), (0,)), ((), ())), preferred_element_type=F32)


def nt(a, b):
    return lax.dot_general(a, b, (((1,), (1,)), ((), ())), preferred_element_type=F32)


def pick_rows(rank, slots):
    at_slot = lax.broadcasted_iota(jnp.int32, (slots, rank.shape[1]), 0).astype(F32)
    return jnp.concatenate(
        [(rank[e : e + 1, :] == at_slot).astype(F32).astype(BF) for e in range(rank.shape[0])],
        axis=0,
    )


def pick_cols(rank, slots):
    at_slot = lax.broadcasted_iota(jnp.int32, (rank.shape[0], slots), 1).astype(F32)
    return jnp.concatenate(
        [(rank[:, e : e + 1] == at_slot).astype(F32).astype(BF) for e in range(rank.shape[1])],
        axis=1,
    )


def put_rows(rank, parts, rows):
    x1a, x1b, x2a, x2b, x5, x6 = parts
    slots = rows.shape[2] // 2
    n = x1a.shape[2]
    rest = []
    for dx, x2 in enumerate((x2a, x2b)):
        pick = pick_rows(rank[dx], slots)
        low, high = pick[:, :n], pick[:, n:]
        block1 = nn(low, x1a[dx, 0]) + nn(high, x1b[dx, 0])
        block2 = nn(low, x2[0, 0]) + nn(high, x2[1, 0])
        block5 = nn(low, x5[0, 0, dx]) + nn(high, x5[0, 1, dx])
        block6 = nn(low, x6[0, dx, 0]) + nn(high, x6[0, dx, 1])
        at = dx * slots
        for e in range(2):
            part = slice(e * slots, (e + 1) * slots)
            rows[e, 0, at : at + slots, 0:768] = block1[part].astype(BF)
            rows[e, 0, at : at + slots, 768:1536] = block2[part].astype(BF)
            rows[e, 0, at : at + slots, 1536:1792] = block5[part, :256].astype(BF)
            rows[e, 0, at : at + slots, 1792:2048] = block6[part].astype(BF)
            rest.append(block5[part, 256:])
    return rest


def cot_kernel(rank, x1a, x1b, x2a, x2b, x5, x6, down, cots, d_act):
    put_rows(rank, (x1a, x1b, x2a, x2b, x5, x6), cots)
    for e in range(2):
        d_act[e, 0] = nt(cots[e, 0], down[e])


def expert_kernel(
    rank, rank_t, cols, d_act, x1a, x1b, x2a, x2b, x5, x6, weights,
    rows, scaled, d_g, d_u, t1, t2, t5, t6, back,
):
    slots = rows.shape[2] // 2
    rest = put_rows(rank, (x1a, x1b, x2a, x2b, x5, x6), rows)
    gates = []
    for i, part in enumerate(rest):
        both = cols[i % 2, 0:1, :] + cols[i % 2, 1:2, :]
        gates.append(jnp.sum(part * both, axis=1, keepdims=True))
    extras = []
    for e in range(2):
        gate = jnp.concatenate([gates[e], gates[2 + e]], axis=0)
        g = nn(rows[e, 0], weights[e])
        g, u = jnp.split(g, 2, axis=1)
        da = d_act[e, 0]
        sig = 1.0 / (1.0 + jnp.exp(-g))
        silu = g * sig
        act = silu * u
        scaled[e, 0] = (act * gate).astype(BF)
        d_gate = jnp.sum(act * da, axis=1, keepdims=True)
        da = da * gate
        dg = (da * u * sig * (1.0 + g * (1.0 - sig))).astype(BF)
        du = (da * silu).astype(BF)
        d_g[e, 0] = dg
        d_u[e, 0] = du
        high = d_gate.astype(BF).astype(F32)
        extras.append(high * cols[e, 0:1, :] + (d_gate - high) * cols[e, 1:2, :])
        dr = nt(jnp.concatenate([dg, du], axis=1), weights[e]).astype(BF)
        for dx in range(2):
            back[dx, e * slots : (e + 1) * slots, :] = dr[dx * slots : (dx + 1) * slots]
    extra = [
        jnp.concatenate([extras[e][dx * slots : (dx + 1) * slots] for e in range(2)], axis=0)
        for dx in range(2)
    ]
    put_back(rank_t, back, t1, t2, t5, t6, slots, extra)


def put_back(rank_t, back, t1, t2, t5, t6, slots, extra=None):
    for dx in range(2):
        pick_t = pick_cols(rank_t[dx], slots)
        n = pick_t.shape[0] // 2
        p1, p2, p5, p6 = [
            nn(pick_t, back[dx, :, a:b]).astype(BF) for a, b in zip(SPLIT[:-1], SPLIT[1:])
        ]
        for dy in range(2):
            half = slice(dy * n, (dy + 1) * n)
            t1[dy, dx, 0] = p1[half]
            t2[dx, dy, 0] = p2[half]
            t5[0, dy, dx, :, 0:256] = p5[half]
            t6[0, dx, dy] = p6[half]
        if extra is not None:
            p7 = nn(pick_t, extra[dx].astype(BF)).astype(BF)
            for dy in range(2):
                t5[0, dy, dx, :, 256:] = p7[dy * n : (dy + 1) * n]


def out_kernel(rank_t, scaled, down, t1, t2, t5, t6, back):
    slots = scaled.shape[2] // 2
    for e in range(2):
        y = nn(scaled[e, 0], down[e]).astype(BF)
        for dx in range(2):
            back[dx, e * slots : (e + 1) * slots, :] = y[dx * slots : (dx + 1) * slots]
    put_back(rank_t, back, t1, t2, t5, t6, slots)


def grad_kernel(where, left, right, small, heads, a, b):
    both = lax.dot_general(
        left[...], right[...], (((0,), (0,)), ((), ())), preferred_element_type=F32
    ).astype(BF)
    width = a.shape[-1]
    a[0, 0] = both[:, :width]
    b[0, 0, :, : both.shape[1] - width] = both[:, width:]
    rest = jnp.zeros((small.shape[0] - heads.shape[0], small.shape[1]), F32)
    both_small = small[...] + jnp.concatenate([heads[...], rest], axis=0)
    b[0, 0, :, both.shape[1] - width :] = both_small.astype(BF)


def run_grad(where, left, right, small, heads):
    count, columns = right.shape
    rest = small.shape[1]
    width = columns * 9 // 16 // 128 * 128
    shard = left.shape[1] // 16
    return pl.pallas_call(
        grad_kernel,
        grid_spec=pltpu.PrefetchScalarGridSpec(
            num_scalar_prefetch=1,
            grid=(2, 4),
            in_specs=[
                pl.BlockSpec((count, shard), lambda dx, dz, w: (0, w[2 * dz + dx])),
                pl.BlockSpec((count, columns), lambda dx, dz, w: (0, 0)),
                pl.BlockSpec((shard, rest), lambda dx, dz, w: (w[2 * dz + dx], 0)),
                pl.BlockSpec((HEAD // 16, rest), lambda dx, dz, w: (w[2 * dz + dx], 0)),
            ],
            out_specs=[
                pl.BlockSpec((1, 1, shard, width), lambda dx, dz, w: (dx, dz, 0, 0)),
                pl.BlockSpec((1, 1, shard, columns - width + rest), lambda dx, dz, w: (dz, dx, 0, 0)),
            ],
        ),
        out_shape=[
            shaped((2, 4, shard, width), BF),
            shaped((4, 2, shard, columns - width + rest), BF),
        ],
        compiler_params=LIMIT,
        name="grad",
    )(where, left, right, small, heads)


def pair(*tail):
    return pl.BlockSpec((2, *tail), lambda i, *_: (i,) + (0,) * len(tail))


def z_last(*lead):
    def spec(rows, columns):
        return pl.BlockSpec(
            (*lead, 1, rows, columns), lambda i, *_: (0,) * len(lead) + (i, 0, 0)
        )

    return spec


def z_first(rows, columns):
    return pl.BlockSpec((1, 2, 2, rows, columns), lambda i, *_: (i, 0, 0, 0, 0))


def block_specs(n, extra):
    return [z_last(2, 2)(n, 768), z_last(2, 2)(n, 768), z_first(n, 256 + extra), z_first(n, 256)]


def block_shapes(n, extra):
    shapes = [(2, 2, 4, n, 768), (2, 2, 4, n, 768), (4, 2, 2, n, 256 + extra), (4, 2, 2, n, 256)]
    return [shaped(v, BF) for v in shapes]


def by_expert(*tail):
    return pl.BlockSpec((2, 1, *tail), lambda i, *_: (0, i) + (0,) * len(tail))


def fixed(*shape):
    return pl.BlockSpec(
        shape, lambda i, *_: (0,) * len(shape), pipeline_mode=pl.Buffered(1)
    )


def shaped(shape, kind):
    return jax.ShapeDtypeStruct(shape, kind)


LIMIT = pltpu.CompilerParams(vmem_limit_bytes=58 * 1024 * 1024)


def part_specs(n, extra):
    return [z_last(2)(n, 768)] * 4 + [z_first(n, 256 + extra), z_first(n, 256)]


def run_cots(rank, parts, down, slots):
    n = parts[0].shape[2]
    ff, width = down.shape[1:]
    return pl.pallas_call(
        cot_kernel,
        grid=(4,),
        in_specs=[pair(2, 2 * n), *part_specs(n, 0), fixed(2, ff, width)],
        out_specs=[by_expert(2 * slots, width), by_expert(2 * slots, ff)],
        out_shape=[shaped((2, 4, 2 * slots, width), BF), shaped((2, 4, 2 * slots, ff), F32)],
        compiler_params=LIMIT,
        name="cots",
    )(rank, *parts, down)


def run_experts(rank, rank_t, cols, d_act, parts, weights, slots):
    s1, s1y, s2, s2x, o5, o6 = parts
    n = s1.shape[2]
    seq, width, ff = 2 * n, weights.shape[1], weights.shape[2] // 2
    return pl.pallas_call(
        expert_kernel,
        grid=(4,),
        in_specs=[
            pair(2, seq),
            pair(seq, 2),
            fixed(*cols.shape),
            by_expert(2 * slots, ff),
            *part_specs(n, 128),
            fixed(2, width, 2 * ff),
        ],
        out_specs=[
            by_expert(2 * slots, width),
            by_expert(2 * slots, ff),
            by_expert(2 * slots, ff),
            by_expert(2 * slots, ff),
        ]
        + block_specs(n, 128),
        out_shape=[
            shaped((2, 4, 2 * slots, width), BF),
            shaped((2, 4, 2 * slots, ff), BF),
            shaped((2, 4, 2 * slots, ff), BF),
            shaped((2, 4, 2 * slots, ff), BF),
        ]
        + block_shapes(n, 128),
        scratch_shapes=[pltpu.VMEM((2, 2 * slots, width), BF)],
        compiler_params=LIMIT,
        name="experts",
    )(
        rank, rank_t, cols, d_act, s1, s1y, s2, s2x, o5, o6, weights,
    )


def run_outs(rank_t, scaled, down, slots):
    seq, ff, width = rank_t.shape[1], down.shape[1], down.shape[2]
    return pl.pallas_call(
        out_kernel,
        grid=(4,),
        in_specs=[pair(seq, 2), by_expert(2 * slots, ff), fixed(2, ff, width)],
        out_specs=block_specs(seq // 2, 0),
        out_shape=block_shapes(seq // 2, 0),
        scratch_shapes=[pltpu.VMEM((2, 2 * slots, width), BF)],
        compiler_params=LIMIT,
        name="outs",
    )(rank_t, scaled, down)


def flip(v, axis, y):
    a, b = jnp.split(v, 2, axis=axis)
    return jnp.where(y == 0, v, jnp.concatenate([b, a], axis=axis))


def slot_plan(ids_all, experts):
    y = lax.axis_index("tensor")
    seq = ids_all.shape[1]
    mine = lax.axis_index("dp") * 2 + jnp.arange(2, dtype=jnp.int32)
    mask = jnp.any(ids_all[:, None, :, :] == mine[None, :, None, None], axis=3)
    before = (jnp.arange(seq)[:, None] < jnp.arange(seq)[None, :]).astype(BF)
    rank = jnp.einsum("gea,ab->geb", mask.astype(BF), before, preferred_element_type=F32)
    rank = jnp.where(mask, rank, -1.0)
    d = jnp.arange(16)
    where = sequence_at(d // 8, d // 2 % 4, d % 2)
    rank_rel = flip(jnp.take(rank, where, axis=0), 2, y)
    rank_t = jnp.swapaxes(rank_rel, 1, 2)
    column = jnp.arange(128)
    cols = (
        column[None, None, :] == (mine[:, None] + jnp.array([[0, experts]]))[:, :, None]
    ).astype(F32)
    halves = lambda v: (v[:8], v[8:])
    return halves(where.astype(jnp.int32)), halves(rank_rel), halves(rank_t), cols


def moe_small(plan, cot_parts, ffn_in, gate_x, weights, down_weight, slots):
    def cot_rows(k):
        return run_cots(plan[1][k], cot_parts[k], down_weight, slots)

    v1, v2, v5, v6 = split_columns(ffn_in)
    state = gather_a(v1, v2, jnp.concatenate([v5, gate_x], axis=1), v6)
    state, plan = tied(state, plan)
    further = gather_c(*state)
    further, far = tied(further, cot_rows(1))
    s1, s1y, s2, s2x, o5, o6 = gather_d(*state, *further)
    o5, o6, plan = lax.optimization_barrier((o5, o6, plan))
    (s1y, s2x), near = tied((s1y, s2x), cot_rows(0))
    first = (s1, s1y, s2, s2x, o5, o6)
    parts = (first, tuple(swap_c(v) for v in first))
    cots, d_act = zip(near, far)
    rank_rel, rank_t, cols = plan[1:]
    far, near = [
        run_experts(rank_rel[k], rank_t[k], cols, d_act[k], parts[k], weights, slots)
        for k in (1, 0)
    ]
    p1, p2, p5, p6 = scatter_core(near[4:], far[4:])
    kept = lambda i: (near[i], far[i])
    total = lambda spec, a, b: jnp.einsum(spec, a[0], b[0], preferred_element_type=F32) + jnp.einsum(
        spec, a[1], b[1], preferred_element_type=F32
    )
    p5 = reduce_z(p5, 1)
    p6 = reduce_z(p6, -1)
    p1 = step_y(p1)
    p2 = step_x(p2)
    down_grad = total("egsf,egsd->efd", kept(1), cots)
    outs = []
    for k in (0, 1):
        outs.append(run_outs(rank_t[k], kept(1)[k], down_weight, slots))
    (p1, p2, p5, p6), (outs, down_grad) = tied((p1, p2, p5, p6), (outs, down_grad))
    p5 = step_y(p5)
    p6 = step_x(p6)
    p1 = step_x(p1)
    p2 = step_y(p2)
    up_grad = total("egsd,egsf->edf", kept(0), kept(3))
    (p1, p2, p5, p6), up_grad = tied((p1, p2, p5, p6), up_grad)
    d5 = step_x(p5)
    d6 = step_y(p6)
    d1 = reduce_z(p1, 1)
    d2 = reduce_z(p2, -1)
    p1, p2, p5, p6 = scatter_core(*outs)
    p2, (d5, d6) = tied(p2, (d5, d6))
    p2 = step_x(p2)
    d_sum = jnp.concatenate([d1, d2, d5[:, :256], d6, d5[:, 256:]], axis=1)
    d_sum, (p1, p5, p6) = tied(d_sum, (p1, p5, p6))
    d_sum = d_sum.astype(F32)

    def gate_later(aside):
        (rows, grads), aside = tied((kept(0), kept(2)), aside)
        return total("egsd,egsf->edf", rows, grads), aside

    return d_sum, (p1, p2, p5, p6), gate_later, up_grad, down_grad


def moe_large(
    ids_all, cotangent, ffn_in, gate_x, gate_weight, up_weight, down_weight, experts, slots
):
    dp, seq = ids_all.shape[:2]
    local = gate_weight.shape[0]
    dp_at = lax.axis_index("dp")
    mine = dp_at * local + jnp.arange(local, dtype=jnp.int32)
    mask = jnp.any(ids_all[:, :, None, :] == mine[None, None, :, None], axis=3).astype(BF)
    gate_all = gather_all(gate_x).reshape(dp, seq, -1)
    before = (jnp.arange(seq)[:, None] > jnp.arange(seq)[None, :]).astype(BF)
    rank = jnp.einsum("ab,gbe->gea", before, mask, preferred_element_type=F32)
    rank = jnp.where(jnp.swapaxes(mask, 1, 2) > 0, rank, -1.0)
    pick = (rank[:, :, None, :] == jnp.arange(slots, dtype=F32)[None, None, :, None]).astype(BF)

    cots = dispatch(pick, cotangent, dp, seq, None)
    rows = dispatch(pick, ffn_in, dp, seq, cots)
    gate_tok = lax.dynamic_slice_in_dim(gate_all, dp_at * local, local, 2).astype(
        F32
    ) + lax.dynamic_slice_in_dim(gate_all, experts + dp_at * local, local, 2).astype(F32)
    gate_slot = jnp.sum(pick.astype(F32) * jnp.swapaxes(gate_tok, 1, 2)[:, :, None, :], axis=3)

    g_proj = jnp.einsum("gesd,edf->gesf", rows, gate_weight, preferred_element_type=F32)
    u_proj = jnp.einsum("gesd,edf->gesf", rows, up_weight, preferred_element_type=F32)
    d_act = jnp.einsum("gesd,efd->gesf", cots, down_weight, preferred_element_type=F32)
    sig = 1.0 / (1.0 + jnp.exp(-g_proj))
    silu = g_proj * sig
    act = silu * u_proj
    scaled = (act * gate_slot[..., None]).astype(BF)
    d_gate_slot = jnp.sum(act * d_act, axis=3)
    d_act = d_act * gate_slot[..., None]
    d_g = (d_act * u_proj * sig * (1.0 + g_proj * (1.0 - sig))).astype(BF)
    d_u = (d_act * silu).astype(BF)
    d_rows = (
        jnp.einsum("gesf,edf->gesd", d_g, gate_weight, preferred_element_type=F32)
        + jnp.einsum("gesf,edf->gesd", d_u, up_weight, preferred_element_type=F32)
    ).astype(BF)
    dg_high, dg_low = split2(d_gate_slot)
    column = jnp.arange(lanes(2 * experts))
    high_col = (column[None, :] == mine[:, None])[None, :, None, :]
    low_col = (column[None, :] == experts + mine[:, None])[None, :, None, :]
    extra = jnp.where(high_col, dg_high[..., None], jnp.where(low_col, dg_low[..., None], 0.0))
    d_rows = jnp.concatenate([d_rows, extra.astype(BF)], axis=3)
    d_sum = combine(pick, d_rows, dp, seq, None)

    y_rows = jnp.einsum("gesf,efd->gesd", scaled, down_weight, preferred_element_type=F32)
    y_sum = combine(pick, y_rows.astype(BF), dp, seq, d_sum)
    down_grad = jnp.einsum("gesf,gesd->efd", scaled, cots, preferred_element_type=F32)
    gate_grad = jnp.einsum("gesd,gesf->edf", rows, d_g, preferred_element_type=F32)
    up_grad = jnp.einsum("gesd,gesf->edf", rows, d_u, preferred_element_type=F32)

    return d_sum, y_sum, gate_grad, up_grad, down_grad


def pad_to(v, width):
    return jnp.pad(v, ((0, 0), (0, width - v.shape[1])))


def lanes(count):
    return -(-count // 128) * 128


def on_device(
    tokens,
    attn_gain,
    q_weight,
    key_matrix,
    value_matrix,
    o_weight,
    query_norm_gain,
    k_gain,
    ffn_gain,
    router_weight,
    gate_weight,
    up_weight,
    down_weight,
    expert_ids,
    cotangent,
):
    dp = lax.axis_size("dp")
    tensor = lax.axis_size("tensor")
    own, width = tokens.shape
    seq = expert_ids.shape[0]
    begin = lax.axis_index("tensor") * own
    local = gate_weight.shape[0]
    experts = local * dp
    slots = 10 * seq * expert_ids.shape[1] // (8 * experts)
    slots = -(-slots // 16) * 16
    shard = q_weight.shape[0]
    gshard = query_norm_gain.shape[0]
    hq = q_weight.shape[1] // HEAD
    hk = key_matrix.shape[1] // HEAD
    qkv_width = (hq + 2 * hk) * HEAD
    top = expert_ids.shape[1]
    fast = (dp, tensor, local, seq, width) == (16, 2, 2, 384, 2048)

    arange_e = jnp.arange(experts, dtype=jnp.int32)
    own_ids = lax.dynamic_slice_in_dim(expert_ids, begin, own, 0)
    own_mask = jnp.any(own_ids[:, :, None] == arange_e[None, None, :], axis=1)

    gain_rows = jnp.stack(
        [
            attn_gain,
            ffn_gain,
            jnp.pad(query_norm_gain, (0, shard - gshard)),
            jnp.pad(k_gain, (0, shard - gshard)),
        ],
        axis=1,
    )
    ids_rows = expert_ids.reshape(shard, -1).astype(BF)
    small = jnp.concatenate([router_weight, gain_rows, ids_rows], axis=1)
    small = pad_to(small, lanes(small.shape[1]))
    small_end = qkv_width + small.shape[1]
    all_in = gather_dp(
        jnp.concatenate([q_weight, key_matrix, value_matrix, small, o_weight.T], axis=1)
    )
    layer_in = gather_y(tokens)
    if fast:
        weights = jnp.concatenate([gate_weight, up_weight], axis=2)
        layer_in, weights = tied(layer_in, weights)
    o_t = all_in[:, small_end:]
    if fast:
        cot_own, all_in = tied(cotangent, all_in)
        cot_state = gather_a(*split_columns(cot_own))

    w_qkv = all_in[:, :qkv_width]
    router = all_in[:, qkv_width : qkv_width + experts]
    gains = all_in[:, qkv_width + experts : qkv_width + experts + 4].astype(F32)
    ids_all = all_in[:, qkv_width + experts + 4 :][:, : seq * top // shard]
    ids_all = ids_all.astype(jnp.int32).reshape(dp, seq, top)
    attn_gain32 = gains[:, 0]
    ffn_gain32 = gains[:, 1]
    q_gain32 = gains[:, 2].reshape(dp, shard)[:, :gshard].reshape(-1)
    k_gain32 = gains[:, 3].reshape(dp, shard)[:, :gshard].reshape(-1)

    residual = layer_in.astype(F32)
    normed = rms(residual, attn_gain32).astype(BF)
    qkv = dot(normed, w_qkv, 1, 0)
    cos, sin = rope_tables(seq)
    head_gains = jnp.pad(jnp.stack([q_gain32, k_gain32]), ((0, 6), (0, 0)))
    context = run_attend(qkv, head_gains, cos, sin, hq, hk)
    attn_part = dot(context, o_t, 1, 1)
    if fast:
        attn_part, ids_all = tied(attn_part, ids_all)
        plan = slot_plan(ids_all, experts)
        cot_parts = gather_d(*cot_state, *gather_c(*cot_state))
        cot_parts = (cot_parts, tuple(swap_c(v) for v in cot_parts))
    hidden = tokens.astype(F32) + scatter_y(attn_part)

    ffn_in = rms(hidden, ffn_gain32).astype(BF)
    logits = dot(ffn_in, router, 1, 0)
    chosen = jnp.where(own_mask, jnp.exp(logits), 0.0)
    gates = chosen / jnp.sum(chosen, axis=1, keepdims=True)
    gate_high, gate_low = split2(gates)
    gate_x = pad_to(jnp.concatenate([gate_high, gate_low], axis=1), lanes(2 * experts))
    args = (gate_weight, up_weight, down_weight)
    if fast:
        d_sum, y_sum, gate_later, up_grad, down_grad = moe_small(
            plan, cot_parts, ffn_in, gate_x, weights, down_weight, slots
        )
    else:
        d_sum, y_sum, gate_grad, up_grad, down_grad = moe_large(
            ids_all, cotangent, ffn_in, gate_x, *args, experts, slots
        )
    d_gates = d_sum[:, width : width + experts] + d_sum[:, width + experts : width + 2 * experts]
    d_logits = gates * (d_gates - jnp.sum(gates * d_gates, axis=1, keepdims=True))
    d_high, d_low = split2(d_logits)
    d_ffn = d_sum[:, :width] + dot(d_high, router, 1, 1) + dot(d_low, router, 1, 1)
    router_part = dot(ffn_in, d_high, 0, 0) + dot(ffn_in, d_low, 0, 0)
    d_hidden, ffn_gain_rows = rms_back(hidden, ffn_gain32, d_ffn)
    ffn_gain_part = jnp.sum(ffn_gain_rows, axis=0)
    d_hidden = d_hidden + cotangent.astype(F32)
    d_attn = gather_y(d_hidden.astype(BF))

    o_part = dot(d_attn, context, 0, 0).astype(BF)
    d_attn, o_part = tied(d_attn, o_part)
    o_sum = scatter_dp(o_part).astype(F32)
    if fast:
        p1, p2, p5, p6 = y_sum
        d_attn, p1 = tied(d_attn, p1)
        p1 = step_y(p1)
        two5, two6 = first_hop(p5, 1), first_hop(p6, -1)
        gate_grad, d_attn = gate_later(d_attn)
    d_context = dot(d_attn, o_t, 1, 0).astype(BF)
    heads = []
    for head in range(hk):
        heads.append(run_attend_back(head, qkv, d_context, head_gains, cos, sin, hq, hk))
        if fast and head == 0:
            aside = (p1, p2, two5, two6, gate_grad)
            d_context, heads, aside = lax.optimization_barrier((d_context, heads, aside))
            p1, p2, two5, two6, gate_grad = aside
            p1 = step_x(p1)
            p2 = step_y(p2)
            p5 = reduce_z(p5, 1, two5)
            p6 = reduce_z(p6, -1, two6)
    d_qkv = jnp.concatenate([h[k] for k in range(3) for h in heads], axis=1)
    small_part = jnp.concatenate([router_part, ffn_gain_part[:, None]], axis=1)
    small_part = pad_to(small_part, lanes(experts + 3))
    column = jnp.arange(small_part.shape[1])[None, :]
    head_part = sum(h[3][0] for h in heads)[:, None] * (column == experts + 1).astype(F32)
    head_part += sum(h[3][1] for h in heads)[:, None] * (column == experts + 2).astype(F32)
    if fast:
        d_qkv, (p1, p2, p5, p6) = tied(d_qkv, (p1, p2, p5, p6))
        y_sum = (reduce_z(p1, 1), reduce_z(p2, -1), step_x(step_y(p5)), step_y(step_x(p6)))
        far = run_grad(plan[0][1], normed, d_qkv, small_part, head_part)
        near = run_grad(plan[0][0], normed, d_qkv, small_part, head_part)
        a, b = scatter_rows_core(near, far)
        qkv_sum = scatter_rows(a, b).astype(F32)
        qkv_sum, small_sum = qkv_sum[:, :qkv_width], qkv_sum[:, qkv_width:]
        y_sum = jnp.concatenate(y_sum, axis=1).astype(F32)
    else:
        qkv_sum = scatter_dp(dot(normed, d_qkv, 0, 0).astype(BF)).astype(F32)
        head_part = jnp.pad(
            head_part.reshape(dp, gshard, -1), ((0, 0), (0, shard - gshard), (0, 0))
        )
        small_sum = scatter_dp(small_part + head_part.reshape(small_part.shape))
    output = (hidden + y_sum).astype(BF)
    d_normed = dot(d_qkv, w_qkv, 1, 1)
    d_normed = scatter_y(d_normed)
    d_tokens, _ = rms_back(tokens.astype(F32), attn_gain32, d_normed)
    tokens_grad = d_tokens + d_hidden

    weights = jnp.concatenate([q_weight, key_matrix, value_matrix], axis=1).astype(F32)
    gain_part = jnp.sum(weights * qkv_sum, axis=1) / attn_gain.astype(F32)
    small_sum = jnp.concatenate([small_sum, gain_part[:, None]], axis=1)
    small_sum = small_sum + swap_y(small_sum)
    return (
        output,
        tokens_grad,
        small_sum[:, -1],
        qkv_sum[:, : hq * HEAD],
        qkv_sum[:, hq * HEAD : (hq + hk) * HEAD],
        qkv_sum[:, (hq + hk) * HEAD :],
        o_sum.T,
        small_sum[:gshard, experts + 1],
        small_sum[:gshard, experts + 2],
        small_sum[:, experts],
        small_sum[:, :experts],
        gate_grad,
        up_grad,
        down_grad,
    )


def solution(mesh):
    rows = P(("dp", "tensor"), None)
    both = P("dp", "tensor")
    return jax.shard_map(
        on_device,
        mesh=mesh,
        in_specs=(
            rows,
            P("dp"),
            both,
            both,
            both,
            P("tensor", "dp"),
            P("dp"),
            P("dp"),
            P("dp"),
            P("dp", None),
            P("dp", None, "tensor"),
            P("dp", None, "tensor"),
            P("dp", "tensor", None),
            P("dp", None),
            rows,
        ),
        out_specs=(
            rows,
            rows,
            P("dp"),
            both,
            both,
            both,
            P("tensor", "dp"),
            P("dp"),
            P("dp"),
            P("dp"),
            P("dp", None),
            P("dp", None, "tensor"),
            P("dp", None, "tensor"),
            P("dp", "tensor", None),
        ),
        check_vma=False,
    )
```

```python
import jax
import jax.numpy as jnp
from jax import lax
from jax.experimental import pallas as pl
from jax.experimental.pallas import tpu as pltpu
from jax.sharding import PartitionSpec as P


HEAD = 128
EPS = 1e-06
THETA = 1000000.0
BF = jnp.bfloat16
F32 = jnp.float32


def dot(a, b, ca, cb):
    return lax.dot_general(a, b, (((ca,), (cb,)), ((), ())), preferred_element_type=F32)


def rms(v, gain):
    return v * lax.rsqrt(jnp.mean(v * v, axis=-1, keepdims=True) + EPS) * gain


def rms_back(v, gain, u):
    inv = lax.rsqrt(jnp.mean(v * v, axis=-1, keepdims=True) + EPS)
    ug = u * gain
    grad = ug * inv - v * (jnp.mean(ug * v, axis=-1, keepdims=True) * inv * inv * inv)
    return grad, u * v * inv


def rope_tables(count):
    inverse = THETA ** (-(jnp.arange(HEAD // 2, dtype=F32) * 2.0 / HEAD))
    angles = jnp.arange(count, dtype=F32)[:, None] * inverse[None, :]
    cos, sin = jnp.cos(angles), jnp.sin(angles)
    return jnp.concatenate([cos, cos], axis=1), jnp.concatenate([-sin, sin], axis=1)


def half_turn(v):
    return pltpu.roll(v, HEAD // 2, 1)


def turned(raw, gain, cos, sin):
    v = rms(raw, gain)
    return (v * cos + half_turn(v) * sin).astype(BF)


def soft(q, k):
    scores = lax.dot_general(q, k, (((1,), (1,)), ((), ())), preferred_element_type=F32)
    scores = scores * HEAD ** (-0.5)
    row = lax.broadcasted_iota(jnp.int32, scores.shape, 0)
    column = lax.broadcasted_iota(jnp.int32, scores.shape, 1)
    e = jnp.where(row >= column, jnp.exp(scores), 0.0)
    return e * (1.0 / jnp.sum(e, axis=1, keepdims=True))


def attend_kernel(q_raw, k_raw, v_raw, gains, cos, sin, context, keys):
    @pl.when(pl.program_id(1) == 0)
    def _():
        keys[...] = turned(k_raw[...], gains[1:2], cos[...], sin[...])

    v = v_raw[...].astype(BF)
    for h in range(2):
        part = slice(h * HEAD, (h + 1) * HEAD)
        q = turned(q_raw[:, part], gains[0:1], cos[...], sin[...])
        p = soft(q, keys[...]).astype(BF)
        context[:, part] = lax.dot_general(
            p, v, (((1,), (0,)), ((), ())), preferred_element_type=F32
        ).astype(BF)


def attend_back_kernel(
    q_raw, k_raw, v_raw, d_context, gains, cos, sin, d_q, d_k, d_v, d_gains, keys, k_sum, v_sum
):
    at = pl.program_id(0)

    @pl.when(at == 0)
    def _():
        keys[...] = turned(k_raw[...], gains[1:2], cos[...], sin[...])
        k_sum[...] = jnp.zeros_like(k_sum)
        v_sum[...] = jnp.zeros_like(v_sum)
        d_gains[...] = jnp.zeros_like(d_gains)

    def back(raw, gain, u):
        return rms_back(raw, gain, u * cos[...] - half_turn(u) * sin[...])

    v = v_raw[...].astype(BF)
    scale = HEAD ** (-0.5)
    for h in range(2):
        part = slice(h * HEAD, (h + 1) * HEAD)
        raw = q_raw[:, part]
        q = turned(raw, gains[0:1], cos[...], sin[...])
        p = soft(q, keys[...])
        dc = d_context[:, part]
        dp = lax.dot_general(dc, v, (((1,), (1,)), ((), ())), preferred_element_type=F32)
        v_sum[...] += lax.dot_general(
            p.astype(BF), dc, (((0,), (0,)), ((), ())), preferred_element_type=F32
        )
        ds = (p * (dp - jnp.sum(p * dp, axis=1, keepdims=True))).astype(BF)
        dq = lax.dot_general(
            ds, keys[...], (((1,), (0,)), ((), ())), preferred_element_type=F32
        )
        k_sum[...] += lax.dot_general(ds, q, (((0,), (0,)), ((), ())), preferred_element_type=F32)
        grad, gain_rows = back(raw, gains[0:1], dq * scale)
        d_q[:, part] = grad.astype(BF)
        d_gains[0:1, :] += jnp.sum(gain_rows, axis=0, keepdims=True)

    @pl.when(at == pl.num_programs(0) - 1)
    def _():
        grad, gain_rows = back(k_raw[...], gains[1:2], k_sum[...] * scale)
        d_k[...] = grad.astype(BF)
        d_v[...] = v_sum[...].astype(BF)
        d_gains[1:2, :] += jnp.sum(gain_rows, axis=0, keepdims=True)


def run_attend(qkv, gains, cos, sin, hq, hk):
    seq = qkv.shape[0]
    pairs = hq // hk // 2
    block = lambda width, index: pl.BlockSpec((seq, width * HEAD), index)
    whole = lambda rows: pl.BlockSpec((rows, HEAD), lambda i, j: (0, 0))
    return pl.pallas_call(
        attend_kernel,
        grid=(hk, pairs),
        in_specs=[
            block(2, lambda i, j: (0, i * pairs + j)),
            block(1, lambda i, j: (0, hq + i)),
            block(1, lambda i, j: (0, hq + hk + i)),
            whole(8),
            whole(seq),
            whole(seq),
        ],
        out_specs=block(2, lambda i, j: (0, i * pairs + j)),
        out_shape=jax.ShapeDtypeStruct((seq, hq * HEAD), BF),
        scratch_shapes=[pltpu.VMEM((seq, HEAD), BF)],
        name="attend",
    )(qkv, qkv, qkv, gains, cos, sin)


def run_attend_back(head, qkv, d_context, gains, cos, sin, hq, hk):
    seq = qkv.shape[0]
    pairs = hq // hk // 2
    block = lambda width, index: pl.BlockSpec((seq, width * HEAD), index)
    whole = lambda rows: pl.BlockSpec((rows, HEAD), lambda j: (0, 0))
    return pl.pallas_call(
        attend_back_kernel,
        grid=(pairs,),
        in_specs=[
            block(2, lambda j: (0, head * pairs + j)),
            block(1, lambda j: (0, hq + head)),
            block(1, lambda j: (0, hq + hk + head)),
            block(2, lambda j: (0, head * pairs + j)),
            whole(8),
            whole(seq),
            whole(seq),
        ],
        out_specs=[block(2, lambda j: (0, j)), whole(seq), whole(seq), whole(8)],
        out_shape=[
            jax.ShapeDtypeStruct((seq, 2 * pairs * HEAD), BF),
            jax.ShapeDtypeStruct((seq, HEAD), BF),
            jax.ShapeDtypeStruct((seq, HEAD), BF),
            jax.ShapeDtypeStruct((8, HEAD), F32),
        ],
        scratch_shapes=[
            pltpu.VMEM((seq, HEAD), BF),
            pltpu.VMEM((seq, HEAD), F32),
            pltpu.VMEM((seq, HEAD), F32),
        ],
        name="attend_back",
    )(qkv, qkv, qkv, d_context, gains, cos, sin)


def split2(v):
    high = v.astype(BF)
    return high, (v - high.astype(F32)).astype(BF)


def gather_dp(v):
    return lax.all_gather(v, "dp", axis=0, tiled=True)


def gather_all(v):
    return lax.all_gather(v, ("dp", "tensor"), axis=0, tiled=True)


def scatter_all(v):
    return lax.psum_scatter(v, ("dp", "tensor"), scatter_dimension=0, tiled=True)


def scatter_dp(v):
    return lax.psum_scatter(v, "dp", scatter_dimension=0, tiled=True)


def pieces(width, dp, seq):
    count = 1 if dp * seq <= 8192 else 4
    step = width // count // 128 * 128
    edges = [step * i for i in range(count)] + [width]
    return list(zip(edges[:-1], edges[1:]))


def after(v, earlier):
    return v if earlier is None else lax.optimization_barrier((v, earlier))[0]


def dispatch(pick, own, dp, seq, earlier):
    blocks = []
    for low, high in pieces(own.shape[1], dp, seq):
        every = gather_all(after(own[:, low:high], earlier)).reshape(dp, seq, high - low)
        block = jnp.einsum("gest,gtd->gesd", pick, every, preferred_element_type=F32).astype(BF)
        blocks.append(block)
        earlier = block if len(pieces(own.shape[1], dp, seq)) > 1 else None
    return jnp.concatenate(blocks, axis=3)


def combine(pick, rows, dp, seq, earlier):
    blocks = []
    for low, high in pieces(rows.shape[3], dp, seq):
        tok = jnp.einsum(
            "gest,gesd->gtd",
            pick,
            after(rows[:, :, :, low:high], earlier),
            preferred_element_type=F32,
        ).astype(BF)
        blocks.append(scatter_all(tok.reshape(dp * seq, high - low)))
        earlier = blocks[-1] if len(pieces(rows.shape[3], dp, seq)) > 1 else None
    return jnp.concatenate(blocks, axis=1).astype(F32)


GRID = [(z, x, c) for z in range(4) for x in range(2) for c in range(2)]
SPLIT = (0, 768, 1536, 1792, 2048)


def at(z, x, c):
    return z % 4 * 4 + x % 2 * 2 + c % 2


def shift_z(v, k):
    return lax.ppermute(v, "dp", [(at(z, x, c), at(z + k, x, c)) for z, x, c in GRID])


def swap_x(v):
    return lax.ppermute(v, "dp", [(at(z, x, c), at(z, x + 1, c)) for z, x, c in GRID])


def swap_c(v):
    return lax.ppermute(v, "dp", [(at(z, x, c), at(z, x, c + 1)) for z, x, c in GRID])


def swap_y(v):
    return lax.ppermute(v, "tensor", [(0, 1), (1, 0)])


def gather_y(v):
    other = swap_y(v)
    first = lax.axis_index("tensor") == 0
    return jnp.concatenate([jnp.where(first, v, other), jnp.where(first, other, v)])


def scatter_y(v):
    a, b = jnp.split(v, 2)
    first = lax.axis_index("tensor") == 0
    kept, sent = jnp.where(first, a, b), jnp.where(first, b, a)
    other = swap_y(sent.astype(BF))
    return kept.astype(F32) + other.astype(F32)


def gather_z(v, way):
    one, three = shift_z(v, 1), shift_z(v, -1)
    two = shift_z(one, 1) if way > 0 else shift_z(three, -1)
    return jnp.stack([v, one, two, three])


def add2(a, b):
    return (a.astype(F32) + b.astype(F32)).astype(BF)


def reduce_z(v, way, two=None):
    if two is None:
        two = first_hop(v, way)
    side = shift_z(v[3 if way > 0 else 1], way)
    relay = shift_z(add2(v[1 if way > 0 else 3], two), -way)
    return (v[0].astype(F32) + side.astype(F32) + relay.astype(F32)).astype(BF)


def first_hop(v, way):
    return shift_z(v[2], -way)


def tied(v, w):
    return lax.optimization_barrier((v, w))


def gather_rel(v1, v2, v5, v6, plan, aside):
    w5 = jnp.stack([v5, swap_x(v5)])
    w6 = jnp.stack([v6, swap_y(v6)])
    s1 = gather_z(v1, 1)
    s2 = gather_z(v2, -1)
    w5 = jnp.stack([w5, swap_y(w5)])
    w6 = jnp.stack([w6, swap_x(w6)])
    s1, s2, w5, w6, plan = lax.optimization_barrier((s1, s2, w5, w6, plan))
    five = [shift_z(w5, 1), shift_z(w5, -1)]
    six = [shift_z(w6, 1), shift_z(w6, -1)]
    s1x, s2y = swap_x(s1), swap_y(s2)
    s1 = jnp.stack([s1, s1x])
    s2 = jnp.stack([s2, s2y])
    s1y, s2x = swap_y(s1), swap_x(s2)
    five.append(shift_z(five[0], 1))
    six.append(shift_z(six[1], -1))
    o5 = jnp.stack([w5, five[0], five[2], five[1]])
    o6 = jnp.stack([w6, six[0], six[2], six[1]])
    far = aside(1, plan)
    near = aside(0, plan)
    (s1y, s2x), (near, far) = tied((s1y, s2x), (near, far))
    first = (s1, s1y, s2, s2x, o5, o6)
    return first, tuple(swap_c(v) for v in first), plan, (near, far)


def scatter_core(near, far):
    p5, p6, p1, p2 = [add2(near[i], swap_c(far[i])) for i in (2, 3, 0, 1)]
    return p1, p2, p5, p6


def step_x(v):
    other = swap_x(v[1])
    return add2(v[0], other)


def step_y(v):
    other = swap_y(v[1])
    return add2(v[0], other)


def scatter_rows_core(near, far):
    a = swap_c(far[0])
    b = swap_c(far[1])
    return add2(near[0], a), add2(near[1], b)


def scatter_rows(a, b):
    b = reduce_z(b, -1)
    a = step_x(a)
    b = step_x(b)
    return jnp.concatenate([reduce_z(a, 1), b], axis=1)


def sequence_at(dc, dz, dx):
    at = lax.axis_index("dp")
    return (at // 4 - dz) % 4 * 4 + (at // 2 % 2 + dx) % 2 * 2 + (at % 2 + dc) % 2


def nn(a, b):
    return lax.dot_general(a, b, (((1,), (0,)), ((), ())), preferred_element_type=F32)


def nt(a, b):
    return lax.dot_general(a, b, (((1,), (1,)), ((), ())), preferred_element_type=F32)


def pick_rows(rank, slots):
    at_slot = lax.broadcasted_iota(jnp.int32, (slots, rank.shape[1]), 0).astype(F32)
    return jnp.concatenate(
        [(rank[e : e + 1, :] == at_slot).astype(F32).astype(BF) for e in range(rank.shape[0])],
        axis=0,
    )


def pick_cols(rank, slots):
    at_slot = lax.broadcasted_iota(jnp.int32, (rank.shape[0], slots), 1).astype(F32)
    return jnp.concatenate(
        [(rank[:, e : e + 1] == at_slot).astype(F32).astype(BF) for e in range(rank.shape[1])],
        axis=1,
    )


def cot_kernel(where, rank, cot_a, cot_b, down, cots, d_act):
    slots = cots.shape[2] // 2
    for dx, cot in enumerate((cot_a, cot_b)):
        both = nn(pick_rows(rank[dx], slots), cot[0]).astype(BF)
        for e in range(2):
            cots[e, 0, dx * slots : (dx + 1) * slots, :] = both[e * slots : (e + 1) * slots]
    for e in range(2):
        d_act[e, 0] = nt(cots[e, 0], down[e])


def expert_kernel(
    rank, rank_t, cols, d_act, x1a, x1b, x2a, x2b, x5, x6, weights,
    rows, scaled, d_g, d_u, t1, t2, t5, t6, back,
):
    slots = rows.shape[2] // 2
    n = x1a.shape[2]
    gates = []
    for dx, x2 in enumerate((x2a, x2b)):
        pick = pick_rows(rank[dx], slots)
        low, high = pick[:, :n], pick[:, n:]
        block1 = nn(low, x1a[dx, 0]) + nn(high, x1b[dx, 0])
        block2 = nn(low, x2[0, 0]) + nn(high, x2[1, 0])
        block5 = nn(low, x5[0, 0, dx]) + nn(high, x5[0, 1, dx])
        block6 = nn(low, x6[0, dx, 0]) + nn(high, x6[0, dx, 1])
        low = dx * slots
        for e in range(2):
            part = slice(e * slots, (e + 1) * slots)
            rows[e, 0, low : low + slots, 0:768] = block1[part].astype(BF)
            rows[e, 0, low : low + slots, 768:1536] = block2[part].astype(BF)
            rows[e, 0, low : low + slots, 1536:1792] = block5[part, :256].astype(BF)
            rows[e, 0, low : low + slots, 1792:2048] = block6[part].astype(BF)
            both = cols[e, 0:1, :] + cols[e, 1:2, :]
            gates.append(jnp.sum(block5[part, 256:] * both, axis=1, keepdims=True))
    extras = []
    for e in range(2):
        gate = jnp.concatenate([gates[e], gates[2 + e]], axis=0)
        g = nn(rows[e, 0], weights[e])
        g, u = jnp.split(g, 2, axis=1)
        da = d_act[e, 0]
        sig = 1.0 / (1.0 + jnp.exp(-g))
        silu = g * sig
        act = silu * u
        scaled[e, 0] = (act * gate).astype(BF)
        d_gate = jnp.sum(act * da, axis=1, keepdims=True)
        da = da * gate
        dg = (da * u * sig * (1.0 + g * (1.0 - sig))).astype(BF)
        du = (da * silu).astype(BF)
        d_g[e, 0] = dg
        d_u[e, 0] = du
        high = d_gate.astype(BF).astype(F32)
        extras.append(high * cols[e, 0:1, :] + (d_gate - high) * cols[e, 1:2, :])
        dr = nt(jnp.concatenate([dg, du], axis=1), weights[e]).astype(BF)
        for dx in range(2):
            back[dx, e * slots : (e + 1) * slots, :] = dr[dx * slots : (dx + 1) * slots]
    extra = [
        jnp.concatenate([extras[e][dx * slots : (dx + 1) * slots] for e in range(2)], axis=0)
        for dx in range(2)
    ]
    put_back(rank_t, back, t1, t2, t5, t6, slots, extra)


def put_back(rank_t, back, t1, t2, t5, t6, slots, extra=None):
    for dx in range(2):
        pick_t = pick_cols(rank_t[dx], slots)
        n = pick_t.shape[0] // 2
        p1, p2, p5, p6 = [
            nn(pick_t, back[dx, :, a:b]).astype(BF) for a, b in zip(SPLIT[:-1], SPLIT[1:])
        ]
        for dy in range(2):
            half = slice(dy * n, (dy + 1) * n)
            t1[dy, dx, 0] = p1[half]
            t2[dx, dy, 0] = p2[half]
            t5[0, dy, dx, :, 0:256] = p5[half]
            t6[0, dx, dy] = p6[half]
        if extra is not None:
            p7 = nn(pick_t, extra[dx].astype(BF)).astype(BF)
            for dy in range(2):
                t5[0, dy, dx, :, 256:] = p7[dy * n : (dy + 1) * n]


def out_kernel(rank_t, scaled, down, t1, t2, t5, t6, back):
    slots = scaled.shape[2] // 2
    for e in range(2):
        y = nn(scaled[e, 0], down[e]).astype(BF)
        for dx in range(2):
            back[dx, e * slots : (e + 1) * slots, :] = y[dx * slots : (dx + 1) * slots]
    put_back(rank_t, back, t1, t2, t5, t6, slots)


def grad_kernel(where, left, right, small, heads, a, b):
    both = lax.dot_general(
        left[...], right[...], (((0,), (0,)), ((), ())), preferred_element_type=F32
    ).astype(BF)
    width = a.shape[-1]
    a[0, 0] = both[:, :width]
    b[0, 0, :, : both.shape[1] - width] = both[:, width:]
    rest = jnp.zeros((small.shape[0] - heads.shape[0], small.shape[1]), F32)
    both_small = small[...] + jnp.concatenate([heads[...], rest], axis=0)
    b[0, 0, :, both.shape[1] - width :] = both_small.astype(BF)


def run_grad(where, left, right, small, heads):
    count, columns = right.shape
    rest = small.shape[1]
    width = columns * 9 // 16 // 128 * 128
    shard = left.shape[1] // 16
    return pl.pallas_call(
        grad_kernel,
        grid_spec=pltpu.PrefetchScalarGridSpec(
            num_scalar_prefetch=1,
            grid=(2, 4),
            in_specs=[
                pl.BlockSpec((count, shard), lambda dx, dz, w: (0, w[2 * dz + dx])),
                pl.BlockSpec((count, columns), lambda dx, dz, w: (0, 0)),
                pl.BlockSpec((shard, rest), lambda dx, dz, w: (w[2 * dz + dx], 0)),
                pl.BlockSpec((HEAD // 16, rest), lambda dx, dz, w: (w[2 * dz + dx], 0)),
            ],
            out_specs=[
                pl.BlockSpec((1, 1, shard, width), lambda dx, dz, w: (dx, dz, 0, 0)),
                pl.BlockSpec((1, 1, shard, columns - width + rest), lambda dx, dz, w: (dz, dx, 0, 0)),
            ],
        ),
        out_shape=[
            shaped((2, 4, shard, width), BF),
            shaped((4, 2, shard, columns - width + rest), BF),
        ],
        compiler_params=LIMIT,
        name="grad",
    )(where, left, right, small, heads)


def pair(*tail):
    return pl.BlockSpec((2, *tail), lambda i, *_: (i,) + (0,) * len(tail))


def z_last(*lead):
    def spec(rows, columns):
        return pl.BlockSpec(
            (*lead, 1, rows, columns), lambda i, *_: (0,) * len(lead) + (i, 0, 0)
        )

    return spec


def z_first(rows, columns):
    return pl.BlockSpec((1, 2, 2, rows, columns), lambda i, *_: (i, 0, 0, 0, 0))


def block_specs(n, extra):
    return [z_last(2, 2)(n, 768), z_last(2, 2)(n, 768), z_first(n, 256 + extra), z_first(n, 256)]


def block_shapes(n, extra):
    shapes = [(2, 2, 4, n, 768), (2, 2, 4, n, 768), (4, 2, 2, n, 256 + extra), (4, 2, 2, n, 256)]
    return [shaped(v, BF) for v in shapes]


def by_expert(*tail):
    return pl.BlockSpec((2, 1, *tail), lambda i, *_: (0, i) + (0,) * len(tail))


def fixed(*shape):
    return pl.BlockSpec(
        shape, lambda i, *_: (0,) * len(shape), pipeline_mode=pl.Buffered(1)
    )


def shaped(shape, kind):
    return jax.ShapeDtypeStruct(shape, kind)


LIMIT = pltpu.CompilerParams(vmem_limit_bytes=58 * 1024 * 1024)


def run_cots(where, rank, cot_all, down, slots):
    seq, width = cot_all.shape[1:]
    ff = down.shape[1]
    return pl.pallas_call(
        cot_kernel,
        grid_spec=pltpu.PrefetchScalarGridSpec(
            num_scalar_prefetch=1,
            grid=(4,),
            in_specs=[
                pair(2, seq),
                pl.BlockSpec((1, seq, width), lambda i, w: (w[2 * i], 0, 0)),
                pl.BlockSpec((1, seq, width), lambda i, w: (w[2 * i + 1], 0, 0)),
                fixed(2, ff, width),
            ],
            out_specs=[by_expert(2 * slots, width), by_expert(2 * slots, ff)],
        ),
        out_shape=[shaped((2, 4, 2 * slots, width), BF), shaped((2, 4, 2 * slots, ff), F32)],
        compiler_params=LIMIT,
        name="cots",
    )(where, rank, cot_all, cot_all, down)


def run_experts(rank, rank_t, cols, d_act, parts, weights, slots):
    s1, s1y, s2, s2x, o5, o6 = parts
    n = s1.shape[2]
    seq, width, ff = 2 * n, weights.shape[1], weights.shape[2] // 2
    return pl.pallas_call(
        expert_kernel,
        grid=(4,),
        in_specs=[
            pair(2, seq),
            pair(seq, 2),
            fixed(*cols.shape),
            by_expert(2 * slots, ff),
            z_last(2)(n, 768),
            z_last(2)(n, 768),
            z_last(2)(n, 768),
            z_last(2)(n, 768),
            z_first(n, 384),
            z_first(n, 256),
            fixed(2, width, 2 * ff),
        ],
        out_specs=[
            by_expert(2 * slots, width),
            by_expert(2 * slots, ff),
            by_expert(2 * slots, ff),
            by_expert(2 * slots, ff),
        ]
        + block_specs(n, 128),
        out_shape=[
            shaped((2, 4, 2 * slots, width), BF),
            shaped((2, 4, 2 * slots, ff), BF),
            shaped((2, 4, 2 * slots, ff), BF),
            shaped((2, 4, 2 * slots, ff), BF),
        ]
        + block_shapes(n, 128),
        scratch_shapes=[pltpu.VMEM((2, 2 * slots, width), BF)],
        compiler_params=LIMIT,
        name="experts",
    )(
        rank, rank_t, cols, d_act, s1, s1y, s2, s2x, o5, o6, weights,
    )


def run_outs(rank_t, scaled, down, slots):
    seq, ff, width = rank_t.shape[1], down.shape[1], down.shape[2]
    return pl.pallas_call(
        out_kernel,
        grid=(4,),
        in_specs=[pair(seq, 2), by_expert(2 * slots, ff), fixed(2, ff, width)],
        out_specs=block_specs(seq // 2, 0),
        out_shape=block_shapes(seq // 2, 0),
        scratch_shapes=[pltpu.VMEM((2, 2 * slots, width), BF)],
        compiler_params=LIMIT,
        name="outs",
    )(rank_t, scaled, down)


def flip(v, axis, y):
    a, b = jnp.split(v, 2, axis=axis)
    return jnp.where(y == 0, v, jnp.concatenate([b, a], axis=axis))


def slot_plan(ids_all, experts):
    y = lax.axis_index("tensor")
    seq = ids_all.shape[1]
    mine = lax.axis_index("dp") * 2 + jnp.arange(2, dtype=jnp.int32)
    mask = jnp.any(ids_all[:, None, :, :] == mine[None, :, None, None], axis=3)
    before = (jnp.arange(seq)[:, None] < jnp.arange(seq)[None, :]).astype(BF)
    rank = jnp.einsum("gea,ab->geb", mask.astype(BF), before, preferred_element_type=F32)
    rank = jnp.where(mask, rank, -1.0)
    d = jnp.arange(16)
    where = sequence_at(d // 8, d // 2 % 4, d % 2)
    rank = jnp.take(rank, where, axis=0)
    rank_rel = flip(rank, 2, y)
    rank_t = jnp.swapaxes(rank_rel, 1, 2)
    column = jnp.arange(128)
    cols = (
        column[None, None, :] == (mine[:, None] + jnp.array([[0, experts]]))[:, :, None]
    ).astype(F32)
    halves = lambda v: (v[:8], v[8:])
    return halves(where.astype(jnp.int32)), halves(rank), halves(rank_rel), halves(rank_t), cols


def moe_small(plan, cot_all, ffn_in, gate_x, weights, down_weight, slots):

    def cot_rows(k, plan):
        return run_cots(plan[0][k], plan[1][k], cot_all, down_weight, slots)

    v1, v2, v5, v6 = [ffn_in[:, a:b] for a, b in zip(SPLIT[:-1], SPLIT[1:])]
    v5 = jnp.concatenate([v5, gate_x], axis=1)
    *parts, plan, both = gather_rel(v1, v2, v5, v6, plan, cot_rows)
    rank_rel, rank_t, cols = plan[2:]
    cots, d_act = zip(*both)
    far, near = [
        run_experts(rank_rel[k], rank_t[k], cols, d_act[k], parts[k], weights, slots)
        for k in (1, 0)
    ]
    p1, p2, p5, p6 = scatter_core(near[4:], far[4:])
    kept = lambda i: (near[i], far[i])
    total = lambda spec, a, b: jnp.einsum(spec, a[0], b[0], preferred_element_type=F32) + jnp.einsum(
        spec, a[1], b[1], preferred_element_type=F32
    )
    p5 = reduce_z(p5, 1)
    p6 = reduce_z(p6, -1)
    p1 = step_y(p1)
    p2 = step_x(p2)
    down_grad = total("egsf,egsd->efd", kept(1), cots)
    outs = []
    for k in (0, 1):
        outs.append(run_outs(rank_t[k], kept(1)[k], down_weight, slots))
    (p1, p2, p5, p6), (outs, down_grad) = tied((p1, p2, p5, p6), (outs, down_grad))
    p5 = step_y(p5)
    p6 = step_x(p6)
    p1 = step_x(p1)
    p2 = step_y(p2)
    up_grad = total("egsd,egsf->edf", kept(0), kept(3))
    (p1, p2, p5, p6), up_grad = tied((p1, p2, p5, p6), up_grad)
    d5 = step_x(p5)
    d6 = step_y(p6)
    d1 = reduce_z(p1, 1)
    d2 = reduce_z(p2, -1)
    p1, p2, p5, p6 = scatter_core(*outs)
    p2, (d5, d6) = tied(p2, (d5, d6))
    p2 = step_x(p2)
    d_sum = jnp.concatenate([d1, d2, d5[:, :256], d6, d5[:, 256:]], axis=1)
    d_sum, (p1, p5, p6) = tied(d_sum, (p1, p5, p6))
    d_sum = d_sum.astype(F32)

    def gate_later(aside):
        (rows, grads), aside = tied((kept(0), kept(2)), aside)
        return total("egsd,egsf->edf", rows, grads), aside

    return d_sum, (p1, p2, p5, p6), gate_later, up_grad, down_grad


def moe_large(
    ids_all, cotangent, ffn_in, gate_x, gate_weight, up_weight, down_weight, experts, slots
):
    dp, seq = ids_all.shape[:2]
    local = gate_weight.shape[0]
    dp_at = lax.axis_index("dp")
    mine = dp_at * local + jnp.arange(local, dtype=jnp.int32)
    mask = jnp.any(ids_all[:, :, None, :] == mine[None, None, :, None], axis=3).astype(BF)
    gate_all = gather_all(gate_x).reshape(dp, seq, -1)
    before = (jnp.arange(seq)[:, None] > jnp.arange(seq)[None, :]).astype(BF)
    rank = jnp.einsum("ab,gbe->gea", before, mask, preferred_element_type=F32)
    rank = jnp.where(jnp.swapaxes(mask, 1, 2) > 0, rank, -1.0)
    pick = (rank[:, :, None, :] == jnp.arange(slots, dtype=F32)[None, None, :, None]).astype(BF)

    cots = dispatch(pick, cotangent, dp, seq, None)
    rows = dispatch(pick, ffn_in, dp, seq, cots)
    gate_tok = lax.dynamic_slice_in_dim(gate_all, dp_at * local, local, 2).astype(
        F32
    ) + lax.dynamic_slice_in_dim(gate_all, experts + dp_at * local, local, 2).astype(F32)
    gate_slot = jnp.sum(pick.astype(F32) * jnp.swapaxes(gate_tok, 1, 2)[:, :, None, :], axis=3)

    g_proj = jnp.einsum("gesd,edf->gesf", rows, gate_weight, preferred_element_type=F32)
    u_proj = jnp.einsum("gesd,edf->gesf", rows, up_weight, preferred_element_type=F32)
    d_act = jnp.einsum("gesd,efd->gesf", cots, down_weight, preferred_element_type=F32)
    sig = 1.0 / (1.0 + jnp.exp(-g_proj))
    silu = g_proj * sig
    act = silu * u_proj
    scaled = (act * gate_slot[..., None]).astype(BF)
    d_gate_slot = jnp.sum(act * d_act, axis=3)
    d_act = d_act * gate_slot[..., None]
    d_g = (d_act * u_proj * sig * (1.0 + g_proj * (1.0 - sig))).astype(BF)
    d_u = (d_act * silu).astype(BF)
    d_rows = (
        jnp.einsum("gesf,edf->gesd", d_g, gate_weight, preferred_element_type=F32)
        + jnp.einsum("gesf,edf->gesd", d_u, up_weight, preferred_element_type=F32)
    ).astype(BF)
    dg_high, dg_low = split2(d_gate_slot)
    column = jnp.arange(lanes(2 * experts))
    high_col = (column[None, :] == mine[:, None])[None, :, None, :]
    low_col = (column[None, :] == experts + mine[:, None])[None, :, None, :]
    extra = jnp.where(high_col, dg_high[..., None], jnp.where(low_col, dg_low[..., None], 0.0))
    d_rows = jnp.concatenate([d_rows, extra.astype(BF)], axis=3)
    d_sum = combine(pick, d_rows, dp, seq, None)

    y_rows = jnp.einsum("gesf,efd->gesd", scaled, down_weight, preferred_element_type=F32)
    y_sum = combine(pick, y_rows.astype(BF), dp, seq, d_sum)
    down_grad = jnp.einsum("gesf,gesd->efd", scaled, cots, preferred_element_type=F32)
    gate_grad = jnp.einsum("gesd,gesf->edf", rows, d_g, preferred_element_type=F32)
    up_grad = jnp.einsum("gesd,gesf->edf", rows, d_u, preferred_element_type=F32)

    return d_sum, y_sum, gate_grad, up_grad, down_grad


def pad_to(v, width):
    return jnp.pad(v, ((0, 0), (0, width - v.shape[1])))


def lanes(count):
    return -(-count // 128) * 128


def on_device(
    tokens,
    attn_gain,
    q_weight,
    key_matrix,
    value_matrix,
    o_weight,
    query_norm_gain,
    k_gain,
    ffn_gain,
    router_weight,
    gate_weight,
    up_weight,
    down_weight,
    expert_ids,
    cotangent,
):
    dp = lax.axis_size("dp")
    tensor = lax.axis_size("tensor")
    own, width = tokens.shape
    seq = expert_ids.shape[0]
    begin = lax.axis_index("tensor") * own
    local = gate_weight.shape[0]
    experts = local * dp
    slots = 10 * seq * expert_ids.shape[1] // (8 * experts)
    slots = -(-slots // 16) * 16
    shard = q_weight.shape[0]
    gshard = query_norm_gain.shape[0]
    hq = q_weight.shape[1] // HEAD
    hk = key_matrix.shape[1] // HEAD
    qkv_width = (hq + 2 * hk) * HEAD
    top = expert_ids.shape[1]
    fast = (dp, tensor, local, seq, width) == (16, 2, 2, 384, 2048)

    arange_e = jnp.arange(experts, dtype=jnp.int32)
    own_ids = lax.dynamic_slice_in_dim(expert_ids, begin, own, 0)
    own_mask = jnp.any(own_ids[:, :, None] == arange_e[None, None, :], axis=1)

    gain_rows = jnp.stack(
        [
            attn_gain,
            ffn_gain,
            jnp.pad(query_norm_gain, (0, shard - gshard)),
            jnp.pad(k_gain, (0, shard - gshard)),
        ],
        axis=1,
    )
    ids_rows = expert_ids.reshape(shard, -1).astype(BF)
    small = jnp.concatenate([router_weight, gain_rows, ids_rows], axis=1)
    small = pad_to(small, lanes(small.shape[1]))
    small_end = qkv_width + small.shape[1]
    all_in = gather_dp(
        jnp.concatenate([q_weight, key_matrix, value_matrix, small, o_weight.T], axis=1)
    )
    layer_in = gather_y(tokens)
    if fast:
        weights = jnp.concatenate([gate_weight, up_weight], axis=2)
        layer_in, weights = tied(layer_in, weights)
    o_t = all_in[:, small_end:]
    if fast:
        cot_all = gather_dp(gather_y(cotangent)).reshape(dp, seq, width)

    w_qkv = all_in[:, :qkv_width]
    router = all_in[:, qkv_width : qkv_width + experts]
    gains = all_in[:, qkv_width + experts : qkv_width + experts + 4].astype(F32)
    ids_all = all_in[:, qkv_width + experts + 4 :][:, : seq * top // shard]
    ids_all = ids_all.astype(jnp.int32).reshape(dp, seq, top)
    attn_gain32 = gains[:, 0]
    ffn_gain32 = gains[:, 1]
    q_gain32 = gains[:, 2].reshape(dp, shard)[:, :gshard].reshape(-1)
    k_gain32 = gains[:, 3].reshape(dp, shard)[:, :gshard].reshape(-1)

    residual = layer_in.astype(F32)
    normed = rms(residual, attn_gain32).astype(BF)
    qkv = dot(normed, w_qkv, 1, 0)
    cos, sin = rope_tables(seq)
    head_gains = jnp.pad(jnp.stack([q_gain32, k_gain32]), ((0, 6), (0, 0)))
    context = run_attend(qkv, head_gains, cos, sin, hq, hk)
    attn_part = dot(context, o_t, 1, 1)
    if fast:
        attn_part, ids_all = tied(attn_part, ids_all)
        plan = slot_plan(ids_all, experts)
    hidden = tokens.astype(F32) + scatter_y(attn_part)

    ffn_in = rms(hidden, ffn_gain32).astype(BF)
    logits = dot(ffn_in, router, 1, 0)
    chosen = jnp.where(own_mask, jnp.exp(logits), 0.0)
    gates = chosen / jnp.sum(chosen, axis=1, keepdims=True)
    gate_high, gate_low = split2(gates)
    gate_x = pad_to(jnp.concatenate([gate_high, gate_low], axis=1), lanes(2 * experts))
    args = (gate_weight, up_weight, down_weight)
    if fast:
        d_sum, y_sum, gate_later, up_grad, down_grad = moe_small(
            plan, cot_all, ffn_in, gate_x, weights, down_weight, slots
        )
    else:
        d_sum, y_sum, gate_grad, up_grad, down_grad = moe_large(
            ids_all, cotangent, ffn_in, gate_x, *args, experts, slots
        )
    d_gates = d_sum[:, width : width + experts] + d_sum[:, width + experts : width + 2 * experts]
    d_logits = gates * (d_gates - jnp.sum(gates * d_gates, axis=1, keepdims=True))
    d_high, d_low = split2(d_logits)
    d_ffn = d_sum[:, :width] + dot(d_high, router, 1, 1) + dot(d_low, router, 1, 1)
    router_part = dot(ffn_in, d_high, 0, 0) + dot(ffn_in, d_low, 0, 0)
    d_hidden, ffn_gain_rows = rms_back(hidden, ffn_gain32, d_ffn)
    ffn_gain_part = jnp.sum(ffn_gain_rows, axis=0)
    d_hidden = d_hidden + cotangent.astype(F32)
    d_attn = gather_y(d_hidden.astype(BF))

    o_part = dot(d_attn, context, 0, 0).astype(BF)
    d_attn, o_part = tied(d_attn, o_part)
    o_sum = scatter_dp(o_part).astype(F32)
    if fast:
        p1, p2, p5, p6 = y_sum
        d_attn, p1 = tied(d_attn, p1)
        p1 = step_y(p1)
        two5, two6 = first_hop(p5, 1), first_hop(p6, -1)
        gate_grad, d_attn = gate_later(d_attn)
    d_context = dot(d_attn, o_t, 1, 0).astype(BF)
    heads = []
    for head in range(hk):
        heads.append(run_attend_back(head, qkv, d_context, head_gains, cos, sin, hq, hk))
        if fast and head == 0:
            aside = (p1, p2, two5, two6, gate_grad)
            d_context, heads, aside = lax.optimization_barrier((d_context, heads, aside))
            p1, p2, two5, two6, gate_grad = aside
            p1 = step_x(p1)
            p2 = step_y(p2)
            p5 = reduce_z(p5, 1, two5)
            p6 = reduce_z(p6, -1, two6)
    d_qkv = jnp.concatenate([h[k] for k in range(3) for h in heads], axis=1)
    small_part = jnp.concatenate([router_part, ffn_gain_part[:, None]], axis=1)
    small_part = pad_to(small_part, lanes(experts + 3))
    column = jnp.arange(small_part.shape[1])[None, :]
    head_part = sum(h[3][0] for h in heads)[:, None] * (column == experts + 1).astype(F32)
    head_part += sum(h[3][1] for h in heads)[:, None] * (column == experts + 2).astype(F32)
    if fast:
        d_qkv, (p1, p2, p5, p6) = tied(d_qkv, (p1, p2, p5, p6))
        y_sum = (reduce_z(p1, 1), reduce_z(p2, -1), step_x(step_y(p5)), step_y(step_x(p6)))
        far = run_grad(plan[0][1], normed, d_qkv, small_part, head_part)
        near = run_grad(plan[0][0], normed, d_qkv, small_part, head_part)
        a, b = scatter_rows_core(near, far)
        qkv_sum = scatter_rows(a, b).astype(F32)
        qkv_sum, small_sum = qkv_sum[:, :qkv_width], qkv_sum[:, qkv_width:]
        y_sum = jnp.concatenate(y_sum, axis=1).astype(F32)
    else:
        qkv_sum = scatter_dp(dot(normed, d_qkv, 0, 0).astype(BF)).astype(F32)
        head_part = jnp.pad(
            head_part.reshape(dp, gshard, -1), ((0, 0), (0, shard - gshard), (0, 0))
        )
        small_sum = scatter_dp(small_part + head_part.reshape(small_part.shape))
    output = (hidden + y_sum).astype(BF)
    d_normed = dot(d_qkv, w_qkv, 1, 1)
    d_normed = scatter_y(d_normed)
    d_tokens, _ = rms_back(tokens.astype(F32), attn_gain32, d_normed)
    tokens_grad = d_tokens + d_hidden

    weights = jnp.concatenate([q_weight, key_matrix, value_matrix], axis=1).astype(F32)
    gain_part = jnp.sum(weights * qkv_sum, axis=1) / attn_gain.astype(F32)
    small_sum = jnp.concatenate([small_sum, gain_part[:, None]], axis=1)
    small_sum = small_sum + swap_y(small_sum)
    return (
        output,
        tokens_grad,
        small_sum[:, -1],
        qkv_sum[:, : hq * HEAD],
        qkv_sum[:, hq * HEAD : (hq + hk) * HEAD],
        qkv_sum[:, (hq + hk) * HEAD :],
        o_sum.T,
        small_sum[:gshard, experts + 1],
        small_sum[:gshard, experts + 2],
        small_sum[:, experts],
        small_sum[:, :experts],
        gate_grad,
        up_grad,
        down_grad,
    )


def solution(mesh):
    rows = P(("dp", "tensor"), None)
    both = P("dp", "tensor")
    return jax.shard_map(
        on_device,
        mesh=mesh,
        in_specs=(
            rows,
            P("dp"),
            both,
            both,
            both,
            P("tensor", "dp"),
            P("dp"),
            P("dp"),
            P("dp"),
            P("dp", None),
            P("dp", None, "tensor"),
            P("dp", None, "tensor"),
            P("dp", "tensor", None),
            P("dp", None),
            rows,
        ),
        out_specs=(
            rows,
            rows,
            P("dp"),
            both,
            both,
            both,
            P("tensor", "dp"),
            P("dp"),
            P("dp"),
            P("dp"),
            P("dp", None),
            P("dp", None, "tensor"),
            P("dp", None, "tensor"),
            P("dp", "tensor", None),
        ),
        check_vma=False,
    )
```

```python
import jax
import jax.numpy as jnp
from jax import lax
from jax.experimental import pallas as pl
from jax.experimental.pallas import tpu as pltpu
from jax.sharding import PartitionSpec as P


HEAD = 128
EPS = 1e-06
THETA = 1000000.0
BF = jnp.bfloat16
F32 = jnp.float32


def dot(a, b, ca, cb):
    return lax.dot_general(a, b, (((ca,), (cb,)), ((), ())), preferred_element_type=F32)


def rms(v, gain):
    return v * lax.rsqrt(jnp.mean(v * v, axis=-1, keepdims=True) + EPS) * gain


def rms_back(v, gain, u):
    inv = lax.rsqrt(jnp.mean(v * v, axis=-1, keepdims=True) + EPS)
    ug = u * gain
    grad = ug * inv - v * (jnp.mean(ug * v, axis=-1, keepdims=True) * inv * inv * inv)
    return grad, u * v * inv


def rope_tables(count):
    inverse = THETA ** (-(jnp.arange(HEAD // 2, dtype=F32) * 2.0 / HEAD))
    angles = jnp.arange(count, dtype=F32)[:, None] * inverse[None, :]
    cos, sin = jnp.cos(angles), jnp.sin(angles)
    return jnp.concatenate([cos, cos], axis=1), jnp.concatenate([-sin, sin], axis=1)


def half_turn(v):
    return pltpu.roll(v, HEAD // 2, 1)


def turned(raw, gain, cos, sin):
    v = rms(raw, gain)
    return (v * cos + half_turn(v) * sin).astype(BF)


def soft(q, k):
    scores = lax.dot_general(q, k, (((1,), (1,)), ((), ())), preferred_element_type=F32)
    scores = scores * HEAD ** (-0.5)
    row = lax.broadcasted_iota(jnp.int32, scores.shape, 0)
    column = lax.broadcasted_iota(jnp.int32, scores.shape, 1)
    e = jnp.where(row >= column, jnp.exp(scores), 0.0)
    return e * (1.0 / jnp.sum(e, axis=1, keepdims=True))


def attend_kernel(q_raw, k_raw, v_raw, gains, cos, sin, context, keys):
    @pl.when(pl.program_id(1) == 0)
    def _():
        keys[...] = turned(k_raw[...], gains[1:2], cos[...], sin[...])

    v = v_raw[...].astype(BF)
    for h in range(2):
        part = slice(h * HEAD, (h + 1) * HEAD)
        q = turned(q_raw[:, part], gains[0:1], cos[...], sin[...])
        p = soft(q, keys[...]).astype(BF)
        context[:, part] = lax.dot_general(
            p, v, (((1,), (0,)), ((), ())), preferred_element_type=F32
        ).astype(BF)


def attend_back_kernel(
    q_raw, k_raw, v_raw, d_context, gains, cos, sin, d_q, d_k, d_v, d_gains, keys, k_sum, v_sum
):
    at = pl.program_id(0)

    @pl.when(at == 0)
    def _():
        keys[...] = turned(k_raw[...], gains[1:2], cos[...], sin[...])
        k_sum[...] = jnp.zeros_like(k_sum)
        v_sum[...] = jnp.zeros_like(v_sum)
        d_gains[...] = jnp.zeros_like(d_gains)

    def back(raw, gain, u):
        return rms_back(raw, gain, u * cos[...] - half_turn(u) * sin[...])

    v = v_raw[...].astype(BF)
    scale = HEAD ** (-0.5)
    for h in range(2):
        part = slice(h * HEAD, (h + 1) * HEAD)
        raw = q_raw[:, part]
        q = turned(raw, gains[0:1], cos[...], sin[...])
        p = soft(q, keys[...])
        dc = d_context[:, part]
        dp = lax.dot_general(dc, v, (((1,), (1,)), ((), ())), preferred_element_type=F32)
        v_sum[...] += lax.dot_general(
            p.astype(BF), dc, (((0,), (0,)), ((), ())), preferred_element_type=F32
        )
        ds = (p * (dp - jnp.sum(p * dp, axis=1, keepdims=True))).astype(BF)
        dq = lax.dot_general(
            ds, keys[...], (((1,), (0,)), ((), ())), preferred_element_type=F32
        )
        k_sum[...] += lax.dot_general(ds, q, (((0,), (0,)), ((), ())), preferred_element_type=F32)
        grad, gain_rows = back(raw, gains[0:1], dq * scale)
        d_q[:, part] = grad.astype(BF)
        d_gains[0:1, :] += jnp.sum(gain_rows, axis=0, keepdims=True)

    @pl.when(at == pl.num_programs(0) - 1)
    def _():
        grad, gain_rows = back(k_raw[...], gains[1:2], k_sum[...] * scale)
        d_k[...] = grad.astype(BF)
        d_v[...] = v_sum[...].astype(BF)
        d_gains[1:2, :] += jnp.sum(gain_rows, axis=0, keepdims=True)


def run_attend(qkv, gains, cos, sin, hq, hk):
    seq = qkv.shape[0]
    pairs = hq // hk // 2
    block = lambda width, index: pl.BlockSpec((seq, width * HEAD), index)
    whole = lambda rows: pl.BlockSpec((rows, HEAD), lambda i, j: (0, 0))
    return pl.pallas_call(
        attend_kernel,
        grid=(hk, pairs),
        in_specs=[
            block(2, lambda i, j: (0, i * pairs + j)),
            block(1, lambda i, j: (0, hq + i)),
            block(1, lambda i, j: (0, hq + hk + i)),
            whole(8),
            whole(seq),
            whole(seq),
        ],
        out_specs=block(2, lambda i, j: (0, i * pairs + j)),
        out_shape=jax.ShapeDtypeStruct((seq, hq * HEAD), BF),
        scratch_shapes=[pltpu.VMEM((seq, HEAD), BF)],
        name="attend",
    )(qkv, qkv, qkv, gains, cos, sin)


def run_attend_back(head, qkv, d_context, gains, cos, sin, hq, hk):
    seq = qkv.shape[0]
    pairs = hq // hk // 2
    block = lambda width, index: pl.BlockSpec((seq, width * HEAD), index)
    whole = lambda rows: pl.BlockSpec((rows, HEAD), lambda j: (0, 0))
    return pl.pallas_call(
        attend_back_kernel,
        grid=(pairs,),
        in_specs=[
            block(2, lambda j: (0, head * pairs + j)),
            block(1, lambda j: (0, hq + head)),
            block(1, lambda j: (0, hq + hk + head)),
            block(2, lambda j: (0, head * pairs + j)),
            whole(8),
            whole(seq),
            whole(seq),
        ],
        out_specs=[block(2, lambda j: (0, j)), whole(seq), whole(seq), whole(8)],
        out_shape=[
            jax.ShapeDtypeStruct((seq, 2 * pairs * HEAD), BF),
            jax.ShapeDtypeStruct((seq, HEAD), BF),
            jax.ShapeDtypeStruct((seq, HEAD), BF),
            jax.ShapeDtypeStruct((8, HEAD), F32),
        ],
        scratch_shapes=[
            pltpu.VMEM((seq, HEAD), BF),
            pltpu.VMEM((seq, HEAD), F32),
            pltpu.VMEM((seq, HEAD), F32),
        ],
        name="attend_back",
    )(qkv, qkv, qkv, d_context, gains, cos, sin)


def split2(v):
    high = v.astype(BF)
    return high, (v - high.astype(F32)).astype(BF)


def gather_dp(v):
    return lax.all_gather(v, "dp", axis=0, tiled=True)


def gather_all(v):
    return lax.all_gather(v, ("dp", "tensor"), axis=0, tiled=True)


def scatter_all(v):
    return lax.psum_scatter(v, ("dp", "tensor"), scatter_dimension=0, tiled=True)


def scatter_dp(v):
    return lax.psum_scatter(v, "dp", scatter_dimension=0, tiled=True)


def pieces(width, dp, seq):
    count = 1 if dp * seq <= 8192 else 4
    step = width // count // 128 * 128
    edges = [step * i for i in range(count)] + [width]
    return list(zip(edges[:-1], edges[1:]))


def after(v, earlier):
    return v if earlier is None else lax.optimization_barrier((v, earlier))[0]


def dispatch(pick, own, dp, seq, earlier):
    blocks = []
    for low, high in pieces(own.shape[1], dp, seq):
        every = gather_all(after(own[:, low:high], earlier)).reshape(dp, seq, high - low)
        block = jnp.einsum("gest,gtd->gesd", pick, every, preferred_element_type=F32).astype(BF)
        blocks.append(block)
        earlier = block if len(pieces(own.shape[1], dp, seq)) > 1 else None
    return jnp.concatenate(blocks, axis=3)


def combine(pick, rows, dp, seq, earlier):
    blocks = []
    for low, high in pieces(rows.shape[3], dp, seq):
        tok = jnp.einsum(
            "gest,gesd->gtd",
            pick,
            after(rows[:, :, :, low:high], earlier),
            preferred_element_type=F32,
        ).astype(BF)
        blocks.append(scatter_all(tok.reshape(dp * seq, high - low)))
        earlier = blocks[-1] if len(pieces(rows.shape[3], dp, seq)) > 1 else None
    return jnp.concatenate(blocks, axis=1).astype(F32)


GRID = [(z, x, c) for z in range(4) for x in range(2) for c in range(2)]
SPLIT = (0, 768, 1536, 1792, 2048)


def at(z, x, c):
    return z % 4 * 4 + x % 2 * 2 + c % 2


def shift_z(v, k):
    return lax.ppermute(v, "dp", [(at(z, x, c), at(z + k, x, c)) for z, x, c in GRID])


def swap_x(v):
    return lax.ppermute(v, "dp", [(at(z, x, c), at(z, x + 1, c)) for z, x, c in GRID])


def swap_c(v):
    return lax.ppermute(v, "dp", [(at(z, x, c), at(z, x, c + 1)) for z, x, c in GRID])


def swap_y(v):
    return lax.ppermute(v, "tensor", [(0, 1), (1, 0)])


def gather_y(v):
    other = swap_y(v)
    first = lax.axis_index("tensor") == 0
    return jnp.concatenate([jnp.where(first, v, other), jnp.where(first, other, v)])


def scatter_y(v):
    a, b = jnp.split(v, 2)
    first = lax.axis_index("tensor") == 0
    kept, sent = jnp.where(first, a, b), jnp.where(first, b, a)
    other = swap_y(sent.astype(BF))
    return kept.astype(F32) + other.astype(F32)


def gather_z(v, way):
    one, three = shift_z(v, 1), shift_z(v, -1)
    two = shift_z(one, 1) if way > 0 else shift_z(three, -1)
    return jnp.stack([v, one, two, three])


def add2(a, b):
    return (a.astype(F32) + b.astype(F32)).astype(BF)


def reduce_z(v, way, two=None):
    if two is None:
        two = first_hop(v, way)
    side = shift_z(v[3 if way > 0 else 1], way)
    relay = shift_z(add2(v[1 if way > 0 else 3], two), -way)
    return (v[0].astype(F32) + side.astype(F32) + relay.astype(F32)).astype(BF)


def first_hop(v, way):
    return shift_z(v[2], -way)


def tied(v, w):
    return lax.optimization_barrier((v, w))


def gather_rel(v1, v2, v5, v6, plan, aside):
    w5 = jnp.stack([v5, swap_x(v5)])
    w6 = jnp.stack([v6, swap_y(v6)])
    s1 = gather_z(v1, 1)
    s2 = gather_z(v2, -1)
    w5 = jnp.stack([w5, swap_y(w5)])
    w6 = jnp.stack([w6, swap_x(w6)])
    s1, s2, w5, w6, plan = lax.optimization_barrier((s1, s2, w5, w6, plan))
    five = [shift_z(w5, 1), shift_z(w5, -1)]
    six = [shift_z(w6, 1), shift_z(w6, -1)]
    s1x, s2y = swap_x(s1), swap_y(s2)
    s1 = jnp.stack([s1, s1x])
    s2 = jnp.stack([s2, s2y])
    s1y, s2x = swap_y(s1), swap_x(s2)
    five.append(shift_z(five[0], 1))
    six.append(shift_z(six[1], -1))
    o5 = jnp.stack([w5, five[0], five[2], five[1]])
    o6 = jnp.stack([w6, six[0], six[2], six[1]])
    far = aside(1, plan)
    near = aside(0, plan)
    (s1y, s2x), (near, far) = tied((s1y, s2x), (near, far))
    first = (s1, s1y, s2, s2x, o5, o6)
    return first, tuple(swap_c(v) for v in first), plan, (near, far)


def scatter_core(near, far):
    p5, p6, p1, p2 = [add2(near[i], swap_c(far[i])) for i in (2, 3, 0, 1)]
    return p1, p2, p5, p6


def step_x(v):
    other = swap_x(v[1])
    return add2(v[0], other)


def step_y(v):
    other = swap_y(v[1])
    return add2(v[0], other)


def scatter_rows_core(near, far):
    a = swap_c(far[0])
    b = swap_c(far[1])
    return add2(near[0], a), add2(near[1], b)


def scatter_rows(a, b):
    b = reduce_z(b, -1)
    a = step_x(a)
    b = step_x(b)
    return jnp.concatenate([reduce_z(a, 1), b], axis=1)


def sequence_at(dc, dz, dx):
    at = lax.axis_index("dp")
    return (at // 4 - dz) % 4 * 4 + (at // 2 % 2 + dx) % 2 * 2 + (at % 2 + dc) % 2


def nn(a, b):
    return lax.dot_general(a, b, (((1,), (0,)), ((), ())), preferred_element_type=F32)


def nt(a, b):
    return lax.dot_general(a, b, (((1,), (1,)), ((), ())), preferred_element_type=F32)


def pick_rows(rank, slots):
    at_slot = lax.broadcasted_iota(jnp.int32, (slots, rank.shape[1]), 0).astype(F32)
    return jnp.concatenate(
        [(rank[e : e + 1, :] == at_slot).astype(F32).astype(BF) for e in range(rank.shape[0])],
        axis=0,
    )


def pick_cols(rank, slots):
    at_slot = lax.broadcasted_iota(jnp.int32, (rank.shape[0], slots), 1).astype(F32)
    return jnp.concatenate(
        [(rank[:, e : e + 1] == at_slot).astype(F32).astype(BF) for e in range(rank.shape[1])],
        axis=1,
    )


def cot_kernel(where, rank, cot_a, cot_b, down, cots, d_act):
    slots = cots.shape[2] // 2
    for dx, cot in enumerate((cot_a, cot_b)):
        both = nn(pick_rows(rank[dx], slots), cot[0]).astype(BF)
        for e in range(2):
            cots[e, 0, dx * slots : (dx + 1) * slots, :] = both[e * slots : (e + 1) * slots]
    for e in range(2):
        d_act[e, 0] = nt(cots[e, 0], down[e])


def expert_kernel(
    rank, rank_t, cols, d_act, x1a, x1b, x2a, x2b, x5, x6, weights,
    rows, scaled, d_g, d_u, t1, t2, t5, t6, back,
):
    slots = rows.shape[2] // 2
    n = x1a.shape[2]
    gates = []
    for dx, x2 in enumerate((x2a, x2b)):
        pick = pick_rows(rank[dx], slots)
        low, high = pick[:, :n], pick[:, n:]
        block1 = nn(low, x1a[dx, 0]) + nn(high, x1b[dx, 0])
        block2 = nn(low, x2[0, 0]) + nn(high, x2[1, 0])
        block5 = nn(low, x5[0, 0, dx]) + nn(high, x5[0, 1, dx])
        block6 = nn(low, x6[0, dx, 0]) + nn(high, x6[0, dx, 1])
        low = dx * slots
        for e in range(2):
            part = slice(e * slots, (e + 1) * slots)
            rows[e, 0, low : low + slots, 0:768] = block1[part].astype(BF)
            rows[e, 0, low : low + slots, 768:1536] = block2[part].astype(BF)
            rows[e, 0, low : low + slots, 1536:1792] = block5[part, :256].astype(BF)
            rows[e, 0, low : low + slots, 1792:2048] = block6[part].astype(BF)
            both = cols[e, 0:1, :] + cols[e, 1:2, :]
            gates.append(jnp.sum(block5[part, 256:] * both, axis=1, keepdims=True))
    extras = []
    for e in range(2):
        gate = jnp.concatenate([gates[e], gates[2 + e]], axis=0)
        g = nn(rows[e, 0], weights[e])
        g, u = jnp.split(g, 2, axis=1)
        da = d_act[e, 0]
        sig = 1.0 / (1.0 + jnp.exp(-g))
        silu = g * sig
        act = silu * u
        scaled[e, 0] = (act * gate).astype(BF)
        d_gate = jnp.sum(act * da, axis=1, keepdims=True)
        da = da * gate
        dg = (da * u * sig * (1.0 + g * (1.0 - sig))).astype(BF)
        du = (da * silu).astype(BF)
        d_g[e, 0] = dg
        d_u[e, 0] = du
        high = d_gate.astype(BF).astype(F32)
        extras.append(high * cols[e, 0:1, :] + (d_gate - high) * cols[e, 1:2, :])
        dr = nt(jnp.concatenate([dg, du], axis=1), weights[e]).astype(BF)
        for dx in range(2):
            back[dx, e * slots : (e + 1) * slots, :] = dr[dx * slots : (dx + 1) * slots]
    extra = [
        jnp.concatenate([extras[e][dx * slots : (dx + 1) * slots] for e in range(2)], axis=0)
        for dx in range(2)
    ]
    put_back(rank_t, back, t1, t2, t5, t6, slots, extra)


def put_back(rank_t, back, t1, t2, t5, t6, slots, extra=None):
    for dx in range(2):
        pick_t = pick_cols(rank_t[dx], slots)
        n = pick_t.shape[0] // 2
        p1, p2, p5, p6 = [
            nn(pick_t, back[dx, :, a:b]).astype(BF) for a, b in zip(SPLIT[:-1], SPLIT[1:])
        ]
        for dy in range(2):
            half = slice(dy * n, (dy + 1) * n)
            t1[dy, dx, 0] = p1[half]
            t2[dx, dy, 0] = p2[half]
            t5[0, dy, dx, :, 0:256] = p5[half]
            t6[0, dx, dy] = p6[half]
        if extra is not None:
            p7 = nn(pick_t, extra[dx].astype(BF)).astype(BF)
            for dy in range(2):
                t5[0, dy, dx, :, 256:] = p7[dy * n : (dy + 1) * n]


def out_kernel(rank_t, scaled, down, t1, t2, t5, t6, back):
    slots = scaled.shape[2] // 2
    for e in range(2):
        y = nn(scaled[e, 0], down[e]).astype(BF)
        for dx in range(2):
            back[dx, e * slots : (e + 1) * slots, :] = y[dx * slots : (dx + 1) * slots]
    put_back(rank_t, back, t1, t2, t5, t6, slots)


def grad_kernel(where, left, right, small, heads, a, b):
    both = lax.dot_general(
        left[...], right[...], (((0,), (0,)), ((), ())), preferred_element_type=F32
    ).astype(BF)
    width = a.shape[-1]
    a[0, 0] = both[:, :width]
    b[0, 0, :, : both.shape[1] - width] = both[:, width:]
    rest = jnp.zeros((small.shape[0] - heads.shape[0], small.shape[1]), F32)
    both_small = small[...] + jnp.concatenate([heads[...], rest], axis=0)
    b[0, 0, :, both.shape[1] - width :] = both_small.astype(BF)


def run_grad(where, left, right, small, heads):
    count, columns = right.shape
    rest = small.shape[1]
    width = columns * 9 // 16 // 128 * 128
    shard = left.shape[1] // 16
    return pl.pallas_call(
        grad_kernel,
        grid_spec=pltpu.PrefetchScalarGridSpec(
            num_scalar_prefetch=1,
            grid=(2, 4),
            in_specs=[
                pl.BlockSpec((count, shard), lambda dx, dz, w: (0, w[2 * dz + dx])),
                pl.BlockSpec((count, columns), lambda dx, dz, w: (0, 0)),
                pl.BlockSpec((shard, rest), lambda dx, dz, w: (w[2 * dz + dx], 0)),
                pl.BlockSpec((HEAD // 16, rest), lambda dx, dz, w: (w[2 * dz + dx], 0)),
            ],
            out_specs=[
                pl.BlockSpec((1, 1, shard, width), lambda dx, dz, w: (dx, dz, 0, 0)),
                pl.BlockSpec((1, 1, shard, columns - width + rest), lambda dx, dz, w: (dz, dx, 0, 0)),
            ],
        ),
        out_shape=[
            shaped((2, 4, shard, width), BF),
            shaped((4, 2, shard, columns - width + rest), BF),
        ],
        compiler_params=LIMIT,
        name="grad",
    )(where, left, right, small, heads)


def pair(*tail):
    return pl.BlockSpec((2, *tail), lambda i, *_: (i,) + (0,) * len(tail))


def z_last(*lead):
    def spec(rows, columns):
        return pl.BlockSpec(
            (*lead, 1, rows, columns), lambda i, *_: (0,) * len(lead) + (i, 0, 0)
        )

    return spec


def z_first(rows, columns):
    return pl.BlockSpec((1, 2, 2, rows, columns), lambda i, *_: (i, 0, 0, 0, 0))


def block_specs(n, extra):
    return [z_last(2, 2)(n, 768), z_last(2, 2)(n, 768), z_first(n, 256 + extra), z_first(n, 256)]


def block_shapes(n, extra):
    shapes = [(2, 2, 4, n, 768), (2, 2, 4, n, 768), (4, 2, 2, n, 256 + extra), (4, 2, 2, n, 256)]
    return [shaped(v, BF) for v in shapes]


def by_expert(*tail):
    return pl.BlockSpec((2, 1, *tail), lambda i, *_: (0, i) + (0,) * len(tail))


def fixed(*shape):
    return pl.BlockSpec(
        shape, lambda i, *_: (0,) * len(shape), pipeline_mode=pl.Buffered(1)
    )


def shaped(shape, kind):
    return jax.ShapeDtypeStruct(shape, kind)


LIMIT = pltpu.CompilerParams(vmem_limit_bytes=58 * 1024 * 1024)


def run_cots(where, rank, cot_all, down, slots):
    seq, width = cot_all.shape[1:]
    ff = down.shape[1]
    return pl.pallas_call(
        cot_kernel,
        grid_spec=pltpu.PrefetchScalarGridSpec(
            num_scalar_prefetch=1,
            grid=(4,),
            in_specs=[
                pair(2, seq),
                pl.BlockSpec((1, seq, width), lambda i, w: (w[2 * i], 0, 0)),
                pl.BlockSpec((1, seq, width), lambda i, w: (w[2 * i + 1], 0, 0)),
                fixed(2, ff, width),
            ],
            out_specs=[by_expert(2 * slots, width), by_expert(2 * slots, ff)],
        ),
        out_shape=[shaped((2, 4, 2 * slots, width), BF), shaped((2, 4, 2 * slots, ff), F32)],
        compiler_params=LIMIT,
        name="cots",
    )(where, rank, cot_all, cot_all, down)


def run_experts(rank, rank_t, cols, d_act, parts, weights, slots):
    s1, s1y, s2, s2x, o5, o6 = parts
    n = s1.shape[2]
    seq, width, ff = 2 * n, weights.shape[1], weights.shape[2] // 2
    return pl.pallas_call(
        expert_kernel,
        grid=(4,),
        in_specs=[
            pair(2, seq),
            pair(seq, 2),
            fixed(*cols.shape),
            by_expert(2 * slots, ff),
            z_last(2)(n, 768),
            z_last(2)(n, 768),
            z_last(2)(n, 768),
            z_last(2)(n, 768),
            z_first(n, 384),
            z_first(n, 256),
            fixed(2, width, 2 * ff),
        ],
        out_specs=[
            by_expert(2 * slots, width),
            by_expert(2 * slots, ff),
            by_expert(2 * slots, ff),
            by_expert(2 * slots, ff),
        ]
        + block_specs(n, 128),
        out_shape=[
            shaped((2, 4, 2 * slots, width), BF),
            shaped((2, 4, 2 * slots, ff), BF),
            shaped((2, 4, 2 * slots, ff), BF),
            shaped((2, 4, 2 * slots, ff), BF),
        ]
        + block_shapes(n, 128),
        scratch_shapes=[pltpu.VMEM((2, 2 * slots, width), BF)],
        compiler_params=LIMIT,
        name="experts",
    )(
        rank, rank_t, cols, d_act, s1, s1y, s2, s2x, o5, o6, weights,
    )


def run_outs(rank_t, scaled, down, slots):
    seq, ff, width = rank_t.shape[1], down.shape[1], down.shape[2]
    return pl.pallas_call(
        out_kernel,
        grid=(4,),
        in_specs=[pair(seq, 2), by_expert(2 * slots, ff), fixed(2, ff, width)],
        out_specs=block_specs(seq // 2, 0),
        out_shape=block_shapes(seq // 2, 0),
        scratch_shapes=[pltpu.VMEM((2, 2 * slots, width), BF)],
        compiler_params=LIMIT,
        name="outs",
    )(rank_t, scaled, down)


def flip(v, axis, y):
    a, b = jnp.split(v, 2, axis=axis)
    return jnp.where(y == 0, v, jnp.concatenate([b, a], axis=axis))


def slot_plan(ids_all, experts):
    y = lax.axis_index("tensor")
    seq = ids_all.shape[1]
    mine = lax.axis_index("dp") * 2 + jnp.arange(2, dtype=jnp.int32)
    mask = jnp.any(ids_all[:, None, :, :] == mine[None, :, None, None], axis=3)
    before = (jnp.arange(seq)[:, None] < jnp.arange(seq)[None, :]).astype(BF)
    rank = jnp.einsum("gea,ab->geb", mask.astype(BF), before, preferred_element_type=F32)
    rank = jnp.where(mask, rank, -1.0)
    d = jnp.arange(16)
    where = sequence_at(d // 8, d // 2 % 4, d % 2)
    rank = jnp.take(rank, where, axis=0)
    rank_rel = flip(rank, 2, y)
    rank_t = jnp.swapaxes(rank_rel, 1, 2)
    column = jnp.arange(128)
    cols = (
        column[None, None, :] == (mine[:, None] + jnp.array([[0, experts]]))[:, :, None]
    ).astype(F32)
    halves = lambda v: (v[:8], v[8:])
    return halves(where.astype(jnp.int32)), halves(rank), halves(rank_rel), halves(rank_t), cols


def moe_small(plan, cot_all, ffn_in, gate_x, weights, down_weight, slots):

    def cot_rows(k, plan):
        return run_cots(plan[0][k], plan[1][k], cot_all, down_weight, slots)

    v1, v2, v5, v6 = [ffn_in[:, a:b] for a, b in zip(SPLIT[:-1], SPLIT[1:])]
    v5 = jnp.concatenate([v5, gate_x], axis=1)
    *parts, plan, both = gather_rel(v1, v2, v5, v6, plan, cot_rows)
    rank_rel, rank_t, cols = plan[2:]
    cots, d_act = zip(*both)
    far, near = [
        run_experts(rank_rel[k], rank_t[k], cols, d_act[k], parts[k], weights, slots)
        for k in (1, 0)
    ]
    p1, p2, p5, p6 = scatter_core(near[4:], far[4:])
    kept = lambda i: (near[i], far[i])
    total = lambda spec, a, b: jnp.einsum(spec, a[0], b[0], preferred_element_type=F32) + jnp.einsum(
        spec, a[1], b[1], preferred_element_type=F32
    )
    p5 = reduce_z(p5, 1)
    p6 = reduce_z(p6, -1)
    p1 = step_y(p1)
    p2 = step_x(p2)
    down_grad = total("egsf,egsd->efd", kept(1), cots)
    outs = []
    for k in (0, 1):
        outs.append(run_outs(rank_t[k], kept(1)[k], down_weight, slots))
    (p1, p2, p5, p6), (outs, down_grad) = tied((p1, p2, p5, p6), (outs, down_grad))
    p5 = step_y(p5)
    p6 = step_x(p6)
    p1 = step_x(p1)
    p2 = step_y(p2)
    up_grad = total("egsd,egsf->edf", kept(0), kept(3))
    (p1, p2, p5, p6), up_grad = tied((p1, p2, p5, p6), up_grad)
    d5 = step_x(p5)
    d6 = step_y(p6)
    d1 = reduce_z(p1, 1)
    d2 = reduce_z(p2, -1)
    p1, p2, p5, p6 = scatter_core(*outs)
    p2, (d5, d6) = tied(p2, (d5, d6))
    p2 = step_x(p2)
    d_sum = jnp.concatenate([d1, d2, d5[:, :256], d6, d5[:, 256:]], axis=1)
    d_sum, (p1, p5, p6) = tied(d_sum, (p1, p5, p6))
    d_sum = d_sum.astype(F32)

    def gate_later(aside):
        (rows, grads), aside = tied((kept(0), kept(2)), aside)
        return total("egsd,egsf->edf", rows, grads), aside

    return d_sum, (p1, p2, p5, p6), gate_later, up_grad, down_grad


def moe_large(
    ids_all, cotangent, ffn_in, gate_x, gate_weight, up_weight, down_weight, experts, slots
):
    dp, seq = ids_all.shape[:2]
    local = gate_weight.shape[0]
    dp_at = lax.axis_index("dp")
    mine = dp_at * local + jnp.arange(local, dtype=jnp.int32)
    mask = jnp.any(ids_all[:, :, None, :] == mine[None, None, :, None], axis=3).astype(BF)
    gate_all = gather_all(gate_x).reshape(dp, seq, -1)
    before = (jnp.arange(seq)[:, None] > jnp.arange(seq)[None, :]).astype(BF)
    rank = jnp.einsum("ab,gbe->gea", before, mask, preferred_element_type=F32)
    rank = jnp.where(jnp.swapaxes(mask, 1, 2) > 0, rank, -1.0)
    pick = (rank[:, :, None, :] == jnp.arange(slots, dtype=F32)[None, None, :, None]).astype(BF)

    cots = dispatch(pick, cotangent, dp, seq, None)
    rows = dispatch(pick, ffn_in, dp, seq, cots)
    gate_tok = lax.dynamic_slice_in_dim(gate_all, dp_at * local, local, 2).astype(
        F32
    ) + lax.dynamic_slice_in_dim(gate_all, experts + dp_at * local, local, 2).astype(F32)
    gate_slot = jnp.sum(pick.astype(F32) * jnp.swapaxes(gate_tok, 1, 2)[:, :, None, :], axis=3)

    g_proj = jnp.einsum("gesd,edf->gesf", rows, gate_weight, preferred_element_type=F32)
    u_proj = jnp.einsum("gesd,edf->gesf", rows, up_weight, preferred_element_type=F32)
    d_act = jnp.einsum("gesd,efd->gesf", cots, down_weight, preferred_element_type=F32)
    sig = 1.0 / (1.0 + jnp.exp(-g_proj))
    silu = g_proj * sig
    act = silu * u_proj
    scaled = (act * gate_slot[..., None]).astype(BF)
    d_gate_slot = jnp.sum(act * d_act, axis=3)
    d_act = d_act * gate_slot[..., None]
    d_g = (d_act * u_proj * sig * (1.0 + g_proj * (1.0 - sig))).astype(BF)
    d_u = (d_act * silu).astype(BF)
    d_rows = (
        jnp.einsum("gesf,edf->gesd", d_g, gate_weight, preferred_element_type=F32)
        + jnp.einsum("gesf,edf->gesd", d_u, up_weight, preferred_element_type=F32)
    ).astype(BF)
    dg_high, dg_low = split2(d_gate_slot)
    column = jnp.arange(lanes(2 * experts))
    high_col = (column[None, :] == mine[:, None])[None, :, None, :]
    low_col = (column[None, :] == experts + mine[:, None])[None, :, None, :]
    extra = jnp.where(high_col, dg_high[..., None], jnp.where(low_col, dg_low[..., None], 0.0))
    d_rows = jnp.concatenate([d_rows, extra.astype(BF)], axis=3)
    d_sum = combine(pick, d_rows, dp, seq, None)

    y_rows = jnp.einsum("gesf,efd->gesd", scaled, down_weight, preferred_element_type=F32)
    y_sum = combine(pick, y_rows.astype(BF), dp, seq, d_sum)
    down_grad = jnp.einsum("gesf,gesd->efd", scaled, cots, preferred_element_type=F32)
    gate_grad = jnp.einsum("gesd,gesf->edf", rows, d_g, preferred_element_type=F32)
    up_grad = jnp.einsum("gesd,gesf->edf", rows, d_u, preferred_element_type=F32)

    return d_sum, y_sum, gate_grad, up_grad, down_grad


def pad_to(v, width):
    return jnp.pad(v, ((0, 0), (0, width - v.shape[1])))


def lanes(count):
    return -(-count // 128) * 128


def on_device(
    tokens,
    attn_gain,
    q_weight,
    key_matrix,
    value_matrix,
    o_weight,
    query_norm_gain,
    k_gain,
    ffn_gain,
    router_weight,
    gate_weight,
    up_weight,
    down_weight,
    expert_ids,
    cotangent,
):
    dp = lax.axis_size("dp")
    tensor = lax.axis_size("tensor")
    own, width = tokens.shape
    seq = expert_ids.shape[0]
    begin = lax.axis_index("tensor") * own
    local = gate_weight.shape[0]
    experts = local * dp
    slots = 10 * seq * expert_ids.shape[1] // (8 * experts)
    slots = -(-slots // 16) * 16
    shard = q_weight.shape[0]
    gshard = query_norm_gain.shape[0]
    hq = q_weight.shape[1] // HEAD
    hk = key_matrix.shape[1] // HEAD
    qkv_width = (hq + 2 * hk) * HEAD
    top = expert_ids.shape[1]
    fast = (dp, tensor, local, seq, width) == (16, 2, 2, 384, 2048)

    arange_e = jnp.arange(experts, dtype=jnp.int32)
    own_ids = lax.dynamic_slice_in_dim(expert_ids, begin, own, 0)
    own_mask = jnp.any(own_ids[:, :, None] == arange_e[None, None, :], axis=1)

    gain_rows = jnp.stack(
        [
            attn_gain,
            ffn_gain,
            jnp.pad(query_norm_gain, (0, shard - gshard)),
            jnp.pad(k_gain, (0, shard - gshard)),
        ],
        axis=1,
    )
    ids_rows = expert_ids.reshape(shard, -1).astype(BF)
    small = jnp.concatenate([router_weight, gain_rows, ids_rows], axis=1)
    small = pad_to(small, lanes(small.shape[1]))
    small_end = qkv_width + small.shape[1]
    all_in = gather_dp(
        jnp.concatenate([q_weight, key_matrix, value_matrix, small, o_weight.T], axis=1)
    )
    layer_in = gather_y(tokens)
    if fast:
        weights = jnp.concatenate([gate_weight, up_weight], axis=2)
        layer_in, weights = tied(layer_in, weights)
    o_t = all_in[:, small_end:]
    if fast:
        cot_all = gather_dp(gather_y(cotangent)).reshape(dp, seq, width)

    w_qkv = all_in[:, :qkv_width]
    router = all_in[:, qkv_width : qkv_width + experts]
    gains = all_in[:, qkv_width + experts : qkv_width + experts + 4].astype(F32)
    ids_all = all_in[:, qkv_width + experts + 4 :][:, : seq * top // shard]
    ids_all = ids_all.astype(jnp.int32).reshape(dp, seq, top)
    attn_gain32 = gains[:, 0]
    ffn_gain32 = gains[:, 1]
    q_gain32 = gains[:, 2].reshape(dp, shard)[:, :gshard].reshape(-1)
    k_gain32 = gains[:, 3].reshape(dp, shard)[:, :gshard].reshape(-1)

    residual = layer_in.astype(F32)
    normed = rms(residual, attn_gain32).astype(BF)
    qkv = dot(normed, w_qkv, 1, 0)
    cos, sin = rope_tables(seq)
    head_gains = jnp.pad(jnp.stack([q_gain32, k_gain32]), ((0, 6), (0, 0)))
    context = run_attend(qkv, head_gains, cos, sin, hq, hk)
    attn_part = dot(context, o_t, 1, 1)
    if fast:
        attn_part, ids_all = tied(attn_part, ids_all)
        plan = slot_plan(ids_all, experts)
    hidden = tokens.astype(F32) + scatter_y(attn_part)

    ffn_in = rms(hidden, ffn_gain32).astype(BF)
    logits = dot(ffn_in, router, 1, 0)
    chosen = jnp.where(own_mask, jnp.exp(logits), 0.0)
    gates = chosen / jnp.sum(chosen, axis=1, keepdims=True)
    gate_high, gate_low = split2(gates)
    gate_x = pad_to(jnp.concatenate([gate_high, gate_low], axis=1), lanes(2 * experts))
    args = (gate_weight, up_weight, down_weight)
    if fast:
        d_sum, y_sum, gate_later, up_grad, down_grad = moe_small(
            plan, cot_all, ffn_in, gate_x, weights, down_weight, slots
        )
    else:
        d_sum, y_sum, gate_grad, up_grad, down_grad = moe_large(
            ids_all, cotangent, ffn_in, gate_x, *args, experts, slots
        )
    d_gates = d_sum[:, width : width + experts] + d_sum[:, width + experts : width + 2 * experts]
    d_logits = gates * (d_gates - jnp.sum(gates * d_gates, axis=1, keepdims=True))
    d_high, d_low = split2(d_logits)
    d_ffn = d_sum[:, :width] + dot(d_high, router, 1, 1) + dot(d_low, router, 1, 1)
    router_part = dot(ffn_in, d_high, 0, 0) + dot(ffn_in, d_low, 0, 0)
    d_hidden, ffn_gain_rows = rms_back(hidden, ffn_gain32, d_ffn)
    ffn_gain_part = jnp.sum(ffn_gain_rows, axis=0)
    d_hidden = d_hidden + cotangent.astype(F32)
    d_attn = d_hidden.astype(BF)
    if fast:
        gate_grad, d_attn = gate_later(d_attn)
    d_attn = gather_y(d_attn)
    if fast:
        d_attn, gate_grad = tied(d_attn, gate_grad)

    if fast:
        p1, p2, p5, p6 = y_sum
        d_attn, p1 = tied(d_attn, p1)
        p1 = step_y(p1)
    o_part = dot(d_attn, context, 0, 0).astype(BF)
    d_attn, o_part = tied(d_attn, o_part)
    o_sum = scatter_dp(o_part).astype(F32)
    if fast:
        two5, two6 = first_hop(p5, 1), first_hop(p6, -1)
    d_context = dot(d_attn, o_t, 1, 0).astype(BF)
    heads = []
    for head in range(hk):
        heads.append(run_attend_back(head, qkv, d_context, head_gains, cos, sin, hq, hk))
        if fast and head == 0:
            aside = (p1, p2, two5, two6, gate_grad)
            d_context, heads, aside = lax.optimization_barrier((d_context, heads, aside))
            p1, p2, two5, two6, gate_grad = aside
            p1 = step_x(p1)
            p2 = step_y(p2)
            p5 = reduce_z(p5, 1, two5)
            p6 = reduce_z(p6, -1, two6)
    d_qkv = jnp.concatenate([h[k] for k in range(3) for h in heads], axis=1)
    small_part = jnp.concatenate([router_part, ffn_gain_part[:, None]], axis=1)
    small_part = pad_to(small_part, lanes(experts + 3))
    column = jnp.arange(small_part.shape[1])[None, :]
    head_part = sum(h[3][0] for h in heads)[:, None] * (column == experts + 1).astype(F32)
    head_part += sum(h[3][1] for h in heads)[:, None] * (column == experts + 2).astype(F32)
    if fast:
        d_qkv, (p1, p2, p5, p6) = tied(d_qkv, (p1, p2, p5, p6))
        y_sum = (reduce_z(p1, 1), reduce_z(p2, -1), step_x(step_y(p5)), step_y(step_x(p6)))
        far = run_grad(plan[0][1], normed, d_qkv, small_part, head_part)
        near = run_grad(plan[0][0], normed, d_qkv, small_part, head_part)
        a, b = scatter_rows_core(near, far)
        qkv_sum = scatter_rows(a, b).astype(F32)
        qkv_sum, small_sum = qkv_sum[:, :qkv_width], qkv_sum[:, qkv_width:]
        y_sum = jnp.concatenate(y_sum, axis=1).astype(F32)
    else:
        qkv_sum = scatter_dp(dot(normed, d_qkv, 0, 0).astype(BF)).astype(F32)
        head_part = jnp.pad(
            head_part.reshape(dp, gshard, -1), ((0, 0), (0, shard - gshard), (0, 0))
        )
        small_sum = scatter_dp(small_part + head_part.reshape(small_part.shape))
    output = (hidden + y_sum).astype(BF)
    d_normed = dot(d_qkv, w_qkv, 1, 1)
    d_normed = scatter_y(d_normed)
    d_tokens, _ = rms_back(tokens.astype(F32), attn_gain32, d_normed)
    tokens_grad = d_tokens + d_hidden

    weights = jnp.concatenate([q_weight, key_matrix, value_matrix], axis=1).astype(F32)
    gain_part = jnp.sum(weights * qkv_sum, axis=1) / attn_gain.astype(F32)
    small_sum = jnp.concatenate([small_sum, gain_part[:, None]], axis=1)
    small_sum = small_sum + swap_y(small_sum)
    return (
        output,
        tokens_grad,
        small_sum[:, -1],
        qkv_sum[:, : hq * HEAD],
        qkv_sum[:, hq * HEAD : (hq + hk) * HEAD],
        qkv_sum[:, (hq + hk) * HEAD :],
        o_sum.T,
        small_sum[:gshard, experts + 1],
        small_sum[:gshard, experts + 2],
        small_sum[:, experts],
        small_sum[:, :experts],
        gate_grad,
        up_grad,
        down_grad,
    )


def solution(mesh):
    rows = P(("dp", "tensor"), None)
    both = P("dp", "tensor")
    return jax.shard_map(
        on_device,
        mesh=mesh,
        in_specs=(
            rows,
            P("dp"),
            both,
            both,
            both,
            P("tensor", "dp"),
            P("dp"),
            P("dp"),
            P("dp"),
            P("dp", None),
            P("dp", None, "tensor"),
            P("dp", None, "tensor"),
            P("dp", "tensor", None),
            P("dp", None),
            rows,
        ),
        out_specs=(
            rows,
            rows,
            P("dp"),
            both,
            both,
            both,
            P("tensor", "dp"),
            P("dp"),
            P("dp"),
            P("dp"),
            P("dp", None),
            P("dp", None, "tensor"),
            P("dp", None, "tensor"),
            P("dp", "tensor", None),
        ),
        check_vma=False,
    )
```
